32 devices in a mesh: dp: 8 (over z, y), expert: 4 (over x, core).
Axes of the slice: x: 2, y: 2, z: 4, core: 2. Of those that a mesh axis runs over, the one named last changes fastest.
Arguments:
- tokens: bfloat16 [8, 1024, 2048], P('dp', 'expert'), may hold values from -6 to 6
- cotangent: bfloat16 [8, 1024, 2048], P('dp', 'expert'), may hold values from -6 to 6
- attention_routes: int32 [8, 1024, 2], P('dp'), may hold values from 0 to 3, all different within a row; in each aligned block of 256 rows (0 to 255, 256 to 511, ..., all dimensions but the last counted through in order) at most 160 rows name the same one
- feedforward_routes: int32 [8, 1024, 2], P('dp'), may hold values from 0 to 3, all different within a row; in each aligned block of 256 rows (0 to 255, 256 to 511, ..., all dimensions but the last counted through in order) at most 160 rows name the same one
- prefix_length: int32 [8], P('dp'), may hold values from 102 to 512
- gain_attention: float32 [2048], replicated, may hold values from 0.25 to 1.75
- gain_feedforward: float32 [2048], replicated, may hold values from 0.25 to 1.75
- keyvalue_weight: bfloat16 [2048, 4096], P('dp'), may hold values from -0.125 to 0.125
- router_weight: bfloat16 [2048, 8], P('dp'), may hold values from -0.25 to 0.25
- query_weight: bfloat16 [4, 2048, 2048], P('expert', 'dp'), may hold values from -0.125 to 0.125
- output_weight: bfloat16 [4, 2048, 2048], P('expert', 'dp'), may hold values from -3 to 3
- gate_weight: bfloat16 [4, 5632, 2048], P('expert', 'dp'), may hold values from -0.125 to 0.125
- up_weight: bfloat16 [4, 5632, 2048], P('expert', 'dp'), may hold values from -0.125 to 0.125
- down_weight: bfloat16 [4, 5632, 2048], P('expert', 'dp'), may hold values from -0.15625 to 0.15625
Outputs:
- layer_output: bfloat16 [8, 1024, 2048], P('dp', 'expert')
- grad_tokens: float32 [8, 1024, 2048], P('dp', 'expert')
- grad_gain_attention: float32 [2048], P('dp')
- grad_gain_feedforward: float32 [2048], P('dp')
- grad_keyvalue: float32 [2048, 4096], P('dp')
- grad_router: float32 [2048, 8], P('dp')
- grad_query: float32 [4, 2048, 2048], P('expert', 'dp')
- grad_projection: float32 [4, 2048, 2048], P('expert', 'dp')
- grad_gate: float32 [4, 5632, 2048], P('expert', 'dp')
- grad_up: float32 [4, 5632, 2048], P('expert', 'dp')
- grad_down: float32 [4, 5632, 2048], P('expert', 'dp')
The draws below stay inside these ranges and needn't reach their ends.
Inputs may be any that keep to these rules, and one draw needn't show every extreme that they name: `attention_routes`: the two ids of a token differ. Among the 256 tokens of one device (aligned blocks of each sequence) no expert is named more than 160 times, a bound that some block reaches. `feedforward_routes`: the two ids of a token differ. Among the 256 tokens of one device (aligned blocks of each sequence) no expert is named more than 160 times, a bound that some block reaches.
All inputs are finite; a program needn't handle non-finite values.
Results may differ from the reference program's by a relative error of at most 0.025.
Values may be sent and summed in bfloat16 or wider, within the bound.
A program may use at most 448 MiB of HBM per device.

```python
import math
import jax
import jax.numpy as jnp
import numpy as np
from jax import lax

D = 2048
HEAD_DIM = 128
FF = 5632
TOP = 2
SEQ_LEN = 1024
EXPERTS = 4
QW = 2048
TOK_DEV = 256
SEQUENCES = 8
CAP = 160


def touch_ends(values, key, smallest, high):
    index_at = [jax.random.randint(jax.random.fold_in(key, axis), (), 0, length) for axis, length in enumerate(values.shape)]
    widest = values.shape.index(max(values.shape))
    next_to = index_at[:widest] + [(index_at[widest] + 1) % values.shape[widest]] + index_at[widest + 1:]
    return values.at[tuple(index_at)].set(smallest).at[tuple(next_to)].set(high)


def block_levels(rng, dims, shards, least, high):
    factor_of, own = 1.0, jax.random.fold_in(rng, 6)
    for dim, blocks in shards:
        draws = jnp.exp(jax.random.uniform(jax.random.fold_in(own, dim), (blocks,), jnp.float32, least / len(shards), high / len(shards)))
        factor_of = factor_of * jnp.repeat(draws, dims[dim] // blocks).reshape([-1 if axis == dim else 1 for axis in range(len(dims))])
    return factor_of


def shared_out(key, own, number, rows, amount, top, limit, lean):
    order = jax.random.permutation(key, amount)
    packed, usual = load_shares(amount, rows * top, limit, lean, True), load_shares(amount, rows * top, limit, lean, False)
    places = jnp.arange(amount)

    def named(lengths, rotation):
        used = int((lengths > 0).sum())
        fixed = max(1, used // 4)
        passed = fixed + (places - fixed + rotation * (used - fixed)) % max(1, amount - fixed)
        return jnp.zeros((amount,), jnp.int32).at[order[jnp.where(places < fixed, places, passed)]].set(jnp.asarray(lengths, jnp.int32))

    lengths = jnp.where(number % 4 == 0, named(packed, number // 4), named(usual, number - number // 4 - 1))
    mixed = jax.random.permutation(jax.random.fold_in(own, 3), amount)
    donor, receiver = mixed[0:amount // 2 * 2:2], mixed[1:amount // 2 * 2:2]
    margin = jnp.minimum(lengths[donor] - 1, limit - lengths[receiver]) // 2
    margin = jnp.where((donor == order[0]) | (receiver == order[0]) | (lengths[receiver] == 0), 0, jnp.maximum(margin, 0))
    passed = jax.random.randint(jax.random.fold_in(own, 4), (amount // 2,), 0, 1 << 20) % (margin + 1)
    lengths = lengths.at[donor].add(-passed).at[receiver].add(passed)
    items = jnp.searchsorted(jnp.cumsum(lengths), jnp.arange(rows * top), side="right").astype(jnp.int32)
    grid = items.reshape(top, rows).T
    grid = grid[jax.random.permutation(jax.random.fold_in(own, 1), rows)]
    rotation = jax.random.randint(jax.random.fold_in(own, 2), (rows, 1), 0, top)
    return jnp.take_along_axis(grid, (jnp.arange(top)[None, :] + rotation) % top, axis=1)


def load_shares(amount, total, bound, skew, full):
    portions = [(1 << 20) // math.isqrt(standing ** skew) + 1 for standing in range(1, amount + 1)]
    largest = bound if full else min(bound, max(-(-total // amount), total * portions[0] // sum(portions)))
    least = 1 if total - largest >= amount - 1 else 0
    holding, spare = [largest] + [least] * (amount - 1), total - largest - least * (amount - 1)
    while spare > 0:
        movable = [i for i in range(1, amount) if holding[i] < largest] or [i for i in range(1, amount) if holding[i] < bound]
        whole, remaining = sum([portions[i] for i in movable]), spare
        for i in movable:
            more = min(bound - holding[i], max(1, remaining * portions[i] // whole), spare)
            holding[i] = holding[i] + more
            spare = spare - more
    return np.array(holding)


def centred(stream_key, shape, spread, limit, cuts=(), held_as=jnp.bfloat16):
    level = block_levels(stream_key, shape, cuts, -0.22, 0.18) if cuts else 1.0
    drawn = jax.random.normal(stream_key, shape, jnp.float32) * spread * level
    return jnp.minimum(jnp.maximum(drawn, -limit), limit).astype(held_as)


def setup_inputs(seed: int = 0) -> dict:
    arg_keys = jax.random.split(jax.random.key(seed), 15)
    tokens = centred(arg_keys[0], (SEQUENCES, SEQ_LEN, D), 1.0, 6.0, ((0, 8), (1, 4)))
    cotangent = centred(arg_keys[1], (SEQUENCES, SEQ_LEN, D), 1.0, 6.0, ((0, 8), (1, 4)))
    attention_routes_keys = jax.random.split(jax.random.fold_in(arg_keys[2], 1), SEQUENCES * SEQ_LEN // TOK_DEV)
    attention_routes_turns = jax.random.permutation(jax.random.fold_in(arg_keys[2], 3), SEQUENCES * SEQ_LEN // TOK_DEV)
    attention_routes = jax.vmap(lambda own, number: shared_out(jax.random.fold_in(arg_keys[2], 2), own, number, TOK_DEV, EXPERTS, TOP, CAP, 1))(attention_routes_keys, attention_routes_turns).reshape((SEQUENCES, SEQ_LEN, TOP))
    feedforward_routes_keys = jax.random.split(jax.random.fold_in(arg_keys[3], 1), SEQUENCES * SEQ_LEN // TOK_DEV)
    feedforward_routes_turns = jax.random.permutation(jax.random.fold_in(arg_keys[3], 3), SEQUENCES * SEQ_LEN // TOK_DEV)
    feedforward_routes = jax.vmap(lambda own, number: shared_out(jax.random.fold_in(arg_keys[3], 2), own, number, TOK_DEV, EXPERTS, TOP, CAP, 2))(feedforward_routes_keys, feedforward_routes_turns).reshape((SEQUENCES, SEQ_LEN, TOP))
    prefix_length = touch_ends(jax.random.randint(arg_keys[4], (SEQUENCES,), SEQ_LEN // 10, SEQ_LEN // 2 + 1), jax.random.fold_in(arg_keys[4], 1), SEQ_LEN // 10, (SEQ_LEN // 2 + 1) - 1).astype(jnp.int32)
    gain_attention = jnp.clip(1.0 + 0.15 * jax.random.normal(arg_keys[5], (D,), jnp.float32), 0.25, 1.75)
    gain_feedforward = jnp.clip(1.0 + 0.15 * jax.random.normal(arg_keys[6], (D,), jnp.float32), 0.25, 1.75)
    keyvalue_weight = centred(arg_keys[7], (D, 2 * QW), D ** -0.5, 0.125, ((0, 8),))
    router_weight = centred(arg_keys[8], (D, 2 * EXPERTS), (D // 4) ** -0.5, 0.25, ((0, 8),))
    query_weight = centred(arg_keys[9], (EXPERTS, D, QW), D ** -0.5, 0.125, ((0, 4), (1, 8)))
    output_weight = centred(arg_keys[10], (EXPERTS, QW, D), (max(2 * QW // SEQ_LEN, 1)) ** -0.5, 3.0, ((0, 4), (1, 8)))
    gate_weight = centred(arg_keys[11], (EXPERTS, FF, D), D ** -0.5, 0.125, ((0, 4), (1, 8)))
    up_weight = centred(arg_keys[12], (EXPERTS, FF, D), D ** -0.5, 0.125, ((0, 4), (1, 8)))
    down_weight = centred(arg_keys[13], (EXPERTS, FF, D), (FF // 4) ** -0.5, 0.15625, ((0, 4), (1, 8)))
    return {"tokens": tokens, "cotangent": cotangent, "attention_routes": attention_routes, "feedforward_routes": feedforward_routes, "prefix_length": prefix_length, "gain_attention": gain_attention, "gain_feedforward": gain_feedforward, "keyvalue_weight": keyvalue_weight, "router_weight": router_weight, "query_weight": query_weight, "output_weight": output_weight, "gate_weight": gate_weight, "up_weight": up_weight, "down_weight": down_weight}


EPS = 1e-06
NEG = -1e+30
HIGH = lax.Precision.HIGHEST

@jax.custom_vjp
def low(v):
    return lax.optimization_barrier(v.astype(jnp.bfloat16)).astype(jnp.float32)

@jax.custom_vjp
def low_back(v):
    return v

def low_keep(v):
    return (low(v), None)

def low_pass(kept, grad):
    return (grad,)

def back_keep(v):
    return (v, None)

def back_low(kept, grad):
    return (low(grad),)
low.defvjp(low_keep, low_pass)
low_back.defvjp(back_keep, back_low)

def matmul(left_rows, right_rows):
    return jnp.dot(left_rows, right_rows, precision=HIGH)

def matmul_across(left_rows, right_rows):
    return lax.dot_general(left_rows, right_rows, (((1,), (1,)), ((), ())), precision=HIGH)

def rms_scale(vector, gain_vector):
    return vector * lax.rsqrt(lax.optimization_barrier(jnp.mean(vector * vector, axis=-1, keepdims=True)) + EPS) * gain_vector

def pair_softmax(logits, chosen_ids):
    selected = jnp.take_along_axis(logits, chosen_ids, axis=1)
    largest = lax.optimization_barrier(jnp.max(selected, axis=1, keepdims=True))
    exponent = jnp.exp(selected - largest)
    weights = exponent / lax.optimization_barrier(jnp.sum(exponent, axis=1, keepdims=True))
    matches = (chosen_ids[:, :, None] == jnp.arange(logits.shape[1], dtype=jnp.int32)[None, None, :]).astype(jnp.float32)
    return lax.optimization_barrier(jnp.sum(weights[:, :, None] * matches, axis=1))

def one_sequence(inputs, gain_attention, gain_feedforward, keyvalue_weight, router_weight, query_weight, output_weight, gate_weight, up_weight, down_weight, attention_ids, feed_ids, prefix):
    length = inputs.shape[0]
    query_width = query_weight.shape[2]
    head_count = query_width // HEAD_DIM
    experts = query_weight.shape[0]
    scaling = HEAD_DIM ** (-0.5)
    attention_in = low(rms_scale(inputs, gain_attention))
    keyvalue = low(low_back(matmul(attention_in, keyvalue_weight)))
    key_rows = keyvalue[:, :query_width].reshape(length, head_count, HEAD_DIM)
    value_rows = keyvalue[:, query_width:].reshape(length, head_count, HEAD_DIM)
    attention_gate = pair_softmax(matmul(attention_in, router_weight[:, :experts]), attention_ids)
    positions = jnp.arange(length, dtype=jnp.int32)
    allowed = (positions[None, :] <= positions[:, None]) | (positions[None, :] < prefix)
    expert_ids = jnp.arange(experts, dtype=jnp.int32)

    def attention_expert(running, expert):
        queries = low(low_back(matmul(attention_in, query_weight[expert]))).reshape(length, head_count, HEAD_DIM)
        scores = low_back(jnp.einsum('qhd,khd->hqk', queries, key_rows, precision=HIGH) * scaling)
        scores = jnp.where(allowed[None], scores, NEG)
        largest = lax.optimization_barrier(jnp.max(scores, axis=2, keepdims=True))
        exponent = jnp.exp(scores - largest)
        probs = low(exponent / lax.optimization_barrier(jnp.sum(exponent, axis=2, keepdims=True)))
        mixture = low(low_back(jnp.einsum('hqk,khd->qhd', probs, value_rows, precision=HIGH).reshape(length, query_width)))
        branch = low(low_back(matmul(mixture, output_weight[expert])))
        column = lax.optimization_barrier(jnp.sum(attention_gate * (expert_ids == expert).astype(jnp.float32)[None, :], axis=1, keepdims=True))
        return (running + column * branch, None)
    attended, _ = lax.scan(jax.checkpoint(attention_expert), jnp.zeros_like(inputs), expert_ids)
    hidden = inputs + attended
    feed_in = low(rms_scale(hidden, gain_feedforward))
    feed_gate = pair_softmax(matmul(feed_in, router_weight[:, experts:]), feed_ids)

    def feed_expert(running, expert):
        pre_gate = low_back(matmul_across(feed_in, gate_weight[expert]))
        pre_up = low_back(matmul_across(feed_in, up_weight[expert]))
        activation = low(pre_gate * jax.nn.sigmoid(pre_gate) * pre_up)
        branch = low(low_back(matmul(activation, down_weight[expert])))
        column = lax.optimization_barrier(jnp.sum(feed_gate * (expert_ids == expert).astype(jnp.float32)[None, :], axis=1, keepdims=True))
        return (running + column * branch, None)
    fed, _ = lax.scan(jax.checkpoint(feed_expert), jnp.zeros_like(inputs), expert_ids)
    return hidden + fed

def reference(tokens, cotangent, attention_routes, feedforward_routes, prefix_length, gain_attention, gain_feedforward, keyvalue_weight, router_weight, query_weight, output_weight, gate_weight, up_weight, down_weight):
    floats = tuple((array.astype(jnp.float32) for array in (tokens, gain_attention, gain_feedforward, keyvalue_weight, router_weight, query_weight, output_weight, gate_weight, up_weight, down_weight)))

    def forward(*params):
        rest = params[1:]

        def step(carry, element):
            seq_inputs, attention_ids, feed_ids, prefix = element
            return (carry, jax.checkpoint(one_sequence)(seq_inputs, *rest, attention_ids, feed_ids, prefix))
        _, result = lax.scan(step, jnp.zeros((), jnp.float32), (params[0], attention_routes, feedforward_routes, prefix_length))
        return result
    result, pullback = jax.vjp(forward, *floats)
    grads = pullback(cotangent.astype(jnp.float32))
    return (result.astype(jnp.bfloat16), grads[0], grads[1], grads[2], grads[3], grads[4], grads[5], grads[6], grads[7], grads[8], grads[9])
```

```python
import functools

import jax
import jax.numpy as jnp
from jax import lax
from jax.experimental import pallas as pl
from jax.experimental.pallas import tpu as pltpu
from jax.sharding import PartitionSpec as P

HEADS = 16
HEAD_DIM = 128


EPS = 1e-06
NEG = -1e30
HIGH = lax.Precision.HIGHEST
ACROSS = (((1,), (1,)), ((), ()))
DOWNWARD = (((0,), (0,)), ((), ()))


def norm_parts(vector, gain_vector):
    factor = lax.rsqrt(jnp.mean(vector * vector, axis=-1, keepdims=True) + EPS)
    normed = vector * factor
    return (normed * gain_vector, normed, factor)


def norm_back(incoming, gain_vector, normed, factor):
    dnormed = incoming * gain_vector
    return factor * (dnormed - normed * jnp.mean(dnormed * normed, axis=-1, keepdims=True))


def route_plan(sequence_ids, my_index, group_size, tok_rows, slot_count):
    expert_range = jnp.arange(group_size, dtype=jnp.int32)
    matches_all = (sequence_ids[:, :, None] == expert_range[None, None, :]).astype(jnp.int32)
    chosen = jnp.sum(matches_all, axis=1).reshape(group_size, tok_rows, group_size)
    ranking = jnp.cumsum(chosen, axis=1) - chosen
    slot_ids = jnp.arange(slot_count, dtype=jnp.int32)[None, :, None]
    block_pick = (expert_range == my_index).astype(jnp.int32)
    my_chosen = jnp.sum(chosen * block_pick[:, None, None], axis=0).T
    my_ranking = jnp.sum(ranking * block_pick[:, None, None], axis=0).T
    send_table = (
        my_chosen[:, None, :] * (my_ranking[:, None, :] == slot_ids).astype(jnp.int32)
    ).astype(jnp.float32)
    column_chosen = jnp.sum(chosen * block_pick[None, None, :], axis=2)
    column_ranking = jnp.sum(ranking * block_pick[None, None, :], axis=2)
    taken = column_chosen[:, None, :] * (column_ranking[:, None, :] == slot_ids).astype(jnp.int32)
    positions = (
        expert_range[:, None, None] * tok_rows
        + jnp.arange(tok_rows, dtype=jnp.int32)[None, None, :]
    )
    arrival_places = jnp.sum(taken * positions, axis=2).reshape(-1)
    my_ids = lax.dynamic_slice_in_dim(sequence_ids, my_index * tok_rows, tok_rows, 0)
    matches = (my_ids[:, :, None] == expert_range[None, None, :]).astype(jnp.float32)
    return (send_table, arrival_places, matches)


def pair_gates(logits, matches):
    selected = jnp.sum(matches * logits[:, None, :], axis=2)
    largest = jnp.max(selected, axis=1, keepdims=True)
    exponent = jnp.exp(selected - largest)
    weights = exponent / jnp.sum(exponent, axis=1, keepdims=True)
    return (weights, jnp.sum(weights[:, :, None] * matches, axis=1))


def gates_back(dgate, weights, matches):
    dweights = jnp.sum(dgate[:, None, :] * matches, axis=2)
    dselected = weights * (dweights - jnp.sum(weights * dweights, axis=1, keepdims=True))
    return jnp.sum(dselected[:, :, None] * matches, axis=1)


def merge_back(send_table, gate_table, returned):
    weighted = send_table * gate_table.T[:, None, :]
    return jnp.einsum("ect,ecd->td", weighted, returned.astype(jnp.float32), precision=HIGH)


def branch_cotangent(send_table, gate_table, returned, incoming):
    spread_grad = jnp.einsum("ect,td->ecd", send_table, incoming, precision=HIGH)
    slot_gate = jnp.sum(send_table * gate_table.T[:, None, :], axis=2)
    cotangent_rows = (spread_grad * slot_gate[:, :, None]).astype(jnp.bfloat16)
    slot_dgate = jnp.sum(spread_grad * returned.astype(jnp.float32), axis=2)
    dgate = jnp.einsum("ect,ec->te", send_table, slot_dgate, precision=HIGH)
    return (cotangent_rows, dgate)


def expert_matches(ids, group_size):
    expert_range = jnp.arange(group_size, dtype=jnp.int32)
    return (ids[:, :, None] == expert_range[None, None, :]).astype(jnp.float32)


def expert_table(ids, my_index, group_size, tok_rows, slot_count):
    blocks = ids.reshape(-1, tok_rows, 2)
    chosen = jnp.sum((blocks == my_index).astype(jnp.float32), axis=2)
    before = jnp.triu(jnp.ones((tok_rows, tok_rows), jnp.float32), 1)
    ranking = jnp.dot(chosen, before)
    slot_ids = jnp.arange(slot_count, dtype=jnp.float32)[None, :, None]
    taken = chosen[:, None, :] * (ranking[:, None, :] == slot_ids).astype(jnp.float32)
    other = jnp.sum(blocks, axis=2) - my_index
    slot_other = jnp.sum(taken * other[:, None, :].astype(jnp.float32), axis=2)
    return (taken.astype(jnp.bfloat16), slot_other.reshape(-1).astype(jnp.int32))


def own_gate(logits, other, my_index):
    expert_range = jnp.arange(logits.shape[1], dtype=jnp.int32)[None]
    mine = jnp.sum(jnp.where(expert_range == my_index, logits, 0.0), axis=1, keepdims=True)
    theirs = jnp.sum(jnp.where(expert_range == other[:, None], logits, 0.0), axis=1, keepdims=True)
    return jax.nn.sigmoid(mine - theirs)


def pick_rows(taken, rows):
    blocks, slots, tokens = taken.shape
    picked = jnp.einsum(
        "bct,btd->bcd",
        taken,
        rows.reshape(blocks, tokens, -1),
        preferred_element_type=jnp.float32,
    )
    return picked.astype(jnp.bfloat16).reshape(blocks * slots, -1)


def return_rows(taken, rows):
    blocks, slots, tokens = taken.shape
    placed = jnp.einsum(
        "bct,bcd->btd",
        taken,
        rows.reshape(blocks, slots, -1),
        preferred_element_type=jnp.float32,
    )
    return placed.astype(jnp.bfloat16).reshape(blocks * tokens, -1)


def gather_all(rows):
    return lax.all_gather(rows, ("dp", "expert"), axis=0, tiled=True)


def scatter_all(rows):
    return lax.psum_scatter(rows, ("dp", "expert"), scatter_dimension=0, tiled=True)


def dispatch(rows):
    return lax.all_to_all(rows, "expert", split_axis=0, concat_axis=0, tiled=True)


def collect(rows):
    return lax.all_to_all(rows, "expert", split_axis=0, concat_axis=0, tiled=True)


def spread_rows(rows):
    return lax.all_gather(rows, "dp", axis=0, tiled=True)


def sum_rows(terms):
    return lax.psum_scatter(
        terms.astype(jnp.bfloat16), "dp", scatter_dimension=0, tiled=True
    ).astype(jnp.float32)


def send_rows(send_table, rows):
    return jnp.einsum(
        "ect,td->ecd", send_table.astype(jnp.bfloat16), rows, preferred_element_type=jnp.float32
    ).astype(jnp.bfloat16)


def per_device(
    tokens,
    cotangent,
    attention_routes,
    feedforward_routes,
    prefix_length,
    gain_attention,
    gain_feedforward,
    keyvalue_weight,
    router_weight,
    query_weight,
    output_weight,
    gate_weight,
    up_weight,
    down_weight,
):
    my_index = lax.axis_index("expert")
    group_size = lax.axis_size("expert")
    inputs = tokens[0].astype(jnp.float32)
    tok_rows = inputs.shape[0]
    model_width = inputs.shape[1]
    seq_total = tok_rows * group_size
    slot_count = 5 * 2 * tok_rows // (4 * group_size)
    query_width = HEADS * HEAD_DIM
    scaling = HEAD_DIM ** (-0.5)
    keyvalue_full, router_full, query_full, output_full = (
        lax.all_gather(keyvalue_weight, "dp", axis=0, tiled=True),
        lax.all_gather(router_weight, "dp", axis=0, tiled=True),
        lax.all_gather(query_weight[0], "dp", axis=0, tiled=True),
        lax.all_gather(output_weight[0], "dp", axis=0, tiled=True),
    )
    every_route = lax.all_gather(feedforward_routes[0], "dp", axis=0, tiled=True)
    cot_everyone = gather_all(cotangent[0])
    attention_cols = router_full[:, :group_size]
    feedforward_cols = router_full[:, group_size:]
    normed_attention, unit_attention, factor_attention = norm_parts(inputs, gain_attention)
    attention_in = normed_attention.astype(jnp.bfloat16)
    keyvalue_rows = jnp.dot(attention_in, keyvalue_full, preferred_element_type=jnp.float32).astype(
        jnp.bfloat16
    )
    keyvalue_seq = lax.all_gather(keyvalue_rows, "expert", axis=0, tiled=True)
    key_rows = keyvalue_seq[:, :query_width].reshape(seq_total, HEADS, HEAD_DIM)
    value_rows = keyvalue_seq[:, query_width:].reshape(seq_total, HEADS, HEAD_DIM)
    attend_table, attend_places, attend_matches = route_plan(
        attention_routes[0], my_index, group_size, tok_rows, slot_count
    )
    attend_logits = jnp.dot(attention_in, attention_cols, preferred_element_type=jnp.float32)
    attend_weights, attend_gate = pair_gates(attend_logits, attend_matches)
    arrived = dispatch(send_rows(attend_table, attention_in)).reshape(-1, model_width)
    queries = jnp.dot(arrived, query_full, preferred_element_type=jnp.float32).astype(jnp.bfloat16)
    queries = queries.reshape(-1, HEADS, HEAD_DIM)
    key_places = jnp.arange(seq_total, dtype=jnp.int32)
    allowed = (key_places[None, :] <= attend_places[:, None]) | (
        key_places[None, :] < prefix_length[0]
    )
    scores = (
        jnp.einsum("rhd,khd->hrk", queries, key_rows, preferred_element_type=jnp.float32) * scaling
    )
    scores = jnp.where(allowed[None], scores, NEG)
    row_max = jnp.max(scores, axis=2, keepdims=True)
    exponent = jnp.exp(scores - row_max)
    row_total = jnp.sum(exponent, axis=2, keepdims=True)
    log_total = row_max + jnp.log(row_total)
    attention_low = (exponent / row_total).astype(jnp.bfloat16)
    mixture = jnp.einsum(
        "hrk,khd->rhd", attention_low, value_rows, preferred_element_type=jnp.float32
    )
    mixture = mixture.astype(jnp.bfloat16).reshape(-1, query_width)
    attend_branch = jnp.dot(mixture, output_full, preferred_element_type=jnp.float32).astype(
        jnp.bfloat16
    )
    attend_returned = collect(attend_branch.reshape(group_size, slot_count, model_width))
    hidden = inputs + merge_back(attend_table, attend_gate, attend_returned)
    normed_feed, unit_feed, factor_feed = norm_parts(hidden, gain_feedforward)
    feed_in = normed_feed.astype(jnp.bfloat16)
    feed_ids = lax.dynamic_slice_in_dim(
        feedforward_routes[0], my_index * tok_rows, tok_rows, 0
    )
    feed_matches = expert_matches(feed_ids, group_size)
    feed_logits = jnp.dot(feed_in, feedforward_cols, preferred_element_type=jnp.float32)
    feed_weights, feed_gate = pair_gates(feed_logits, feed_matches)
    everyone = gather_all(feed_in)
    feed_taken, feed_pairs = expert_table(every_route, my_index, group_size, tok_rows, slot_count)
    pick = functools.partial(pick_rows, feed_taken)
    feed_rows = pick(everyone)
    cot_rows = pick(cot_everyone)
    row_logits = jnp.dot(feed_rows, feedforward_cols, preferred_element_type=jnp.float32)
    row_gate = own_gate(row_logits, feed_pairs, my_index)
    pre_gate = lax.dot_general(feed_rows, gate_weight[0], ACROSS, preferred_element_type=jnp.float32)
    pre_up = lax.dot_general(feed_rows, up_weight[0], ACROSS, preferred_element_type=jnp.float32)
    sigmoid_gate = jax.nn.sigmoid(pre_gate)
    act = pre_gate * sigmoid_gate * pre_up
    act_low = act.astype(jnp.bfloat16)
    act_scaled = (act * row_gate).astype(jnp.bfloat16)
    act_grad = lax.dot_general(cot_rows, down_weight[0], ACROSS, preferred_element_type=jnp.float32)
    slot_dgate = jnp.sum(act_low.astype(jnp.float32) * act_grad, axis=1)
    act_grad = act_grad * row_gate
    dgate_low = (act_grad * pre_up * sigmoid_gate * (1.0 + pre_gate * (1.0 - sigmoid_gate))).astype(
        jnp.bfloat16
    )
    dup_low = (act_grad * pre_gate * sigmoid_gate).astype(jnp.bfloat16)
    feed_dx = (
        jnp.dot(dgate_low, gate_weight[0], preferred_element_type=jnp.float32)
        + jnp.dot(dup_low, up_weight[0], preferred_element_type=jnp.float32)
    ).astype(jnp.bfloat16)
    feed_branch = jnp.dot(act_scaled, down_weight[0], preferred_element_type=jnp.float32).astype(
        jnp.bfloat16
    )
    grad_gate = lax.dot_general(dgate_low, feed_rows, DOWNWARD, preferred_element_type=jnp.float32)
    grad_up = lax.dot_general(dup_low, feed_rows, DOWNWARD, preferred_element_type=jnp.float32)
    grad_down = lax.dot_general(act_scaled, cot_rows, DOWNWARD, preferred_element_type=jnp.float32)
    token_dgate = jnp.einsum(
        "bct,bc->bt",
        feed_taken.astype(jnp.float32),
        slot_dgate.reshape(-1, slot_count),
        precision=HIGH,
    ).reshape(-1, 1)
    own_column = (jnp.arange(group_size) == my_index).astype(jnp.float32)[None]
    feed_dgate = scatter_all(token_dgate * own_column)
    feed_home = scatter_all(return_rows(feed_taken, feed_dx)).astype(jnp.float32)
    feed_sum = scatter_all(return_rows(feed_taken, feed_branch)).astype(jnp.float32)
    layer_output = hidden + feed_sum
    gradient = cotangent[0].astype(jnp.float32)
    feed_dlogits = gates_back(feed_dgate, feed_weights, feed_matches)
    feed_dnorm = feed_home + jnp.dot(
        feed_dlogits, feedforward_cols.astype(jnp.float32).T, precision=HIGH
    )
    grad_gain_feed = jnp.sum(feed_dnorm * unit_feed, axis=0)
    hidden_grad = gradient + norm_back(feed_dnorm, gain_feedforward, unit_feed, factor_feed)
    attend_cot, attend_dgate = branch_cotangent(
        attend_table, attend_gate, attend_returned, hidden_grad
    )
    attend_dlogits = gates_back(attend_dgate, attend_weights, attend_matches)
    attend_cot_rows = dispatch(attend_cot).reshape(-1, model_width)
    dmixture = lax.dot_general(
        attend_cot_rows, output_full, ACROSS, preferred_element_type=jnp.float32
    )
    dmixture = dmixture.astype(jnp.bfloat16).reshape(-1, HEADS, HEAD_DIM)
    grad_projection = lax.dot_general(
        mixture, attend_cot_rows, DOWNWARD, preferred_element_type=jnp.float32
    )
    scores_again = (
        jnp.einsum("rhd,khd->hrk", queries, key_rows, preferred_element_type=jnp.float32) * scaling
    )
    attention = jnp.where(allowed[None], jnp.exp(scores_again - log_total), 0.0)
    attention_again = attention.astype(jnp.bfloat16)
    dattention = jnp.einsum(
        "rhd,khd->hrk", dmixture, value_rows, preferred_element_type=jnp.float32
    )
    row_dot = jnp.sum(attention * dattention, axis=2, keepdims=True)
    dscores = (attention * (dattention - row_dot)).astype(jnp.bfloat16)
    dqueries = (
        jnp.einsum("hrk,khd->rhd", dscores, key_rows, preferred_element_type=jnp.float32) * scaling
    )
    dqueries = dqueries.astype(jnp.bfloat16).reshape(-1, query_width)
    dkeys = (
        jnp.einsum("hrk,rhd->khd", dscores, queries, preferred_element_type=jnp.float32) * scaling
    )
    dvalues = jnp.einsum(
        "hrk,rhd->khd", attention_again, dmixture, preferred_element_type=jnp.float32
    )
    grad_query = lax.dot_general(arrived, dqueries, DOWNWARD, preferred_element_type=jnp.float32)
    attend_dx = lax.dot_general(dqueries, query_full, ACROSS, preferred_element_type=jnp.float32)
    keyvalue_terms = jnp.concatenate(
        [dkeys.reshape(seq_total, query_width), dvalues.reshape(seq_total, query_width)], axis=1
    ).reshape(group_size, tok_rows, 2 * query_width)
    attend_home, keyvalue_home = (
        lax.all_to_all(
            attend_dx.reshape(group_size, slot_count, model_width).astype(jnp.bfloat16),
            "expert",
            split_axis=0,
            concat_axis=0,
            tiled=True,
        ).astype(jnp.float32),
        lax.all_to_all(
            keyvalue_terms.astype(jnp.bfloat16), "expert", split_axis=0, concat_axis=0, tiled=True
        ).astype(keyvalue_terms.dtype),
    )
    dkeyvalue = jnp.sum(keyvalue_home, axis=0).astype(jnp.bfloat16)
    attend_dnorm = (
        jnp.einsum("ect,ecd->td", attend_table, attend_home, precision=HIGH)
        + lax.dot_general(dkeyvalue, keyvalue_full, ACROSS, preferred_element_type=jnp.float32)
        + jnp.dot(attend_dlogits, attention_cols.astype(jnp.float32).T, precision=HIGH)
    )
    grad_keyvalue = lax.dot_general(
        attention_in, dkeyvalue, DOWNWARD, preferred_element_type=jnp.float32
    )
    grad_router = jnp.concatenate(
        [
            jnp.dot(attention_in.astype(jnp.float32).T, attend_dlogits, precision=HIGH),
            jnp.dot(feed_in.astype(jnp.float32).T, feed_dlogits, precision=HIGH),
        ],
        axis=1,
    )
    grad_gain_attend = jnp.sum(attend_dnorm * unit_attention, axis=0)
    grad_tokens = hidden_grad + norm_back(
        attend_dnorm, gain_attention, unit_attention, factor_attention
    )
    reduced = (
        lax.psum_scatter(
            grad_keyvalue.astype(jnp.bfloat16), "dp", scatter_dimension=0, tiled=True
        ).astype(jnp.float32),
        lax.psum_scatter(
            grad_router.astype(jnp.bfloat16), "dp", scatter_dimension=0, tiled=True
        ).astype(jnp.float32),
        lax.psum_scatter(
            grad_query.astype(jnp.bfloat16), "dp", scatter_dimension=0, tiled=True
        ).astype(jnp.float32),
        lax.psum_scatter(
            grad_projection.astype(jnp.bfloat16), "dp", scatter_dimension=0, tiled=True
        ).astype(jnp.float32),
        lax.psum_scatter(
            grad_gain_attend.astype(jnp.bfloat16), "dp", scatter_dimension=0, tiled=True
        ).astype(jnp.float32),
        lax.psum_scatter(
            grad_gain_feed.astype(jnp.bfloat16), "dp", scatter_dimension=0, tiled=True
        ).astype(jnp.float32),
    )
    shared = (
        lax.psum(reduced[0].astype(jnp.bfloat16), "expert").astype(jnp.float32),
        lax.psum(reduced[1].astype(jnp.bfloat16), "expert").astype(jnp.float32),
        lax.psum(reduced[4].astype(jnp.bfloat16), "expert").astype(jnp.float32),
        lax.psum(reduced[5].astype(jnp.bfloat16), "expert").astype(jnp.float32),
    )
    return (
        layer_output.astype(jnp.bfloat16)[None],
        grad_tokens[None],
        shared[2],
        shared[3],
        shared[0],
        shared[1],
        reduced[2][None],
        reduced[3][None],
        grad_gate[None],
        grad_up[None],
        grad_down[None],
    )


MESH = pl.DeviceIdType.MESH
CHIPS_Z = 4
TURNS = ((3, 2, 1, 0), (3, 0, 2, 1), (0, 3, 1, 2), (0, 1, 2, 3))


class Place:
    def __init__(self):
        self.dp, self.expert = lax.axis_index("dp"), lax.axis_index("expert")
        self.at = {
            "z": self.dp // 2,
            "y": self.dp % 2,
            "x": self.expert // 2,
            "c": self.expert % 2,
        }

    def across(self, axis):
        back = 1 - 2 * self.at[axis]
        if axis == "c":
            return (self.dp, self.expert + back)
        if axis == "x":
            return (self.dp, self.expert + 2 * back)
        return (self.dp + back, self.expert)

    def along(self, step):
        return (self.dp + 2 * step, self.expert)

    def block(self, whose, z, flips):
        at = {a: self.at[a] + flips.get(a, 0) * (1 - 2 * self.at[a]) for a in "xyc"}
        dp, expert = z * 2 + at["y"], at["x"] * 2 + at["c"]
        return {"all": dp * 4 + expert, "dp": dp, "expert": expert}[whose]


def enter(place, axes):
    barrier, count = pltpu.get_barrier_semaphore(), 0
    for axis in axes:
        if axis != "z":
            pl.semaphore_signal(
                barrier, inc=1, device_id=place.across(axis), device_id_type=MESH
            )
            count += 1
    if "z" in axes:
        z = place.at["z"]
        for step, there in ((-1, z > 0), (1, z < CHIPS_Z - 1)):

            @pl.when(there)
            def _(step=step):
                pl.semaphore_signal(
                    barrier, inc=1, device_id=place.along(step), device_id_type=MESH
                )

            count = count + there.astype(jnp.int32)
    pl.semaphore_wait(barrier, count)


def on(condition, action):
    if condition is None:
        action()
    else:
        pl.when(condition)(action)


def both(a, b):
    return b if a is None else a if b is None else a & b


class Post:
    def __init__(self, sems, place):
        self.sems, self.place, self.sent = sems, place, []

    def send(self, source, target, arrival, device, condition=None):
        number = len(self.sent)

        def copy():
            return pltpu.make_async_remote_copy(
                src_ref=source,
                dst_ref=target,
                send_sem=self.sems.at[number],
                recv_sem=arrival,
                device_id=device,
                device_id_type=MESH,
            )

        self.sent.append((condition, copy))
        on(condition, lambda: copy().start())

    def arrived(self, target, arrival):
        pltpu.make_async_remote_copy(
            src_ref=target,
            dst_ref=target,
            send_sem=self.sems.at[0],
            recv_sem=arrival,
            device_id=self.place.across("c"),
            device_id_type=MESH,
        ).wait_recv()

    def close(self):
        for condition, copy in self.sent:
            on(condition, lambda copy=copy: copy().wait_send())


FLIPS = {"x": 4, "y": 2, "c": 1}


def gather_kernel(jobs, axes, *refs):
    count = len(jobs)
    sources, targets = refs[:count], refs[count : 2 * count]
    send_sems, arrive_sems, own_sems = refs[2 * count :]
    place = Place()
    enter(place, axes)
    post = Post(send_sems, place)
    z_here = place.at["z"]
    line = 0
    waves, owns = {}, []
    for j, (whose, rows, pieces) in enumerate(jobs):
        own = pltpu.make_async_copy(
            sources[j],
            targets[j].at[pl.ds(place.block(whose, z_here, {}) * rows, rows)],
            own_sems.at[j],
        )
        own.start()
        owns.append(own)
        for first, length, order in pieces:

            def part(z, flips, j=j, whose=whose, rows=rows, first=first, length=length):
                at = place.block(whose, z, flips) * rows + first
                return targets[j].at[pl.ds(at, length)]

            def mark(z, flips, line=line):
                return arrive_sems.at[line, z * 8 + sum(FLIPS[a] * v for a, v in flips.items())]

            def hand_on(source, z, flips, depth, side, wave, condition, order=order, part=part, mark=mark):
                for axis in order[max(depth, 0) :]:
                    if axis == "z" and (depth < 0 or order[depth] != "z"):
                        for step in (1, -1):
                            there = (z_here < CHIPS_Z - 1) if step > 0 else (z_here > 0)
                            post.send(source, part(z, flips), mark(z, flips), place.along(step), both(condition, there))
                    elif axis == "z":
                        there = (z_here < CHIPS_Z - 1) if side > 0 else (z_here > 0)
                        post.send(source, part(z, flips), mark(z, flips), place.along(side), both(condition, there))
                    elif depth < 0 or axis != order[depth]:
                        seen = dict(flips)
                        seen[axis] = 1
                        post.send(source, part(z, flips), mark(z, seen), place.across(axis), condition)

            def come(z, flips, depth, side, hops, wave, condition, order=order, part=part, mark=mark, hand_on=hand_on):
                def act():
                    on(condition, lambda: post.arrived(part(z, flips), mark(z, flips)))
                    hand_on(part(z, flips), z, flips, depth, side, wave, condition)

                waves.setdefault(wave, []).append(act)
                spread(z, flips, depth, side, hops, wave, condition, order, come)

            hand_on(sources[j].at[pl.ds(first, length)], z_here, {}, -1, 0, 0, None)
            spread(z_here, {}, -1, 0, 0, 0, None, order, come)
            line += 1
    for wave in sorted(waves):
        for act in waves[wave]:
            act()
    for own in owns:
        own.wait()
    post.close()


def spread(z, flips, depth, side, hops, wave, condition, order, come):
    z_here = lax.axis_index("dp") // 2
    for later in range(max(depth, 0), len(order)):
        axis = order[later]
        if axis == "z":
            if depth >= 0 and order[depth] == "z":
                if hops < CHIPS_Z - 1:
                    far = hops + 1
                    there = (z_here >= far) if side > 0 else (z_here + far < CHIPS_Z)
                    come(z_here - side * far, flips, later, side, far, wave + 1, there)
            else:
                for step in (1, -1):
                    there = (z_here >= 1) if step > 0 else (z_here + 1 < CHIPS_Z)
                    come(z_here - step, flips, later, step, 1, wave + 1, both(condition, there))
        elif later > depth:
            seen = dict(flips)
            seen[axis] = 1
            come(z, seen, later, 0, 0, wave + 1, condition)


def gather(jobs, collective_id, name):
    arrays = [rows for rows, _, _ in jobs]
    sizes = {"all": 32, "dp": 8, "expert": 4}
    plan = tuple((whose, rows.shape[0], pieces) for rows, whose, pieces in jobs)
    axes = "".join(a for a in "cxyz" if any(a in order for _, _, ps in plan for _, _, order in ps))
    lines = sum(len(ps) for _, _, ps in plan)
    any_spec = pl.BlockSpec(memory_space=pltpu.HBM)
    return pl.pallas_call(
        functools.partial(gather_kernel, plan, axes),
        out_shape=[
            jax.ShapeDtypeStruct((sizes[whose] * r.shape[0], r.shape[1]), r.dtype)
            for r, whose, _ in jobs
        ],
        in_specs=[any_spec] * len(jobs),
        out_specs=[any_spec] * len(jobs),
        scratch_shapes=[
            pltpu.SemaphoreType.DMA((110 * lines,)),
            pltpu.SemaphoreType.DMA((lines, 32)),
            pltpu.SemaphoreType.DMA((len(jobs),)),
        ],
        compiler_params=pltpu.CompilerParams(
            collective_id=collective_id, has_side_effects=True
        ),
        name=name,
    )(*arrays)


def scatter_kernel(whose, rows, pieces, source, result, acc, *refs):
    place = Place()
    orders = [order for _, _, order in pieces]
    flat = [order.replace("z", "") for order in orders]
    steps = len(flat[0])
    lined = "z" in orders[0]
    turns = CHIPS_Z if lined else 1
    bins = refs[:steps]
    line = refs[steps] if lined else None
    send_sems, load_sems, bin_sems, line_sems = refs[-4:]
    z_here = place.at["z"]
    if lined:
        turn = [
            sum((z_here == z).astype(jnp.int32) * seq[k] for z, seq in enumerate(TURNS))
            for k in range(CHIPS_Z)
        ]
    else:
        turn = [z_here]
    slot_z = lambda k: turn[k] if lined else 0
    post = Post(send_sems, place)

    def flips_of(p, stage, code):
        later = flat[p][stage + 1 :]
        flips = {a: (code >> i) & 1 for i, a in enumerate(later)}
        if stage < steps:
            flips[flat[p][stage]] = 1
        return flips

    def kept(p, flips):
        names = sorted(flat[p][1:])
        return sum(flips.get(a, 0) << i for i, a in enumerate(names))

    def code_after(p, stage, flips):
        return sum(flips.get(a, 0) << i for i, a in enumerate(flat[p][stage + 1 :]))

    keep = 2 ** (steps - 1)
    names = sorted(flat[0][1:])
    loads = {}
    for k in range(turns):
        for n in reversed(range(keep)):
            flips = {a: (n >> i) & 1 for i, a in enumerate(names)}
            at = slot_z(k) * keep + n
            loads[k, n] = pltpu.make_async_copy(
                source.at[pl.ds(place.block(whose, turn[k], flips) * rows, rows)],
                acc.at[at],
                load_sems.at[at],
            )
            loads[k, n].start()
    enter(place, "".join(flat[0]) + ("z" if lined else ""))
    loaded = set()

    def add(target, terms, length):
        @pl.loop(0, length // 16)
        def _(r):
            at = pl.ds(pl.multiple_of(r * 16, 16), 16)
            total = target[at, :].astype(jnp.float32)
            for term in terms:
                total = total + term[at, :].astype(jnp.float32)
            target[at, :] = total.astype(jnp.bfloat16)

    def mine(p, ref):
        first, length, _ = pieces[p]
        return ref.at[pl.ds(first, length)]

    def gathered(p, k, stage, flips):
        n = kept(p, flips)
        at = slot_z(k) * keep + n
        if (k, n) not in loaded:
            loads[k, n].wait()
            loaded.add((k, n))
        terms = []
        for before in range(stage):
            code = code_after(p, before, flips)
            width = 2 ** (steps - 1 - before)
            ref = mine(p, bins[before].at[slot_z(k) * width + code])
            post.arrived(ref, bin_sems.at[p, before, slot_z(k) * width + code])
            terms.append(ref)
        block = mine(p, acc.at[at])
        add(block, terms, pieces[p][1])
        return block

    def leave(p, k, stage, code, block, flips):
        axis = flat[p][stage]
        width = 2 ** (steps - 1 - stage)
        at = slot_z(k) * width + code
        post.send(block, mine(p, bins[stage].at[at]), bin_sems.at[p, stage, at], place.across(axis))

    def work(k, stage):
        if stage < steps:
            for code in reversed(range(2 ** (steps - 1 - stage))):
                for p in range(len(pieces)):
                    flips = flips_of(p, stage, code)
                    if stage == 0:
                        first, length, _ = pieces[p]
                        at = place.block(whose, turn[k], flips) * rows + first
                        leave(p, k, stage, code, source.at[pl.ds(at, length)], flips)
                    else:
                        leave(p, k, stage, code, gathered(p, k, stage, flips), flips)
            return
        for p in range(len(pieces)):
            block = gathered(p, k, steps, {})
            if not lined or k == turns - 1:
                continue
            t = turn[k]
            right = t > z_here

            def pass_on(p=p, t=t, block=block):
                ref = mine(p, line.at[t])
                post.arrived(ref, line_sems.at[p, t])
                add(block, [ref], pieces[p][1])

            pl.when((right & (z_here > 0)) | (~right & (z_here < CHIPS_Z - 1)))(pass_on)
            slot = jnp.where(t == z_here - 1, CHIPS_Z, t)
            post.send(
                block,
                mine(p, line.at[slot]),
                line_sems.at[p, slot],
                place.along(jnp.where(right, 1, -1)),
            )

    for k in range(turns):
        work(k, 0)
    for time in range(turns + steps):
        for stage in range(1, steps + 1):
            k = time - stage + 1
            if 0 <= k < turns:
                work(k, stage)
    for p in range(len(pieces)):
        first, length, _ = pieces[p]
        block = mine(p, acc.at[z_here * keep if lined else 0])
        if lined:
            for slot, there in ((z_here, z_here > 0), (CHIPS_Z, z_here < CHIPS_Z - 1)):

                def last(p=p, slot=slot, block=block):
                    ref = mine(p, line.at[slot])
                    post.arrived(ref, line_sems.at[p, slot])
                    add(block, [ref], pieces[p][1])

                pl.when(there)(last)

        @pl.loop(0, length // 16)
        def _(r, first=first, block=block):
            at = pl.ds(pl.multiple_of(r * 16, 16), 16)
            result[pl.ds(pl.multiple_of(first + r * 16, 16), 16), :] = block[at, :].astype(
                result.dtype
            )

    post.close()


def scatter(array, whose, pieces, collective_id, name, dtype=jnp.float32):
    size = {"all": 32, "dp": 8, "expert": 4}[whose]
    rows, width = array.shape[0] // size, array.shape[1]
    flat = pieces[0][2].replace("z", "")
    steps, lined = len(flat), "z" in pieces[0][2]
    turns = CHIPS_Z if lined else 1
    room = lambda blocks: pltpu.VMEM((blocks, rows, width), jnp.bfloat16)
    scratch = [room(turns * 2 ** (steps - 1))]
    scratch += [room(turns * 2 ** (steps - 1 - stage)) for stage in range(steps)]
    if lined:
        scratch.append(room(CHIPS_Z + 1))
    count = len(pieces)
    scratch += [
        pltpu.SemaphoreType.DMA((count * (turns * 2**steps + 4),)),
        pltpu.SemaphoreType.DMA((turns * 2 ** (steps - 1),)),
        pltpu.SemaphoreType.DMA((count, steps, turns * 2 ** (steps - 1))),
        pltpu.SemaphoreType.DMA((count, CHIPS_Z + 1)),
    ]
    return pl.pallas_call(
        functools.partial(scatter_kernel, whose, rows, pieces),
        out_shape=jax.ShapeDtypeStruct((rows, width), dtype),
        in_specs=[pl.BlockSpec(memory_space=pltpu.HBM)],
        out_specs=pl.BlockSpec(memory_space=pltpu.VMEM),
        scratch_shapes=scratch,
        compiler_params=pltpu.CompilerParams(
            collective_id=collective_id, has_side_effects=True, vmem_limit_bytes=62 * 2**20
        ),
        name=name,
    )(array)


def attention_bias(bias, block, rows, width, prefix):
    query = block * rows + lax.broadcasted_iota(jnp.int32, (rows, width), 0)
    key = lax.broadcasted_iota(jnp.int32, (rows, width), 1)
    bias[:, :width] = jnp.where((key <= query) | (key < prefix), 0.0, NEG)


def pick_expert(ref, lane, experts, span, chosen):
    total = None
    for e in range(experts):
        cols = ref[:, pl.ds(pl.multiple_of(e * span + lane, HEAD_DIM), HEAD_DIM)]
        term = jnp.where(chosen == e, cols.astype(jnp.float32), 0.0)
        total = term if total is None else total + term
    return total.astype(jnp.bfloat16)


def key_limits(blocks, rows):
    return [max((i + 1) * rows, blocks * rows // 2) for i in range(blocks)]


def for_each_limit(blocks, rows, body):
    block = pl.program_id(0)
    limits = key_limits(blocks, rows)
    for width in sorted(set(limits)):
        members = [i for i, limit in enumerate(limits) if limit == width]
        pl.when((block >= members[0]) & (block <= members[-1]))(lambda width=width: body(width))


def attention_kernel(experts, prefix, q, k, v, side, mixed, log_total, bias):
    rows, span = q.shape[0], k.shape[1]
    heads = span // HEAD_DIM
    block = pl.program_id(0)
    chosen = [side[:, 0:1], side[:, 1:2]]
    gates = [side[:, 2:3], side[:, 3:4]]

    def body(width):
        attention_bias(bias, block, rows, width, prefix[0])

        @pl.loop(0, heads)
        def _(head):
            lane = head * HEAD_DIM
            lanes = pl.ds(pl.multiple_of(lane, HEAD_DIM), HEAD_DIM)
            weighted = []
            for j in range(2):
                query = pick_expert(q, lane, experts, span, chosen[j])
                scores = lax.dot_general(
                    query, k[:width, lanes], ACROSS, preferred_element_type=jnp.float32
                )
                scores = scores * (HEAD_DIM**-0.5) + bias[:, :width]
                largest = jnp.max(scores, axis=1, keepdims=True)
                exponent = jnp.exp(scores - largest)
                total = jnp.sum(exponent, axis=1, keepdims=True)
                low = (exponent * (1.0 / total)).astype(jnp.bfloat16)
                out = jnp.dot(low, v[:width, lanes], preferred_element_type=jnp.float32)
                weighted.append(out * gates[j])
                at = pl.ds(pl.multiple_of((2 * head + j) * HEAD_DIM, HEAD_DIM), HEAD_DIM)
                log_total[:, at] = jnp.broadcast_to(
                    largest + jnp.log(total), (rows, HEAD_DIM)
                )
            for e in range(experts):
                cols = jnp.where(chosen[0] == e, weighted[0], 0.0) + jnp.where(
                    chosen[1] == e, weighted[1], 0.0
                )
                at = pl.ds(pl.multiple_of(e * span + lane, HEAD_DIM), HEAD_DIM)
                mixed[:, at] = cols.astype(jnp.bfloat16)

    for_each_limit(k.shape[0] // rows, rows, body)


def attention(projected, side, prefix, experts, rows):
    length = projected.shape[0]
    span = projected.shape[1] // (experts + 2)
    wide = experts * span
    return pl.pallas_call(
        functools.partial(attention_kernel, experts),
        grid=(length // rows,),
        in_specs=[
            pl.BlockSpec(memory_space=pltpu.SMEM),
            pl.BlockSpec((rows, wide), lambda i: (i, 0)),
            pl.BlockSpec((length, span), lambda i: (0, experts)),
            pl.BlockSpec((length, span), lambda i: (0, experts + 1)),
            pl.BlockSpec((rows, 128), lambda i: (i, 0)),
        ],
        out_specs=[
            pl.BlockSpec((rows, wide), lambda i: (i, 0)),
            pl.BlockSpec((rows, 2 * span), lambda i: (i, 0)),
        ],
        out_shape=[
            jax.ShapeDtypeStruct((length, wide), jnp.bfloat16),
            jax.ShapeDtypeStruct((length, 2 * span), jnp.float32),
        ],
        scratch_shapes=[pltpu.VMEM((rows, length), jnp.float32)],
        compiler_params=pltpu.CompilerParams(vmem_limit_bytes=48 * 2**20),
        name="attention",
    )(prefix, projected, projected, projected, side)


def attention_back_kernel(
    experts, prefix, q, k, v, side, log_total, dmix, dprojected, dgate, bias, dk, dv
):
    rows, span = q.shape[0], k.shape[1]
    length = k.shape[0]
    heads = span // HEAD_DIM
    block = pl.program_id(0)
    scaling = HEAD_DIM**-0.5
    chosen = [side[:, 0:1], side[:, 1:2]]
    gates = [side[:, 2:3], side[:, 3:4]]
    row_at = pl.ds(pl.multiple_of(block * rows, rows), rows)
    column = lax.broadcasted_iota(jnp.int32, (rows, 128), 1)

    @pl.when(block == 0)
    def _():
        dk[...] = jnp.zeros_like(dk)
        dv[...] = jnp.zeros_like(dv)

    dgate[...] = jnp.zeros_like(dgate)

    def body(width):
        attention_bias(bias, block, rows, width, prefix[0])

        @pl.loop(0, heads)
        def _(head):
            lane = head * HEAD_DIM
            lanes = pl.ds(pl.multiple_of(lane, HEAD_DIM), HEAD_DIM)
            keys, values = k[:width, lanes], v[:width, lanes]
            dqueries = []
            for j in range(2):
                query = pick_expert(q, lane, experts, span, chosen[j])
                dm = pick_expert(dmix, lane, experts, span, chosen[j])
                at = pl.ds(pl.multiple_of((2 * head + j) * HEAD_DIM, HEAD_DIM), HEAD_DIM)
                logs = jnp.tile(log_total[:, at], (1, width // HEAD_DIM))
                scores = lax.dot_general(query, keys, ACROSS, preferred_element_type=jnp.float32)
                probs = jnp.exp(scores * scaling + bias[:, :width] - logs)
                dprobs = lax.dot_general(dm, values, ACROSS, preferred_element_type=jnp.float32)
                inner = jnp.sum(probs * dprobs, axis=1, keepdims=True)
                dgate[...] += jnp.where(column == j, inner, 0.0)
                probs = probs * gates[j]
                dscores = (probs * (dprobs - inner)).astype(jnp.bfloat16)
                low = probs.astype(jnp.bfloat16)
                dquery = jnp.dot(dscores, keys, preferred_element_type=jnp.float32) * scaling
                dqueries.append(dquery)
                dk[:width, lanes] += lax.dot_general(
                    dscores, query, DOWNWARD, preferred_element_type=jnp.float32
                )
                dv[:width, lanes] += lax.dot_general(
                    low, dm, DOWNWARD, preferred_element_type=jnp.float32
                )
            for e in range(experts):
                cols = jnp.where(chosen[0] == e, dqueries[0], 0.0) + jnp.where(
                    chosen[1] == e, dqueries[1], 0.0
                )
                at = pl.ds(pl.multiple_of(e * span + lane, HEAD_DIM), HEAD_DIM)
                dprojected[row_at, at] = cols.astype(jnp.bfloat16)

    for_each_limit(length // rows, rows, body)

    @pl.when(block == pl.num_programs(0) - 1)
    def _():
        dprojected[:, experts * span : (experts + 1) * span] = (dk[...] * scaling).astype(
            jnp.bfloat16
        )
        dprojected[:, (experts + 1) * span :] = dv[...].astype(jnp.bfloat16)


def attention_back(projected, side, prefix, log_total, dmix, experts, rows):
    length, total = projected.shape
    span = total // (experts + 2)
    wide = experts * span
    return pl.pallas_call(
        functools.partial(attention_back_kernel, experts),
        grid=(length // rows,),
        in_specs=[
            pl.BlockSpec(memory_space=pltpu.SMEM),
            pl.BlockSpec((rows, wide), lambda i: (i, 0)),
            pl.BlockSpec((length, span), lambda i: (0, experts)),
            pl.BlockSpec((length, span), lambda i: (0, experts + 1)),
            pl.BlockSpec((rows, 128), lambda i: (i, 0)),
            pl.BlockSpec((rows, 2 * span), lambda i: (i, 0)),
            pl.BlockSpec((rows, wide), lambda i: (i, 0)),
        ],
        out_specs=[
            pl.BlockSpec((length, total), lambda i: (0, 0)),
            pl.BlockSpec((rows, 128), lambda i: (i, 0)),
        ],
        out_shape=[
            jax.ShapeDtypeStruct((length, total), jnp.bfloat16),
            jax.ShapeDtypeStruct((length, 128), jnp.float32),
        ],
        scratch_shapes=[
            pltpu.VMEM((rows, length), jnp.float32),
            pltpu.VMEM((length, span), jnp.float32),
            pltpu.VMEM((length, span), jnp.float32),
        ],
        compiler_params=pltpu.CompilerParams(vmem_limit_bytes=56 * 2**20),
        name="attention_back",
    )(prefix, projected, projected, projected, side, log_total, dmix)


def per_device_torus(
    tokens,
    cotangent,
    attention_routes,
    feedforward_routes,
    prefix_length,
    gain_attention,
    gain_feedforward,
    keyvalue_weight,
    router_weight,
    query_weight,
    output_weight,
    gate_weight,
    up_weight,
    down_weight,
):
    my_index = lax.axis_index("expert")
    group_size = lax.axis_size("expert")
    dp_size = lax.axis_size("dp")
    inputs = tokens[0].astype(jnp.float32)
    tok_rows, model_width = inputs.shape
    slot_count = 5 * 2 * tok_rows // (4 * group_size)
    query_width = HEADS * HEAD_DIM
    span = query_width // group_size
    low = jnp.bfloat16
    f32 = jnp.float32

    half = dp_size // group_size
    swap = [
        ((z * half + y) * group_size + e, (e * half + y) * group_size + z)
        for z in range(group_size)
        for y in range(half)
        for e in range(group_size)
    ]
    cot_everyone = lax.all_gather(cotangent[0], ("dp", "expert"), axis=0, tiled=True)
    router_full = lax.all_gather(router_weight, "dp", axis=0, tiled=True)
    every_route = lax.all_gather(feedforward_routes[0], "dp", axis=0, tiled=True)
    query_cols = lax.all_to_all(query_weight[0], "expert", split_axis=1, concat_axis=1, tiled=True)
    key_cols = lax.dynamic_slice_in_dim(keyvalue_weight, my_index * span, span, 1)
    value_cols = lax.dynamic_slice_in_dim(keyvalue_weight, query_width + my_index * span, span, 1)
    in_shard = jnp.concatenate([query_cols, key_cols, value_cols], axis=1)
    out_shard = lax.ppermute(output_weight[0], ("dp", "expert"), swap)

    normed_attention, unit_attention, factor_attention = norm_parts(inputs, gain_attention)
    attention_in = normed_attention.astype(low)
    quarters = lambda order: tuple(
        (i * tok_rows // 4, tok_rows // 4, order) for i in range(4)
    )
    rows_in = in_shard.shape[0]
    sequence_in, in_weight, out_weight = gather(
        [
            (attention_in, "expert", quarters("xc")),
            (in_shard, "dp", ((0, rows_in, "zy"),)),
            (out_shard, "dp", ((0, rows_in, "zy"),)),
        ],
        1,
        "gather_weights",
    )
    attention_cols = router_full[:, :group_size]
    feedforward_cols = router_full[:, group_size:]
    projected = jnp.dot(sequence_in, in_weight, preferred_element_type=f32).astype(low)
    attend_matches_all = expert_matches(attention_routes[0], group_size)
    attend_logits = jnp.dot(sequence_in, attention_cols, preferred_element_type=f32)
    attend_weights_all, _ = pair_gates(attend_logits, attend_matches_all)
    side = jnp.concatenate([attention_routes[0].astype(f32), attend_weights_all], axis=1)
    side = jnp.pad(side, ((0, 0), (0, 128 - side.shape[1])))
    mixed, log_total = attention(projected, side, prefix_length, group_size, tok_rows)
    attend_part = jnp.dot(mixed, out_weight, preferred_element_type=f32).astype(low)
    attended = scatter(attend_part, "expert", quarters("cx"), 2, "sum_attention")
    hidden = inputs + attended
    normed_feed, unit_feed, factor_feed = norm_parts(hidden, gain_feedforward)
    feed_in = normed_feed.astype(low)
    everywhere = lambda a, b: ((0, tok_rows // 2, a), (tok_rows // 2, tok_rows // 2, b))
    (everyone,) = gather([(feed_in, "all", everywhere("zxyc", "zyxc"))], 3, "gather_rows")

    mine = lambda a: lax.dynamic_slice_in_dim(a, my_index * tok_rows, tok_rows, 0)
    feed_matches = expert_matches(mine(feedforward_routes[0]), group_size)
    feed_logits = jnp.dot(feed_in, feedforward_cols, preferred_element_type=f32)
    feed_weights, _ = pair_gates(feed_logits, feed_matches)
    feed_taken, feed_pairs = expert_table(every_route, my_index, group_size, tok_rows, slot_count)
    feed_rows = pick_rows(feed_taken, everyone)
    cot_rows = pick_rows(feed_taken, cot_everyone)
    row_logits = jnp.dot(feed_rows, feedforward_cols, preferred_element_type=f32)
    row_gate = own_gate(row_logits, feed_pairs, my_index)
    pre_gate = lax.dot_general(feed_rows, gate_weight[0], ACROSS, preferred_element_type=f32)
    pre_up = lax.dot_general(feed_rows, up_weight[0], ACROSS, preferred_element_type=f32)
    sigmoid_gate = jax.nn.sigmoid(pre_gate)
    act = pre_gate * sigmoid_gate * pre_up
    act_low = act.astype(low)
    act_scaled = (act * row_gate).astype(low)
    act_grad = lax.dot_general(cot_rows, down_weight[0], ACROSS, preferred_element_type=f32)
    slot_dgate = jnp.sum(act_low.astype(f32) * act_grad, axis=1)
    act_grad = act_grad * row_gate
    dgate_low = (act_grad * pre_up * sigmoid_gate * (1.0 + pre_gate * (1.0 - sigmoid_gate))).astype(
        low
    )
    dup_low = (act_grad * pre_gate * sigmoid_gate).astype(low)
    feed_dx = (
        jnp.dot(dgate_low, gate_weight[0], preferred_element_type=f32)
        + jnp.dot(dup_low, up_weight[0], preferred_element_type=f32)
    ).astype(low)
    feed_branch = jnp.dot(act_scaled, down_weight[0], preferred_element_type=f32).astype(low)
    grad_gate = lax.dot_general(dgate_low, feed_rows, DOWNWARD, preferred_element_type=f32)
    grad_up = lax.dot_general(dup_low, feed_rows, DOWNWARD, preferred_element_type=f32)
    grad_down = lax.dot_general(act_scaled, cot_rows, DOWNWARD, preferred_element_type=f32)
    token_dgate = jnp.einsum(
        "bct,bc->bt", feed_taken.astype(f32), slot_dgate.reshape(-1, slot_count), precision=HIGH
    )
    own_row = (jnp.arange(group_size) == my_index).astype(f32)[None, :, None]
    feed_dgate = lax.psum_scatter(
        (token_dgate[:, None, :] * own_row).reshape(-1, tok_rows),
        ("dp", "expert"),
        scatter_dimension=0,
        tiled=True,
    ).T
    feed_home = scatter(
        return_rows(feed_taken, feed_dx), "all", everywhere("cxyz", "cyxz"), 4, "sum_rows"
    )
    feed_sum = scatter(
        return_rows(feed_taken, feed_branch), "all", everywhere("cxyz", "cyxz"), 4, "sum_rows"
    )
    layer_output = hidden + feed_sum
    gradient = cotangent[0].astype(f32)
    feed_dlogits = gates_back(feed_dgate, feed_weights, feed_matches)
    feed_dnorm = feed_home + jnp.dot(feed_dlogits, feedforward_cols.astype(f32).T, precision=HIGH)
    grad_gain_feed = jnp.sum(feed_dnorm * unit_feed, axis=0)
    hidden_grad = gradient + norm_back(feed_dnorm, gain_feedforward, unit_feed, factor_feed)

    (sequence_grad,) = gather(
        [(hidden_grad.astype(low), "expert", quarters("xc"))], 5, "gather_cotangents"
    )
    dmix = lax.dot_general(sequence_grad, out_weight, ACROSS, preferred_element_type=f32).astype(low)
    grad_out = lax.dot_general(mixed, sequence_grad, DOWNWARD, preferred_element_type=f32)
    dprojected, gate_parts = attention_back(
        projected, side, prefix_length, log_total, dmix, group_size, tok_rows
    )
    attend_dx = lax.dot_general(dprojected, in_weight, ACROSS, preferred_element_type=f32)
    grad_in = lax.dot_general(sequence_in, dprojected, DOWNWARD, preferred_element_type=f32)
    attend_home = scatter(attend_dx.astype(low), "expert", quarters("cx"), 2, "sum_attention")
    pair_dgate = lax.psum_scatter(
        gate_parts[:, :2].reshape(group_size, tok_rows, 2).transpose(0, 2, 1).reshape(-1, tok_rows),
        "expert",
        scatter_dimension=0,
        tiled=True,
    ).T
    matches = mine(attend_matches_all)
    weights = mine(attend_weights_all)
    dselected = weights * (pair_dgate - jnp.sum(weights * pair_dgate, axis=1, keepdims=True))
    attend_dlogits = jnp.sum(dselected[:, :, None] * matches, axis=1)
    attend_dnorm = attend_home + jnp.dot(
        attend_dlogits, attention_cols.astype(f32).T, precision=HIGH
    )
    grad_gain_attend = jnp.sum(attend_dnorm * unit_attention, axis=0)
    grad_tokens = hidden_grad + norm_back(
        attend_dnorm, gain_attention, unit_attention, factor_attention
    )
    small = jnp.concatenate(
        [
            lax.dot_general(attend_dlogits, attention_in.astype(f32), DOWNWARD, precision=HIGH),
            lax.dot_general(feed_dlogits, feed_in.astype(f32), DOWNWARD, precision=HIGH),
            grad_gain_attend[None],
            grad_gain_feed[None],
        ],
        axis=0,
    )
    small = lax.psum(small.astype(f32), ("dp", "expert"))
    small = lax.dynamic_slice_in_dim(small, lax.axis_index("dp") * rows_in, rows_in, 1)

    down_dp = ((0, rows_in, "yz"),)
    out_rows = scatter(grad_out.astype(low), "dp", down_dp, 6, "sum_output_weight")
    in_rows = scatter(grad_in.astype(low), "dp", down_dp, 7, "sum_input_weight").astype(low)
    grad_projection = lax.ppermute(out_rows.astype(low), ("dp", "expert"), swap).astype(f32)
    wide = group_size * span
    grad_query = lax.all_to_all(
        in_rows[:, :wide], "expert", split_axis=1, concat_axis=1, tiled=True
    ).astype(f32)
    grad_keyvalue = lax.all_gather(in_rows[:, wide:], "expert", axis=0, tiled=False)
    grad_keyvalue = (
        grad_keyvalue.reshape(group_size, rows_in, 2, span)
        .transpose(1, 2, 0, 3)
        .reshape(rows_in, 2 * query_width)
        .astype(f32)
    )
    return (
        layer_output.astype(low)[None],
        grad_tokens[None],
        small[2 * group_size],
        small[2 * group_size + 1],
        grad_keyvalue,
        small[: 2 * group_size].T,
        grad_query[None],
        grad_projection[None],
        grad_gate[None],
        grad_up[None],
        grad_down[None],
    )


def solution(mesh):
    in_specs = (
        P("dp", "expert", None),
        P("dp", "expert", None),
        P("dp", None, None),
        P("dp", None, None),
        P("dp"),
        P(),
        P(),
        P("dp", None),
        P("dp", None),
        P("expert", "dp", None),
        P("expert", "dp", None),
        P("expert", "dp", None),
        P("expert", "dp", None),
        P("expert", "dp", None),
    )
    out_specs = (
        P("dp", "expert", None),
        P("dp", "expert", None),
        P("dp"),
        P("dp"),
        P("dp", None),
        P("dp", None),
        P("expert", "dp", None),
        P("expert", "dp", None),
        P("expert", "dp", None),
        P("expert", "dp", None),
        P("expert", "dp", None),
    )
    torus = (mesh.shape["dp"], mesh.shape["expert"]) == (8, 4)
    body = per_device_torus if torus else per_device
    return jax.shard_map(
        body, mesh=mesh, in_specs=in_specs, out_specs=out_specs, check_vma=False
    )
```

```python
import functools

import jax
import jax.numpy as jnp
from jax import lax
from jax.experimental import pallas as pl
from jax.experimental.pallas import tpu as pltpu
from jax.sharding import PartitionSpec as P

HEADS = 16
HEAD_DIM = 128


EPS = 1e-06
NEG = -1e30
HIGH = lax.Precision.HIGHEST
ACROSS = (((1,), (1,)), ((), ()))
DOWNWARD = (((0,), (0,)), ((), ()))


def norm_parts(vector, gain_vector):
    factor = lax.rsqrt(jnp.mean(vector * vector, axis=-1, keepdims=True) + EPS)
    normed = vector * factor
    return (normed * gain_vector, normed, factor)


def norm_back(incoming, gain_vector, normed, factor):
    dnormed = incoming * gain_vector
    return factor * (dnormed - normed * jnp.mean(dnormed * normed, axis=-1, keepdims=True))


def route_plan(sequence_ids, my_index, group_size, tok_rows, slot_count):
    expert_range = jnp.arange(group_size, dtype=jnp.int32)
    matches_all = (sequence_ids[:, :, None] == expert_range[None, None, :]).astype(jnp.int32)
    chosen = jnp.sum(matches_all, axis=1).reshape(group_size, tok_rows, group_size)
    ranking = jnp.cumsum(chosen, axis=1) - chosen
    slot_ids = jnp.arange(slot_count, dtype=jnp.int32)[None, :, None]
    block_pick = (expert_range == my_index).astype(jnp.int32)
    my_chosen = jnp.sum(chosen * block_pick[:, None, None], axis=0).T
    my_ranking = jnp.sum(ranking * block_pick[:, None, None], axis=0).T
    send_table = (
        my_chosen[:, None, :] * (my_ranking[:, None, :] == slot_ids).astype(jnp.int32)
    ).astype(jnp.float32)
    column_chosen = jnp.sum(chosen * block_pick[None, None, :], axis=2)
    column_ranking = jnp.sum(ranking * block_pick[None, None, :], axis=2)
    taken = column_chosen[:, None, :] * (column_ranking[:, None, :] == slot_ids).astype(jnp.int32)
    positions = (
        expert_range[:, None, None] * tok_rows
        + jnp.arange(tok_rows, dtype=jnp.int32)[None, None, :]
    )
    arrival_places = jnp.sum(taken * positions, axis=2).reshape(-1)
    my_ids = lax.dynamic_slice_in_dim(sequence_ids, my_index * tok_rows, tok_rows, 0)
    matches = (my_ids[:, :, None] == expert_range[None, None, :]).astype(jnp.float32)
    return (send_table, arrival_places, matches)


def pair_gates(logits, matches):
    selected = jnp.sum(matches * logits[:, None, :], axis=2)
    largest = jnp.max(selected, axis=1, keepdims=True)
    exponent = jnp.exp(selected - largest)
    weights = exponent / jnp.sum(exponent, axis=1, keepdims=True)
    return (weights, jnp.sum(weights[:, :, None] * matches, axis=1))


def gates_back(dgate, weights, matches):
    dweights = jnp.sum(dgate[:, None, :] * matches, axis=2)
    dselected = weights * (dweights - jnp.sum(weights * dweights, axis=1, keepdims=True))
    return jnp.sum(dselected[:, :, None] * matches, axis=1)


def merge_back(send_table, gate_table, returned):
    weighted = send_table * gate_table.T[:, None, :]
    return jnp.einsum("ect,ecd->td", weighted, returned.astype(jnp.float32), precision=HIGH)


def branch_cotangent(send_table, gate_table, returned, incoming):
    spread_grad = jnp.einsum("ect,td->ecd", send_table, incoming, precision=HIGH)
    slot_gate = jnp.sum(send_table * gate_table.T[:, None, :], axis=2)
    cotangent_rows = (spread_grad * slot_gate[:, :, None]).astype(jnp.bfloat16)
    slot_dgate = jnp.sum(spread_grad * returned.astype(jnp.float32), axis=2)
    dgate = jnp.einsum("ect,ec->te", send_table, slot_dgate, precision=HIGH)
    return (cotangent_rows, dgate)


def expert_matches(ids, group_size):
    expert_range = jnp.arange(group_size, dtype=jnp.int32)
    return (ids[:, :, None] == expert_range[None, None, :]).astype(jnp.float32)


def expert_table(ids, my_index, group_size, tok_rows, slot_count):
    blocks = ids.reshape(-1, tok_rows, 2)
    chosen = jnp.sum((blocks == my_index).astype(jnp.float32), axis=2)
    before = jnp.triu(jnp.ones((tok_rows, tok_rows), jnp.float32), 1)
    ranking = jnp.dot(chosen, before)
    slot_ids = jnp.arange(slot_count, dtype=jnp.float32)[None, :, None]
    taken = chosen[:, None, :] * (ranking[:, None, :] == slot_ids).astype(jnp.float32)
    other = jnp.sum(blocks, axis=2) - my_index
    slot_other = jnp.sum(taken * other[:, None, :].astype(jnp.float32), axis=2)
    return (taken.astype(jnp.bfloat16), slot_other.reshape(-1).astype(jnp.int32))


def own_gate(logits, other, my_index):
    expert_range = jnp.arange(logits.shape[1], dtype=jnp.int32)[None]
    mine = jnp.sum(jnp.where(expert_range == my_index, logits, 0.0), axis=1, keepdims=True)
    theirs = jnp.sum(jnp.where(expert_range == other[:, None], logits, 0.0), axis=1, keepdims=True)
    return jax.nn.sigmoid(mine - theirs)


def pick_rows(taken, rows):
    blocks, slots, tokens = taken.shape
    picked = jnp.einsum(
        "bct,btd->bcd",
        taken,
        rows.reshape(blocks, tokens, -1),
        preferred_element_type=jnp.float32,
    )
    return picked.astype(jnp.bfloat16).reshape(blocks * slots, -1)


def return_rows(taken, rows):
    blocks, slots, tokens = taken.shape
    placed = jnp.einsum(
        "bct,bcd->btd",
        taken,
        rows.reshape(blocks, slots, -1),
        preferred_element_type=jnp.float32,
    )
    return placed.astype(jnp.bfloat16).reshape(blocks * tokens, -1)


def gather_all(rows):
    return lax.all_gather(rows, ("dp", "expert"), axis=0, tiled=True)


def scatter_all(rows):
    return lax.psum_scatter(rows, ("dp", "expert"), scatter_dimension=0, tiled=True)


def dispatch(rows):
    return lax.all_to_all(rows, "expert", split_axis=0, concat_axis=0, tiled=True)


def collect(rows):
    return lax.all_to_all(rows, "expert", split_axis=0, concat_axis=0, tiled=True)


def spread_rows(rows):
    return lax.all_gather(rows, "dp", axis=0, tiled=True)


def sum_rows(terms):
    return lax.psum_scatter(
        terms.astype(jnp.bfloat16), "dp", scatter_dimension=0, tiled=True
    ).astype(jnp.float32)


def send_rows(send_table, rows):
    return jnp.einsum(
        "ect,td->ecd", send_table.astype(jnp.bfloat16), rows, preferred_element_type=jnp.float32
    ).astype(jnp.bfloat16)


def per_device(
    tokens,
    cotangent,
    attention_routes,
    feedforward_routes,
    prefix_length,
    gain_attention,
    gain_feedforward,
    keyvalue_weight,
    router_weight,
    query_weight,
    output_weight,
    gate_weight,
    up_weight,
    down_weight,
):
    my_index = lax.axis_index("expert")
    group_size = lax.axis_size("expert")
    inputs = tokens[0].astype(jnp.float32)
    tok_rows = inputs.shape[0]
    model_width = inputs.shape[1]
    seq_total = tok_rows * group_size
    slot_count = 5 * 2 * tok_rows // (4 * group_size)
    query_width = HEADS * HEAD_DIM
    scaling = HEAD_DIM ** (-0.5)
    keyvalue_full, router_full, query_full, output_full = (
        lax.all_gather(keyvalue_weight, "dp", axis=0, tiled=True),
        lax.all_gather(router_weight, "dp", axis=0, tiled=True),
        lax.all_gather(query_weight[0], "dp", axis=0, tiled=True),
        lax.all_gather(output_weight[0], "dp", axis=0, tiled=True),
    )
    every_route = lax.all_gather(feedforward_routes[0], "dp", axis=0, tiled=True)
    cot_everyone = gather_all(cotangent[0])
    attention_cols = router_full[:, :group_size]
    feedforward_cols = router_full[:, group_size:]
    normed_attention, unit_attention, factor_attention = norm_parts(inputs, gain_attention)
    attention_in = normed_attention.astype(jnp.bfloat16)
    keyvalue_rows = jnp.dot(attention_in, keyvalue_full, preferred_element_type=jnp.float32).astype(
        jnp.bfloat16
    )
    keyvalue_seq = lax.all_gather(keyvalue_rows, "expert", axis=0, tiled=True)
    key_rows = keyvalue_seq[:, :query_width].reshape(seq_total, HEADS, HEAD_DIM)
    value_rows = keyvalue_seq[:, query_width:].reshape(seq_total, HEADS, HEAD_DIM)
    attend_table, attend_places, attend_matches = route_plan(
        attention_routes[0], my_index, group_size, tok_rows, slot_count
    )
    attend_logits = jnp.dot(attention_in, attention_cols, preferred_element_type=jnp.float32)
    attend_weights, attend_gate = pair_gates(attend_logits, attend_matches)
    arrived = dispatch(send_rows(attend_table, attention_in)).reshape(-1, model_width)
    queries = jnp.dot(arrived, query_full, preferred_element_type=jnp.float32).astype(jnp.bfloat16)
    queries = queries.reshape(-1, HEADS, HEAD_DIM)
    key_places = jnp.arange(seq_total, dtype=jnp.int32)
    allowed = (key_places[None, :] <= attend_places[:, None]) | (
        key_places[None, :] < prefix_length[0]
    )
    scores = (
        jnp.einsum("rhd,khd->hrk", queries, key_rows, preferred_element_type=jnp.float32) * scaling
    )
    scores = jnp.where(allowed[None], scores, NEG)
    row_max = jnp.max(scores, axis=2, keepdims=True)
    exponent = jnp.exp(scores - row_max)
    row_total = jnp.sum(exponent, axis=2, keepdims=True)
    log_total = row_max + jnp.log(row_total)
    attention_low = (exponent / row_total).astype(jnp.bfloat16)
    mixture = jnp.einsum(
        "hrk,khd->rhd", attention_low, value_rows, preferred_element_type=jnp.float32
    )
    mixture = mixture.astype(jnp.bfloat16).reshape(-1, query_width)
    attend_branch = jnp.dot(mixture, output_full, preferred_element_type=jnp.float32).astype(
        jnp.bfloat16
    )
    attend_returned = collect(attend_branch.reshape(group_size, slot_count, model_width))
    hidden = inputs + merge_back(attend_table, attend_gate, attend_returned)
    normed_feed, unit_feed, factor_feed = norm_parts(hidden, gain_feedforward)
    feed_in = normed_feed.astype(jnp.bfloat16)
    feed_ids = lax.dynamic_slice_in_dim(
        feedforward_routes[0], my_index * tok_rows, tok_rows, 0
    )
    feed_matches = expert_matches(feed_ids, group_size)
    feed_logits = jnp.dot(feed_in, feedforward_cols, preferred_element_type=jnp.float32)
    feed_weights, feed_gate = pair_gates(feed_logits, feed_matches)
    everyone = gather_all(feed_in)
    feed_taken, feed_pairs = expert_table(every_route, my_index, group_size, tok_rows, slot_count)
    pick = functools.partial(pick_rows, feed_taken)
    feed_rows = pick(everyone)
    cot_rows = pick(cot_everyone)
    row_logits = jnp.dot(feed_rows, feedforward_cols, preferred_element_type=jnp.float32)
    row_gate = own_gate(row_logits, feed_pairs, my_index)
    pre_gate = lax.dot_general(feed_rows, gate_weight[0], ACROSS, preferred_element_type=jnp.float32)
    pre_up = lax.dot_general(feed_rows, up_weight[0], ACROSS, preferred_element_type=jnp.float32)
    sigmoid_gate = jax.nn.sigmoid(pre_gate)
    act = pre_gate * sigmoid_gate * pre_up
    act_low = act.astype(jnp.bfloat16)
    act_scaled = (act * row_gate).astype(jnp.bfloat16)
    act_grad = lax.dot_general(cot_rows, down_weight[0], ACROSS, preferred_element_type=jnp.float32)
    slot_dgate = jnp.sum(act_low.astype(jnp.float32) * act_grad, axis=1)
    act_grad = act_grad * row_gate
    dgate_low = (act_grad * pre_up * sigmoid_gate * (1.0 + pre_gate * (1.0 - sigmoid_gate))).astype(
        jnp.bfloat16
    )
    dup_low = (act_grad * pre_gate * sigmoid_gate).astype(jnp.bfloat16)
    feed_dx = (
        jnp.dot(dgate_low, gate_weight[0], preferred_element_type=jnp.float32)
        + jnp.dot(dup_low, up_weight[0], preferred_element_type=jnp.float32)
    ).astype(jnp.bfloat16)
    feed_branch = jnp.dot(act_scaled, down_weight[0], preferred_element_type=jnp.float32).astype(
        jnp.bfloat16
    )
    grad_gate = lax.dot_general(dgate_low, feed_rows, DOWNWARD, preferred_element_type=jnp.float32)
    grad_up = lax.dot_general(dup_low, feed_rows, DOWNWARD, preferred_element_type=jnp.float32)
    grad_down = lax.dot_general(act_scaled, cot_rows, DOWNWARD, preferred_element_type=jnp.float32)
    token_dgate = jnp.einsum(
        "bct,bc->bt",
        feed_taken.astype(jnp.float32),
        slot_dgate.reshape(-1, slot_count),
        precision=HIGH,
    ).reshape(-1, 1)
    own_column = (jnp.arange(group_size) == my_index).astype(jnp.float32)[None]
    feed_dgate = scatter_all(token_dgate * own_column)
    feed_home = scatter_all(return_rows(feed_taken, feed_dx)).astype(jnp.float32)
    feed_sum = scatter_all(return_rows(feed_taken, feed_branch)).astype(jnp.float32)
    layer_output = hidden + feed_sum
    gradient = cotangent[0].astype(jnp.float32)
    feed_dlogits = gates_back(feed_dgate, feed_weights, feed_matches)
    feed_dnorm = feed_home + jnp.dot(
        feed_dlogits, feedforward_cols.astype(jnp.float32).T, precision=HIGH
    )
    grad_gain_feed = jnp.sum(feed_dnorm * unit_feed, axis=0)
    hidden_grad = gradient + norm_back(feed_dnorm, gain_feedforward, unit_feed, factor_feed)
    attend_cot, attend_dgate = branch_cotangent(
        attend_table, attend_gate, attend_returned, hidden_grad
    )
    attend_dlogits = gates_back(attend_dgate, attend_weights, attend_matches)
    attend_cot_rows = dispatch(attend_cot).reshape(-1, model_width)
    dmixture = lax.dot_general(
        attend_cot_rows, output_full, ACROSS, preferred_element_type=jnp.float32
    )
    dmixture = dmixture.astype(jnp.bfloat16).reshape(-1, HEADS, HEAD_DIM)
    grad_projection = lax.dot_general(
        mixture, attend_cot_rows, DOWNWARD, preferred_element_type=jnp.float32
    )
    scores_again = (
        jnp.einsum("rhd,khd->hrk", queries, key_rows, preferred_element_type=jnp.float32) * scaling
    )
    attention = jnp.where(allowed[None], jnp.exp(scores_again - log_total), 0.0)
    attention_again = attention.astype(jnp.bfloat16)
    dattention = jnp.einsum(
        "rhd,khd->hrk", dmixture, value_rows, preferred_element_type=jnp.float32
    )
    row_dot = jnp.sum(attention * dattention, axis=2, keepdims=True)
    dscores = (attention * (dattention - row_dot)).astype(jnp.bfloat16)
    dqueries = (
        jnp.einsum("hrk,khd->rhd", dscores, key_rows, preferred_element_type=jnp.float32) * scaling
    )
    dqueries = dqueries.astype(jnp.bfloat16).reshape(-1, query_width)
    dkeys = (
        jnp.einsum("hrk,rhd->khd", dscores, queries, preferred_element_type=jnp.float32) * scaling
    )
    dvalues = jnp.einsum(
        "hrk,rhd->khd", attention_again, dmixture, preferred_element_type=jnp.float32
    )
    grad_query = lax.dot_general(arrived, dqueries, DOWNWARD, preferred_element_type=jnp.float32)
    attend_dx = lax.dot_general(dqueries, query_full, ACROSS, preferred_element_type=jnp.float32)
    keyvalue_terms = jnp.concatenate(
        [dkeys.reshape(seq_total, query_width), dvalues.reshape(seq_total, query_width)], axis=1
    ).reshape(group_size, tok_rows, 2 * query_width)
    attend_home, keyvalue_home = (
        lax.all_to_all(
            attend_dx.reshape(group_size, slot_count, model_width).astype(jnp.bfloat16),
            "expert",
            split_axis=0,
            concat_axis=0,
            tiled=True,
        ).astype(jnp.float32),
        lax.all_to_all(
            keyvalue_terms.astype(jnp.bfloat16), "expert", split_axis=0, concat_axis=0, tiled=True
        ).astype(keyvalue_terms.dtype),
    )
    dkeyvalue = jnp.sum(keyvalue_home, axis=0).astype(jnp.bfloat16)
    attend_dnorm = (
        jnp.einsum("ect,ecd->td", attend_table, attend_home, precision=HIGH)
        + lax.dot_general(dkeyvalue, keyvalue_full, ACROSS, preferred_element_type=jnp.float32)
        + jnp.dot(attend_dlogits, attention_cols.astype(jnp.float32).T, precision=HIGH)
    )
    grad_keyvalue = lax.dot_general(
        attention_in, dkeyvalue, DOWNWARD, preferred_element_type=jnp.float32
    )
    grad_router = jnp.concatenate(
        [
            jnp.dot(attention_in.astype(jnp.float32).T, attend_dlogits, precision=HIGH),
            jnp.dot(feed_in.astype(jnp.float32).T, feed_dlogits, precision=HIGH),
        ],
        axis=1,
    )
    grad_gain_attend = jnp.sum(attend_dnorm * unit_attention, axis=0)
    grad_tokens = hidden_grad + norm_back(
        attend_dnorm, gain_attention, unit_attention, factor_attention
    )
    reduced = (
        lax.psum_scatter(
            grad_keyvalue.astype(jnp.bfloat16), "dp", scatter_dimension=0, tiled=True
        ).astype(jnp.float32),
        lax.psum_scatter(
            grad_router.astype(jnp.bfloat16), "dp", scatter_dimension=0, tiled=True
        ).astype(jnp.float32),
        lax.psum_scatter(
            grad_query.astype(jnp.bfloat16), "dp", scatter_dimension=0, tiled=True
        ).astype(jnp.float32),
        lax.psum_scatter(
            grad_projection.astype(jnp.bfloat16), "dp", scatter_dimension=0, tiled=True
        ).astype(jnp.float32),
        lax.psum_scatter(
            grad_gain_attend.astype(jnp.bfloat16), "dp", scatter_dimension=0, tiled=True
        ).astype(jnp.float32),
        lax.psum_scatter(
            grad_gain_feed.astype(jnp.bfloat16), "dp", scatter_dimension=0, tiled=True
        ).astype(jnp.float32),
    )
    shared = (
        lax.psum(reduced[0].astype(jnp.bfloat16), "expert").astype(jnp.float32),
        lax.psum(reduced[1].astype(jnp.bfloat16), "expert").astype(jnp.float32),
        lax.psum(reduced[4].astype(jnp.bfloat16), "expert").astype(jnp.float32),
        lax.psum(reduced[5].astype(jnp.bfloat16), "expert").astype(jnp.float32),
    )
    return (
        layer_output.astype(jnp.bfloat16)[None],
        grad_tokens[None],
        shared[2],
        shared[3],
        shared[0],
        shared[1],
        reduced[2][None],
        reduced[3][None],
        grad_gate[None],
        grad_up[None],
        grad_down[None],
    )


MESH = pl.DeviceIdType.MESH
CHIPS_Z = 4
TURNS = ((3, 2, 1, 0), (3, 0, 2, 1), (0, 3, 1, 2), (0, 1, 2, 3))


class Place:
    def __init__(self):
        self.dp, self.expert = lax.axis_index("dp"), lax.axis_index("expert")
        self.at = {
            "z": self.dp // 2,
            "y": self.dp % 2,
            "x": self.expert // 2,
            "c": self.expert % 2,
        }

    def across(self, axis):
        back = 1 - 2 * self.at[axis]
        if axis == "c":
            return (self.dp, self.expert + back)
        if axis == "x":
            return (self.dp, self.expert + 2 * back)
        return (self.dp + back, self.expert)

    def along(self, step):
        return (self.dp + 2 * step, self.expert)

    def block(self, whose, z, flips):
        at = {a: self.at[a] + flips.get(a, 0) * (1 - 2 * self.at[a]) for a in "xyc"}
        dp, expert = z * 2 + at["y"], at["x"] * 2 + at["c"]
        return {"all": dp * 4 + expert, "dp": dp, "expert": expert}[whose]


def enter(place, axes):
    barrier, count = pltpu.get_barrier_semaphore(), 0
    for axis in axes:
        if axis != "z":
            pl.semaphore_signal(
                barrier, inc=1, device_id=place.across(axis), device_id_type=MESH
            )
            count += 1
    if "z" in axes:
        z = place.at["z"]
        for step, there in ((-1, z > 0), (1, z < CHIPS_Z - 1)):

            @pl.when(there)
            def _(step=step):
                pl.semaphore_signal(
                    barrier, inc=1, device_id=place.along(step), device_id_type=MESH
                )

            count = count + there.astype(jnp.int32)
    pl.semaphore_wait(barrier, count)


def on(condition, action):
    if condition is None:
        action()
    else:
        pl.when(condition)(action)


def both(a, b):
    return b if a is None else a if b is None else a & b


class Post:
    def __init__(self, sems, place):
        self.sems, self.place, self.sent = sems, place, []

    def send(self, source, target, arrival, device, condition=None):
        number = len(self.sent)

        def copy():
            return pltpu.make_async_remote_copy(
                src_ref=source,
                dst_ref=target,
                send_sem=self.sems.at[number],
                recv_sem=arrival,
                device_id=device,
                device_id_type=MESH,
            )

        self.sent.append((condition, copy))
        on(condition, lambda: copy().start())

    def arrived(self, target, arrival):
        pltpu.make_async_remote_copy(
            src_ref=target,
            dst_ref=target,
            send_sem=self.sems.at[0],
            recv_sem=arrival,
            device_id=self.place.across("c"),
            device_id_type=MESH,
        ).wait_recv()

    def close(self):
        for condition, copy in self.sent:
            on(condition, lambda copy=copy: copy().wait_send())


FLIPS = {"x": 4, "y": 2, "c": 1}


def gather_kernel(jobs, axes, *refs):
    count = len(jobs)
    sources, targets = refs[:count], refs[count : 2 * count]
    send_sems, arrive_sems, own_sems = refs[2 * count :]
    place = Place()
    enter(place, axes)
    post = Post(send_sems, place)
    z_here = place.at["z"]
    line = 0
    waves, owns = {}, []
    for j, (whose, rows, pieces) in enumerate(jobs):
        own = pltpu.make_async_copy(
            sources[j],
            targets[j].at[pl.ds(place.block(whose, z_here, {}) * rows, rows)],
            own_sems.at[j],
        )
        own.start()
        owns.append(own)
        for first, length, order in pieces:

            def part(z, flips, j=j, whose=whose, rows=rows, first=first, length=length):
                at = place.block(whose, z, flips) * rows + first
                return targets[j].at[pl.ds(at, length)]

            def mark(z, flips, line=line):
                return arrive_sems.at[line, z * 8 + sum(FLIPS[a] * v for a, v in flips.items())]

            def hand_on(source, z, flips, depth, side, wave, condition, order=order, part=part, mark=mark):
                for axis in order[max(depth, 0) :]:
                    if axis == "z" and (depth < 0 or order[depth] != "z"):
                        for step in (1, -1):
                            there = (z_here < CHIPS_Z - 1) if step > 0 else (z_here > 0)
                            post.send(source, part(z, flips), mark(z, flips), place.along(step), both(condition, there))
                    elif axis == "z":
                        there = (z_here < CHIPS_Z - 1) if side > 0 else (z_here > 0)
                        post.send(source, part(z, flips), mark(z, flips), place.along(side), both(condition, there))
                    elif depth < 0 or axis != order[depth]:
                        seen = dict(flips)
                        seen[axis] = 1
                        post.send(source, part(z, flips), mark(z, seen), place.across(axis), condition)

            def come(z, flips, depth, side, hops, wave, condition, order=order, part=part, mark=mark, hand_on=hand_on):
                def act():
                    on(condition, lambda: post.arrived(part(z, flips), mark(z, flips)))
                    hand_on(part(z, flips), z, flips, depth, side, wave, condition)

                waves.setdefault(wave, []).append(act)
                spread(z, flips, depth, side, hops, wave, condition, order, come)

            hand_on(sources[j].at[pl.ds(first, length)], z_here, {}, -1, 0, 0, None)
            spread(z_here, {}, -1, 0, 0, 0, None, order, come)
            line += 1
    for wave in sorted(waves):
        for act in waves[wave]:
            act()
    for own in owns:
        own.wait()
    post.close()


def spread(z, flips, depth, side, hops, wave, condition, order, come):
    z_here = lax.axis_index("dp") // 2
    for later in range(max(depth, 0), len(order)):
        axis = order[later]
        if axis == "z":
            if depth >= 0 and order[depth] == "z":
                if hops < CHIPS_Z - 1:
                    far = hops + 1
                    there = (z_here >= far) if side > 0 else (z_here + far < CHIPS_Z)
                    come(z_here - side * far, flips, later, side, far, wave + 1, there)
            else:
                for step in (1, -1):
                    there = (z_here >= 1) if step > 0 else (z_here + 1 < CHIPS_Z)
                    come(z_here - step, flips, later, step, 1, wave + 1, both(condition, there))
        elif later > depth:
            seen = dict(flips)
            seen[axis] = 1
            come(z, seen, later, 0, 0, wave + 1, condition)


def gather(jobs, collective_id, name):
    arrays = [rows for rows, _, _ in jobs]
    sizes = {"all": 32, "dp": 8, "expert": 4}
    plan = tuple((whose, rows.shape[0], pieces) for rows, whose, pieces in jobs)
    axes = "".join(a for a in "cxyz" if any(a in order for _, _, ps in plan for _, _, order in ps))
    lines = sum(len(ps) for _, _, ps in plan)
    any_spec = pl.BlockSpec(memory_space=pltpu.HBM)
    return pl.pallas_call(
        functools.partial(gather_kernel, plan, axes),
        out_shape=[
            jax.ShapeDtypeStruct((sizes[whose] * r.shape[0], r.shape[1]), r.dtype)
            for r, whose, _ in jobs
        ],
        in_specs=[any_spec] * len(jobs),
        out_specs=[any_spec] * len(jobs),
        scratch_shapes=[
            pltpu.SemaphoreType.DMA((110 * lines,)),
            pltpu.SemaphoreType.DMA((lines, 32)),
            pltpu.SemaphoreType.DMA((len(jobs),)),
        ],
        compiler_params=pltpu.CompilerParams(
            collective_id=collective_id, has_side_effects=True
        ),
        name=name,
    )(*arrays)


def scatter_kernel(whose, rows, pieces, source, result, acc, *refs):
    place = Place()
    orders = [order for _, _, order in pieces]
    flat = [order.replace("z", "") for order in orders]
    steps = len(flat[0])
    lined = "z" in orders[0]
    turns = CHIPS_Z if lined else 1
    bins = refs[:steps]
    line = refs[steps] if lined else None
    send_sems, load_sems, bin_sems, line_sems = refs[-4:]
    z_here = place.at["z"]
    if lined:
        turn = [
            sum((z_here == z).astype(jnp.int32) * seq[k] for z, seq in enumerate(TURNS))
            for k in range(CHIPS_Z)
        ]
    else:
        turn = [z_here]
    slot_z = lambda k: turn[k] if lined else 0
    post = Post(send_sems, place)

    def flips_of(p, stage, code):
        later = flat[p][stage + 1 :]
        flips = {a: (code >> i) & 1 for i, a in enumerate(later)}
        if stage < steps:
            flips[flat[p][stage]] = 1
        return flips

    def kept(p, flips):
        names = sorted(flat[p][1:])
        return sum(flips.get(a, 0) << i for i, a in enumerate(names))

    def code_after(p, stage, flips):
        return sum(flips.get(a, 0) << i for i, a in enumerate(flat[p][stage + 1 :]))

    keep = 2 ** (steps - 1)
    names = sorted(flat[0][1:])
    loads = {}
    for k in range(turns):
        for n in reversed(range(keep)):
            flips = {a: (n >> i) & 1 for i, a in enumerate(names)}
            at = slot_z(k) * keep + n
            loads[k, n] = pltpu.make_async_copy(
                source.at[pl.ds(place.block(whose, turn[k], flips) * rows, rows)],
                acc.at[at],
                load_sems.at[at],
            )
            loads[k, n].start()
    enter(place, "".join(flat[0]) + ("z" if lined else ""))
    loaded = set()

    def add(target, terms, length):
        @pl.loop(0, length // 16)
        def _(r):
            at = pl.ds(pl.multiple_of(r * 16, 16), 16)
            total = target[at, :].astype(jnp.float32)
            for term in terms:
                total = total + term[at, :].astype(jnp.float32)
            target[at, :] = total.astype(jnp.bfloat16)

    def mine(p, ref):
        first, length, _ = pieces[p]
        return ref.at[pl.ds(first, length)]

    def gathered(p, k, stage, flips):
        n = kept(p, flips)
        at = slot_z(k) * keep + n
        if (k, n) not in loaded:
            loads[k, n].wait()
            loaded.add((k, n))
        terms = []
        for before in range(stage):
            code = code_after(p, before, flips)
            width = 2 ** (steps - 1 - before)
            ref = mine(p, bins[before].at[slot_z(k) * width + code])
            post.arrived(ref, bin_sems.at[p, before, slot_z(k) * width + code])
            terms.append(ref)
        block = mine(p, acc.at[at])
        add(block, terms, pieces[p][1])
        return block

    def leave(p, k, stage, code, block, flips):
        axis = flat[p][stage]
        width = 2 ** (steps - 1 - stage)
        at = slot_z(k) * width + code
        post.send(block, mine(p, bins[stage].at[at]), bin_sems.at[p, stage, at], place.across(axis))

    def work(k, stage):
        if stage < steps:
            for code in reversed(range(2 ** (steps - 1 - stage))):
                for p in range(len(pieces)):
                    flips = flips_of(p, stage, code)
                    if stage == 0:
                        first, length, _ = pieces[p]
                        at = place.block(whose, turn[k], flips) * rows + first
                        leave(p, k, stage, code, source.at[pl.ds(at, length)], flips)
                    else:
                        leave(p, k, stage, code, gathered(p, k, stage, flips), flips)
            return
        for p in range(len(pieces)):
            block = gathered(p, k, steps, {})
            if not lined or k == turns - 1:
                continue
            t = turn[k]
            right = t > z_here

            def pass_on(p=p, t=t, block=block):
                ref = mine(p, line.at[t])
                post.arrived(ref, line_sems.at[p, t])
                add(block, [ref], pieces[p][1])

            pl.when((right & (z_here > 0)) | (~right & (z_here < CHIPS_Z - 1)))(pass_on)
            slot = jnp.where(t == z_here - 1, CHIPS_Z, t)
            post.send(
                block,
                mine(p, line.at[slot]),
                line_sems.at[p, slot],
                place.along(jnp.where(right, 1, -1)),
            )

    for k in range(turns):
        work(k, 0)
    for time in range(turns + steps):
        for stage in range(1, steps + 1):
            k = time - stage + 1
            if 0 <= k < turns:
                work(k, stage)
    for p in range(len(pieces)):
        first, length, _ = pieces[p]
        block = mine(p, acc.at[z_here * keep if lined else 0])
        if lined:
            for slot, there in ((z_here, z_here > 0), (CHIPS_Z, z_here < CHIPS_Z - 1)):

                def last(p=p, slot=slot, block=block):
                    ref = mine(p, line.at[slot])
                    post.arrived(ref, line_sems.at[p, slot])
                    add(block, [ref], pieces[p][1])

                pl.when(there)(last)

        @pl.loop(0, length // 16)
        def _(r, first=first, block=block):
            at = pl.ds(pl.multiple_of(r * 16, 16), 16)
            result[pl.ds(pl.multiple_of(first + r * 16, 16), 16), :] = block[at, :].astype(
                result.dtype
            )

    post.close()


def scatter(array, whose, pieces, collective_id, name, dtype=jnp.float32):
    size = {"all": 32, "dp": 8, "expert": 4}[whose]
    rows, width = array.shape[0] // size, array.shape[1]
    flat = pieces[0][2].replace("z", "")
    steps, lined = len(flat), "z" in pieces[0][2]
    turns = CHIPS_Z if lined else 1
    room = lambda blocks: pltpu.VMEM((blocks, rows, width), jnp.bfloat16)
    scratch = [room(turns * 2 ** (steps - 1))]
    scratch += [room(turns * 2 ** (steps - 1 - stage)) for stage in range(steps)]
    if lined:
        scratch.append(room(CHIPS_Z + 1))
    count = len(pieces)
    scratch += [
        pltpu.SemaphoreType.DMA((count * (turns * 2**steps + 4),)),
        pltpu.SemaphoreType.DMA((turns * 2 ** (steps - 1),)),
        pltpu.SemaphoreType.DMA((count, steps, turns * 2 ** (steps - 1))),
        pltpu.SemaphoreType.DMA((count, CHIPS_Z + 1)),
    ]
    return pl.pallas_call(
        functools.partial(scatter_kernel, whose, rows, pieces),
        out_shape=jax.ShapeDtypeStruct((rows, width), dtype),
        in_specs=[pl.BlockSpec(memory_space=pltpu.HBM)],
        out_specs=pl.BlockSpec(memory_space=pltpu.VMEM),
        scratch_shapes=scratch,
        compiler_params=pltpu.CompilerParams(
            collective_id=collective_id, has_side_effects=True, vmem_limit_bytes=62 * 2**20
        ),
        name=name,
    )(array)


def attention_bias(bias, block, rows, width, prefix):
    query = block * rows + lax.broadcasted_iota(jnp.int32, (rows, width), 0)
    key = lax.broadcasted_iota(jnp.int32, (rows, width), 1)
    bias[:, :width] = jnp.where((key <= query) | (key < prefix), 0.0, NEG)


def pick_expert(ref, lane, experts, span, chosen):
    total = None
    for e in range(experts):
        cols = ref[:, pl.ds(pl.multiple_of(e * span + lane, HEAD_DIM), HEAD_DIM)]
        term = jnp.where(chosen == e, cols.astype(jnp.float32), 0.0)
        total = term if total is None else total + term
    return total.astype(jnp.bfloat16)


def key_limits(blocks, rows):
    return [max((i + 1) * rows, blocks * rows // 2) for i in range(blocks)]


def for_each_limit(blocks, rows, body):
    block = pl.program_id(0)
    limits = key_limits(blocks, rows)
    for width in sorted(set(limits)):
        members = [i for i, limit in enumerate(limits) if limit == width]
        pl.when((block >= members[0]) & (block <= members[-1]))(lambda width=width: body(width))


def attention_kernel(experts, prefix, q, k, v, side, mixed, log_total, bias):
    rows, span = q.shape[0], k.shape[1]
    heads = span // HEAD_DIM
    block = pl.program_id(0)
    chosen = [side[:, 0:1], side[:, 1:2]]
    gates = [side[:, 2:3], side[:, 3:4]]

    def body(width):
        attention_bias(bias, block, rows, width, prefix[0])

        @pl.loop(0, heads)
        def _(head):
            lane = head * HEAD_DIM
            lanes = pl.ds(pl.multiple_of(lane, HEAD_DIM), HEAD_DIM)
            weighted = []
            for j in range(2):
                query = pick_expert(q, lane, experts, span, chosen[j])
                scores = lax.dot_general(
                    query, k[:width, lanes], ACROSS, preferred_element_type=jnp.float32
                )
                scores = scores * (HEAD_DIM**-0.5) + bias[:, :width]
                largest = jnp.max(scores, axis=1, keepdims=True)
                exponent = jnp.exp(scores - largest)
                total = jnp.sum(exponent, axis=1, keepdims=True)
                low = (exponent * (1.0 / total)).astype(jnp.bfloat16)
                out = jnp.dot(low, v[:width, lanes], preferred_element_type=jnp.float32)
                weighted.append(out * gates[j])
                at = pl.ds(pl.multiple_of((2 * head + j) * HEAD_DIM, HEAD_DIM), HEAD_DIM)
                log_total[:, at] = jnp.broadcast_to(
                    largest + jnp.log(total), (rows, HEAD_DIM)
                )
            for e in range(experts):
                cols = jnp.where(chosen[0] == e, weighted[0], 0.0) + jnp.where(
                    chosen[1] == e, weighted[1], 0.0
                )
                at = pl.ds(pl.multiple_of(e * span + lane, HEAD_DIM), HEAD_DIM)
                mixed[:, at] = cols.astype(jnp.bfloat16)

    for_each_limit(k.shape[0] // rows, rows, body)


def attention(projected, side, prefix, experts, rows):
    length = projected.shape[0]
    span = projected.shape[1] // (experts + 2)
    wide = experts * span
    return pl.pallas_call(
        functools.partial(attention_kernel, experts),
        grid=(length // rows,),
        in_specs=[
            pl.BlockSpec(memory_space=pltpu.SMEM),
            pl.BlockSpec((rows, wide), lambda i: (i, 0)),
            pl.BlockSpec((length, span), lambda i: (0, experts)),
            pl.BlockSpec((length, span), lambda i: (0, experts + 1)),
            pl.BlockSpec((rows, 128), lambda i: (i, 0)),
        ],
        out_specs=[
            pl.BlockSpec((rows, wide), lambda i: (i, 0)),
            pl.BlockSpec((rows, 2 * span), lambda i: (i, 0)),
        ],
        out_shape=[
            jax.ShapeDtypeStruct((length, wide), jnp.bfloat16),
            jax.ShapeDtypeStruct((length, 2 * span), jnp.float32),
        ],
        scratch_shapes=[pltpu.VMEM((rows, length), jnp.float32)],
        compiler_params=pltpu.CompilerParams(vmem_limit_bytes=48 * 2**20),
        name="attention",
    )(prefix, projected, projected, projected, side)


def attention_back_kernel(
    experts, prefix, q, k, v, side, log_total, dmix, dprojected, dgate, bias, dk, dv
):
    rows, span = q.shape[0], k.shape[1]
    length = k.shape[0]
    heads = span // HEAD_DIM
    block = pl.program_id(0)
    scaling = HEAD_DIM**-0.5
    chosen = [side[:, 0:1], side[:, 1:2]]
    gates = [side[:, 2:3], side[:, 3:4]]
    row_at = pl.ds(pl.multiple_of(block * rows, rows), rows)
    column = lax.broadcasted_iota(jnp.int32, (rows, 128), 1)

    @pl.when(block == 0)
    def _():
        dk[...] = jnp.zeros_like(dk)
        dv[...] = jnp.zeros_like(dv)

    dgate[...] = jnp.zeros_like(dgate)

    def body(width):
        attention_bias(bias, block, rows, width, prefix[0])

        @pl.loop(0, heads)
        def _(head):
            lane = head * HEAD_DIM
            lanes = pl.ds(pl.multiple_of(lane, HEAD_DIM), HEAD_DIM)
            keys, values = k[:width, lanes], v[:width, lanes]
            dqueries = []
            for j in range(2):
                query = pick_expert(q, lane, experts, span, chosen[j])
                dm = pick_expert(dmix, lane, experts, span, chosen[j])
                at = pl.ds(pl.multiple_of((2 * head + j) * HEAD_DIM, HEAD_DIM), HEAD_DIM)
                logs = jnp.tile(log_total[:, at], (1, width // HEAD_DIM))
                scores = lax.dot_general(query, keys, ACROSS, preferred_element_type=jnp.float32)
                probs = jnp.exp(scores * scaling + bias[:, :width] - logs)
                dprobs = lax.dot_general(dm, values, ACROSS, preferred_element_type=jnp.float32)
                inner = jnp.sum(probs * dprobs, axis=1, keepdims=True)
                dgate[...] += jnp.where(column == j, inner, 0.0)
                probs = probs * gates[j]
                dscores = (probs * (dprobs - inner)).astype(jnp.bfloat16)
                low = probs.astype(jnp.bfloat16)
                dquery = jnp.dot(dscores, keys, preferred_element_type=jnp.float32) * scaling
                dqueries.append(dquery)
                dk[:width, lanes] += lax.dot_general(
                    dscores, query, DOWNWARD, preferred_element_type=jnp.float32
                )
                dv[:width, lanes] += lax.dot_general(
                    low, dm, DOWNWARD, preferred_element_type=jnp.float32
                )
            for e in range(experts):
                cols = jnp.where(chosen[0] == e, dqueries[0], 0.0) + jnp.where(
                    chosen[1] == e, dqueries[1], 0.0
                )
                at = pl.ds(pl.multiple_of(e * span + lane, HEAD_DIM), HEAD_DIM)
                dprojected[row_at, at] = cols.astype(jnp.bfloat16)

    for_each_limit(length // rows, rows, body)

    @pl.when(block == pl.num_programs(0) - 1)
    def _():
        dprojected[:, experts * span : (experts + 1) * span] = (dk[...] * scaling).astype(
            jnp.bfloat16
        )
        dprojected[:, (experts + 1) * span :] = dv[...].astype(jnp.bfloat16)


def attention_back(projected, side, prefix, log_total, dmix, experts, rows):
    length, total = projected.shape
    span = total // (experts + 2)
    wide = experts * span
    return pl.pallas_call(
        functools.partial(attention_back_kernel, experts),
        grid=(length // rows,),
        in_specs=[
            pl.BlockSpec(memory_space=pltpu.SMEM),
            pl.BlockSpec((rows, wide), lambda i: (i, 0)),
            pl.BlockSpec((length, span), lambda i: (0, experts)),
            pl.BlockSpec((length, span), lambda i: (0, experts + 1)),
            pl.BlockSpec((rows, 128), lambda i: (i, 0)),
            pl.BlockSpec((rows, 2 * span), lambda i: (i, 0)),
            pl.BlockSpec((rows, wide), lambda i: (i, 0)),
        ],
        out_specs=[
            pl.BlockSpec((length, total), lambda i: (0, 0)),
            pl.BlockSpec((rows, 128), lambda i: (i, 0)),
        ],
        out_shape=[
            jax.ShapeDtypeStruct((length, total), jnp.bfloat16),
            jax.ShapeDtypeStruct((length, 128), jnp.float32),
        ],
        scratch_shapes=[
            pltpu.VMEM((rows, length), jnp.float32),
            pltpu.VMEM((length, span), jnp.float32),
            pltpu.VMEM((length, span), jnp.float32),
        ],
        compiler_params=pltpu.CompilerParams(vmem_limit_bytes=56 * 2**20),
        name="attention_back",
    )(prefix, projected, projected, projected, side, log_total, dmix)


NEAREST = ((0, 1, 2, 3), (1, 2, 0, 3), (2, 1, 3, 0), (3, 2, 1, 0))


def expert_slots(ids, my_index, tok_rows):
    blocks = ids.reshape(-1, tok_rows, 2)
    chosen = jnp.sum((blocks == my_index).astype(jnp.float32), axis=2)
    before = jnp.triu(jnp.ones((tok_rows, tok_rows), jnp.float32), 1)
    slots = jnp.where(chosen > 0, jnp.dot(chosen, before), -1.0).astype(jnp.int32)
    return slots, jnp.sum(blocks, axis=2) - my_index


def feed_kernel(
    tok,
    slot_count,
    own_rows,
    cots,
    gate_weight,
    up_weight,
    down_weight,
    router_rows,
    slots,
    others,
    everyone,
    dx_part,
    out_part,
    x_kept,
    g_kept,
    d_kept,
    a_kept,
    dgate,
    w_in,
    w_down,
    rows_buf,
    cots_buf,
    xs,
    gs,
    pre,
    back,
    ds,
    acts,
    dx_buf,
    out_buf,
    send_sems,
    arrive_sems,
    own_sem,
    weight_sems,
    load_sems,
    keep_sems,
):
    place = Place()
    z_here = place.at["z"]
    hidden = gate_weight.shape[0]
    padded = w_down.shape[0]
    width = own_rows.shape[1]
    half = tok // 2
    chips = 4 * CHIPS_Z
    pair = 2 * slot_count
    f32, low = jnp.float32, jnp.bfloat16

    loads = [
        pltpu.make_async_copy(gate_weight, w_in.at[pl.ds(0, hidden)], weight_sems.at[0]),
        pltpu.make_async_copy(
            router_rows, w_in.at[pl.ds(hidden, padded - hidden)], weight_sems.at[1]
        ),
        pltpu.make_async_copy(up_weight, w_in.at[pl.ds(padded, hidden)], weight_sems.at[2]),
        pltpu.make_async_copy(down_weight, w_down.at[pl.ds(0, hidden)], weight_sems.at[3]),
        pltpu.make_async_copy(
            own_rows, everyone.at[pl.ds(place.block("all", z_here, {}) * tok, tok)], own_sem
        ),
    ]
    for load in loads:
        load.start()
    w_in[padded + hidden :, :] = jnp.zeros((padded - hidden, width), low)
    w_down[hidden:, :] = jnp.zeros((padded - hidden, width), low)
    enter(place, "cxyz")

    def chip(u):
        k, xr, yr = u // 4, u % 2, (u // 2) % 2
        z = sum(
            ((z_here == at) & (k == i)).astype(jnp.int32) * seq[i]
            for at, seq in enumerate(NEAREST)
            for i in range(CHIPS_Z)
        )
        return z, xr, yr

    def first_block(u):
        z, xr, yr = chip(u)
        x = place.at["x"] + xr * (1 - 2 * place.at["x"])
        y = place.at["y"] + yr * (1 - 2 * place.at["y"])
        return (z * 2 + y) * 4 + x * 2

    def part(p, u, core):
        return everyone.at[pl.ds((first_block(u) + core) * tok + p * half, half)]

    def remote(source, target, number, mark, device):
        return pltpu.make_async_remote_copy(
            src_ref=source,
            dst_ref=target,
            send_sem=send_sems.at[number],
            recv_sem=arrive_sems.at[mark],
            device_id=device,
            device_id_type=MESH,
        )

    def routes(u, p):
        z, xr, yr = chip(u)
        plain = (xr + yr) == 0
        mark = (p * CHIPS_Z + z) * 8
        here = xr * 4 + yr * 2
        base = (u * 2 + p) * 5
        own = z == z_here
        right = plain & (z <= z_here) & (z_here < CHIPS_Z - 1)
        left = plain & (z >= z_here) & (z_here > 0)
        over_x = plain if p == 0 else xr == 0
        over_y = yr == 0 if p == 0 else plain
        return [
            (right, base, mark, place.along(1)),
            (left, base + 1, mark, place.along(-1)),
            (over_x, base + 2, mark + 4 + yr * 2, place.across("x")),
            (over_y, base + 3, mark + xr * 4 + 2, place.across("y")),
            (None, base + 4, mark + here + 1, place.across("c")),
        ]

    def hand_on(u, sources):
        for p in range(2):
            for condition, number, mark, device in routes(u, p):
                target = part(p, u, place.at["c"])
                source = target if sources is None else sources[p]
                on(
                    condition,
                    lambda source=source, target=target, number=number, mark=mark, device=device: remote(
                        source, target, number, mark, device
                    ).start(),
                )

    def sibling_came(u):
        z, xr, yr = chip(u)
        for p in range(2):
            ref = part(p, u, 1 - place.at["c"])
            mark = (p * CHIPS_Z + z) * 8 + xr * 4 + yr * 2 + 1
            remote(ref, ref, 0, mark, place.across("c")).wait_recv()

    def take_in(u):
        z, xr, yr = chip(u)
        for p in range(2):
            ref = part(p, u, place.at["c"])
            mark = (p * CHIPS_Z + z) * 8 + xr * 4 + yr * 2
            remote(ref, ref, 0, mark, place.across("c")).wait_recv()
        hand_on(u, None)
        sibling_came(u)

    def fetch(u):
        at = pl.ds(first_block(u) * tok, 2 * tok)
        return [
            pltpu.make_async_copy(everyone.at[at], rows_buf.at[u % 2], load_sems.at[u % 2, 0]),
            pltpu.make_async_copy(cots.at[at], cots_buf.at[u % 2], load_sems.at[u % 2, 1]),
        ]

    def keep(u):
        rows = pl.ds(u * pair, pair)
        blocks = pl.ds(first_block(u) * tok, 2 * tok)
        s = u % 2
        return [
            pltpu.make_async_copy(xs.at[s], x_kept.at[rows], keep_sems.at[s, 0]),
            pltpu.make_async_copy(gs.at[s], g_kept.at[rows], keep_sems.at[s, 1]),
            pltpu.make_async_copy(ds.at[s], d_kept.at[rows], keep_sems.at[s, 2]),
            pltpu.make_async_copy(acts.at[s], a_kept.at[rows], keep_sems.at[s, 3]),
            pltpu.make_async_copy(dx_buf.at[s], dx_part.at[blocks], keep_sems.at[s, 4]),
            pltpu.make_async_copy(out_buf.at[s], out_part.at[blocks], keep_sems.at[s, 5]),
        ]

    hand_on(0, [own_rows.at[pl.ds(0, half)], own_rows.at[pl.ds(half, half)]])
    loads[4].wait()
    sibling_came(0)
    for copy in fetch(0):
        copy.start()
    take_in(1)
    for load in loads[:4]:
        load.wait()

    def compute(u):
        s = u % 2
        block = first_block(u)
        spread = []
        for b in range(2):
            row = slots[pl.ds(block + b, 1), :]
            table = lax.broadcasted_iota(jnp.int32, (slot_count, tok), 0) == row
            table = table.astype(f32)
            spread.append(table)
            at = pl.ds(b * slot_count, slot_count)
            from_rows = pl.ds(b * tok, tok)
            xs[s, at, :] = jnp.dot(
                table.astype(low), rows_buf[s, from_rows, :], preferred_element_type=f32
            ).astype(low)
            gs[s, at, :] = jnp.dot(
                table.astype(low), cots_buf[s, from_rows, :], preferred_element_type=f32
            ).astype(low)

        @pl.loop(0, 2 * padded // 256)
        def _(n):
            at = pl.ds(pl.multiple_of(n * 256, 256), 256)
            pre[:, at] = lax.dot_general(xs[s], w_in[at, :], ACROSS, preferred_element_type=f32)

        @pl.loop(0, padded // 256)
        def _(n):
            at = pl.ds(pl.multiple_of(n * 256, 256), 256)
            back[:, at] = lax.dot_general(gs[s], w_down[at, :], ACROSS, preferred_element_type=f32)

        for b in range(2):
            at = pl.ds(b * slot_count, slot_count)
            last = pre[at, padded - 128 : padded]
            column = lax.broadcasted_iota(jnp.int32, (slot_count, 128), 1) - (
                hidden - (padded - 128)
            )
            other = jnp.sum(
                spread[b] * others[pl.ds(block + b, 1), :].astype(f32), axis=1, keepdims=True
            )
            mine = jnp.sum(jnp.where(column == place.expert, last, 0.0), axis=1, keepdims=True)
            theirs = jnp.sum(
                jnp.where(column == other.astype(jnp.int32), last, 0.0), axis=1, keepdims=True
            )
            gate = 1.0 / (1.0 + jnp.exp(theirs - mine))
            inner = jnp.zeros((slot_count, 1), f32)
            for n in range(padded // 256):
                cols = pl.ds(n * 256, 256)
                pre_gate, pre_up = pre[at, cols], pre[at, pl.ds(padded + n * 256, 256)]
                dact = back[at, cols]
                sig = 1.0 / (1.0 + jnp.exp(-pre_gate))
                silu = pre_gate * sig
                act = silu * pre_up
                acts[s, at, cols] = (act * gate).astype(low)
                inner += jnp.sum(act * dact, axis=1, keepdims=True)
                dact = dact * gate
                ds[s, at, cols] = (dact * pre_up * sig * (1.0 + pre_gate * (1.0 - sig))).astype(low)
                ds[s, at, pl.ds(padded + n * 256, 256)] = (dact * silu).astype(low)
            dgate[pl.ds(block + b, 1), :] = jnp.sum(spread[b] * inner, axis=0, keepdims=True)

        @pl.loop(0, width // 256)
        def _(n):
            cols = pl.ds(pl.multiple_of(n * 256, 256), 256)
            dx = jnp.dot(ds[s], w_in[:, cols], preferred_element_type=f32).astype(low)
            out = jnp.dot(acts[s], w_down[:, cols], preferred_element_type=f32).astype(low)
            for b in range(2):
                at = slice(b * slot_count, (b + 1) * slot_count)
                table = spread[b].astype(low)
                to = pl.ds(b * tok, tok)
                dx_buf[s, to, cols] = lax.dot_general(
                    table, dx[at], DOWNWARD, preferred_element_type=f32
                ).astype(low)
                out_buf[s, to, cols] = lax.dot_general(
                    table, out[at], DOWNWARD, preferred_element_type=f32
                ).astype(low)

    @pl.loop(0, chips)
    def _(u):
        @pl.when(u + 2 < chips)
        def _():
            take_in(u + 2)

        @pl.when(u + 1 < chips)
        def _():
            for copy in fetch(u + 1):
                copy.start()

        for copy in fetch(u):
            copy.wait()

        @pl.when(u >= 2)
        def _():
            for copy in keep(u - 2):
                copy.wait()

        compute(u)
        for copy in keep(u):
            copy.start()

    for u in (chips - 2, chips - 1):
        for copy in keep(jnp.int32(u)):
            copy.wait()

    @pl.loop(0, chips)
    def _(u):
        for p in range(2):
            for condition, number, mark, device in routes(u, p):
                ref = part(p, u, place.at["c"])
                on(
                    condition,
                    lambda ref=ref, number=number, mark=mark, device=device: remote(
                        ref, ref, number, mark, device
                    ).wait_send(),
                )


def feed(own_rows, cots, gate_weight, up_weight, down_weight, router_rows, slots, others, slot_count):
    tok, width = own_rows.shape
    hidden = gate_weight.shape[0]
    padded = hidden + router_rows.shape[0]
    total = cots.shape[0]
    kept = total // tok * slot_count
    low = jnp.bfloat16
    hbm = pl.BlockSpec(memory_space=pltpu.HBM)
    vmem = pl.BlockSpec(memory_space=pltpu.VMEM)
    shape = jax.ShapeDtypeStruct
    pair = 2 * slot_count
    chips = 4 * CHIPS_Z
    return pl.pallas_call(
        functools.partial(feed_kernel, tok, slot_count),
        in_specs=[hbm] * 6 + [vmem] * 2,
        out_specs=[hbm] * 7 + [vmem],
        out_shape=[
            shape((total, width), low),
            shape((total, width), low),
            shape((total, width), low),
            shape((kept, width), low),
            shape((kept, width), low),
            shape((kept, 2 * padded), low),
            shape((kept, padded), low),
            shape(slots.shape, jnp.float32),
        ],
        scratch_shapes=[
            pltpu.VMEM((2 * padded, width), low),
            pltpu.VMEM((padded, width), low),
            pltpu.VMEM((2, 2 * tok, width), low),
            pltpu.VMEM((2, 2 * tok, width), low),
            pltpu.VMEM((2, pair, width), low),
            pltpu.VMEM((2, pair, width), low),
            pltpu.VMEM((pair, 2 * padded), jnp.float32),
            pltpu.VMEM((pair, padded), jnp.float32),
            pltpu.VMEM((2, pair, 2 * padded), low),
            pltpu.VMEM((2, pair, padded), low),
            pltpu.VMEM((2, 2 * tok, width), low),
            pltpu.VMEM((2, 2 * tok, width), low),
            pltpu.SemaphoreType.DMA((10 * chips,)),
            pltpu.SemaphoreType.DMA((16 * CHIPS_Z,)),
            pltpu.SemaphoreType.DMA,
            pltpu.SemaphoreType.DMA((4,)),
            pltpu.SemaphoreType.DMA((2, 2)),
            pltpu.SemaphoreType.DMA((2, 6)),
        ],
        compiler_params=pltpu.CompilerParams(
            collective_id=3, has_side_effects=True, vmem_limit_bytes=60 * 2**20
        ),
        name="feed_forward",
    )(own_rows, cots, gate_weight, up_weight, down_weight, router_rows, slots, others)


def per_device_torus(
    tokens,
    cotangent,
    attention_routes,
    feedforward_routes,
    prefix_length,
    gain_attention,
    gain_feedforward,
    keyvalue_weight,
    router_weight,
    query_weight,
    output_weight,
    gate_weight,
    up_weight,
    down_weight,
):
    my_index = lax.axis_index("expert")
    group_size = lax.axis_size("expert")
    dp_size = lax.axis_size("dp")
    inputs = tokens[0].astype(jnp.float32)
    tok_rows, model_width = inputs.shape
    slot_count = 5 * 2 * tok_rows // (4 * group_size)
    query_width = HEADS * HEAD_DIM
    span = query_width // group_size
    low = jnp.bfloat16
    f32 = jnp.float32

    half = dp_size // group_size
    swap = [
        ((z * half + y) * group_size + e, (e * half + y) * group_size + z)
        for z in range(group_size)
        for y in range(half)
        for e in range(group_size)
    ]
    query_cols = lax.all_to_all(query_weight[0], "expert", split_axis=1, concat_axis=1, tiled=True)
    key_cols = lax.dynamic_slice_in_dim(keyvalue_weight, my_index * span, span, 1)
    value_cols = lax.dynamic_slice_in_dim(keyvalue_weight, query_width + my_index * span, span, 1)
    in_shard = jnp.concatenate([query_cols, key_cols, value_cols], axis=1)
    out_shard = lax.ppermute(output_weight[0], ("dp", "expert"), swap)

    normed_attention, unit_attention, factor_attention = norm_parts(inputs, gain_attention)
    attention_in = normed_attention.astype(low)
    quarters = lambda order: tuple(
        (i * tok_rows // 4, tok_rows // 4, order) for i in range(4)
    )
    rows_in = in_shard.shape[0]
    route_shard = feedforward_routes[0].astype(low).reshape(-1, 128)
    router_shard = router_weight.T.reshape(-1, 128)
    whole = lambda a: ((0, a.shape[0], "zy"),)
    out_weight = lax.all_gather(out_shard, "dp", axis=0, tiled=True)
    cut = rows_in * 13 // 16
    sequence_in, in_weight, every_route, router_full = gather(
        [
            (attention_in, "expert", quarters("xc")),
            (in_shard, "dp", ((0, cut, "zy"), (cut, rows_in - cut, "yz"))),
            (route_shard, "dp", whole(route_shard)),
            (router_shard, "dp", whole(router_shard)),
        ],
        1,
        "gather_weights",
    )
    cot_late, sequence_in = lax.optimization_barrier((cotangent[0], sequence_in))
    cot_everyone = lax.all_gather(cot_late, ("dp", "expert"), axis=0, tiled=True)
    every_route = every_route.reshape(-1, 2).astype(jnp.int32)
    router_full = (
        router_full.reshape(dp_size, 2 * group_size, rows_in)
        .transpose(0, 2, 1)
        .reshape(-1, 2 * group_size)
    )
    attention_cols = router_full[:, :group_size]
    feedforward_cols = router_full[:, group_size:]
    projected = jnp.dot(sequence_in, in_weight, preferred_element_type=f32).astype(low)
    attend_matches_all = expert_matches(attention_routes[0], group_size)
    attend_logits = jnp.dot(sequence_in, attention_cols, preferred_element_type=f32)
    attend_weights_all, _ = pair_gates(attend_logits, attend_matches_all)
    side = jnp.concatenate([attention_routes[0].astype(f32), attend_weights_all], axis=1)
    side = jnp.pad(side, ((0, 0), (0, 128 - side.shape[1])))
    mixed, log_total = attention(projected, side, prefix_length, group_size, tok_rows)
    attend_part = jnp.dot(mixed, out_weight, preferred_element_type=f32).astype(low)
    attended = scatter(attend_part, "expert", quarters("cx"), 2, "sum_attention")
    hidden = inputs + attended
    normed_feed, unit_feed, factor_feed = norm_parts(hidden, gain_feedforward)
    feed_in = normed_feed.astype(low)
    everywhere = lambda a, b: ((0, tok_rows // 2, a), (tok_rows // 2, tok_rows // 2, b))
    mine = lambda a: lax.dynamic_slice_in_dim(a, my_index * tok_rows, tok_rows, 0)
    feed_matches = expert_matches(mine(feedforward_routes[0]), group_size)
    feed_logits = jnp.dot(feed_in, feedforward_cols, preferred_element_type=f32)
    feed_weights, _ = pair_gates(feed_logits, feed_matches)
    slots, others = expert_slots(every_route, my_index, tok_rows)
    hidden_rows = gate_weight.shape[1]
    padded = -(-hidden_rows // 256) * 256
    router_rows = jnp.pad(
        feedforward_cols.T, ((0, padded - hidden_rows - group_size), (0, 0))
    )
    _, dx_part, out_part, kept_rows, kept_cots, kept_back, kept_act, token_dgate = feed(
        feed_in,
        cot_everyone,
        gate_weight[0],
        up_weight[0],
        down_weight[0],
        router_rows,
        slots,
        others,
        slot_count,
    )
    grad_in_feed = lax.dot_general(kept_back, kept_rows, DOWNWARD, preferred_element_type=f32)
    grad_gate = grad_in_feed[:hidden_rows]
    grad_up = grad_in_feed[padded : padded + hidden_rows]
    grad_down = lax.dot_general(
        kept_act[:, :hidden_rows], kept_cots, DOWNWARD, preferred_element_type=f32
    )
    own_row = (jnp.arange(group_size) == my_index).astype(f32)[None, :, None]
    feed_dgate = lax.psum_scatter(
        (token_dgate[:, None, :] * own_row).reshape(-1, tok_rows),
        ("dp", "expert"),
        scatter_dimension=0,
        tiled=True,
    ).T
    feed_home = scatter(dx_part, "all", everywhere("cxyz", "cyxz"), 4, "sum_rows")
    feed_sum = lax.psum_scatter(
        out_part,
        ("dp", "expert"),
        scatter_dimension=0,
        tiled=True,
    ).astype(f32)
    layer_output = hidden + feed_sum
    gradient = cotangent[0].astype(f32)
    feed_dlogits = gates_back(feed_dgate, feed_weights, feed_matches)
    feed_dnorm = feed_home + jnp.dot(feed_dlogits, feedforward_cols.astype(f32).T, precision=HIGH)
    grad_gain_feed = jnp.sum(feed_dnorm * unit_feed, axis=0)
    hidden_grad = gradient + norm_back(feed_dnorm, gain_feedforward, unit_feed, factor_feed)

    (sequence_grad,) = gather(
        [(hidden_grad.astype(low), "expert", quarters("xc"))], 5, "gather_cotangents"
    )
    dmix = lax.dot_general(sequence_grad, out_weight, ACROSS, preferred_element_type=f32).astype(low)
    grad_out = lax.dot_general(mixed, sequence_grad, DOWNWARD, preferred_element_type=f32)
    dprojected, gate_parts = attention_back(
        projected, side, prefix_length, log_total, dmix, group_size, tok_rows
    )
    attend_dx = lax.dot_general(dprojected, in_weight, ACROSS, preferred_element_type=f32)
    grad_in = lax.dot_general(sequence_in, dprojected, DOWNWARD, preferred_element_type=f32)
    attend_home = scatter(attend_dx.astype(low), "expert", quarters("cx"), 2, "sum_attention")
    pair_dgate = lax.psum_scatter(
        gate_parts[:, :2].reshape(group_size, tok_rows, 2).transpose(0, 2, 1).reshape(-1, tok_rows),
        "expert",
        scatter_dimension=0,
        tiled=True,
    ).T
    matches = mine(attend_matches_all)
    weights = mine(attend_weights_all)
    dselected = weights * (pair_dgate - jnp.sum(weights * pair_dgate, axis=1, keepdims=True))
    attend_dlogits = jnp.sum(dselected[:, :, None] * matches, axis=1)
    attend_dnorm = attend_home + jnp.dot(
        attend_dlogits, attention_cols.astype(f32).T, precision=HIGH
    )
    grad_gain_attend = jnp.sum(attend_dnorm * unit_attention, axis=0)
    grad_tokens = hidden_grad + norm_back(
        attend_dnorm, gain_attention, unit_attention, factor_attention
    )
    small = jnp.concatenate(
        [
            lax.dot_general(attend_dlogits, attention_in.astype(f32), DOWNWARD, precision=HIGH),
            lax.dot_general(feed_dlogits, feed_in.astype(f32), DOWNWARD, precision=HIGH),
            grad_gain_attend[None],
            grad_gain_feed[None],
        ],
        axis=0,
    )
    small = lax.psum(small.astype(f32), ("dp", "expert"))
    small = lax.dynamic_slice_in_dim(small, lax.axis_index("dp") * rows_in, rows_in, 1)

    down_dp = ((0, rows_in, "yz"),)
    out_rows = scatter(grad_out.astype(low), "dp", down_dp, 6, "sum_output_weight")
    in_rows = scatter(grad_in.astype(low), "dp", down_dp, 7, "sum_input_weight").astype(low)
    grad_projection = lax.ppermute(out_rows.astype(low), ("dp", "expert"), swap).astype(f32)
    wide = group_size * span
    grad_query = lax.all_to_all(
        in_rows[:, :wide], "expert", split_axis=1, concat_axis=1, tiled=True
    ).astype(f32)
    grad_keyvalue = lax.all_gather(in_rows[:, wide:], "expert", axis=0, tiled=False)
    grad_keyvalue = (
        grad_keyvalue.reshape(group_size, rows_in, 2, span)
        .transpose(1, 2, 0, 3)
        .reshape(rows_in, 2 * query_width)
        .astype(f32)
    )
    return (
        layer_output.astype(low)[None],
        grad_tokens[None],
        small[2 * group_size],
        small[2 * group_size + 1],
        grad_keyvalue,
        small[: 2 * group_size].T,
        grad_query[None],
        grad_projection[None],
        grad_gate[None],
        grad_up[None],
        grad_down[None],
    )


def solution(mesh):
    in_specs = (
        P("dp", "expert", None),
        P("dp", "expert", None),
        P("dp", None, None),
        P("dp", None, None),
        P("dp"),
        P(),
        P(),
        P("dp", None),
        P("dp", None),
        P("expert", "dp", None),
        P("expert", "dp", None),
        P("expert", "dp", None),
        P("expert", "dp", None),
        P("expert", "dp", None),
    )
    out_specs = (
        P("dp", "expert", None),
        P("dp", "expert", None),
        P("dp"),
        P("dp"),
        P("dp", None),
        P("dp", None),
        P("expert", "dp", None),
        P("expert", "dp", None),
        P("expert", "dp", None),
        P("expert", "dp", None),
        P("expert", "dp", None),
    )
    torus = (mesh.shape["dp"], mesh.shape["expert"]) == (8, 4)
    body = per_device_torus if torus else per_device
    return jax.shard_map(
        body, mesh=mesh, in_specs=in_specs, out_specs=out_specs, check_vma=False
    )
```

```python
import functools

import jax
import jax.numpy as jnp
from jax import lax
from jax.experimental import pallas as pl
from jax.experimental.pallas import tpu as pltpu
from jax.sharding import PartitionSpec as P

HEADS = 16
HEAD_DIM = 128


EPS = 1e-06
NEG = -1e30
HIGH = lax.Precision.HIGHEST
ACROSS = (((1,), (1,)), ((), ()))
DOWNWARD = (((0,), (0,)), ((), ()))


def norm_parts(vector, gain_vector):
    factor = lax.rsqrt(jnp.mean(vector * vector, axis=-1, keepdims=True) + EPS)
    normed = vector * factor
    return (normed * gain_vector, normed, factor)


def norm_back(incoming, gain_vector, normed, factor):
    dnormed = incoming * gain_vector
    return factor * (dnormed - normed * jnp.mean(dnormed * normed, axis=-1, keepdims=True))


def route_plan(sequence_ids, my_index, group_size, tok_rows, slot_count):
    expert_range = jnp.arange(group_size, dtype=jnp.int32)
    matches_all = (sequence_ids[:, :, None] == expert_range[None, None, :]).astype(jnp.int32)
    chosen = jnp.sum(matches_all, axis=1).reshape(group_size, tok_rows, group_size)
    ranking = jnp.cumsum(chosen, axis=1) - chosen
    slot_ids = jnp.arange(slot_count, dtype=jnp.int32)[None, :, None]
    block_pick = (expert_range == my_index).astype(jnp.int32)
    my_chosen = jnp.sum(chosen * block_pick[:, None, None], axis=0).T
    my_ranking = jnp.sum(ranking * block_pick[:, None, None], axis=0).T
    send_table = (
        my_chosen[:, None, :] * (my_ranking[:, None, :] == slot_ids).astype(jnp.int32)
    ).astype(jnp.float32)
    column_chosen = jnp.sum(chosen * block_pick[None, None, :], axis=2)
    column_ranking = jnp.sum(ranking * block_pick[None, None, :], axis=2)
    taken = column_chosen[:, None, :] * (column_ranking[:, None, :] == slot_ids).astype(jnp.int32)
    positions = (
        expert_range[:, None, None] * tok_rows
        + jnp.arange(tok_rows, dtype=jnp.int32)[None, None, :]
    )
    arrival_places = jnp.sum(taken * positions, axis=2).reshape(-1)
    my_ids = lax.dynamic_slice_in_dim(sequence_ids, my_index * tok_rows, tok_rows, 0)
    matches = (my_ids[:, :, None] == expert_range[None, None, :]).astype(jnp.float32)
    return (send_table, arrival_places, matches)


def pair_gates(logits, matches):
    selected = jnp.sum(matches * logits[:, None, :], axis=2)
    largest = jnp.max(selected, axis=1, keepdims=True)
    exponent = jnp.exp(selected - largest)
    weights = exponent / jnp.sum(exponent, axis=1, keepdims=True)
    return (weights, jnp.sum(weights[:, :, None] * matches, axis=1))


def gates_back(dgate, weights, matches):
    dweights = jnp.sum(dgate[:, None, :] * matches, axis=2)
    dselected = weights * (dweights - jnp.sum(weights * dweights, axis=1, keepdims=True))
    return jnp.sum(dselected[:, :, None] * matches, axis=1)


def merge_back(send_table, gate_table, returned):
    weighted = send_table * gate_table.T[:, None, :]
    return jnp.einsum("ect,ecd->td", weighted, returned.astype(jnp.float32), precision=HIGH)


def branch_cotangent(send_table, gate_table, returned, incoming):
    spread_grad = jnp.einsum("ect,td->ecd", send_table, incoming, precision=HIGH)
    slot_gate = jnp.sum(send_table * gate_table.T[:, None, :], axis=2)
    cotangent_rows = (spread_grad * slot_gate[:, :, None]).astype(jnp.bfloat16)
    slot_dgate = jnp.sum(spread_grad * returned.astype(jnp.float32), axis=2)
    dgate = jnp.einsum("ect,ec->te", send_table, slot_dgate, precision=HIGH)
    return (cotangent_rows, dgate)


def expert_matches(ids, group_size):
    expert_range = jnp.arange(group_size, dtype=jnp.int32)
    return (ids[:, :, None] == expert_range[None, None, :]).astype(jnp.float32)


def expert_table(ids, my_index, group_size, tok_rows, slot_count):
    blocks = ids.reshape(-1, tok_rows, 2)
    chosen = jnp.sum((blocks == my_index).astype(jnp.float32), axis=2)
    before = jnp.triu(jnp.ones((tok_rows, tok_rows), jnp.float32), 1)
    ranking = jnp.dot(chosen, before)
    slot_ids = jnp.arange(slot_count, dtype=jnp.float32)[None, :, None]
    taken = chosen[:, None, :] * (ranking[:, None, :] == slot_ids).astype(jnp.float32)
    other = jnp.sum(blocks, axis=2) - my_index
    slot_other = jnp.sum(taken * other[:, None, :].astype(jnp.float32), axis=2)
    return (taken.astype(jnp.bfloat16), slot_other.reshape(-1).astype(jnp.int32))


def own_gate(logits, other, my_index):
    expert_range = jnp.arange(logits.shape[1], dtype=jnp.int32)[None]
    mine = jnp.sum(jnp.where(expert_range == my_index, logits, 0.0), axis=1, keepdims=True)
    theirs = jnp.sum(jnp.where(expert_range == other[:, None], logits, 0.0), axis=1, keepdims=True)
    return jax.nn.sigmoid(mine - theirs)


def pick_rows(taken, rows):
    blocks, slots, tokens = taken.shape
    picked = jnp.einsum(
        "bct,btd->bcd",
        taken,
        rows.reshape(blocks, tokens, -1),
        preferred_element_type=jnp.float32,
    )
    return picked.astype(jnp.bfloat16).reshape(blocks * slots, -1)


def return_rows(taken, rows):
    blocks, slots, tokens = taken.shape
    placed = jnp.einsum(
        "bct,bcd->btd",
        taken,
        rows.reshape(blocks, slots, -1),
        preferred_element_type=jnp.float32,
    )
    return placed.astype(jnp.bfloat16).reshape(blocks * tokens, -1)


def gather_all(rows):
    return lax.all_gather(rows, ("dp", "expert"), axis=0, tiled=True)


def scatter_all(rows):
    return lax.psum_scatter(rows, ("dp", "expert"), scatter_dimension=0, tiled=True)


def dispatch(rows):
    return lax.all_to_all(rows, "expert", split_axis=0, concat_axis=0, tiled=True)


def collect(rows):
    return lax.all_to_all(rows, "expert", split_axis=0, concat_axis=0, tiled=True)


def spread_rows(rows):
    return lax.all_gather(rows, "dp", axis=0, tiled=True)


def sum_rows(terms):
    return lax.psum_scatter(
        terms.astype(jnp.bfloat16), "dp", scatter_dimension=0, tiled=True
    ).astype(jnp.float32)


def send_rows(send_table, rows):
    return jnp.einsum(
        "ect,td->ecd", send_table.astype(jnp.bfloat16), rows, preferred_element_type=jnp.float32
    ).astype(jnp.bfloat16)


def per_device(
    tokens,
    cotangent,
    attention_routes,
    feedforward_routes,
    prefix_length,
    gain_attention,
    gain_feedforward,
    keyvalue_weight,
    router_weight,
    query_weight,
    output_weight,
    gate_weight,
    up_weight,
    down_weight,
):
    my_index = lax.axis_index("expert")
    group_size = lax.axis_size("expert")
    inputs = tokens[0].astype(jnp.float32)
    tok_rows = inputs.shape[0]
    model_width = inputs.shape[1]
    seq_total = tok_rows * group_size
    slot_count = 5 * 2 * tok_rows // (4 * group_size)
    query_width = HEADS * HEAD_DIM
    scaling = HEAD_DIM ** (-0.5)
    keyvalue_full, router_full, query_full, output_full = (
        lax.all_gather(keyvalue_weight, "dp", axis=0, tiled=True),
        lax.all_gather(router_weight, "dp", axis=0, tiled=True),
        lax.all_gather(query_weight[0], "dp", axis=0, tiled=True),
        lax.all_gather(output_weight[0], "dp", axis=0, tiled=True),
    )
    every_route = lax.all_gather(feedforward_routes[0], "dp", axis=0, tiled=True)
    cot_everyone = gather_all(cotangent[0])
    attention_cols = router_full[:, :group_size]
    feedforward_cols = router_full[:, group_size:]
    normed_attention, unit_attention, factor_attention = norm_parts(inputs, gain_attention)
    attention_in = normed_attention.astype(jnp.bfloat16)
    keyvalue_rows = jnp.dot(attention_in, keyvalue_full, preferred_element_type=jnp.float32).astype(
        jnp.bfloat16
    )
    keyvalue_seq = lax.all_gather(keyvalue_rows, "expert", axis=0, tiled=True)
    key_rows = keyvalue_seq[:, :query_width].reshape(seq_total, HEADS, HEAD_DIM)
    value_rows = keyvalue_seq[:, query_width:].reshape(seq_total, HEADS, HEAD_DIM)
    attend_table, attend_places, attend_matches = route_plan(
        attention_routes[0], my_index, group_size, tok_rows, slot_count
    )
    attend_logits = jnp.dot(attention_in, attention_cols, preferred_element_type=jnp.float32)
    attend_weights, attend_gate = pair_gates(attend_logits, attend_matches)
    arrived = dispatch(send_rows(attend_table, attention_in)).reshape(-1, model_width)
    queries = jnp.dot(arrived, query_full, preferred_element_type=jnp.float32).astype(jnp.bfloat16)
    queries = queries.reshape(-1, HEADS, HEAD_DIM)
    key_places = jnp.arange(seq_total, dtype=jnp.int32)
    allowed = (key_places[None, :] <= attend_places[:, None]) | (
        key_places[None, :] < prefix_length[0]
    )
    scores = (
        jnp.einsum("rhd,khd->hrk", queries, key_rows, preferred_element_type=jnp.float32) * scaling
    )
    scores = jnp.where(allowed[None], scores, NEG)
    row_max = jnp.max(scores, axis=2, keepdims=True)
    exponent = jnp.exp(scores - row_max)
    row_total = jnp.sum(exponent, axis=2, keepdims=True)
    log_total = row_max + jnp.log(row_total)
    attention_low = (exponent / row_total).astype(jnp.bfloat16)
    mixture = jnp.einsum(
        "hrk,khd->rhd", attention_low, value_rows, preferred_element_type=jnp.float32
    )
    mixture = mixture.astype(jnp.bfloat16).reshape(-1, query_width)
    attend_branch = jnp.dot(mixture, output_full, preferred_element_type=jnp.float32).astype(
        jnp.bfloat16
    )
    attend_returned = collect(attend_branch.reshape(group_size, slot_count, model_width))
    hidden = inputs + merge_back(attend_table, attend_gate, attend_returned)
    normed_feed, unit_feed, factor_feed = norm_parts(hidden, gain_feedforward)
    feed_in = normed_feed.astype(jnp.bfloat16)
    feed_ids = lax.dynamic_slice_in_dim(
        feedforward_routes[0], my_index * tok_rows, tok_rows, 0
    )
    feed_matches = expert_matches(feed_ids, group_size)
    feed_logits = jnp.dot(feed_in, feedforward_cols, preferred_element_type=jnp.float32)
    feed_weights, feed_gate = pair_gates(feed_logits, feed_matches)
    everyone = gather_all(feed_in)
    feed_taken, feed_pairs = expert_table(every_route, my_index, group_size, tok_rows, slot_count)
    pick = functools.partial(pick_rows, feed_taken)
    feed_rows = pick(everyone)
    cot_rows = pick(cot_everyone)
    row_logits = jnp.dot(feed_rows, feedforward_cols, preferred_element_type=jnp.float32)
    row_gate = own_gate(row_logits, feed_pairs, my_index)
    pre_gate = lax.dot_general(feed_rows, gate_weight[0], ACROSS, preferred_element_type=jnp.float32)
    pre_up = lax.dot_general(feed_rows, up_weight[0], ACROSS, preferred_element_type=jnp.float32)
    sigmoid_gate = jax.nn.sigmoid(pre_gate)
    act = pre_gate * sigmoid_gate * pre_up
    act_low = act.astype(jnp.bfloat16)
    act_scaled = (act * row_gate).astype(jnp.bfloat16)
    act_grad = lax.dot_general(cot_rows, down_weight[0], ACROSS, preferred_element_type=jnp.float32)
    slot_dgate = jnp.sum(act_low.astype(jnp.float32) * act_grad, axis=1)
    act_grad = act_grad * row_gate
    dgate_low = (act_grad * pre_up * sigmoid_gate * (1.0 + pre_gate * (1.0 - sigmoid_gate))).astype(
        jnp.bfloat16
    )
    dup_low = (act_grad * pre_gate * sigmoid_gate).astype(jnp.bfloat16)
    feed_dx = (
        jnp.dot(dgate_low, gate_weight[0], preferred_element_type=jnp.float32)
        + jnp.dot(dup_low, up_weight[0], preferred_element_type=jnp.float32)
    ).astype(jnp.bfloat16)
    feed_branch = jnp.dot(act_scaled, down_weight[0], preferred_element_type=jnp.float32).astype(
        jnp.bfloat16
    )
    grad_gate = lax.dot_general(dgate_low, feed_rows, DOWNWARD, preferred_element_type=jnp.float32)
    grad_up = lax.dot_general(dup_low, feed_rows, DOWNWARD, preferred_element_type=jnp.float32)
    grad_down = lax.dot_general(act_scaled, cot_rows, DOWNWARD, preferred_element_type=jnp.float32)
    token_dgate = jnp.einsum(
        "bct,bc->bt",
        feed_taken.astype(jnp.float32),
        slot_dgate.reshape(-1, slot_count),
        precision=HIGH,
    ).reshape(-1, 1)
    own_column = (jnp.arange(group_size) == my_index).astype(jnp.float32)[None]
    feed_dgate = scatter_all(token_dgate * own_column)
    feed_home = scatter_all(return_rows(feed_taken, feed_dx)).astype(jnp.float32)
    feed_sum = scatter_all(return_rows(feed_taken, feed_branch)).astype(jnp.float32)
    layer_output = hidden + feed_sum
    gradient = cotangent[0].astype(jnp.float32)
    feed_dlogits = gates_back(feed_dgate, feed_weights, feed_matches)
    feed_dnorm = feed_home + jnp.dot(
        feed_dlogits, feedforward_cols.astype(jnp.float32).T, precision=HIGH
    )
    grad_gain_feed = jnp.sum(feed_dnorm * unit_feed, axis=0)
    hidden_grad = gradient + norm_back(feed_dnorm, gain_feedforward, unit_feed, factor_feed)
    attend_cot, attend_dgate = branch_cotangent(
        attend_table, attend_gate, attend_returned, hidden_grad
    )
    attend_dlogits = gates_back(attend_dgate, attend_weights, attend_matches)
    attend_cot_rows = dispatch(attend_cot).reshape(-1, model_width)
    dmixture = lax.dot_general(
        attend_cot_rows, output_full, ACROSS, preferred_element_type=jnp.float32
    )
    dmixture = dmixture.astype(jnp.bfloat16).reshape(-1, HEADS, HEAD_DIM)
    grad_projection = lax.dot_general(
        mixture, attend_cot_rows, DOWNWARD, preferred_element_type=jnp.float32
    )
    scores_again = (
        jnp.einsum("rhd,khd->hrk", queries, key_rows, preferred_element_type=jnp.float32) * scaling
    )
    attention = jnp.where(allowed[None], jnp.exp(scores_again - log_total), 0.0)
    attention_again = attention.astype(jnp.bfloat16)
    dattention = jnp.einsum(
        "rhd,khd->hrk", dmixture, value_rows, preferred_element_type=jnp.float32
    )
    row_dot = jnp.sum(attention * dattention, axis=2, keepdims=True)
    dscores = (attention * (dattention - row_dot)).astype(jnp.bfloat16)
    dqueries = (
        jnp.einsum("hrk,khd->rhd", dscores, key_rows, preferred_element_type=jnp.float32) * scaling
    )
    dqueries = dqueries.astype(jnp.bfloat16).reshape(-1, query_width)
    dkeys = (
        jnp.einsum("hrk,rhd->khd", dscores, queries, preferred_element_type=jnp.float32) * scaling
    )
    dvalues = jnp.einsum(
        "hrk,rhd->khd", attention_again, dmixture, preferred_element_type=jnp.float32
    )
    grad_query = lax.dot_general(arrived, dqueries, DOWNWARD, preferred_element_type=jnp.float32)
    attend_dx = lax.dot_general(dqueries, query_full, ACROSS, preferred_element_type=jnp.float32)
    keyvalue_terms = jnp.concatenate(
        [dkeys.reshape(seq_total, query_width), dvalues.reshape(seq_total, query_width)], axis=1
    ).reshape(group_size, tok_rows, 2 * query_width)
    attend_home, keyvalue_home = (
        lax.all_to_all(
            attend_dx.reshape(group_size, slot_count, model_width).astype(jnp.bfloat16),
            "expert",
            split_axis=0,
            concat_axis=0,
            tiled=True,
        ).astype(jnp.float32),
        lax.all_to_all(
            keyvalue_terms.astype(jnp.bfloat16), "expert", split_axis=0, concat_axis=0, tiled=True
        ).astype(keyvalue_terms.dtype),
    )
    dkeyvalue = jnp.sum(keyvalue_home, axis=0).astype(jnp.bfloat16)
    attend_dnorm = (
        jnp.einsum("ect,ecd->td", attend_table, attend_home, precision=HIGH)
        + lax.dot_general(dkeyvalue, keyvalue_full, ACROSS, preferred_element_type=jnp.float32)
        + jnp.dot(attend_dlogits, attention_cols.astype(jnp.float32).T, precision=HIGH)
    )
    grad_keyvalue = lax.dot_general(
        attention_in, dkeyvalue, DOWNWARD, preferred_element_type=jnp.float32
    )
    grad_router = jnp.concatenate(
        [
            jnp.dot(attention_in.astype(jnp.float32).T, attend_dlogits, precision=HIGH),
            jnp.dot(feed_in.astype(jnp.float32).T, feed_dlogits, precision=HIGH),
        ],
        axis=1,
    )
    grad_gain_attend = jnp.sum(attend_dnorm * unit_attention, axis=0)
    grad_tokens = hidden_grad + norm_back(
        attend_dnorm, gain_attention, unit_attention, factor_attention
    )
    reduced = (
        lax.psum_scatter(
            grad_keyvalue.astype(jnp.bfloat16), "dp", scatter_dimension=0, tiled=True
        ).astype(jnp.float32),
        lax.psum_scatter(
            grad_router.astype(jnp.bfloat16), "dp", scatter_dimension=0, tiled=True
        ).astype(jnp.float32),
        lax.psum_scatter(
            grad_query.astype(jnp.bfloat16), "dp", scatter_dimension=0, tiled=True
        ).astype(jnp.float32),
        lax.psum_scatter(
            grad_projection.astype(jnp.bfloat16), "dp", scatter_dimension=0, tiled=True
        ).astype(jnp.float32),
        lax.psum_scatter(
            grad_gain_attend.astype(jnp.bfloat16), "dp", scatter_dimension=0, tiled=True
        ).astype(jnp.float32),
        lax.psum_scatter(
            grad_gain_feed.astype(jnp.bfloat16), "dp", scatter_dimension=0, tiled=True
        ).astype(jnp.float32),
    )
    shared = (
        lax.psum(reduced[0].astype(jnp.bfloat16), "expert").astype(jnp.float32),
        lax.psum(reduced[1].astype(jnp.bfloat16), "expert").astype(jnp.float32),
        lax.psum(reduced[4].astype(jnp.bfloat16), "expert").astype(jnp.float32),
        lax.psum(reduced[5].astype(jnp.bfloat16), "expert").astype(jnp.float32),
    )
    return (
        layer_output.astype(jnp.bfloat16)[None],
        grad_tokens[None],
        shared[2],
        shared[3],
        shared[0],
        shared[1],
        reduced[2][None],
        reduced[3][None],
        grad_gate[None],
        grad_up[None],
        grad_down[None],
    )


MESH = pl.DeviceIdType.MESH
CHIPS_Z = 4
TURNS = ((3, 2, 1, 0), (3, 0, 2, 1), (0, 3, 1, 2), (0, 1, 2, 3))


class Place:
    def __init__(self):
        self.dp, self.expert = lax.axis_index("dp"), lax.axis_index("expert")
        self.at = {
            "z": self.dp // 2,
            "y": self.dp % 2,
            "x": self.expert // 2,
            "c": self.expert % 2,
        }

    def across(self, axis):
        back = 1 - 2 * self.at[axis]
        if axis == "c":
            return (self.dp, self.expert + back)
        if axis == "x":
            return (self.dp, self.expert + 2 * back)
        return (self.dp + back, self.expert)

    def along(self, step):
        return (self.dp + 2 * step, self.expert)

    def block(self, whose, z, flips):
        at = {a: self.at[a] + flips.get(a, 0) * (1 - 2 * self.at[a]) for a in "xyc"}
        dp, expert = z * 2 + at["y"], at["x"] * 2 + at["c"]
        return {"all": dp * 4 + expert, "dp": dp, "expert": expert}[whose]


def enter(place, axes, others=()):
    barrier, count = pltpu.get_barrier_semaphore(), 0
    for device, condition in others:

        def greet(device=device):
            pl.semaphore_signal(barrier, inc=1, device_id=device, device_id_type=MESH)

        on(condition, greet)
        count = count + (1 if condition is None else condition.astype(jnp.int32))
    for axis in axes:
        if axis != "z":
            pl.semaphore_signal(
                barrier, inc=1, device_id=place.across(axis), device_id_type=MESH
            )
            count += 1
    if "z" in axes:
        z = place.at["z"]
        for step, there in ((-1, z > 0), (1, z < CHIPS_Z - 1)):

            @pl.when(there)
            def _(step=step):
                pl.semaphore_signal(
                    barrier, inc=1, device_id=place.along(step), device_id_type=MESH
                )

            count = count + there.astype(jnp.int32)
    pl.semaphore_wait(barrier, count)


def on(condition, action):
    if condition is None:
        action()
    else:
        pl.when(condition)(action)


def both(a, b):
    return b if a is None else a if b is None else a & b


class Post:
    def __init__(self, sems, place):
        self.sems, self.place, self.sent = sems, place, []

    def send(self, source, target, arrival, device, condition=None):
        number = len(self.sent)

        def copy():
            return pltpu.make_async_remote_copy(
                src_ref=source,
                dst_ref=target,
                send_sem=self.sems.at[number],
                recv_sem=arrival,
                device_id=device,
                device_id_type=MESH,
            )

        self.sent.append((condition, copy))
        on(condition, lambda: copy().start())

    def arrived(self, target, arrival):
        pltpu.make_async_remote_copy(
            src_ref=target,
            dst_ref=target,
            send_sem=self.sems.at[0],
            recv_sem=arrival,
            device_id=self.place.across("c"),
            device_id_type=MESH,
        ).wait_recv()

    def close(self):
        for condition, copy in self.sent:
            on(condition, lambda copy=copy: copy().wait_send())


FLIPS = {"x": 4, "y": 2, "c": 1}


def gather_plan(jobs, place, post, sources, targets, arrive_sems, own_sems):
    z_here = place.at["z"]
    line = 0
    waves, owns, starts = {}, [], []
    for j, (whose, rows, pieces) in enumerate(jobs):
        own = pltpu.make_async_copy(
            sources[j],
            targets[j].at[pl.ds(place.block(whose, z_here, {}) * rows, rows)],
            own_sems.at[j],
        )
        owns.append(own)
        begin = [own.start]
        for first, length, order in pieces:
            def part(z, flips, j=j, whose=whose, rows=rows, first=first, length=length):
                at = place.block(whose, z, flips) * rows + first
                return targets[j].at[pl.ds(at, length)]

            def mark(z, flips, line=line):
                return arrive_sems.at[line, z * 8 + sum(FLIPS[a] * v for a, v in flips.items())]

            def hand_on(source, z, flips, depth, side, wave, condition, order=order, part=part, mark=mark):
                for axis in order[max(depth, 0) :]:
                    if axis == "z" and (depth < 0 or order[depth] != "z"):
                        for step in (1, -1):
                            there = (z_here < CHIPS_Z - 1) if step > 0 else (z_here > 0)
                            post.send(source, part(z, flips), mark(z, flips), place.along(step), both(condition, there))
                    elif axis == "z":
                        there = (z_here < CHIPS_Z - 1) if side > 0 else (z_here > 0)
                        post.send(source, part(z, flips), mark(z, flips), place.along(side), both(condition, there))
                    elif depth < 0 or axis != order[depth]:
                        seen = dict(flips)
                        seen[axis] = 1
                        post.send(source, part(z, flips), mark(z, seen), place.across(axis), condition)

            def come(z, flips, depth, side, hops, wave, condition, order=order, part=part, mark=mark, hand_on=hand_on):
                def act():
                    on(condition, lambda: post.arrived(part(z, flips), mark(z, flips)))
                    hand_on(part(z, flips), z, flips, depth, side, wave, condition)

                waves.setdefault(wave, []).append(act)
                spread(z, flips, depth, side, hops, wave, condition, order, come)

            begin.append(
                lambda hand_on=hand_on, j=j, first=first, length=length: hand_on(
                    sources[j].at[pl.ds(first, length)], z_here, {}, -1, 0, 0, None
                )
            )
            spread(z_here, {}, -1, 0, 0, 0, None, order, come)
            line += 1
        starts.append(begin)
    return starts, waves, owns


def gather_kernel(jobs, axes, *refs):
    count = len(jobs)
    sources, targets = refs[:count], refs[count : 2 * count]
    send_sems, arrive_sems, own_sems = refs[2 * count :]
    place = Place()
    enter(place, axes)
    post = Post(send_sems, place)
    starts, waves, owns = gather_plan(jobs, place, post, sources, targets, arrive_sems, own_sems)
    for act in sum(starts, []):
        act()
    for wave in sorted(waves):
        for act in waves[wave]:
            act()
    for own in owns:
        own.wait()
    post.close()


def spread(z, flips, depth, side, hops, wave, condition, order, come):
    z_here = lax.axis_index("dp") // 2
    for later in range(max(depth, 0), len(order)):
        axis = order[later]
        if axis == "z":
            if depth >= 0 and order[depth] == "z":
                if hops < CHIPS_Z - 1:
                    far = hops + 1
                    there = (z_here >= far) if side > 0 else (z_here + far < CHIPS_Z)
                    come(z_here - side * far, flips, later, side, far, wave + 1, there)
            else:
                for step in (1, -1):
                    there = (z_here >= 1) if step > 0 else (z_here + 1 < CHIPS_Z)
                    come(z_here - step, flips, later, step, 1, wave + 1, both(condition, there))
        elif later > depth:
            seen = dict(flips)
            seen[axis] = 1
            come(z, seen, later, 0, 0, wave + 1, condition)


def gather(jobs, collective_id, name):
    arrays = [rows for rows, _, _ in jobs]
    sizes = {"all": 32, "dp": 8, "expert": 4}
    plan = tuple((whose, rows.shape[0], pieces) for rows, whose, pieces in jobs)
    axes = "".join(a for a in "cxyz" if any(a in order for _, _, ps in plan for _, _, order in ps))
    lines = sum(len(ps) for _, _, ps in plan)
    any_spec = pl.BlockSpec(memory_space=pltpu.HBM)
    return pl.pallas_call(
        functools.partial(gather_kernel, plan, axes),
        out_shape=[
            jax.ShapeDtypeStruct((sizes[whose] * r.shape[0], r.shape[1]), r.dtype)
            for r, whose, _ in jobs
        ],
        in_specs=[any_spec] * len(jobs),
        out_specs=[any_spec] * len(jobs),
        scratch_shapes=[
            pltpu.SemaphoreType.DMA((110 * lines,)),
            pltpu.SemaphoreType.DMA((lines, 32)),
            pltpu.SemaphoreType.DMA((len(jobs),)),
        ],
        compiler_params=pltpu.CompilerParams(
            collective_id=collective_id, has_side_effects=True
        ),
        name=name,
    )(*arrays)


def scatter_kernel(whose, rows, pieces, source, _, result, acc, *refs):
    place = Place()
    orders = [order for _, _, order in pieces]
    flat = [order.replace("z", "") for order in orders]
    steps = len(flat[0])
    lined = "z" in orders[0]
    turns = CHIPS_Z if lined else 1
    bins = refs[:steps]
    line = refs[steps] if lined else None
    send_sems, load_sems, bin_sems, line_sems = refs[-4:]
    z_here = place.at["z"]
    if lined:
        turn = [
            sum((z_here == z).astype(jnp.int32) * seq[k] for z, seq in enumerate(TURNS))
            for k in range(CHIPS_Z)
        ]
    else:
        turn = [z_here]
    slot_z = lambda k: turn[k] if lined else 0
    post = Post(send_sems, place)

    def flips_of(p, stage, code):
        later = flat[p][stage + 1 :]
        flips = {a: (code >> i) & 1 for i, a in enumerate(later)}
        if stage < steps:
            flips[flat[p][stage]] = 1
        return flips

    def kept(p, flips):
        names = sorted(flat[p][1:])
        return sum(flips.get(a, 0) << i for i, a in enumerate(names))

    def code_after(p, stage, flips):
        return sum(flips.get(a, 0) << i for i, a in enumerate(flat[p][stage + 1 :]))

    keep = 2 ** (steps - 1)
    names = sorted(flat[0][1:])
    loads = {}
    for k in range(turns):
        for n in reversed(range(keep)):
            flips = {a: (n >> i) & 1 for i, a in enumerate(names)}
            at = slot_z(k) * keep + n
            loads[k, n] = pltpu.make_async_copy(
                source.at[pl.ds(place.block(whose, turn[k], flips) * rows, rows)],
                acc.at[at],
                load_sems.at[at],
            )
            loads[k, n].start()
    enter(place, "".join(flat[0]) + ("z" if lined else ""))
    loaded = set()

    def add(target, terms, length):
        @pl.loop(0, length // 16)
        def _(r):
            at = pl.ds(pl.multiple_of(r * 16, 16), 16)
            total = target[at, :].astype(jnp.float32)
            for term in terms:
                total = total + term[at, :].astype(jnp.float32)
            target[at, :] = total.astype(jnp.bfloat16)

    def mine(p, ref):
        first, length, _ = pieces[p]
        return ref.at[pl.ds(first, length)]

    def gathered(p, k, stage, flips):
        n = kept(p, flips)
        at = slot_z(k) * keep + n
        if (k, n) not in loaded:
            loads[k, n].wait()
            loaded.add((k, n))
        terms = []
        for before in range(stage):
            code = code_after(p, before, flips)
            width = 2 ** (steps - 1 - before)
            ref = mine(p, bins[before].at[slot_z(k) * width + code])
            post.arrived(ref, bin_sems.at[p, before, slot_z(k) * width + code])
            terms.append(ref)
        block = mine(p, acc.at[at])
        add(block, terms, pieces[p][1])
        return block

    def leave(p, k, stage, code, block, flips):
        axis = flat[p][stage]
        width = 2 ** (steps - 1 - stage)
        at = slot_z(k) * width + code
        post.send(block, mine(p, bins[stage].at[at]), bin_sems.at[p, stage, at], place.across(axis))

    def work(k, stage):
        if stage < steps:
            for code in reversed(range(2 ** (steps - 1 - stage))):
                for p in range(len(pieces)):
                    flips = flips_of(p, stage, code)
                    if stage == 0:
                        first, length, _ = pieces[p]
                        at = place.block(whose, turn[k], flips) * rows + first
                        leave(p, k, stage, code, source.at[pl.ds(at, length)], flips)
                    else:
                        leave(p, k, stage, code, gathered(p, k, stage, flips), flips)
            return
        for p in range(len(pieces)):
            block = gathered(p, k, steps, {})
            if not lined or k == turns - 1:
                continue
            t = turn[k]
            right = t > z_here

            def pass_on(p=p, t=t, block=block):
                ref = mine(p, line.at[t])
                post.arrived(ref, line_sems.at[p, t])
                add(block, [ref], pieces[p][1])

            pl.when((right & (z_here > 0)) | (~right & (z_here < CHIPS_Z - 1)))(pass_on)
            slot = jnp.where(t == z_here - 1, CHIPS_Z, t)
            post.send(
                block,
                mine(p, line.at[slot]),
                line_sems.at[p, slot],
                place.along(jnp.where(right, 1, -1)),
            )

    for k in range(turns):
        work(k, 0)
    for time in range(turns + steps):
        for stage in range(1, steps + 1):
            k = time - stage + 1
            if 0 <= k < turns:
                work(k, stage)
    for p in range(len(pieces)):
        first, length, _ = pieces[p]
        block = mine(p, acc.at[z_here * keep if lined else 0])
        if lined:
            for slot, there in ((z_here, z_here > 0), (CHIPS_Z, z_here < CHIPS_Z - 1)):

                def last(p=p, slot=slot, block=block):
                    ref = mine(p, line.at[slot])
                    post.arrived(ref, line_sems.at[p, slot])
                    add(block, [ref], pieces[p][1])

                pl.when(there)(last)

        @pl.loop(0, length // 16)
        def _(r, first=first, block=block):
            at = pl.ds(pl.multiple_of(r * 16, 16), 16)
            result[pl.ds(pl.multiple_of(first + r * 16, 16), 16), :] = block[at, :].astype(
                result.dtype
            )

    post.close()


def scatter(array, whose, pieces, collective_id, name, after=None):
    size = {"all": 32, "dp": 8, "expert": 4}[whose]
    rows, width = array.shape[0] // size, array.shape[1]
    flat = pieces[0][2].replace("z", "")
    steps, lined = len(flat), "z" in pieces[0][2]
    turns = CHIPS_Z if lined else 1
    room = lambda blocks: pltpu.VMEM((blocks, rows, width), jnp.bfloat16)
    scratch = [room(turns * 2 ** (steps - 1))]
    scratch += [room(turns * 2 ** (steps - 1 - stage)) for stage in range(steps)]
    if lined:
        scratch.append(room(CHIPS_Z + 1))
    count = len(pieces)
    scratch += [
        pltpu.SemaphoreType.DMA((count * (turns * 2**steps + 4),)),
        pltpu.SemaphoreType.DMA((turns * 2 ** (steps - 1),)),
        pltpu.SemaphoreType.DMA((count, steps, turns * 2 ** (steps - 1))),
        pltpu.SemaphoreType.DMA((count, CHIPS_Z + 1)),
    ]
    return pl.pallas_call(
        functools.partial(scatter_kernel, whose, rows, pieces),
        out_shape=jax.ShapeDtypeStruct((rows, width), jnp.float32),
        in_specs=[pl.BlockSpec(memory_space=pltpu.HBM), pl.BlockSpec(memory_space=pl.ANY)],
        out_specs=pl.BlockSpec(memory_space=pltpu.VMEM),
        scratch_shapes=scratch,
        compiler_params=pltpu.CompilerParams(
            collective_id=collective_id, has_side_effects=True, vmem_limit_bytes=62 * 2**20
        ),
        name=name,
    )(array, array if after is None else after)


def weights_kernel(jobs, *refs):
    ready = len(jobs) - 2
    sources, (query, keyvalue, output) = refs[:ready], refs[ready : ready + 3]
    in_shard, out_shard = refs[ready + 3 : ready + 5]
    targets = refs[ready + 5 : 2 * ready + 7]
    send_sems, arrive_sems, own_sems, deal_sems = refs[2 * ready + 7 :]
    place = Place()
    z, y, e = place.at["z"], place.at["y"], place.expert
    span = (in_shard.shape[1] - query.shape[1]) // 2
    wide = query.shape[1]
    partner, moves = (e * 2 + y, z), z != e
    peers = []
    for flip_x, flip_c in ((1, 1), (1, 0), (0, 1)):
        x = place.at["x"] + flip_x * (1 - 2 * place.at["x"])
        core = place.at["c"] + flip_c * (1 - 2 * place.at["c"])
        peers.append((x * 2 + core, flip_x * 2 + flip_c))
    enter(place, "cxyz", [((place.dp, peers[0][0]), None), (partner, moves)])
    post = Post(send_sems, place)
    starts, waves, owns = gather_plan(
        jobs, place, post, list(sources) + [in_shard, out_shard], targets, arrive_sems, own_sems
    )
    cols = lambda block: pl.ds(pl.multiple_of(block * span, span), span)
    for peer, flips in peers:
        post.send(
            query.at[:, cols(peer)], in_shard.at[:, cols(e)], deal_sems.at[flips], (place.dp, peer)
        )
    post.send(output, out_shard, deal_sems.at[4], partner, moves)
    local = [
        pltpu.make_async_copy(query.at[:, cols(e)], in_shard.at[:, cols(e)], deal_sems.at[0]),
        pltpu.make_async_copy(
            keyvalue.at[:, cols(e)], in_shard.at[:, pl.ds(wide, span)], deal_sems.at[5]
        ),
        pltpu.make_async_copy(
            keyvalue.at[:, cols(wide // span + e)],
            in_shard.at[:, pl.ds(wide + span, span)],
            deal_sems.at[6],
        ),
    ]
    for copy in local:
        copy.start()
    stay = pltpu.make_async_copy(output, out_shard, deal_sems.at[7])
    pl.when(~moves)(stay.start)
    for act in sum(starts[:ready], []):
        act()
    for copy in local:
        copy.wait()
    for peer, flips in peers:
        post.arrived(in_shard.at[:, cols(peer)], deal_sems.at[flips])
    for act in starts[ready]:
        act()
    pl.when(~moves)(stay.wait)
    pl.when(moves)(lambda: post.arrived(out_shard, deal_sems.at[4]))
    for act in starts[ready + 1]:
        act()
    for wave in sorted(waves):
        for act in waves[wave]:
            act()
    for own in owns:
        own.wait()
    post.close()


def gather_weights(jobs, query, keyvalue, output, pieces, collective_id):
    rows, wide = query.shape
    span = wide // lax.axis_size("expert")
    shards = [
        jax.ShapeDtypeStruct((rows, wide + 2 * span), query.dtype),
        jax.ShapeDtypeStruct(output.shape, output.dtype),
    ]
    sizes = {"all": 32, "dp": 8, "expert": 4}
    plan = tuple((whose, r.shape[0], ps) for r, whose, ps in jobs)
    plan += tuple(("dp", s.shape[0], pieces) for s in shards)
    lines = sum(len(ps) for _, _, ps in plan)
    hbm = pl.BlockSpec(memory_space=pltpu.HBM)
    gathered = [
        jax.ShapeDtypeStruct((sizes[whose] * r.shape[0], r.shape[1]), r.dtype)
        for r, (whose, _, _) in zip([r for r, _, _ in jobs] + shards, plan)
    ]
    out = pl.pallas_call(
        functools.partial(weights_kernel, plan),
        out_shape=shards + gathered,
        in_specs=[hbm] * (len(jobs) + 3),
        out_specs=[hbm] * (2 + len(gathered)),
        scratch_shapes=[
            pltpu.SemaphoreType.DMA((110 * lines,)),
            pltpu.SemaphoreType.DMA((lines, 32)),
            pltpu.SemaphoreType.DMA((len(plan),)),
            pltpu.SemaphoreType.DMA((8,)),
        ],
        compiler_params=pltpu.CompilerParams(collective_id=collective_id, has_side_effects=True),
        name="gather_weights",
    )(*[r for r, _, _ in jobs], query, keyvalue, output)
    return out[2:]


def attention_bias(bias, block, rows, width, prefix):
    query = block * rows + lax.broadcasted_iota(jnp.int32, (rows, width), 0)
    key = lax.broadcasted_iota(jnp.int32, (rows, width), 1)
    bias[:, :width] = jnp.where((key <= query) | (key < prefix), 0.0, NEG)


def pick_expert(ref, lane, experts, span, chosen):
    total = None
    for e in range(experts):
        cols = ref[:, pl.ds(pl.multiple_of(e * span + lane, HEAD_DIM), HEAD_DIM)]
        term = jnp.where(chosen == e, cols.astype(jnp.float32), 0.0)
        total = term if total is None else total + term
    return total.astype(jnp.bfloat16)


def key_limits(blocks, rows):
    return [max((i + 1) * rows, blocks * rows // 2) for i in range(blocks)]


def for_each_limit(blocks, rows, body):
    block = pl.program_id(0)
    limits = key_limits(blocks, rows)
    for width in sorted(set(limits)):
        members = [i for i, limit in enumerate(limits) if limit == width]
        pl.when((block >= members[0]) & (block <= members[-1]))(lambda width=width: body(width))


def attention_kernel(experts, prefix, q, k, v, side, mixed, log_total, bias):
    rows, span = q.shape[0], k.shape[1]
    heads = span // HEAD_DIM
    block = pl.program_id(0)
    chosen = [side[:, 0:1], side[:, 1:2]]
    gates = [side[:, 2:3], side[:, 3:4]]

    def body(width):
        attention_bias(bias, block, rows, width, prefix[0])

        @pl.loop(0, heads)
        def _(head):
            lane = head * HEAD_DIM
            lanes = pl.ds(pl.multiple_of(lane, HEAD_DIM), HEAD_DIM)
            weighted = []
            for j in range(2):
                query = pick_expert(q, lane, experts, span, chosen[j])
                scores = lax.dot_general(
                    query, k[:width, lanes], ACROSS, preferred_element_type=jnp.float32
                )
                scores = scores * (HEAD_DIM**-0.5) + bias[:, :width]
                largest = jnp.max(scores, axis=1, keepdims=True)
                exponent = jnp.exp(scores - largest)
                total = jnp.sum(exponent, axis=1, keepdims=True)
                low = (exponent * (1.0 / total)).astype(jnp.bfloat16)
                out = jnp.dot(low, v[:width, lanes], preferred_element_type=jnp.float32)
                weighted.append(out * gates[j])
                at = pl.ds(pl.multiple_of((2 * head + j) * HEAD_DIM, HEAD_DIM), HEAD_DIM)
                log_total[:, at] = jnp.broadcast_to(
                    largest + jnp.log(total), (rows, HEAD_DIM)
                )
            for e in range(experts):
                cols = jnp.where(chosen[0] == e, weighted[0], 0.0) + jnp.where(
                    chosen[1] == e, weighted[1], 0.0
                )
                at = pl.ds(pl.multiple_of(e * span + lane, HEAD_DIM), HEAD_DIM)
                mixed[:, at] = cols.astype(jnp.bfloat16)

    for_each_limit(k.shape[0] // rows, rows, body)


def attention(projected, side, prefix, experts, rows):
    length = projected.shape[0]
    span = projected.shape[1] // (experts + 2)
    wide = experts * span
    return pl.pallas_call(
        functools.partial(attention_kernel, experts),
        grid=(length // rows,),
        in_specs=[
            pl.BlockSpec(memory_space=pltpu.SMEM),
            pl.BlockSpec((rows, wide), lambda i: (i, 0)),
            pl.BlockSpec((length, span), lambda i: (0, experts)),
            pl.BlockSpec((length, span), lambda i: (0, experts + 1)),
            pl.BlockSpec((rows, 128), lambda i: (i, 0)),
        ],
        out_specs=[
            pl.BlockSpec((rows, wide), lambda i: (i, 0)),
            pl.BlockSpec((rows, 2 * span), lambda i: (i, 0)),
        ],
        out_shape=[
            jax.ShapeDtypeStruct((length, wide), jnp.bfloat16),
            jax.ShapeDtypeStruct((length, 2 * span), jnp.float32),
        ],
        scratch_shapes=[pltpu.VMEM((rows, length), jnp.float32)],
        compiler_params=pltpu.CompilerParams(vmem_limit_bytes=48 * 2**20),
        name="attention",
    )(prefix, projected, projected, projected, side)


def attention_back_kernel(
    experts, prefix, q, k, v, side, log_total, dmix, dprojected, dgate, bias, dk, dv
):
    rows, span = q.shape[0], k.shape[1]
    length = k.shape[0]
    heads = span // HEAD_DIM
    block = pl.program_id(0)
    scaling = HEAD_DIM**-0.5
    chosen = [side[:, 0:1], side[:, 1:2]]
    gates = [side[:, 2:3], side[:, 3:4]]
    row_at = pl.ds(pl.multiple_of(block * rows, rows), rows)
    column = lax.broadcasted_iota(jnp.int32, (rows, 128), 1)

    @pl.when(block == 0)
    def _():
        dk[...] = jnp.zeros_like(dk)
        dv[...] = jnp.zeros_like(dv)

    dgate[...] = jnp.zeros_like(dgate)

    def body(width):
        attention_bias(bias, block, rows, width, prefix[0])

        @pl.loop(0, heads)
        def _(head):
            lane = head * HEAD_DIM
            lanes = pl.ds(pl.multiple_of(lane, HEAD_DIM), HEAD_DIM)
            keys, values = k[:width, lanes], v[:width, lanes]
            dqueries = []
            for j in range(2):
                query = pick_expert(q, lane, experts, span, chosen[j])
                dm = pick_expert(dmix, lane, experts, span, chosen[j])
                at = pl.ds(pl.multiple_of((2 * head + j) * HEAD_DIM, HEAD_DIM), HEAD_DIM)
                logs = jnp.tile(log_total[:, at], (1, width // HEAD_DIM))
                scores = lax.dot_general(query, keys, ACROSS, preferred_element_type=jnp.float32)
                probs = jnp.exp(scores * scaling + bias[:, :width] - logs)
                dprobs = lax.dot_general(dm, values, ACROSS, preferred_element_type=jnp.float32)
                inner = jnp.sum(probs * dprobs, axis=1, keepdims=True)
                dgate[...] += jnp.where(column == j, inner, 0.0)
                probs = probs * gates[j]
                dscores = (probs * (dprobs - inner)).astype(jnp.bfloat16)
                low = probs.astype(jnp.bfloat16)
                dquery = jnp.dot(dscores, keys, preferred_element_type=jnp.float32) * scaling
                dqueries.append(dquery)
                dk[:width, lanes] += lax.dot_general(
                    dscores, query, DOWNWARD, preferred_element_type=jnp.float32
                )
                dv[:width, lanes] += lax.dot_general(
                    low, dm, DOWNWARD, preferred_element_type=jnp.float32
                )
            for e in range(experts):
                cols = jnp.where(chosen[0] == e, dqueries[0], 0.0) + jnp.where(
                    chosen[1] == e, dqueries[1], 0.0
                )
                at = pl.ds(pl.multiple_of(e * span + lane, HEAD_DIM), HEAD_DIM)
                dprojected[row_at, at] = cols.astype(jnp.bfloat16)

    for_each_limit(length // rows, rows, body)

    @pl.when(block == pl.num_programs(0) - 1)
    def _():
        dprojected[:, experts * span : (experts + 1) * span] = (dk[...] * scaling).astype(
            jnp.bfloat16
        )
        dprojected[:, (experts + 1) * span :] = dv[...].astype(jnp.bfloat16)


def attention_back(projected, side, prefix, log_total, dmix, experts, rows):
    length, total = projected.shape
    span = total // (experts + 2)
    wide = experts * span
    return pl.pallas_call(
        functools.partial(attention_back_kernel, experts),
        grid=(length // rows,),
        in_specs=[
            pl.BlockSpec(memory_space=pltpu.SMEM),
            pl.BlockSpec((rows, wide), lambda i: (i, 0)),
            pl.BlockSpec((length, span), lambda i: (0, experts)),
            pl.BlockSpec((length, span), lambda i: (0, experts + 1)),
            pl.BlockSpec((rows, 128), lambda i: (i, 0)),
            pl.BlockSpec((rows, 2 * span), lambda i: (i, 0)),
            pl.BlockSpec((rows, wide), lambda i: (i, 0)),
        ],
        out_specs=[
            pl.BlockSpec((length, total), lambda i: (0, 0)),
            pl.BlockSpec((rows, 128), lambda i: (i, 0)),
        ],
        out_shape=[
            jax.ShapeDtypeStruct((length, total), jnp.bfloat16),
            jax.ShapeDtypeStruct((length, 128), jnp.float32),
        ],
        scratch_shapes=[
            pltpu.VMEM((rows, length), jnp.float32),
            pltpu.VMEM((length, span), jnp.float32),
            pltpu.VMEM((length, span), jnp.float32),
        ],
        compiler_params=pltpu.CompilerParams(vmem_limit_bytes=56 * 2**20),
        name="attention_back",
    )(prefix, projected, projected, projected, side, log_total, dmix)


def expert_slots(ids, my_index, tok_rows):
    blocks = ids.reshape(-1, tok_rows, 2)
    chosen = jnp.sum((blocks == my_index).astype(jnp.float32), axis=2)
    before = jnp.triu(jnp.ones((tok_rows, tok_rows), jnp.float32), 1)
    slots = jnp.where(chosen > 0, jnp.dot(chosen, before), -1.0).astype(jnp.int32)
    return slots, jnp.sum(blocks, axis=2) - my_index


def feed_kernel(
    tok,
    slot_count,
    own_rows,
    cots,
    gate_weight,
    up_weight,
    down_weight,
    router_rows,
    slots,
    others,
    everyone,
    dx_part,
    out_part,
    x_kept,
    g_kept,
    d_kept,
    a_kept,
    dgate,
    w_in,
    w_down,
    rows_buf,
    cots_buf,
    xs,
    gs,
    pre,
    back,
    ds,
    acts,
    dx_buf,
    out_buf,
    send_sems,
    arrive_sems,
    own_sem,
    weight_sems,
    load_sems,
    keep_sems,
):
    place = Place()
    z_here = place.at["z"]
    hidden = gate_weight.shape[0]
    padded = w_down.shape[0]
    width = own_rows.shape[1]
    half = tok // 2
    chips = 4 * CHIPS_Z
    pair = 2 * slot_count
    f32, low = jnp.float32, jnp.bfloat16

    loads = [
        pltpu.make_async_copy(gate_weight, w_in.at[pl.ds(0, hidden)], weight_sems.at[0]),
        pltpu.make_async_copy(
            router_rows, w_in.at[pl.ds(hidden, padded - hidden)], weight_sems.at[1]
        ),
        pltpu.make_async_copy(up_weight, w_in.at[pl.ds(padded, hidden)], weight_sems.at[2]),
        pltpu.make_async_copy(down_weight, w_down.at[pl.ds(0, hidden)], weight_sems.at[3]),
        pltpu.make_async_copy(
            own_rows, everyone.at[pl.ds(place.block("all", z_here, {}) * tok, tok)], own_sem
        ),
    ]
    for load in loads:
        load.start()
    w_in[padded + hidden :, :] = jnp.zeros((padded - hidden, width), low)
    w_down[hidden:, :] = jnp.zeros((padded - hidden, width), low)
    enter(place, "cxyz")

    def chip(u):
        u = jnp.asarray(u, jnp.int32)
        turn, q = u // 4, u % 4
        flip = lambda *at: ((q == at[0]) | (q == at[1])).astype(jnp.int32)
        k, xr, yr = turn + (q == 3) - (q == 0), flip(0, 1), flip(0, 2)
        k = jnp.where(u == 0, 0, jnp.minimum(k, CHIPS_Z - 1))
        xr = jnp.where(u == 0, 0, jnp.where(u == chips - 1, 1, xr))
        yr = jnp.where(u == 0, 0, jnp.where(u == chips - 1, 1, yr))
        inner = (z_here == 1) | (z_here == 2)
        near = jnp.where(inner, jnp.where(k == 3, 3, jnp.where(k == 2, 0, k + 1)), k)
        return jnp.where(z_here < 2, near, CHIPS_Z - 1 - near), xr, yr

    def first_block(u):
        z, xr, yr = chip(u)
        x = place.at["x"] + xr * (1 - 2 * place.at["x"])
        y = place.at["y"] + yr * (1 - 2 * place.at["y"])
        return (z * 2 + y) * 4 + x * 2

    def part(p, u, core):
        return everyone.at[pl.ds((first_block(u) + core) * tok + p * half, half)]

    def remote(source, target, number, mark, device):
        return pltpu.make_async_remote_copy(
            src_ref=source,
            dst_ref=target,
            send_sem=send_sems.at[number],
            recv_sem=arrive_sems.at[mark],
            device_id=device,
            device_id_type=MESH,
        )

    def routes(u, p):
        z, xr, yr = chip(u)
        plain = (xr + yr) == 0
        mark = (p * CHIPS_Z + z) * 8
        here = xr * 4 + yr * 2
        base = (u * 2 + p) * 5
        own = z == z_here
        right = plain & (z <= z_here) & (z_here < CHIPS_Z - 1)
        left = plain & (z >= z_here) & (z_here > 0)
        over_x = plain if p == 0 else xr == 0
        over_y = yr == 0 if p == 0 else plain
        return [
            (right, base, mark, place.along(1)),
            (left, base + 1, mark, place.along(-1)),
            (over_x, base + 2, mark + 4 + yr * 2, place.across("x")),
            (over_y, base + 3, mark + xr * 4 + 2, place.across("y")),
            (None, base + 4, mark + here + 1, place.across("c")),
        ]

    def hand_on(u, sources, pieces=(0, 1)):
        for p in pieces:
            for condition, number, mark, device in routes(u, p):
                target = part(p, u, place.at["c"])
                source = target if sources is None else sources[p]
                on(
                    condition,
                    lambda source=source, target=target, number=number, mark=mark, device=device: remote(
                        source, target, number, mark, device
                    ).start(),
                )

    def sibling_came(u):
        z, xr, yr = chip(u)
        for p in range(2):
            ref = part(p, u, 1 - place.at["c"])
            mark = (p * CHIPS_Z + z) * 8 + xr * 4 + yr * 2 + 1
            remote(ref, ref, 0, mark, place.across("c")).wait_recv()

    def take_in(u, p):
        z, xr, yr = chip(u)
        ref = part(p, u, place.at["c"])
        mark = (p * CHIPS_Z + z) * 8 + xr * 4 + yr * 2
        remote(ref, ref, 0, mark, place.across("c")).wait_recv()
        hand_on(u, None, (p,))

    def fetch(u):
        at = pl.ds(first_block(u) * tok, 2 * tok)
        return [
            pltpu.make_async_copy(everyone.at[at], rows_buf.at[u % 2], load_sems.at[u % 2, 0]),
            pltpu.make_async_copy(cots.at[at], cots_buf.at[u % 2], load_sems.at[u % 2, 1]),
        ]

    def keep(u):
        rows = pl.ds(u * pair, pair)
        blocks = pl.ds(first_block(u) * tok, 2 * tok)
        s = u % 2
        return [
            pltpu.make_async_copy(xs.at[s], x_kept.at[rows], keep_sems.at[s, 0]),
            pltpu.make_async_copy(gs.at[s], g_kept.at[rows], keep_sems.at[s, 1]),
            pltpu.make_async_copy(ds.at[s], d_kept.at[rows], keep_sems.at[s, 2]),
            pltpu.make_async_copy(acts.at[s], a_kept.at[rows], keep_sems.at[s, 3]),
            pltpu.make_async_copy(dx_buf.at[s], dx_part.at[blocks], keep_sems.at[s, 4]),
            pltpu.make_async_copy(out_buf.at[s], out_part.at[blocks], keep_sems.at[s, 5]),
        ]

    hand_on(0, [own_rows.at[pl.ds(0, half)], own_rows.at[pl.ds(half, half)]])
    loads[4].wait()
    sibling_came(0)
    for copy in fetch(0):
        copy.start()
    for p in range(2):
        take_in(1, p)
    for load in loads[:4]:
        load.wait()

    def compute(u):
        s = u % 2
        block = first_block(u)
        spread = []
        for b in range(2):
            row = slots[pl.ds(block + b, 1), :]
            table = lax.broadcasted_iota(jnp.int32, (slot_count, tok), 0) == row
            table = table.astype(f32)
            spread.append(table)
            at = pl.ds(b * slot_count, slot_count)
            from_rows = pl.ds(b * tok, tok)
            xs[s, at, :] = jnp.dot(
                table.astype(low), rows_buf[s, from_rows, :], preferred_element_type=f32
            ).astype(low)
            gs[s, at, :] = jnp.dot(
                table.astype(low), cots_buf[s, from_rows, :], preferred_element_type=f32
            ).astype(low)

        @pl.loop(0, 2 * padded // 256)
        def _(n):
            at = pl.ds(pl.multiple_of(n * 256, 256), 256)
            pre[:, at] = lax.dot_general(xs[s], w_in[at, :], ACROSS, preferred_element_type=f32)

        @pl.when(u + 2 < chips)
        def _():
            take_in(u + 2, 1)

        @pl.loop(0, padded // 256)
        def _(n):
            at = pl.ds(pl.multiple_of(n * 256, 256), 256)
            back[:, at] = lax.dot_general(gs[s], w_down[at, :], ACROSS, preferred_element_type=f32)

        for b in range(2):
            at = pl.ds(b * slot_count, slot_count)
            last = pre[at, padded - 128 : padded]
            column = lax.broadcasted_iota(jnp.int32, (slot_count, 128), 1) - (
                hidden - (padded - 128)
            )
            other = jnp.sum(
                spread[b] * others[pl.ds(block + b, 1), :].astype(f32), axis=1, keepdims=True
            )
            mine = jnp.sum(jnp.where(column == place.expert, last, 0.0), axis=1, keepdims=True)
            theirs = jnp.sum(
                jnp.where(column == other.astype(jnp.int32), last, 0.0), axis=1, keepdims=True
            )
            gate = 1.0 / (1.0 + jnp.exp(theirs - mine))
            inner = jnp.zeros((slot_count, 1), f32)
            for n in range(padded // 256):
                cols = pl.ds(n * 256, 256)
                pre_gate, pre_up = pre[at, cols], pre[at, pl.ds(padded + n * 256, 256)]
                dact = back[at, cols]
                sig = 1.0 / (1.0 + jnp.exp(-pre_gate))
                silu = pre_gate * sig
                act = silu * pre_up
                acts[s, at, cols] = (act * gate).astype(low)
                inner += jnp.sum(act * dact, axis=1, keepdims=True)
                dact = dact * gate
                ds[s, at, cols] = (dact * pre_up * sig * (1.0 + pre_gate * (1.0 - sig))).astype(low)
                ds[s, at, pl.ds(padded + n * 256, 256)] = (dact * silu).astype(low)
            dgate[pl.ds(block + b, 1), :] = jnp.sum(spread[b] * inner, axis=0, keepdims=True)

        @pl.loop(0, width // 256)
        def _(n):
            cols = pl.ds(pl.multiple_of(n * 256, 256), 256)
            dx = jnp.dot(ds[s], w_in[:, cols], preferred_element_type=f32).astype(low)
            out = jnp.dot(acts[s], w_down[:, cols], preferred_element_type=f32).astype(low)
            for b in range(2):
                at = slice(b * slot_count, (b + 1) * slot_count)
                table = spread[b].astype(low)
                to = pl.ds(b * tok, tok)
                dx_buf[s, to, cols] = lax.dot_general(
                    table, dx[at], DOWNWARD, preferred_element_type=f32
                ).astype(low)
                out_buf[s, to, cols] = lax.dot_general(
                    table, out[at], DOWNWARD, preferred_element_type=f32
                ).astype(low)

    @pl.loop(0, chips)
    def _(u):
        @pl.when(u + 1 < chips)
        def _():
            sibling_came(u + 1)
            for copy in fetch(u + 1):
                copy.start()

        @pl.when(u + 2 < chips)
        def _():
            take_in(u + 2, 0)

        for copy in fetch(u):
            copy.wait()

        @pl.when(u >= 2)
        def _():
            for copy in keep(u - 2):
                copy.wait()

        compute(u)
        for copy in keep(u):
            copy.start()

    for u in (chips - 2, chips - 1):
        for copy in keep(jnp.int32(u)):
            copy.wait()

    @pl.loop(0, chips)
    def _(u):
        for p in range(2):
            for condition, number, mark, device in routes(u, p):
                ref = part(p, u, place.at["c"])
                on(
                    condition,
                    lambda ref=ref, number=number, mark=mark, device=device: remote(
                        ref, ref, number, mark, device
                    ).wait_send(),
                )


def feed(own_rows, cots, gate_weight, up_weight, down_weight, router_rows, slots, others, slot_count):
    tok, width = own_rows.shape
    hidden = gate_weight.shape[0]
    padded = hidden + router_rows.shape[0]
    total = cots.shape[0]
    kept = total // tok * slot_count
    low = jnp.bfloat16
    hbm = pl.BlockSpec(memory_space=pltpu.HBM)
    vmem = pl.BlockSpec(memory_space=pltpu.VMEM)
    shape = jax.ShapeDtypeStruct
    pair = 2 * slot_count
    chips = 4 * CHIPS_Z
    return pl.pallas_call(
        functools.partial(feed_kernel, tok, slot_count),
        in_specs=[hbm] * 6 + [vmem] * 2,
        out_specs=[hbm] * 7 + [vmem],
        out_shape=[
            shape((total, width), low),
            shape((total, width), low),
            shape((total, width), low),
            shape((kept, width), low),
            shape((kept, width), low),
            shape((kept, 2 * padded), low),
            shape((kept, padded), low),
            shape(slots.shape, jnp.float32),
        ],
        scratch_shapes=[
            pltpu.VMEM((2 * padded, width), low),
            pltpu.VMEM((padded, width), low),
            pltpu.VMEM((2, 2 * tok, width), low),
            pltpu.VMEM((2, 2 * tok, width), low),
            pltpu.VMEM((2, pair, width), low),
            pltpu.VMEM((2, pair, width), low),
            pltpu.VMEM((pair, 2 * padded), jnp.float32),
            pltpu.VMEM((pair, padded), jnp.float32),
            pltpu.VMEM((2, pair, 2 * padded), low),
            pltpu.VMEM((2, pair, padded), low),
            pltpu.VMEM((2, 2 * tok, width), low),
            pltpu.VMEM((2, 2 * tok, width), low),
            pltpu.SemaphoreType.DMA((10 * chips,)),
            pltpu.SemaphoreType.DMA((16 * CHIPS_Z,)),
            pltpu.SemaphoreType.DMA,
            pltpu.SemaphoreType.DMA((4,)),
            pltpu.SemaphoreType.DMA((2, 2)),
            pltpu.SemaphoreType.DMA((2, 6)),
        ],
        compiler_params=pltpu.CompilerParams(
            collective_id=3, has_side_effects=True, vmem_limit_bytes=60 * 2**20
        ),
        name="feed_forward",
    )(own_rows, cots, gate_weight, up_weight, down_weight, router_rows, slots, others)


def per_device_torus(
    tokens,
    cotangent,
    attention_routes,
    feedforward_routes,
    prefix_length,
    gain_attention,
    gain_feedforward,
    keyvalue_weight,
    router_weight,
    query_weight,
    output_weight,
    gate_weight,
    up_weight,
    down_weight,
):
    my_index = lax.axis_index("expert")
    group_size = lax.axis_size("expert")
    dp_size = lax.axis_size("dp")
    inputs = tokens[0].astype(jnp.float32)
    tok_rows, model_width = inputs.shape
    slot_count = 5 * 2 * tok_rows // (4 * group_size)
    query_width = HEADS * HEAD_DIM
    span = query_width // group_size
    low = jnp.bfloat16
    f32 = jnp.float32

    half = dp_size // group_size
    swap = [
        ((z * half + y) * group_size + e, (e * half + y) * group_size + z)
        for z in range(group_size)
        for y in range(half)
        for e in range(group_size)
    ]
    cot_everyone = lax.all_gather(cotangent[0], ("dp", "expert"), axis=0, tiled=True)

    normed_attention, unit_attention, factor_attention = norm_parts(inputs, gain_attention)
    attention_in = normed_attention.astype(low)
    quarters = lambda order: tuple(
        (i * tok_rows // 4, tok_rows // 4, order) for i in range(4)
    )
    rows_in = keyvalue_weight.shape[0]
    route_shard = feedforward_routes[0].astype(low).reshape(-1, 128)
    router_shard = router_weight.T.reshape(-1, 128)
    whole = lambda a: ((0, a.shape[0], "zy"),)
    cut = rows_in * 13 // 16
    sequence_in, every_route, router_full, in_weight, out_weight = gather_weights(
        [
            (attention_in, "expert", quarters("xc")),
            (route_shard, "dp", whole(route_shard)),
            (router_shard, "dp", whole(router_shard)),
        ],
        query_weight[0],
        keyvalue_weight,
        output_weight[0],
        ((0, cut, "zy"), (cut, rows_in - cut, "yz")),
        1,
    )
    every_route = every_route.reshape(-1, 2).astype(jnp.int32)
    router_full = (
        router_full.reshape(dp_size, 2 * group_size, rows_in)
        .transpose(0, 2, 1)
        .reshape(-1, 2 * group_size)
    )
    attention_cols = router_full[:, :group_size]
    feedforward_cols = router_full[:, group_size:]
    projected = jnp.dot(sequence_in, in_weight, preferred_element_type=f32).astype(low)
    attend_matches_all = expert_matches(attention_routes[0], group_size)
    attend_logits = jnp.dot(sequence_in, attention_cols, preferred_element_type=f32)
    attend_weights_all, _ = pair_gates(attend_logits, attend_matches_all)
    side = jnp.concatenate([attention_routes[0].astype(f32), attend_weights_all], axis=1)
    side = jnp.pad(side, ((0, 0), (0, 128 - side.shape[1])))
    mixed, log_total = attention(projected, side, prefix_length, group_size, tok_rows)
    attend_part = jnp.dot(mixed, out_weight, preferred_element_type=f32).astype(low)
    attended = scatter(attend_part, "expert", quarters("cx"), 2, "sum_attention")
    hidden = inputs + attended
    normed_feed, unit_feed, factor_feed = norm_parts(hidden, gain_feedforward)
    feed_in = normed_feed.astype(low)
    everywhere = lambda a, b: ((0, tok_rows // 2, a), (tok_rows // 2, tok_rows // 2, b))
    mine = lambda a: lax.dynamic_slice_in_dim(a, my_index * tok_rows, tok_rows, 0)
    feed_matches = expert_matches(mine(feedforward_routes[0]), group_size)
    feed_logits = jnp.dot(feed_in, feedforward_cols, preferred_element_type=f32)
    feed_weights, _ = pair_gates(feed_logits, feed_matches)
    slots, others = expert_slots(every_route, my_index, tok_rows)
    hidden_rows = gate_weight.shape[1]
    padded = -(-hidden_rows // 256) * 256
    router_rows = jnp.pad(
        feedforward_cols.T, ((0, padded - hidden_rows - group_size), (0, 0))
    )
    _, dx_part, out_part, kept_rows, kept_cots, kept_back, kept_act, token_dgate = feed(
        feed_in,
        cot_everyone,
        gate_weight[0],
        up_weight[0],
        down_weight[0],
        router_rows,
        slots,
        others,
        slot_count,
    )
    grad_in_feed = lax.dot_general(kept_back, kept_rows, DOWNWARD, preferred_element_type=f32)
    grad_gate = grad_in_feed[:hidden_rows]
    grad_up = grad_in_feed[padded : padded + hidden_rows]
    grad_down = lax.dot_general(
        kept_act[:, :hidden_rows], kept_cots, DOWNWARD, preferred_element_type=f32
    )
    own_row = (jnp.arange(group_size) == my_index).astype(f32)[None, :, None]
    feed_dgate = lax.psum_scatter(
        (token_dgate[:, None, :] * own_row).reshape(-1, tok_rows),
        ("dp", "expert"),
        scatter_dimension=0,
        tiled=True,
    ).T
    feed_home = scatter(dx_part, "all", everywhere("cxyz", "cyxz"), 4, "sum_rows")
    out_part, feed_home = lax.optimization_barrier((out_part, feed_home))
    feed_sum = lax.psum_scatter(
        out_part,
        ("dp", "expert"),
        scatter_dimension=0,
        tiled=True,
    )
    layer_output = hidden + feed_sum.astype(f32)
    gradient = cotangent[0].astype(f32)
    feed_dlogits = gates_back(feed_dgate, feed_weights, feed_matches)
    feed_dnorm = feed_home + jnp.dot(feed_dlogits, feedforward_cols.astype(f32).T, precision=HIGH)
    grad_gain_feed = jnp.sum(feed_dnorm * unit_feed, axis=0)
    hidden_grad = gradient + norm_back(feed_dnorm, gain_feedforward, unit_feed, factor_feed)

    (sequence_grad,) = gather(
        [(hidden_grad.astype(low), "expert", quarters("xc"))], 5, "gather_cotangents"
    )
    dmix = lax.dot_general(sequence_grad, out_weight, ACROSS, preferred_element_type=f32).astype(low)
    grad_out = lax.dot_general(mixed, sequence_grad, DOWNWARD, preferred_element_type=f32)
    dprojected, gate_parts = attention_back(
        projected, side, prefix_length, log_total, dmix, group_size, tok_rows
    )
    attend_dx = lax.dot_general(dprojected, in_weight, ACROSS, preferred_element_type=f32)
    grad_in = lax.dot_general(sequence_in, dprojected, DOWNWARD, preferred_element_type=f32)
    attend_home = scatter(attend_dx.astype(low), "expert", quarters("cx"), 2, "sum_attention")
    pair_dgate = lax.psum_scatter(
        gate_parts[:, :2].reshape(group_size, tok_rows, 2).transpose(0, 2, 1).reshape(-1, tok_rows),
        "expert",
        scatter_dimension=0,
        tiled=True,
    ).T
    matches = mine(attend_matches_all)
    weights = mine(attend_weights_all)
    dselected = weights * (pair_dgate - jnp.sum(weights * pair_dgate, axis=1, keepdims=True))
    attend_dlogits = jnp.sum(dselected[:, :, None] * matches, axis=1)
    attend_dnorm = attend_home + jnp.dot(
        attend_dlogits, attention_cols.astype(f32).T, precision=HIGH
    )
    grad_gain_attend = jnp.sum(attend_dnorm * unit_attention, axis=0)
    grad_tokens = hidden_grad + norm_back(
        attend_dnorm, gain_attention, unit_attention, factor_attention
    )
    small = jnp.concatenate(
        [
            lax.dot_general(attend_dlogits, attention_in.astype(f32), DOWNWARD, precision=HIGH),
            lax.dot_general(feed_dlogits, feed_in.astype(f32), DOWNWARD, precision=HIGH),
            grad_gain_attend[None],
            grad_gain_feed[None],
        ],
        axis=0,
    )
    small = lax.psum(small.astype(f32), ("dp", "expert"))
    small = lax.dynamic_slice_in_dim(small, lax.axis_index("dp") * rows_in, rows_in, 1)

    down_dp = ((0, rows_in, "yz"),)
    out_rows = scatter(grad_out.astype(low), "dp", down_dp, 6, "sum_output_weight")
    in_rows = scatter(
        grad_in.astype(low), "dp", down_dp, 7, "sum_input_weight", feed_sum
    ).astype(low)
    grad_projection = lax.ppermute(out_rows.astype(low), ("dp", "expert"), swap).astype(f32)
    wide = group_size * span
    grad_query = lax.all_to_all(
        in_rows[:, :wide], "expert", split_axis=1, concat_axis=1, tiled=True
    ).astype(f32)
    grad_keyvalue = lax.all_gather(in_rows[:, wide:], "expert", axis=0, tiled=False)
    grad_keyvalue = (
        grad_keyvalue.reshape(group_size, rows_in, 2, span)
        .transpose(1, 2, 0, 3)
        .reshape(rows_in, 2 * query_width)
        .astype(f32)
    )
    return (
        layer_output.astype(low)[None],
        grad_tokens[None],
        small[2 * group_size],
        small[2 * group_size + 1],
        grad_keyvalue,
        small[: 2 * group_size].T,
        grad_query[None],
        grad_projection[None],
        grad_gate[None],
        grad_up[None],
        grad_down[None],
    )


def solution(mesh):
    in_specs = (
        P("dp", "expert", None),
        P("dp", "expert", None),
        P("dp", None, None),
        P("dp", None, None),
        P("dp"),
        P(),
        P(),
        P("dp", None),
        P("dp", None),
        P("expert", "dp", None),
        P("expert", "dp", None),
        P("expert", "dp", None),
        P("expert", "dp", None),
        P("expert", "dp", None),
    )
    out_specs = (
        P("dp", "expert", None),
        P("dp", "expert", None),
        P("dp"),
        P("dp"),
        P("dp", None),
        P("dp", None),
        P("expert", "dp", None),
        P("expert", "dp", None),
        P("expert", "dp", None),
        P("expert", "dp", None),
        P("expert", "dp", None),
    )
    torus = (mesh.shape["dp"], mesh.shape["expert"]) == (8, 4)
    body = per_device_torus if torus else per_device
    return jax.shard_map(
        body, mesh=mesh, in_specs=in_specs, out_specs=out_specs, check_vma=False
    )
```

```python
import functools

import jax
import jax.numpy as jnp
from jax import lax
from jax.experimental import pallas as pl
from jax.experimental.pallas import tpu as pltpu
from jax.sharding import PartitionSpec as P

HEADS = 16
HEAD_DIM = 128


EPS = 1e-06
NEG = -1e30
HIGH = lax.Precision.HIGHEST
ACROSS = (((1,), (1,)), ((), ()))
DOWNWARD = (((0,), (0,)), ((), ()))


def norm_parts(vector, gain_vector):
    factor = lax.rsqrt(jnp.mean(vector * vector, axis=-1, keepdims=True) + EPS)
    normed = vector * factor
    return (normed * gain_vector, normed, factor)


def norm_back(incoming, gain_vector, normed, factor):
    dnormed = incoming * gain_vector
    return factor * (dnormed - normed * jnp.mean(dnormed * normed, axis=-1, keepdims=True))


def route_plan(sequence_ids, my_index, group_size, tok_rows, slot_count):
    expert_range = jnp.arange(group_size, dtype=jnp.int32)
    matches_all = (sequence_ids[:, :, None] == expert_range[None, None, :]).astype(jnp.int32)
    chosen = jnp.sum(matches_all, axis=1).reshape(group_size, tok_rows, group_size)
    ranking = jnp.cumsum(chosen, axis=1) - chosen
    slot_ids = jnp.arange(slot_count, dtype=jnp.int32)[None, :, None]
    block_pick = (expert_range == my_index).astype(jnp.int32)
    my_chosen = jnp.sum(chosen * block_pick[:, None, None], axis=0).T
    my_ranking = jnp.sum(ranking * block_pick[:, None, None], axis=0).T
    send_table = (
        my_chosen[:, None, :] * (my_ranking[:, None, :] == slot_ids).astype(jnp.int32)
    ).astype(jnp.float32)
    column_chosen = jnp.sum(chosen * block_pick[None, None, :], axis=2)
    column_ranking = jnp.sum(ranking * block_pick[None, None, :], axis=2)
    taken = column_chosen[:, None, :] * (column_ranking[:, None, :] == slot_ids).astype(jnp.int32)
    positions = (
        expert_range[:, None, None] * tok_rows
        + jnp.arange(tok_rows, dtype=jnp.int32)[None, None, :]
    )
    arrival_places = jnp.sum(taken * positions, axis=2).reshape(-1)
    my_ids = lax.dynamic_slice_in_dim(sequence_ids, my_index * tok_rows, tok_rows, 0)
    matches = (my_ids[:, :, None] == expert_range[None, None, :]).astype(jnp.float32)
    return (send_table, arrival_places, matches)


def pair_gates(logits, matches):
    selected = jnp.sum(matches * logits[:, None, :], axis=2)
    largest = jnp.max(selected, axis=1, keepdims=True)
    exponent = jnp.exp(selected - largest)
    weights = exponent / jnp.sum(exponent, axis=1, keepdims=True)
    return (weights, jnp.sum(weights[:, :, None] * matches, axis=1))


def gates_back(dgate, weights, matches):
    dweights = jnp.sum(dgate[:, None, :] * matches, axis=2)
    dselected = weights * (dweights - jnp.sum(weights * dweights, axis=1, keepdims=True))
    return jnp.sum(dselected[:, :, None] * matches, axis=1)


def merge_back(send_table, gate_table, returned):
    weighted = send_table * gate_table.T[:, None, :]
    return jnp.einsum("ect,ecd->td", weighted, returned.astype(jnp.float32), precision=HIGH)


def branch_cotangent(send_table, gate_table, returned, incoming):
    spread_grad = jnp.einsum("ect,td->ecd", send_table, incoming, precision=HIGH)
    slot_gate = jnp.sum(send_table * gate_table.T[:, None, :], axis=2)
    cotangent_rows = (spread_grad * slot_gate[:, :, None]).astype(jnp.bfloat16)
    slot_dgate = jnp.sum(spread_grad * returned.astype(jnp.float32), axis=2)
    dgate = jnp.einsum("ect,ec->te", send_table, slot_dgate, precision=HIGH)
    return (cotangent_rows, dgate)


def expert_matches(ids, group_size):
    expert_range = jnp.arange(group_size, dtype=jnp.int32)
    return (ids[:, :, None] == expert_range[None, None, :]).astype(jnp.float32)


def expert_table(ids, my_index, group_size, tok_rows, slot_count):
    blocks = ids.reshape(-1, tok_rows, 2)
    chosen = jnp.sum((blocks == my_index).astype(jnp.float32), axis=2)
    before = jnp.triu(jnp.ones((tok_rows, tok_rows), jnp.float32), 1)
    ranking = jnp.dot(chosen, before)
    slot_ids = jnp.arange(slot_count, dtype=jnp.float32)[None, :, None]
    taken = chosen[:, None, :] * (ranking[:, None, :] == slot_ids).astype(jnp.float32)
    other = jnp.sum(blocks, axis=2) - my_index
    slot_other = jnp.sum(taken * other[:, None, :].astype(jnp.float32), axis=2)
    return (taken.astype(jnp.bfloat16), slot_other.reshape(-1).astype(jnp.int32))


def own_gate(logits, other, my_index):
    expert_range = jnp.arange(logits.shape[1], dtype=jnp.int32)[None]
    mine = jnp.sum(jnp.where(expert_range == my_index, logits, 0.0), axis=1, keepdims=True)
    theirs = jnp.sum(jnp.where(expert_range == other[:, None], logits, 0.0), axis=1, keepdims=True)
    return jax.nn.sigmoid(mine - theirs)


def pick_rows(taken, rows):
    blocks, slots, tokens = taken.shape
    picked = jnp.einsum(
        "bct,btd->bcd",
        taken,
        rows.reshape(blocks, tokens, -1),
        preferred_element_type=jnp.float32,
    )
    return picked.astype(jnp.bfloat16).reshape(blocks * slots, -1)


def return_rows(taken, rows):
    blocks, slots, tokens = taken.shape
    placed = jnp.einsum(
        "bct,bcd->btd",
        taken,
        rows.reshape(blocks, slots, -1),
        preferred_element_type=jnp.float32,
    )
    return placed.astype(jnp.bfloat16).reshape(blocks * tokens, -1)


def gather_all(rows):
    return lax.all_gather(rows, ("dp", "expert"), axis=0, tiled=True)


def scatter_all(rows):
    return lax.psum_scatter(rows, ("dp", "expert"), scatter_dimension=0, tiled=True)


def dispatch(rows):
    return lax.all_to_all(rows, "expert", split_axis=0, concat_axis=0, tiled=True)


def collect(rows):
    return lax.all_to_all(rows, "expert", split_axis=0, concat_axis=0, tiled=True)


def spread_rows(rows):
    return lax.all_gather(rows, "dp", axis=0, tiled=True)


def sum_rows(terms):
    return lax.psum_scatter(
        terms.astype(jnp.bfloat16), "dp", scatter_dimension=0, tiled=True
    ).astype(jnp.float32)


def send_rows(send_table, rows):
    return jnp.einsum(
        "ect,td->ecd", send_table.astype(jnp.bfloat16), rows, preferred_element_type=jnp.float32
    ).astype(jnp.bfloat16)


def per_device(
    tokens,
    cotangent,
    attention_routes,
    feedforward_routes,
    prefix_length,
    gain_attention,
    gain_feedforward,
    keyvalue_weight,
    router_weight,
    query_weight,
    output_weight,
    gate_weight,
    up_weight,
    down_weight,
):
    my_index = lax.axis_index("expert")
    group_size = lax.axis_size("expert")
    inputs = tokens[0].astype(jnp.float32)
    tok_rows = inputs.shape[0]
    model_width = inputs.shape[1]
    seq_total = tok_rows * group_size
    slot_count = 5 * 2 * tok_rows // (4 * group_size)
    query_width = HEADS * HEAD_DIM
    scaling = HEAD_DIM ** (-0.5)
    keyvalue_full, router_full, query_full, output_full = (
        lax.all_gather(keyvalue_weight, "dp", axis=0, tiled=True),
        lax.all_gather(router_weight, "dp", axis=0, tiled=True),
        lax.all_gather(query_weight[0], "dp", axis=0, tiled=True),
        lax.all_gather(output_weight[0], "dp", axis=0, tiled=True),
    )
    every_route = lax.all_gather(feedforward_routes[0], "dp", axis=0, tiled=True)
    cot_everyone = gather_all(cotangent[0])
    attention_cols = router_full[:, :group_size]
    feedforward_cols = router_full[:, group_size:]
    normed_attention, unit_attention, factor_attention = norm_parts(inputs, gain_attention)
    attention_in = normed_attention.astype(jnp.bfloat16)
    keyvalue_rows = jnp.dot(attention_in, keyvalue_full, preferred_element_type=jnp.float32).astype(
        jnp.bfloat16
    )
    keyvalue_seq = lax.all_gather(keyvalue_rows, "expert", axis=0, tiled=True)
    key_rows = keyvalue_seq[:, :query_width].reshape(seq_total, HEADS, HEAD_DIM)
    value_rows = keyvalue_seq[:, query_width:].reshape(seq_total, HEADS, HEAD_DIM)
    attend_table, attend_places, attend_matches = route_plan(
        attention_routes[0], my_index, group_size, tok_rows, slot_count
    )
    attend_logits = jnp.dot(attention_in, attention_cols, preferred_element_type=jnp.float32)
    attend_weights, attend_gate = pair_gates(attend_logits, attend_matches)
    arrived = dispatch(send_rows(attend_table, attention_in)).reshape(-1, model_width)
    queries = jnp.dot(arrived, query_full, preferred_element_type=jnp.float32).astype(jnp.bfloat16)
    queries = queries.reshape(-1, HEADS, HEAD_DIM)
    key_places = jnp.arange(seq_total, dtype=jnp.int32)
    allowed = (key_places[None, :] <= attend_places[:, None]) | (
        key_places[None, :] < prefix_length[0]
    )
    scores = (
        jnp.einsum("rhd,khd->hrk", queries, key_rows, preferred_element_type=jnp.float32) * scaling
    )
    scores = jnp.where(allowed[None], scores, NEG)
    row_max = jnp.max(scores, axis=2, keepdims=True)
    exponent = jnp.exp(scores - row_max)
    row_total = jnp.sum(exponent, axis=2, keepdims=True)
    log_total = row_max + jnp.log(row_total)
    attention_low = (exponent / row_total).astype(jnp.bfloat16)
    mixture = jnp.einsum(
        "hrk,khd->rhd", attention_low, value_rows, preferred_element_type=jnp.float32
    )
    mixture = mixture.astype(jnp.bfloat16).reshape(-1, query_width)
    attend_branch = jnp.dot(mixture, output_full, preferred_element_type=jnp.float32).astype(
        jnp.bfloat16
    )
    attend_returned = collect(attend_branch.reshape(group_size, slot_count, model_width))
    hidden = inputs + merge_back(attend_table, attend_gate, attend_returned)
    normed_feed, unit_feed, factor_feed = norm_parts(hidden, gain_feedforward)
    feed_in = normed_feed.astype(jnp.bfloat16)
    feed_ids = lax.dynamic_slice_in_dim(
        feedforward_routes[0], my_index * tok_rows, tok_rows, 0
    )
    feed_matches = expert_matches(feed_ids, group_size)
    feed_logits = jnp.dot(feed_in, feedforward_cols, preferred_element_type=jnp.float32)
    feed_weights, feed_gate = pair_gates(feed_logits, feed_matches)
    everyone = gather_all(feed_in)
    feed_taken, feed_pairs = expert_table(every_route, my_index, group_size, tok_rows, slot_count)
    pick = functools.partial(pick_rows, feed_taken)
    feed_rows = pick(everyone)
    cot_rows = pick(cot_everyone)
    row_logits = jnp.dot(feed_rows, feedforward_cols, preferred_element_type=jnp.float32)
    row_gate = own_gate(row_logits, feed_pairs, my_index)
    pre_gate = lax.dot_general(feed_rows, gate_weight[0], ACROSS, preferred_element_type=jnp.float32)
    pre_up = lax.dot_general(feed_rows, up_weight[0], ACROSS, preferred_element_type=jnp.float32)
    sigmoid_gate = jax.nn.sigmoid(pre_gate)
    act = pre_gate * sigmoid_gate * pre_up
    act_low = act.astype(jnp.bfloat16)
    act_scaled = (act * row_gate).astype(jnp.bfloat16)
    act_grad = lax.dot_general(cot_rows, down_weight[0], ACROSS, preferred_element_type=jnp.float32)
    slot_dgate = jnp.sum(act_low.astype(jnp.float32) * act_grad, axis=1)
    act_grad = act_grad * row_gate
    dgate_low = (act_grad * pre_up * sigmoid_gate * (1.0 + pre_gate * (1.0 - sigmoid_gate))).astype(
        jnp.bfloat16
    )
    dup_low = (act_grad * pre_gate * sigmoid_gate).astype(jnp.bfloat16)
    feed_dx = (
        jnp.dot(dgate_low, gate_weight[0], preferred_element_type=jnp.float32)
        + jnp.dot(dup_low, up_weight[0], preferred_element_type=jnp.float32)
    ).astype(jnp.bfloat16)
    feed_branch = jnp.dot(act_scaled, down_weight[0], preferred_element_type=jnp.float32).astype(
        jnp.bfloat16
    )
    grad_gate = lax.dot_general(dgate_low, feed_rows, DOWNWARD, preferred_element_type=jnp.float32)
    grad_up = lax.dot_general(dup_low, feed_rows, DOWNWARD, preferred_element_type=jnp.float32)
    grad_down = lax.dot_general(act_scaled, cot_rows, DOWNWARD, preferred_element_type=jnp.float32)
    token_dgate = jnp.einsum(
        "bct,bc->bt",
        feed_taken.astype(jnp.float32),
        slot_dgate.reshape(-1, slot_count),
        precision=HIGH,
    ).reshape(-1, 1)
    own_column = (jnp.arange(group_size) == my_index).astype(jnp.float32)[None]
    feed_dgate = scatter_all(token_dgate * own_column)
    feed_home = scatter_all(return_rows(feed_taken, feed_dx)).astype(jnp.float32)
    feed_sum = scatter_all(return_rows(feed_taken, feed_branch)).astype(jnp.float32)
    layer_output = hidden + feed_sum
    gradient = cotangent[0].astype(jnp.float32)
    feed_dlogits = gates_back(feed_dgate, feed_weights, feed_matches)
    feed_dnorm = feed_home + jnp.dot(
        feed_dlogits, feedforward_cols.astype(jnp.float32).T, precision=HIGH
    )
    grad_gain_feed = jnp.sum(feed_dnorm * unit_feed, axis=0)
    hidden_grad = gradient + norm_back(feed_dnorm, gain_feedforward, unit_feed, factor_feed)
    attend_cot, attend_dgate = branch_cotangent(
        attend_table, attend_gate, attend_returned, hidden_grad
    )
    attend_dlogits = gates_back(attend_dgate, attend_weights, attend_matches)
    attend_cot_rows = dispatch(attend_cot).reshape(-1, model_width)
    dmixture = lax.dot_general(
        attend_cot_rows, output_full, ACROSS, preferred_element_type=jnp.float32
    )
    dmixture = dmixture.astype(jnp.bfloat16).reshape(-1, HEADS, HEAD_DIM)
    grad_projection = lax.dot_general(
        mixture, attend_cot_rows, DOWNWARD, preferred_element_type=jnp.float32
    )
    scores_again = (
        jnp.einsum("rhd,khd->hrk", queries, key_rows, preferred_element_type=jnp.float32) * scaling
    )
    attention = jnp.where(allowed[None], jnp.exp(scores_again - log_total), 0.0)
    attention_again = attention.astype(jnp.bfloat16)
    dattention = jnp.einsum(
        "rhd,khd->hrk", dmixture, value_rows, preferred_element_type=jnp.float32
    )
    row_dot = jnp.sum(attention * dattention, axis=2, keepdims=True)
    dscores = (attention * (dattention - row_dot)).astype(jnp.bfloat16)
    dqueries = (
        jnp.einsum("hrk,khd->rhd", dscores, key_rows, preferred_element_type=jnp.float32) * scaling
    )
    dqueries = dqueries.astype(jnp.bfloat16).reshape(-1, query_width)
    dkeys = (
        jnp.einsum("hrk,rhd->khd", dscores, queries, preferred_element_type=jnp.float32) * scaling
    )
    dvalues = jnp.einsum(
        "hrk,rhd->khd", attention_again, dmixture, preferred_element_type=jnp.float32
    )
    grad_query = lax.dot_general(arrived, dqueries, DOWNWARD, preferred_element_type=jnp.float32)
    attend_dx = lax.dot_general(dqueries, query_full, ACROSS, preferred_element_type=jnp.float32)
    keyvalue_terms = jnp.concatenate(
        [dkeys.reshape(seq_total, query_width), dvalues.reshape(seq_total, query_width)], axis=1
    ).reshape(group_size, tok_rows, 2 * query_width)
    attend_home, keyvalue_home = (
        lax.all_to_all(
            attend_dx.reshape(group_size, slot_count, model_width).astype(jnp.bfloat16),
            "expert",
            split_axis=0,
            concat_axis=0,
            tiled=True,
        ).astype(jnp.float32),
        lax.all_to_all(
            keyvalue_terms.astype(jnp.bfloat16), "expert", split_axis=0, concat_axis=0, tiled=True
        ).astype(keyvalue_terms.dtype),
    )
    dkeyvalue = jnp.sum(keyvalue_home, axis=0).astype(jnp.bfloat16)
    attend_dnorm = (
        jnp.einsum("ect,ecd->td", attend_table, attend_home, precision=HIGH)
        + lax.dot_general(dkeyvalue, keyvalue_full, ACROSS, preferred_element_type=jnp.float32)
        + jnp.dot(attend_dlogits, attention_cols.astype(jnp.float32).T, precision=HIGH)
    )
    grad_keyvalue = lax.dot_general(
        attention_in, dkeyvalue, DOWNWARD, preferred_element_type=jnp.float32
    )
    grad_router = jnp.concatenate(
        [
            jnp.dot(attention_in.astype(jnp.float32).T, attend_dlogits, precision=HIGH),
            jnp.dot(feed_in.astype(jnp.float32).T, feed_dlogits, precision=HIGH),
        ],
        axis=1,
    )
    grad_gain_attend = jnp.sum(attend_dnorm * unit_attention, axis=0)
    grad_tokens = hidden_grad + norm_back(
        attend_dnorm, gain_attention, unit_attention, factor_attention
    )
    reduced = (
        lax.psum_scatter(
            grad_keyvalue.astype(jnp.bfloat16), "dp", scatter_dimension=0, tiled=True
        ).astype(jnp.float32),
        lax.psum_scatter(
            grad_router.astype(jnp.bfloat16), "dp", scatter_dimension=0, tiled=True
        ).astype(jnp.float32),
        lax.psum_scatter(
            grad_query.astype(jnp.bfloat16), "dp", scatter_dimension=0, tiled=True
        ).astype(jnp.float32),
        lax.psum_scatter(
            grad_projection.astype(jnp.bfloat16), "dp", scatter_dimension=0, tiled=True
        ).astype(jnp.float32),
        lax.psum_scatter(
            grad_gain_attend.astype(jnp.bfloat16), "dp", scatter_dimension=0, tiled=True
        ).astype(jnp.float32),
        lax.psum_scatter(
            grad_gain_feed.astype(jnp.bfloat16), "dp", scatter_dimension=0, tiled=True
        ).astype(jnp.float32),
    )
    shared = (
        lax.psum(reduced[0].astype(jnp.bfloat16), "expert").astype(jnp.float32),
        lax.psum(reduced[1].astype(jnp.bfloat16), "expert").astype(jnp.float32),
        lax.psum(reduced[4].astype(jnp.bfloat16), "expert").astype(jnp.float32),
        lax.psum(reduced[5].astype(jnp.bfloat16), "expert").astype(jnp.float32),
    )
    return (
        layer_output.astype(jnp.bfloat16)[None],
        grad_tokens[None],
        shared[2],
        shared[3],
        shared[0],
        shared[1],
        reduced[2][None],
        reduced[3][None],
        grad_gate[None],
        grad_up[None],
        grad_down[None],
    )


MESH = pl.DeviceIdType.MESH
CHIPS_Z = 4
TURNS = ((3, 2, 1, 0), (3, 0, 2, 1), (0, 3, 1, 2), (0, 1, 2, 3))


class Place:
    def __init__(self):
        self.dp, self.expert = lax.axis_index("dp"), lax.axis_index("expert")
        self.at = {
            "z": self.dp // 2,
            "y": self.dp % 2,
            "x": self.expert // 2,
            "c": self.expert % 2,
        }

    def across(self, axis):
        back = 1 - 2 * self.at[axis]
        if axis == "c":
            return (self.dp, self.expert + back)
        if axis == "x":
            return (self.dp, self.expert + 2 * back)
        return (self.dp + back, self.expert)

    def along(self, step):
        return (self.dp + 2 * step, self.expert)

    def block(self, whose, z, flips):
        at = {a: self.at[a] + flips.get(a, 0) * (1 - 2 * self.at[a]) for a in "xyc"}
        dp, expert = z * 2 + at["y"], at["x"] * 2 + at["c"]
        return {"all": dp * 4 + expert, "dp": dp, "expert": expert}[whose]


def enter(place, axes, others=()):
    barrier, count = pltpu.get_barrier_semaphore(), 0
    for device, condition in others:

        def greet(device=device):
            pl.semaphore_signal(barrier, inc=1, device_id=device, device_id_type=MESH)

        on(condition, greet)
        count = count + (1 if condition is None else condition.astype(jnp.int32))
    for axis in axes:
        if axis != "z":
            pl.semaphore_signal(
                barrier, inc=1, device_id=place.across(axis), device_id_type=MESH
            )
            count += 1
    if "z" in axes:
        z = place.at["z"]
        for step, there in ((-1, z > 0), (1, z < CHIPS_Z - 1)):

            @pl.when(there)
            def _(step=step):
                pl.semaphore_signal(
                    barrier, inc=1, device_id=place.along(step), device_id_type=MESH
                )

            count = count + there.astype(jnp.int32)
    pl.semaphore_wait(barrier, count)


def on(condition, action):
    if condition is None:
        action()
    else:
        pl.when(condition)(action)


def both(a, b):
    return b if a is None else a if b is None else a & b


class Post:
    def __init__(self, sems, place):
        self.sems, self.place, self.sent = sems, place, []

    def send(self, source, target, arrival, device, condition=None):
        number = len(self.sent)

        def copy():
            return pltpu.make_async_remote_copy(
                src_ref=source,
                dst_ref=target,
                send_sem=self.sems.at[number],
                recv_sem=arrival,
                device_id=device,
                device_id_type=MESH,
            )

        self.sent.append((condition, copy))
        on(condition, lambda: copy().start())

    def arrived(self, target, arrival):
        pltpu.make_async_remote_copy(
            src_ref=target,
            dst_ref=target,
            send_sem=self.sems.at[0],
            recv_sem=arrival,
            device_id=self.place.across("c"),
            device_id_type=MESH,
        ).wait_recv()

    def close(self):
        for condition, copy in self.sent:
            on(condition, lambda copy=copy: copy().wait_send())


FLIPS = {"x": 4, "y": 2, "c": 1}


def gather_plan(jobs, place, post, sources, targets, arrive_sems, own_sems):
    z_here = place.at["z"]
    line = 0
    waves, owns, starts = {}, [], []
    for j, (whose, rows, pieces) in enumerate(jobs):
        own = pltpu.make_async_copy(
            sources[j],
            targets[j].at[pl.ds(place.block(whose, z_here, {}) * rows, rows)],
            own_sems.at[j],
        )
        owns.append(own)
        begin = [own.start]
        for first, length, order in pieces:
            def part(z, flips, j=j, whose=whose, rows=rows, first=first, length=length):
                at = place.block(whose, z, flips) * rows + first
                return targets[j].at[pl.ds(at, length)]

            def mark(z, flips, line=line):
                return arrive_sems.at[line, z * 8 + sum(FLIPS[a] * v for a, v in flips.items())]

            def hand_on(source, z, flips, depth, side, wave, condition, order=order, part=part, mark=mark):
                for axis in order[max(depth, 0) :]:
                    if axis == "z" and (depth < 0 or order[depth] != "z"):
                        for step in (1, -1):
                            there = (z_here < CHIPS_Z - 1) if step > 0 else (z_here > 0)
                            post.send(source, part(z, flips), mark(z, flips), place.along(step), both(condition, there))
                    elif axis == "z":
                        there = (z_here < CHIPS_Z - 1) if side > 0 else (z_here > 0)
                        post.send(source, part(z, flips), mark(z, flips), place.along(side), both(condition, there))
                    elif depth < 0 or axis != order[depth]:
                        seen = dict(flips)
                        seen[axis] = 1
                        post.send(source, part(z, flips), mark(z, seen), place.across(axis), condition)

            def come(z, flips, depth, side, hops, wave, condition, order=order, part=part, mark=mark, hand_on=hand_on):
                def act():
                    on(condition, lambda: post.arrived(part(z, flips), mark(z, flips)))
                    hand_on(part(z, flips), z, flips, depth, side, wave, condition)

                waves.setdefault(wave, []).append(act)
                spread(z, flips, depth, side, hops, wave, condition, order, come)

            begin.append(
                lambda hand_on=hand_on, j=j, first=first, length=length: hand_on(
                    sources[j].at[pl.ds(first, length)], z_here, {}, -1, 0, 0, None
                )
            )
            spread(z_here, {}, -1, 0, 0, 0, None, order, come)
            line += 1
        starts.append(begin)
    return starts, waves, owns


def gather_kernel(jobs, axes, *refs):
    count = len(jobs)
    sources, targets = refs[:count], refs[count : 2 * count]
    send_sems, arrive_sems, own_sems = refs[2 * count :]
    place = Place()
    enter(place, axes)
    post = Post(send_sems, place)
    starts, waves, owns = gather_plan(jobs, place, post, sources, targets, arrive_sems, own_sems)
    for act in sum(starts, []):
        act()
    for wave in sorted(waves):
        for act in waves[wave]:
            act()
    for own in owns:
        own.wait()
    post.close()


def spread(z, flips, depth, side, hops, wave, condition, order, come):
    z_here = lax.axis_index("dp") // 2
    for later in range(max(depth, 0), len(order)):
        axis = order[later]
        if axis == "z":
            if depth >= 0 and order[depth] == "z":
                if hops < CHIPS_Z - 1:
                    far = hops + 1
                    there = (z_here >= far) if side > 0 else (z_here + far < CHIPS_Z)
                    come(z_here - side * far, flips, later, side, far, wave + 1, there)
            else:
                for step in (1, -1):
                    there = (z_here >= 1) if step > 0 else (z_here + 1 < CHIPS_Z)
                    come(z_here - step, flips, later, step, 1, wave + 1, both(condition, there))
        elif later > depth:
            seen = dict(flips)
            seen[axis] = 1
            come(z, seen, later, 0, 0, wave + 1, condition)


def gather(jobs, collective_id, name):
    arrays = [rows for rows, _, _ in jobs]
    sizes = {"all": 32, "dp": 8, "expert": 4}
    plan = tuple((whose, rows.shape[0], pieces) for rows, whose, pieces in jobs)
    axes = "".join(a for a in "cxyz" if any(a in order for _, _, ps in plan for _, _, order in ps))
    lines = sum(len(ps) for _, _, ps in plan)
    any_spec = pl.BlockSpec(memory_space=pltpu.HBM)
    return pl.pallas_call(
        functools.partial(gather_kernel, plan, axes),
        out_shape=[
            jax.ShapeDtypeStruct((sizes[whose] * r.shape[0], r.shape[1]), r.dtype)
            for r, whose, _ in jobs
        ],
        in_specs=[any_spec] * len(jobs),
        out_specs=[any_spec] * len(jobs),
        scratch_shapes=[
            pltpu.SemaphoreType.DMA((110 * lines,)),
            pltpu.SemaphoreType.DMA((lines, 32)),
            pltpu.SemaphoreType.DMA((len(jobs),)),
        ],
        compiler_params=pltpu.CompilerParams(
            collective_id=collective_id, has_side_effects=True
        ),
        name=name,
    )(*arrays)


def add_into(target, terms, length):
    @pl.loop(0, length // 16)
    def _(r):
        at = pl.ds(pl.multiple_of(r * 16, 16), 16)
        total = target[at, :].astype(jnp.float32)
        for term in terms:
            total = total + term[at, :].astype(jnp.float32)
        target[at, :] = total.astype(jnp.bfloat16)


def scatter_rooms(rows, width, order):
    steps, turns = len(order.replace("z", "")), CHIPS_Z if "z" in order else 1
    blocks = [turns * 2 ** (steps - 1)]
    blocks += [turns * 2 ** (steps - 1 - stage) for stage in range(steps)]
    if "z" in order:
        blocks.append(CHIPS_Z + 1)
    return [pltpu.VMEM((n, rows, width), jnp.bfloat16) for n in blocks]


def scatter_sems(order, pieces):
    steps, turns = len(order.replace("z", "")), CHIPS_Z if "z" in order else 1
    return [
        pltpu.SemaphoreType.DMA((turns * 2 ** (steps - 1),)),
        pltpu.SemaphoreType.DMA((pieces, steps, turns * 2 ** (steps - 1))),
        pltpu.SemaphoreType.DMA((pieces, CHIPS_Z + 1)),
    ]


def scatter_plan(whose, rows, pieces, place, post, source, rooms, sems):
    flat = [order.replace("z", "") for _, _, order in pieces]
    steps = len(flat[0])
    lined = "z" in pieces[0][2]
    turns = CHIPS_Z if lined else 1
    acc, bins, line = rooms[0], rooms[1 : 1 + steps], rooms[-1]
    load_sems, bin_sems, line_sems = sems
    z_here = place.at["z"]
    if lined:
        turn = [
            sum((z_here == z).astype(jnp.int32) * seq[k] for z, seq in enumerate(TURNS))
            for k in range(CHIPS_Z)
        ]
    else:
        turn = [z_here]
    slot_z = lambda k: turn[k] if lined else 0
    keep = 2 ** (steps - 1)
    names = sorted(flat[0][1:])
    loads = {}
    for k in range(turns):
        for n in reversed(range(keep)):
            flips = {a: (n >> i) & 1 for i, a in enumerate(names)}
            at = slot_z(k) * keep + n
            loads[k, n] = pltpu.make_async_copy(
                source.at[pl.ds(place.block(whose, turn[k], flips) * rows, rows)],
                acc.at[at],
                load_sems.at[at],
            )
    loaded = set()

    def mine(p, ref):
        first, length, _ = pieces[p]
        return ref.at[pl.ds(first, length)]

    def code_after(p, stage, flips):
        return sum(flips.get(a, 0) << i for i, a in enumerate(flat[p][stage + 1 :]))

    def gathered(p, k, stage, flips):
        n = sum(flips.get(a, 0) << i for i, a in enumerate(names))
        if (k, n) not in loaded:
            loads[k, n].wait()
            loaded.add((k, n))
        terms = []
        for before in range(stage):
            at = slot_z(k) * 2 ** (steps - 1 - before) + code_after(p, before, flips)
            ref = mine(p, bins[before].at[at])
            post.arrived(ref, bin_sems.at[p, before, at])
            terms.append(ref)
        block = mine(p, acc.at[slot_z(k) * keep + n])
        add_into(block, terms, pieces[p][1])
        return block

    def leave(k, stage):
        for code in reversed(range(2 ** (steps - 1 - stage))):
            for p in range(len(pieces)):
                flips = {a: (code >> i) & 1 for i, a in enumerate(flat[p][stage + 1 :])}
                flips[flat[p][stage]] = 1
                if stage == 0:
                    at = place.block(whose, turn[k], flips) * rows + pieces[p][0]
                    block = source.at[pl.ds(at, pieces[p][1])]
                else:
                    block = gathered(p, k, stage, flips)
                at = slot_z(k) * 2 ** (steps - 1 - stage) + code
                post.send(
                    block,
                    mine(p, bins[stage].at[at]),
                    bin_sems.at[p, stage, at],
                    place.across(flat[p][stage]),
                )

    def settle(k):
        for p in range(len(pieces)):
            block = gathered(p, k, steps, {})
            if not lined or k == turns - 1:
                continue
            t = turn[k]
            right = t > z_here

            def pass_on(p=p, t=t, block=block):
                ref = mine(p, line.at[t])
                post.arrived(ref, line_sems.at[p, t])
                add_into(block, [ref], pieces[p][1])

            pl.when((right & (z_here > 0)) | (~right & (z_here < CHIPS_Z - 1)))(pass_on)
            slot = jnp.where(t == z_here - 1, CHIPS_Z, t)
            post.send(
                block,
                mine(p, line.at[slot]),
                line_sems.at[p, slot],
                place.along(jnp.where(right, 1, -1)),
            )

    def finish(p):
        block = mine(p, acc.at[z_here * keep if lined else 0])
        if lined:
            for slot, there in ((z_here, z_here > 0), (CHIPS_Z, z_here < CHIPS_Z - 1)):

                def last(slot=slot):
                    ref = mine(p, line.at[slot])
                    post.arrived(ref, line_sems.at[p, slot])
                    add_into(block, [ref], pieces[p][1])

                pl.when(there)(last)
        return block

    works = [(-1, lambda k=k: leave(k, 0)) for k in range(turns)]
    for time in range(turns + steps):
        for stage in range(1, steps + 1):
            k = time - stage + 1
            if 0 <= k < turns:
                act = settle if stage == steps else lambda k, stage=stage: leave(k, stage)
                works.append((time, lambda k=k, act=act: act(k)))
    return list(loads.values()), works, finish


def sends_of(order, pieces):
    steps, turns = len(order.replace("z", "")), CHIPS_Z if "z" in order else 1
    return pieces * (turns * 2**steps + 4)


def widen(target, block, length):
    @pl.loop(0, length // 16)
    def _(r):
        at = pl.ds(pl.multiple_of(r * 16, 16), 16)
        target[at, :] = block[at, :].astype(jnp.float32)


def scatter_kernel(whose, rows, pieces, filler, source, *refs):
    given, refs = refs[: filler.operands], refs[filler.operands :]
    result, made, refs = refs[0], refs[1 : 1 + filler.results], refs[1 + filler.results :]
    rooms, refs = refs[: len(refs) - 4 - filler.rooms], refs[len(refs) - 4 - filler.rooms :]
    send_sems, sems, own = refs[0], refs[1:4], refs[4:]
    place = Place()
    post = Post(send_sems, place)
    loads, works, finish = scatter_plan(whose, rows, pieces, place, post, source, rooms, sems)
    for load in loads:
        load.start()
    enter(place, "".join(a for a in "cxyz" if a in pieces[0][2]))
    steps = filler.start(given, made, own)
    slots = sum(1 for time, _ in works if time >= 0)
    done = 0
    for number, (time, act) in enumerate(works):
        act()
        if time >= 0:
            share = steps * (number + 1 - (len(works) - slots)) // slots
            filler.run(given, made, own, done, share)
            done = share
    for p in range(len(pieces)):
        first, length, _ = pieces[p]
        widen(result.at[pl.ds(first, length)], finish(p), length)
    filler.end(given, made, own)
    post.close()


class Nothing:
    operands = results = rooms = 0
    shapes, scratch = [], []

    def start(self, given, made, own):
        return 0

    def run(self, given, made, own, first, last):
        pass

    def end(self, given, made, own):
        pass


class After(Nothing):
    operands = 1


class WeightGrads:
    operands, results, rooms = 4, 2, 6
    TILE, CHUNK = 256, 512

    def __init__(self, rows, wide, narrow, width):
        self.chunks = rows // self.CHUNK
        self.tiles = (wide // self.TILE, narrow // self.TILE)
        self.shapes = [
            jax.ShapeDtypeStruct((wide, width), jnp.float32),
            jax.ShapeDtypeStruct((narrow, width), jnp.float32),
        ]
        self.scratch = [
            pltpu.VMEM((2, self.CHUNK, self.TILE), jnp.bfloat16),
            pltpu.VMEM((2, self.CHUNK, width), jnp.bfloat16),
            pltpu.VMEM((self.TILE, width), jnp.float32),
            pltpu.VMEM((self.TILE, width), jnp.float32),
            pltpu.SemaphoreType.DMA((2, 2)),
            pltpu.SemaphoreType.DMA((2,)),
        ]

    def copies(self, given, own, step, second):
        tile, chunk = step // self.chunks - (self.tiles[0] if second else 0), step % self.chunks
        slot = step % 2
        rows = pl.ds(pl.multiple_of(chunk * self.CHUNK, self.CHUNK), self.CHUNK)
        cols = pl.ds(pl.multiple_of(tile * self.TILE, self.TILE), self.TILE)
        left, right = given[2 * second], given[2 * second + 1]
        return [
            pltpu.make_async_copy(left.at[rows, cols], own[0].at[slot], own[4].at[slot, 0]),
            pltpu.make_async_copy(right.at[rows], own[1].at[slot], own[4].at[slot, 1]),
        ]

    def fetch(self, given, own, step, start):
        edge = self.tiles[0] * self.chunks
        for second in (0, 1):

            @pl.when((step >= edge) if second else (step < edge))
            def _(second=second):
                for copy in self.copies(given, own, step, second):
                    copy.start() if start else copy.wait()

    def put(self, made, own, tile, parity, start):
        for second in (0, 1):

            @pl.when((tile >= self.tiles[0]) if second else (tile < self.tiles[0]))
            def _(second=second):
                at = tile - (self.tiles[0] if second else 0)
                rows = pl.ds(pl.multiple_of(at * self.TILE, self.TILE), self.TILE)
                copy = pltpu.make_async_copy(
                    own[2 + parity], made[second].at[rows], own[5].at[parity]
                )
                copy.start() if start else copy.wait()

    def start(self, given, made, own):
        self.fetch(given, own, jnp.int32(0), True)
        return sum(self.tiles) * self.chunks

    def run(self, given, made, own, first, last):
        total = sum(self.tiles) * self.chunks

        @pl.loop(first, last)
        def _(step):
            tile, chunk = step // self.chunks, step % self.chunks

            @pl.when(step + 1 < total)
            def _():
                self.fetch(given, own, step + 1, True)

            self.fetch(given, own, step, False)
            part = lax.dot_general(
                own[0][step % 2], own[1][step % 2], DOWNWARD, preferred_element_type=jnp.float32
            )
            for parity in (0, 1):

                @pl.when(tile % 2 == parity)
                def _(parity=parity):
                    acc = own[2 + parity]

                    @pl.when(chunk == 0)
                    def _():
                        @pl.when(tile >= 2)
                        def _():
                            self.put(made, own, tile - 2, parity, False)

                        acc[...] = part

                    @pl.when(chunk > 0)
                    def _():
                        acc[...] += part

                    @pl.when(chunk == self.chunks - 1)
                    def _():
                        self.put(made, own, tile, parity, True)

    def end(self, given, made, own):
        tiles = sum(self.tiles)
        for tile in (tiles - 2, tiles - 1):
            self.put(made, own, jnp.int32(tile), tile % 2, False)


def scatter(array, whose, pieces, collective_id, name, filler=Nothing(), operands=()):
    size = {"all": 32, "dp": 8, "expert": 4}[whose]
    rows, width = array.shape[0] // size, array.shape[1]
    order, count = pieces[0][2], len(pieces)
    hbm = pl.BlockSpec(memory_space=pltpu.HBM)
    out = pl.pallas_call(
        functools.partial(scatter_kernel, whose, rows, pieces, filler),
        out_shape=[jax.ShapeDtypeStruct((rows, width), jnp.float32)] + filler.shapes,
        in_specs=[hbm] * (1 + len(operands)),
        out_specs=[pl.BlockSpec(memory_space=pltpu.VMEM)] + [hbm] * filler.results,
        scratch_shapes=scatter_rooms(rows, width, order)
        + [pltpu.SemaphoreType.DMA((sends_of(order, count),))]
        + scatter_sems(order, count)
        + filler.scratch,
        compiler_params=pltpu.CompilerParams(
            collective_id=collective_id, has_side_effects=True, vmem_limit_bytes=63 * 2**20
        ),
        name=name,
    )(array, *operands)
    return out if filler.results else out[0]


def sum_weights_kernel(rows, pieces, in_grad, out_grad, after, query, keyvalue, output, *refs):
    count = len(scatter_rooms(rows, 128, pieces[0][2]))
    in_rooms, out_rooms = refs[:count], refs[count : 2 * count]
    dealt, shared, out_dealt = refs[2 * count : 2 * count + 3]
    send_sems, deal_sems = refs[2 * count + 3 : 2 * count + 5]
    in_sems, out_sems = refs[2 * count + 5 : 2 * count + 8], refs[2 * count + 8 :]
    place = Place()
    post = Post(send_sems, place)
    z, y, e = place.at["z"], place.at["y"], place.expert
    wide = query.shape[1]
    span = (in_grad.shape[1] - wide) // 2
    partner, moves = (e * 2 + y, z), z != e
    peers = []
    for flip_x, flip_c in ((1, 1), (1, 0), (0, 1)):
        x = place.at["x"] + flip_x * (1 - 2 * place.at["x"])
        core = place.at["c"] + flip_c * (1 - 2 * place.at["c"])
        peers.append((x * 2 + core, flip_x * 2 + flip_c))
    in_loads, in_works, in_finish = scatter_plan(
        "dp", rows, pieces, place, post, in_grad, in_rooms, in_sems
    )
    out_loads, out_works, out_finish = scatter_plan(
        "dp", rows, pieces, place, post, out_grad, out_rooms, out_sems
    )
    for load in in_loads + out_loads:
        load.start()
    enter(place, "cxyz", [((place.dp, peers[0][0]), None), (partner, moves)])
    for (_, one), (_, other) in zip(in_works, out_works):
        one()
        other()
    cols = lambda block: pl.ds(pl.multiple_of(block * span, span), span)
    keep = slice(wide, wide + 2 * span)
    for p in range(len(pieces)):
        first, length, _ = pieces[p]
        at = pl.ds(first, length)
        block = in_finish(p)
        for n, (peer, flips) in enumerate(peers):
            post.send(
                block.at[:, cols(peer)],
                dealt.at[at, cols(e)],
                deal_sems.at[p, flips],
                (place.dp, peer),
            )
        post.send(block.at[:, keep], shared.at[2, at], deal_sems.at[p, 4], place.across("x"))
        post.send(block.at[:, keep], shared.at[1, at], deal_sems.at[p, 5], place.across("c"))
        done = out_finish(p)
        post.send(done, out_dealt.at[at], deal_sems.at[p, 6], partner, moves)

    def place_keys(p, flips, block):
        first, length, _ = pieces[p]
        rows_at = pl.ds(first, length)
        x = place.at["x"] + (flips // 2) * (1 - 2 * place.at["x"])
        core = place.at["c"] + (flips % 2) * (1 - 2 * place.at["c"])
        owner = x * 2 + core
        widen(keyvalue.at[rows_at, cols(owner)], block.at[:, pl.ds(0, span)], length)
        widen(
            keyvalue.at[rows_at, cols(wide // span + owner)], block.at[:, pl.ds(span, span)], length
        )

    for p in range(len(pieces)):
        first, length, _ = pieces[p]
        at = pl.ds(first, length)
        post.arrived(shared.at[2, at], deal_sems.at[p, 4])
        post.send(shared.at[2, at], shared.at[3, at], deal_sems.at[p, 7], place.across("c"))
        block = in_rooms[0].at[z, at]
        widen(query.at[at, cols(e)], block.at[:, cols(e)], length)
        place_keys(p, 0, block.at[:, keep])
        place_keys(p, 2, shared.at[2, at])
        post.arrived(shared.at[1, at], deal_sems.at[p, 5])
        place_keys(p, 1, shared.at[1, at])
        for peer, flips in peers:
            post.arrived(dealt.at[at, cols(peer)], deal_sems.at[p, flips])
            widen(query.at[at, cols(peer)], dealt.at[at, cols(peer)], length)

        def came(p=p, at=at, length=length):
            post.arrived(out_dealt.at[at], deal_sems.at[p, 6])
            widen(output.at[at], out_dealt.at[at], length)

        pl.when(moves)(came)
        pl.when(~moves)(
            lambda at=at, length=length: widen(output.at[at], out_rooms[0].at[z, at], length)
        )
        post.arrived(shared.at[3, at], deal_sems.at[p, 7])
        place_keys(p, 3, shared.at[3, at])
    post.close()


def sum_weights(in_grad, out_grad, after, pieces, collective_id):
    rows, wide = out_grad.shape[0] // 8, out_grad.shape[1]
    order, count = pieces[0][2], len(pieces)
    total = in_grad.shape[1]
    hbm = pl.BlockSpec(memory_space=pltpu.HBM)
    vmem = pl.BlockSpec(memory_space=pltpu.VMEM)
    shape = jax.ShapeDtypeStruct
    return pl.pallas_call(
        functools.partial(sum_weights_kernel, rows, pieces),
        out_shape=[
            shape((rows, wide), jnp.float32),
            shape((rows, 2 * wide), jnp.float32),
            shape((rows, wide), jnp.float32),
        ],
        in_specs=[hbm] * 3,
        out_specs=[vmem] * 3,
        scratch_shapes=scatter_rooms(rows, total, order)
        + scatter_rooms(rows, wide, order)
        + [
            pltpu.VMEM((rows, wide), jnp.bfloat16),
            pltpu.VMEM((4, rows, total - wide), jnp.bfloat16),
            pltpu.VMEM((rows, wide), jnp.bfloat16),
            pltpu.SemaphoreType.DMA((2 * sends_of(order, count) + 8 * count,)),
            pltpu.SemaphoreType.DMA((count, 8)),
        ]
        + scatter_sems(order, count)
        + scatter_sems(order, count),
        compiler_params=pltpu.CompilerParams(
            collective_id=collective_id, has_side_effects=True, vmem_limit_bytes=63 * 2**20
        ),
        name="sum_weights",
    )(in_grad, out_grad, after)


def weights_kernel(jobs, *refs):
    ready = len(jobs) - 2
    sources, (query, keyvalue, output) = refs[:ready], refs[ready : ready + 3]
    in_shard, out_shard = refs[ready + 3 : ready + 5]
    targets = refs[ready + 5 : 2 * ready + 7]
    send_sems, arrive_sems, own_sems, deal_sems = refs[2 * ready + 7 :]
    place = Place()
    z, y, e = place.at["z"], place.at["y"], place.expert
    span = (in_shard.shape[1] - query.shape[1]) // 2
    wide = query.shape[1]
    partner, moves = (e * 2 + y, z), z != e
    peers = []
    for flip_x, flip_c in ((1, 1), (1, 0), (0, 1)):
        x = place.at["x"] + flip_x * (1 - 2 * place.at["x"])
        core = place.at["c"] + flip_c * (1 - 2 * place.at["c"])
        peers.append((x * 2 + core, flip_x * 2 + flip_c))
    enter(place, "cxyz", [((place.dp, peers[0][0]), None), (partner, moves)])
    post = Post(send_sems, place)
    starts, waves, owns = gather_plan(
        jobs, place, post, list(sources) + [in_shard, out_shard], targets, arrive_sems, own_sems
    )
    cols = lambda block: pl.ds(pl.multiple_of(block * span, span), span)
    for peer, flips in peers:
        post.send(
            query.at[:, cols(peer)], in_shard.at[:, cols(e)], deal_sems.at[flips], (place.dp, peer)
        )
    post.send(output, out_shard, deal_sems.at[4], partner, moves)
    local = [
        pltpu.make_async_copy(query.at[:, cols(e)], in_shard.at[:, cols(e)], deal_sems.at[0]),
        pltpu.make_async_copy(
            keyvalue.at[:, cols(e)], in_shard.at[:, pl.ds(wide, span)], deal_sems.at[5]
        ),
        pltpu.make_async_copy(
            keyvalue.at[:, cols(wide // span + e)],
            in_shard.at[:, pl.ds(wide + span, span)],
            deal_sems.at[6],
        ),
    ]
    for copy in local:
        copy.start()
    stay = pltpu.make_async_copy(output, out_shard, deal_sems.at[7])
    pl.when(~moves)(stay.start)
    for act in sum(starts[:ready], []):
        act()
    for copy in local:
        copy.wait()
    for peer, flips in peers:
        post.arrived(in_shard.at[:, cols(peer)], deal_sems.at[flips])
    for act in starts[ready]:
        act()
    pl.when(~moves)(stay.wait)
    pl.when(moves)(lambda: post.arrived(out_shard, deal_sems.at[4]))
    for act in starts[ready + 1]:
        act()
    for wave in sorted(waves):
        for act in waves[wave]:
            act()
    for own in owns:
        own.wait()
    post.close()


def gather_weights(jobs, query, keyvalue, output, pieces, collective_id):
    rows, wide = query.shape
    span = wide // lax.axis_size("expert")
    shards = [
        jax.ShapeDtypeStruct((rows, wide + 2 * span), query.dtype),
        jax.ShapeDtypeStruct(output.shape, output.dtype),
    ]
    sizes = {"all": 32, "dp": 8, "expert": 4}
    plan = tuple((whose, r.shape[0], ps) for r, whose, ps in jobs)
    plan += tuple(("dp", s.shape[0], pieces) for s in shards)
    lines = sum(len(ps) for _, _, ps in plan)
    hbm = pl.BlockSpec(memory_space=pltpu.HBM)
    gathered = [
        jax.ShapeDtypeStruct((sizes[whose] * r.shape[0], r.shape[1]), r.dtype)
        for r, (whose, _, _) in zip([r for r, _, _ in jobs] + shards, plan)
    ]
    out = pl.pallas_call(
        functools.partial(weights_kernel, plan),
        out_shape=shards + gathered,
        in_specs=[hbm] * (len(jobs) + 3),
        out_specs=[hbm] * (2 + len(gathered)),
        scratch_shapes=[
            pltpu.SemaphoreType.DMA((110 * lines,)),
            pltpu.SemaphoreType.DMA((lines, 32)),
            pltpu.SemaphoreType.DMA((len(plan),)),
            pltpu.SemaphoreType.DMA((8,)),
        ],
        compiler_params=pltpu.CompilerParams(collective_id=collective_id, has_side_effects=True),
        name="gather_weights",
    )(*[r for r, _, _ in jobs], query, keyvalue, output)
    return out[2:]


def attention_bias(bias, block, rows, width, prefix):
    query = block * rows + lax.broadcasted_iota(jnp.int32, (rows, width), 0)
    key = lax.broadcasted_iota(jnp.int32, (rows, width), 1)
    bias[:, :width] = jnp.where((key <= query) | (key < prefix), 0.0, NEG)


def pick_expert(ref, lane, experts, span, chosen):
    total = None
    for e in range(experts):
        cols = ref[:, pl.ds(pl.multiple_of(e * span + lane, HEAD_DIM), HEAD_DIM)]
        term = jnp.where(chosen == e, cols.astype(jnp.float32), 0.0)
        total = term if total is None else total + term
    return total.astype(jnp.bfloat16)


def key_limits(blocks, rows):
    return [max((i + 1) * rows, blocks * rows // 2) for i in range(blocks)]


def for_each_limit(blocks, rows, body):
    block = pl.program_id(0)
    limits = key_limits(blocks, rows)
    for width in sorted(set(limits)):
        members = [i for i, limit in enumerate(limits) if limit == width]
        pl.when((block >= members[0]) & (block <= members[-1]))(lambda width=width: body(width))


def attention_kernel(experts, prefix, q, k, v, side, mixed, log_total, bias):
    rows, span = q.shape[0], k.shape[1]
    heads = span // HEAD_DIM
    block = pl.program_id(0)
    chosen = [side[:, 0:1], side[:, 1:2]]
    gates = [side[:, 2:3], side[:, 3:4]]

    def body(width):
        attention_bias(bias, block, rows, width, prefix[0])

        @pl.loop(0, heads)
        def _(head):
            lane = head * HEAD_DIM
            lanes = pl.ds(pl.multiple_of(lane, HEAD_DIM), HEAD_DIM)
            weighted = []
            for j in range(2):
                query = pick_expert(q, lane, experts, span, chosen[j])
                scores = lax.dot_general(
                    query, k[:width, lanes], ACROSS, preferred_element_type=jnp.float32
                )
                scores = scores * (HEAD_DIM**-0.5) + bias[:, :width]
                largest = jnp.max(scores, axis=1, keepdims=True)
                exponent = jnp.exp(scores - largest)
                total = jnp.sum(exponent, axis=1, keepdims=True)
                low = (exponent * (1.0 / total)).astype(jnp.bfloat16)
                out = jnp.dot(low, v[:width, lanes], preferred_element_type=jnp.float32)
                weighted.append(out * gates[j])
                at = pl.ds(pl.multiple_of((2 * head + j) * HEAD_DIM, HEAD_DIM), HEAD_DIM)
                log_total[:, at] = jnp.broadcast_to(
                    largest + jnp.log(total), (rows, HEAD_DIM)
                )
            for e in range(experts):
                cols = jnp.where(chosen[0] == e, weighted[0], 0.0) + jnp.where(
                    chosen[1] == e, weighted[1], 0.0
                )
                at = pl.ds(pl.multiple_of(e * span + lane, HEAD_DIM), HEAD_DIM)
                mixed[:, at] = cols.astype(jnp.bfloat16)

    for_each_limit(k.shape[0] // rows, rows, body)


def attention(projected, side, prefix, experts, rows):
    length = projected.shape[0]
    span = projected.shape[1] // (experts + 2)
    wide = experts * span
    return pl.pallas_call(
        functools.partial(attention_kernel, experts),
        grid=(length // rows,),
        in_specs=[
            pl.BlockSpec(memory_space=pltpu.SMEM),
            pl.BlockSpec((rows, wide), lambda i: (i, 0)),
            pl.BlockSpec((length, span), lambda i: (0, experts)),
            pl.BlockSpec((length, span), lambda i: (0, experts + 1)),
            pl.BlockSpec((rows, 128), lambda i: (i, 0)),
        ],
        out_specs=[
            pl.BlockSpec((rows, wide), lambda i: (i, 0)),
            pl.BlockSpec((rows, 2 * span), lambda i: (i, 0)),
        ],
        out_shape=[
            jax.ShapeDtypeStruct((length, wide), jnp.bfloat16),
            jax.ShapeDtypeStruct((length, 2 * span), jnp.float32),
        ],
        scratch_shapes=[pltpu.VMEM((rows, length), jnp.float32)],
        compiler_params=pltpu.CompilerParams(vmem_limit_bytes=48 * 2**20),
        name="attention",
    )(prefix, projected, projected, projected, side)


def attention_back_kernel(
    experts, prefix, q, k, v, side, log_total, dmix, dprojected, dgate, bias, dk, dv
):
    rows, span = q.shape[0], k.shape[1]
    length = k.shape[0]
    heads = span // HEAD_DIM
    block = pl.program_id(0)
    scaling = HEAD_DIM**-0.5
    chosen = [side[:, 0:1], side[:, 1:2]]
    gates = [side[:, 2:3], side[:, 3:4]]
    row_at = pl.ds(pl.multiple_of(block * rows, rows), rows)
    column = lax.broadcasted_iota(jnp.int32, (rows, 128), 1)

    @pl.when(block == 0)
    def _():
        dk[...] = jnp.zeros_like(dk)
        dv[...] = jnp.zeros_like(dv)

    dgate[...] = jnp.zeros_like(dgate)

    def body(width):
        attention_bias(bias, block, rows, width, prefix[0])

        @pl.loop(0, heads)
        def _(head):
            lane = head * HEAD_DIM
            lanes = pl.ds(pl.multiple_of(lane, HEAD_DIM), HEAD_DIM)
            keys, values = k[:width, lanes], v[:width, lanes]
            dqueries = []
            for j in range(2):
                query = pick_expert(q, lane, experts, span, chosen[j])
                dm = pick_expert(dmix, lane, experts, span, chosen[j])
                at = pl.ds(pl.multiple_of((2 * head + j) * HEAD_DIM, HEAD_DIM), HEAD_DIM)
                logs = jnp.tile(log_total[:, at], (1, width // HEAD_DIM))
                scores = lax.dot_general(query, keys, ACROSS, preferred_element_type=jnp.float32)
                probs = jnp.exp(scores * scaling + bias[:, :width] - logs)
                dprobs = lax.dot_general(dm, values, ACROSS, preferred_element_type=jnp.float32)
                inner = jnp.sum(probs * dprobs, axis=1, keepdims=True)
                dgate[...] += jnp.where(column == j, inner, 0.0)
                probs = probs * gates[j]
                dscores = (probs * (dprobs - inner)).astype(jnp.bfloat16)
                low = probs.astype(jnp.bfloat16)
                dquery = jnp.dot(dscores, keys, preferred_element_type=jnp.float32) * scaling
                dqueries.append(dquery)
                dk[:width, lanes] += lax.dot_general(
                    dscores, query, DOWNWARD, preferred_element_type=jnp.float32
                )
                dv[:width, lanes] += lax.dot_general(
                    low, dm, DOWNWARD, preferred_element_type=jnp.float32
                )
            for e in range(experts):
                cols = jnp.where(chosen[0] == e, dqueries[0], 0.0) + jnp.where(
                    chosen[1] == e, dqueries[1], 0.0
                )
                at = pl.ds(pl.multiple_of(e * span + lane, HEAD_DIM), HEAD_DIM)
                dprojected[row_at, at] = cols.astype(jnp.bfloat16)

    for_each_limit(length // rows, rows, body)

    @pl.when(block == pl.num_programs(0) - 1)
    def _():
        dprojected[:, experts * span : (experts + 1) * span] = (dk[...] * scaling).astype(
            jnp.bfloat16
        )
        dprojected[:, (experts + 1) * span :] = dv[...].astype(jnp.bfloat16)


def attention_back(projected, side, prefix, log_total, dmix, experts, rows):
    length, total = projected.shape
    span = total // (experts + 2)
    wide = experts * span
    return pl.pallas_call(
        functools.partial(attention_back_kernel, experts),
        grid=(length // rows,),
        in_specs=[
            pl.BlockSpec(memory_space=pltpu.SMEM),
            pl.BlockSpec((rows, wide), lambda i: (i, 0)),
            pl.BlockSpec((length, span), lambda i: (0, experts)),
            pl.BlockSpec((length, span), lambda i: (0, experts + 1)),
            pl.BlockSpec((rows, 128), lambda i: (i, 0)),
            pl.BlockSpec((rows, 2 * span), lambda i: (i, 0)),
            pl.BlockSpec((rows, wide), lambda i: (i, 0)),
        ],
        out_specs=[
            pl.BlockSpec((length, total), lambda i: (0, 0)),
            pl.BlockSpec((rows, 128), lambda i: (i, 0)),
        ],
        out_shape=[
            jax.ShapeDtypeStruct((length, total), jnp.bfloat16),
            jax.ShapeDtypeStruct((length, 128), jnp.float32),
        ],
        scratch_shapes=[
            pltpu.VMEM((rows, length), jnp.float32),
            pltpu.VMEM((length, span), jnp.float32),
            pltpu.VMEM((length, span), jnp.float32),
        ],
        compiler_params=pltpu.CompilerParams(vmem_limit_bytes=56 * 2**20),
        name="attention_back",
    )(prefix, projected, projected, projected, side, log_total, dmix)


def expert_slots(ids, my_index, tok_rows):
    blocks = ids.reshape(-1, tok_rows, 2)
    chosen = jnp.sum((blocks == my_index).astype(jnp.float32), axis=2)
    before = jnp.triu(jnp.ones((tok_rows, tok_rows), jnp.float32), 1)
    slots = jnp.where(chosen > 0, jnp.dot(chosen, before), -1.0).astype(jnp.int32)
    return slots, jnp.sum(blocks, axis=2) - my_index


def feed_kernel(
    tok,
    slot_count,
    own_rows,
    cots,
    gate_weight,
    up_weight,
    down_weight,
    router_rows,
    slots,
    others,
    everyone,
    dx_part,
    out_part,
    x_kept,
    g_kept,
    d_kept,
    a_kept,
    dgate,
    w_in,
    w_down,
    rows_buf,
    cots_buf,
    xs,
    gs,
    pre,
    back,
    ds,
    acts,
    dx_buf,
    out_buf,
    dxs,
    outs,
    send_sems,
    arrive_sems,
    own_sem,
    weight_sems,
    load_sems,
    keep_sems,
):
    place = Place()
    z_here = place.at["z"]
    hidden = gate_weight.shape[0]
    padded = w_down.shape[0]
    width = own_rows.shape[1]
    half = tok // 2
    chips = 4 * CHIPS_Z
    pair = 2 * slot_count
    f32, low = jnp.float32, jnp.bfloat16

    loads = [
        pltpu.make_async_copy(gate_weight, w_in.at[pl.ds(0, hidden)], weight_sems.at[0]),
        pltpu.make_async_copy(
            router_rows, w_in.at[pl.ds(hidden, padded - hidden)], weight_sems.at[1]
        ),
        pltpu.make_async_copy(up_weight, w_in.at[pl.ds(padded, hidden)], weight_sems.at[2]),
        pltpu.make_async_copy(down_weight, w_down.at[pl.ds(0, hidden)], weight_sems.at[3]),
        pltpu.make_async_copy(
            own_rows, everyone.at[pl.ds(place.block("all", z_here, {}) * tok, tok)], own_sem
        ),
    ]
    for load in loads:
        load.start()
    w_in[padded + hidden :, :] = jnp.zeros((padded - hidden, width), low)
    w_down[hidden:, :] = jnp.zeros((padded - hidden, width), low)
    enter(place, "cxyz")

    def chip(u):
        u = jnp.asarray(u, jnp.int32)
        turn, q = u // 4, u % 4
        flip = lambda *at: ((q == at[0]) | (q == at[1])).astype(jnp.int32)
        k, xr, yr = turn + (q == 3) - (q == 0), flip(0, 1), flip(0, 2)
        k = jnp.where(u == 0, 0, jnp.minimum(k, CHIPS_Z - 1))
        xr = jnp.where(u == 0, 0, jnp.where(u == chips - 1, 1, xr))
        yr = jnp.where(u == 0, 0, jnp.where(u == chips - 1, 1, yr))
        inner = (z_here == 1) | (z_here == 2)
        near = jnp.where(inner, jnp.where(k == 3, 3, jnp.where(k == 2, 0, k + 1)), k)
        return jnp.where(z_here < 2, near, CHIPS_Z - 1 - near), xr, yr

    def first_block(u):
        z, xr, yr = chip(u)
        x = place.at["x"] + xr * (1 - 2 * place.at["x"])
        y = place.at["y"] + yr * (1 - 2 * place.at["y"])
        return (z * 2 + y) * 4 + x * 2

    def part(p, u, core):
        return everyone.at[pl.ds((first_block(u) + core) * tok + p * half, half)]

    def remote(source, target, number, mark, device):
        return pltpu.make_async_remote_copy(
            src_ref=source,
            dst_ref=target,
            send_sem=send_sems.at[number],
            recv_sem=arrive_sems.at[mark],
            device_id=device,
            device_id_type=MESH,
        )

    def routes(u, p):
        z, xr, yr = chip(u)
        plain = (xr + yr) == 0
        mark = (p * CHIPS_Z + z) * 8
        here = xr * 4 + yr * 2
        base = (u * 2 + p) * 5
        own = z == z_here
        right = plain & (z <= z_here) & (z_here < CHIPS_Z - 1)
        left = plain & (z >= z_here) & (z_here > 0)
        over_x = plain if p == 0 else xr == 0
        over_y = yr == 0 if p == 0 else plain
        return [
            (right, base, mark, place.along(1)),
            (left, base + 1, mark, place.along(-1)),
            (over_x, base + 2, mark + 4 + yr * 2, place.across("x")),
            (over_y, base + 3, mark + xr * 4 + 2, place.across("y")),
            (None, base + 4, mark + here + 1, place.across("c")),
        ]

    def hand_on(u, sources, pieces=(0, 1)):
        for p in pieces:
            for condition, number, mark, device in routes(u, p):
                target = part(p, u, place.at["c"])
                source = target if sources is None else sources[p]
                on(
                    condition,
                    lambda source=source, target=target, number=number, mark=mark, device=device: remote(
                        source, target, number, mark, device
                    ).start(),
                )

    def sibling_came(u):
        z, xr, yr = chip(u)
        for p in range(2):
            ref = part(p, u, 1 - place.at["c"])
            mark = (p * CHIPS_Z + z) * 8 + xr * 4 + yr * 2 + 1
            remote(ref, ref, 0, mark, place.across("c")).wait_recv()

    def take_in(u, p):
        z, xr, yr = chip(u)
        ref = part(p, u, place.at["c"])
        mark = (p * CHIPS_Z + z) * 8 + xr * 4 + yr * 2
        remote(ref, ref, 0, mark, place.across("c")).wait_recv()
        hand_on(u, None, (p,))

    def fetch(u):
        at = pl.ds(first_block(u) * tok, 2 * tok)
        return [
            pltpu.make_async_copy(everyone.at[at], rows_buf.at[u % 2], load_sems.at[u % 2, 0]),
            pltpu.make_async_copy(cots.at[at], cots_buf.at[u % 2], load_sems.at[u % 2, 1]),
        ]

    def keep(u):
        rows = pl.ds(u * pair, pair)
        blocks = pl.ds(first_block(u) * tok, 2 * tok)
        s = u % 2
        return [
            pltpu.make_async_copy(xs.at[s], x_kept.at[rows], keep_sems.at[s, 0]),
            pltpu.make_async_copy(gs.at[s], g_kept.at[rows], keep_sems.at[s, 1]),
            pltpu.make_async_copy(ds.at[s], d_kept.at[rows], keep_sems.at[s, 2]),
            pltpu.make_async_copy(acts.at[s], a_kept.at[rows], keep_sems.at[s, 3]),
            pltpu.make_async_copy(dx_buf.at[s], dx_part.at[blocks], keep_sems.at[s, 4]),
            pltpu.make_async_copy(out_buf.at[s], out_part.at[blocks], keep_sems.at[s, 5]),
        ]

    hand_on(0, [own_rows.at[pl.ds(0, half)], own_rows.at[pl.ds(half, half)]])
    loads[4].wait()
    sibling_came(0)
    for copy in fetch(0):
        copy.start()
    for p in range(2):
        take_in(1, p)
    for load in loads[:4]:
        load.wait()

    def compute(u):
        s = u % 2
        block = first_block(u)
        spread = []
        for b in range(2):
            row = slots[pl.ds(block + b, 1), :]
            table = lax.broadcasted_iota(jnp.int32, (slot_count, tok), 0) == row
            table = table.astype(f32)
            spread.append(table)
            at = pl.ds(b * slot_count, slot_count)
            from_rows = pl.ds(b * tok, tok)
            xs[s, at, :] = jnp.dot(
                table.astype(low), rows_buf[s, from_rows, :], preferred_element_type=f32
            ).astype(low)
            gs[s, at, :] = jnp.dot(
                table.astype(low), cots_buf[s, from_rows, :], preferred_element_type=f32
            ).astype(low)

        @pl.loop(0, 2 * padded // 256)
        def _(n):
            at = pl.ds(pl.multiple_of(n * 256, 256), 256)
            pre[:, at] = lax.dot_general(xs[s], w_in[at, :], ACROSS, preferred_element_type=f32)

        @pl.when(u + 2 < chips)
        def _():
            take_in(u + 2, 1)

        @pl.loop(0, padded // 256)
        def _(n):
            at = pl.ds(pl.multiple_of(n * 256, 256), 256)
            back[:, at] = lax.dot_general(gs[s], w_down[at, :], ACROSS, preferred_element_type=f32)

        for b in range(2):
            at = pl.ds(b * slot_count, slot_count)
            last = pre[at, padded - 128 : padded]
            column = lax.broadcasted_iota(jnp.int32, (slot_count, 128), 1) - (
                hidden - (padded - 128)
            )
            other = jnp.sum(
                spread[b] * others[pl.ds(block + b, 1), :].astype(f32), axis=1, keepdims=True
            )
            mine = jnp.sum(jnp.where(column == place.expert, last, 0.0), axis=1, keepdims=True)
            theirs = jnp.sum(
                jnp.where(column == other.astype(jnp.int32), last, 0.0), axis=1, keepdims=True
            )
            gate = 1.0 / (1.0 + jnp.exp(theirs - mine))
            inner = jnp.zeros((slot_count, 1), f32)
            for n in range(padded // 256):
                cols = pl.ds(n * 256, 256)
                pre_gate, pre_up = pre[at, cols], pre[at, pl.ds(padded + n * 256, 256)]
                dact = back[at, cols]
                sig = 1.0 / (1.0 + jnp.exp(-pre_gate))
                silu = pre_gate * sig
                act = silu * pre_up
                acts[s, at, cols] = (act * gate).astype(low)
                inner += jnp.sum(act * dact, axis=1, keepdims=True)
                dact = dact * gate
                ds[s, at, cols] = (dact * pre_up * sig * (1.0 + pre_gate * (1.0 - sig))).astype(low)
                ds[s, at, pl.ds(padded + n * 256, 256)] = (dact * silu).astype(low)
            dgate[pl.ds(block + b, 1), :] = jnp.sum(spread[b] * inner, axis=0, keepdims=True)

        @pl.loop(0, width // 256)
        def _(n):
            cols = pl.ds(pl.multiple_of(n * 256, 256), 256)
            dxs[:, cols] = jnp.dot(ds[s], w_in[:, cols], preferred_element_type=f32).astype(low)
            outs[:, cols] = jnp.dot(acts[s], w_down[:, cols], preferred_element_type=f32).astype(
                low
            )

        for b in range(2):
            at = pl.ds(b * slot_count, slot_count)
            back_table = spread[b].T.astype(low)
            to = pl.ds(b * tok, tok)
            dx_buf[s, to, :] = jnp.dot(
                back_table, dxs[at, :], preferred_element_type=f32
            ).astype(low)
            out_buf[s, to, :] = jnp.dot(
                back_table, outs[at, :], preferred_element_type=f32
            ).astype(low)

    @pl.loop(0, chips)
    def _(u):
        @pl.when(u + 1 < chips)
        def _():
            sibling_came(u + 1)
            for copy in fetch(u + 1):
                copy.start()

        @pl.when(u + 2 < chips)
        def _():
            take_in(u + 2, 0)

        for copy in fetch(u):
            copy.wait()

        @pl.when(u >= 2)
        def _():
            for copy in keep(u - 2):
                copy.wait()

        compute(u)
        for copy in keep(u):
            copy.start()

    for u in (chips - 2, chips - 1):
        for copy in keep(jnp.int32(u)):
            copy.wait()

    @pl.loop(0, chips)
    def _(u):
        for p in range(2):
            for condition, number, mark, device in routes(u, p):
                ref = part(p, u, place.at["c"])
                on(
                    condition,
                    lambda ref=ref, number=number, mark=mark, device=device: remote(
                        ref, ref, number, mark, device
                    ).wait_send(),
                )


def feed(own_rows, cots, gate_weight, up_weight, down_weight, router_rows, slots, others, slot_count):
    tok, width = own_rows.shape
    hidden = gate_weight.shape[0]
    padded = hidden + router_rows.shape[0]
    total = cots.shape[0]
    kept = total // tok * slot_count
    low = jnp.bfloat16
    hbm = pl.BlockSpec(memory_space=pltpu.HBM)
    vmem = pl.BlockSpec(memory_space=pltpu.VMEM)
    shape = jax.ShapeDtypeStruct
    pair = 2 * slot_count
    chips = 4 * CHIPS_Z
    return pl.pallas_call(
        functools.partial(feed_kernel, tok, slot_count),
        in_specs=[hbm] * 6 + [vmem] * 2,
        out_specs=[hbm] * 7 + [vmem],
        out_shape=[
            shape((total, width), low),
            shape((total, width), low),
            shape((total, width), low),
            shape((kept, width), low),
            shape((kept, width), low),
            shape((kept, 2 * padded), low),
            shape((kept, padded), low),
            shape(slots.shape, jnp.float32),
        ],
        scratch_shapes=[
            pltpu.VMEM((2 * padded, width), low),
            pltpu.VMEM((padded, width), low),
            pltpu.VMEM((2, 2 * tok, width), low),
            pltpu.VMEM((2, 2 * tok, width), low),
            pltpu.VMEM((2, pair, width), low),
            pltpu.VMEM((2, pair, width), low),
            pltpu.VMEM((pair, 2 * padded), jnp.float32),
            pltpu.VMEM((pair, padded), jnp.float32),
            pltpu.VMEM((2, pair, 2 * padded), low),
            pltpu.VMEM((2, pair, padded), low),
            pltpu.VMEM((2, 2 * tok, width), low),
            pltpu.VMEM((2, 2 * tok, width), low),
            pltpu.VMEM((pair, width), low),
            pltpu.VMEM((pair, width), low),
            pltpu.SemaphoreType.DMA((10 * chips,)),
            pltpu.SemaphoreType.DMA((16 * CHIPS_Z,)),
            pltpu.SemaphoreType.DMA,
            pltpu.SemaphoreType.DMA((4,)),
            pltpu.SemaphoreType.DMA((2, 2)),
            pltpu.SemaphoreType.DMA((2, 6)),
        ],
        compiler_params=pltpu.CompilerParams(
            collective_id=3, has_side_effects=True, vmem_limit_bytes=60 * 2**20
        ),
        name="feed_forward",
    )(own_rows, cots, gate_weight, up_weight, down_weight, router_rows, slots, others)


def per_device_torus(
    tokens,
    cotangent,
    attention_routes,
    feedforward_routes,
    prefix_length,
    gain_attention,
    gain_feedforward,
    keyvalue_weight,
    router_weight,
    query_weight,
    output_weight,
    gate_weight,
    up_weight,
    down_weight,
):
    my_index = lax.axis_index("expert")
    group_size = lax.axis_size("expert")
    dp_size = lax.axis_size("dp")
    inputs = tokens[0].astype(jnp.float32)
    tok_rows, model_width = inputs.shape
    slot_count = 5 * 2 * tok_rows // (4 * group_size)
    query_width = HEADS * HEAD_DIM
    span = query_width // group_size
    low = jnp.bfloat16
    f32 = jnp.float32

    normed_attention, unit_attention, factor_attention = norm_parts(inputs, gain_attention)
    attention_in = normed_attention.astype(low)
    quarters = lambda order: tuple(
        (i * tok_rows // 4, tok_rows // 4, order) for i in range(4)
    )
    rows_in = keyvalue_weight.shape[0]
    route_shard = feedforward_routes[0].astype(low).reshape(-1, 128)
    router_shard = router_weight.T.reshape(-1, 128)
    whole = lambda a: ((0, a.shape[0], "zy"),)
    cut = rows_in * 12 // 16
    sequence_in, cot_everyone, every_route, router_full, in_weight, out_weight = gather_weights(
        [
            (attention_in, "expert", quarters("xc")),
            (cotangent[0], "all", quarters("zyxc")),
            (route_shard, "dp", whole(route_shard)),
            (router_shard, "dp", whole(router_shard)),
        ],
        query_weight[0],
        keyvalue_weight,
        output_weight[0],
        ((0, cut, "zy"), (cut, rows_in - cut, "yz")),
        1,
    )
    every_route = every_route.reshape(-1, 2).astype(jnp.int32)
    router_full = (
        router_full.reshape(dp_size, 2 * group_size, rows_in)
        .transpose(0, 2, 1)
        .reshape(-1, 2 * group_size)
    )
    attention_cols = router_full[:, :group_size]
    feedforward_cols = router_full[:, group_size:]
    projected = jnp.dot(sequence_in, in_weight, preferred_element_type=f32).astype(low)
    attend_matches_all = expert_matches(attention_routes[0], group_size)
    attend_logits = jnp.dot(sequence_in, attention_cols, preferred_element_type=f32)
    attend_weights_all, _ = pair_gates(attend_logits, attend_matches_all)
    side = jnp.concatenate([attention_routes[0].astype(f32), attend_weights_all], axis=1)
    side = jnp.pad(side, ((0, 0), (0, 128 - side.shape[1])))
    mixed, log_total = attention(projected, side, prefix_length, group_size, tok_rows)
    attend_part = jnp.dot(mixed, out_weight, preferred_element_type=f32).astype(low)
    attended = scatter(attend_part, "expert", quarters("cx"), 2, "sum_attention")
    hidden = inputs + attended
    normed_feed, unit_feed, factor_feed = norm_parts(hidden, gain_feedforward)
    feed_in = normed_feed.astype(low)
    everywhere = lambda a, b: ((0, tok_rows // 2, a), (tok_rows // 2, tok_rows // 2, b))
    mine = lambda a: lax.dynamic_slice_in_dim(a, my_index * tok_rows, tok_rows, 0)
    feed_matches = expert_matches(mine(feedforward_routes[0]), group_size)
    feed_logits = jnp.dot(feed_in, feedforward_cols, preferred_element_type=f32)
    feed_weights, _ = pair_gates(feed_logits, feed_matches)
    slots, others = expert_slots(every_route, my_index, tok_rows)
    hidden_rows = gate_weight.shape[1]
    padded = -(-hidden_rows // 256) * 256
    router_rows = jnp.pad(
        feedforward_cols.T, ((0, padded - hidden_rows - group_size), (0, 0))
    )
    _, dx_part, out_part, kept_rows, kept_cots, kept_back, kept_act, token_dgate = feed(
        feed_in,
        cot_everyone,
        gate_weight[0],
        up_weight[0],
        down_weight[0],
        router_rows,
        slots,
        others,
        slot_count,
    )
    own_row = (jnp.arange(group_size) == my_index).astype(f32)[None, :, None]
    feed_dgate = lax.psum_scatter(
        (token_dgate[:, None, :] * own_row).reshape(-1, tok_rows),
        ("dp", "expert"),
        scatter_dimension=0,
        tiled=True,
    ).T
    feed_home, grad_in_feed, grad_down = scatter(
        dx_part,
        "all",
        everywhere("cxyz", "cyxz"),
        4,
        "sum_rows",
        WeightGrads(kept_rows.shape[0], 2 * padded, padded, model_width),
        (kept_back, kept_rows, kept_act, kept_cots),
    )
    grad_gate = grad_in_feed[:hidden_rows]
    grad_up = grad_in_feed[padded : padded + hidden_rows]
    grad_down = grad_down[:hidden_rows]
    out_part, feed_home = lax.optimization_barrier((out_part, feed_home))
    feed_sum = lax.psum_scatter(
        out_part,
        ("dp", "expert"),
        scatter_dimension=0,
        tiled=True,
    )
    layer_output = hidden + feed_sum.astype(f32)
    gradient = cotangent[0].astype(f32)
    feed_dlogits = gates_back(feed_dgate, feed_weights, feed_matches)
    feed_dnorm = feed_home + jnp.dot(feed_dlogits, feedforward_cols.astype(f32).T, precision=HIGH)
    grad_gain_feed = jnp.sum(feed_dnorm * unit_feed, axis=0)
    hidden_grad = gradient + norm_back(feed_dnorm, gain_feedforward, unit_feed, factor_feed)

    (sequence_grad,) = gather(
        [(hidden_grad.astype(low), "expert", quarters("xc"))], 5, "gather_cotangents"
    )
    dmix = lax.dot_general(sequence_grad, out_weight, ACROSS, preferred_element_type=f32).astype(low)
    grad_out = lax.dot_general(mixed, sequence_grad, DOWNWARD, preferred_element_type=f32)
    dprojected, gate_parts = attention_back(
        projected, side, prefix_length, log_total, dmix, group_size, tok_rows
    )
    attend_dx = lax.dot_general(dprojected, in_weight, ACROSS, preferred_element_type=f32)
    grad_in = lax.dot_general(sequence_in, dprojected, DOWNWARD, preferred_element_type=f32)
    attend_home = scatter(attend_dx.astype(low), "expert", quarters("cx"), 2, "sum_attention")
    pair_dgate = lax.psum_scatter(
        gate_parts[:, :2].reshape(group_size, tok_rows, 2).transpose(0, 2, 1).reshape(-1, tok_rows),
        "expert",
        scatter_dimension=0,
        tiled=True,
    ).T
    matches = mine(attend_matches_all)
    weights = mine(attend_weights_all)
    dselected = weights * (pair_dgate - jnp.sum(weights * pair_dgate, axis=1, keepdims=True))
    attend_dlogits = jnp.sum(dselected[:, :, None] * matches, axis=1)
    attend_dnorm = attend_home + jnp.dot(
        attend_dlogits, attention_cols.astype(f32).T, precision=HIGH
    )
    grad_gain_attend = jnp.sum(attend_dnorm * unit_attention, axis=0)
    grad_tokens = hidden_grad + norm_back(
        attend_dnorm, gain_attention, unit_attention, factor_attention
    )
    small = jnp.concatenate(
        [
            lax.dot_general(attend_dlogits, attention_in.astype(f32), DOWNWARD, precision=HIGH),
            lax.dot_general(feed_dlogits, feed_in.astype(f32), DOWNWARD, precision=HIGH),
            grad_gain_attend[None],
            grad_gain_feed[None],
        ],
        axis=0,
    )
    small = lax.psum(small.astype(f32), ("dp", "expert"))
    small = lax.dynamic_slice_in_dim(small, lax.axis_index("dp") * rows_in, rows_in, 1)

    grad_query, grad_keyvalue, grad_projection = sum_weights(
        grad_in.astype(low), grad_out.astype(low), feed_sum, ((0, rows_in, "yz"),), 6
    )
    return (
        layer_output.astype(low)[None],
        grad_tokens[None],
        small[2 * group_size],
        small[2 * group_size + 1],
        grad_keyvalue,
        small[: 2 * group_size].T,
        grad_query[None],
        grad_projection[None],
        grad_gate[None],
        grad_up[None],
        grad_down[None],
    )


def solution(mesh):
    in_specs = (
        P("dp", "expert", None),
        P("dp", "expert", None),
        P("dp", None, None),
        P("dp", None, None),
        P("dp"),
        P(),
        P(),
        P("dp", None),
        P("dp", None),
        P("expert", "dp", None),
        P("expert", "dp", None),
        P("expert", "dp", None),
        P("expert", "dp", None),
        P("expert", "dp", None),
    )
    out_specs = (
        P("dp", "expert", None),
        P("dp", "expert", None),
        P("dp"),
        P("dp"),
        P("dp", None),
        P("dp", None),
        P("expert", "dp", None),
        P("expert", "dp", None),
        P("expert", "dp", None),
        P("expert", "dp", None),
        P("expert", "dp", None),
    )
    torus = (mesh.shape["dp"], mesh.shape["expert"]) == (8, 4)
    body = per_device_torus if torus else per_device
    return jax.shard_map(
        body, mesh=mesh, in_specs=in_specs, out_specs=out_specs, check_vma=False
    )
```

```python
import functools

import jax
import jax.numpy as jnp
from jax import lax
from jax.experimental import pallas as pl
from jax.experimental.pallas import tpu as pltpu
from jax.sharding import PartitionSpec as P

HEADS = 16
HEAD_DIM = 128


EPS = 1e-06
NEG = -1e30
HIGH = lax.Precision.HIGHEST
ACROSS = (((1,), (1,)), ((), ()))
DOWNWARD = (((0,), (0,)), ((), ()))


def norm_parts(vector, gain_vector):
    factor = lax.rsqrt(jnp.mean(vector * vector, axis=-1, keepdims=True) + EPS)
    normed = vector * factor
    return (normed * gain_vector, normed, factor)


def norm_back(incoming, gain_vector, normed, factor):
    dnormed = incoming * gain_vector
    return factor * (dnormed - normed * jnp.mean(dnormed * normed, axis=-1, keepdims=True))


def route_plan(sequence_ids, my_index, group_size, tok_rows, slot_count):
    expert_range = jnp.arange(group_size, dtype=jnp.int32)
    matches_all = (sequence_ids[:, :, None] == expert_range[None, None, :]).astype(jnp.int32)
    chosen = jnp.sum(matches_all, axis=1).reshape(group_size, tok_rows, group_size)
    ranking = jnp.cumsum(chosen, axis=1) - chosen
    slot_ids = jnp.arange(slot_count, dtype=jnp.int32)[None, :, None]
    block_pick = (expert_range == my_index).astype(jnp.int32)
    my_chosen = jnp.sum(chosen * block_pick[:, None, None], axis=0).T
    my_ranking = jnp.sum(ranking * block_pick[:, None, None], axis=0).T
    send_table = (
        my_chosen[:, None, :] * (my_ranking[:, None, :] == slot_ids).astype(jnp.int32)
    ).astype(jnp.float32)
    column_chosen = jnp.sum(chosen * block_pick[None, None, :], axis=2)
    column_ranking = jnp.sum(ranking * block_pick[None, None, :], axis=2)
    taken = column_chosen[:, None, :] * (column_ranking[:, None, :] == slot_ids).astype(jnp.int32)
    positions = (
        expert_range[:, None, None] * tok_rows
        + jnp.arange(tok_rows, dtype=jnp.int32)[None, None, :]
    )
    arrival_places = jnp.sum(taken * positions, axis=2).reshape(-1)
    my_ids = lax.dynamic_slice_in_dim(sequence_ids, my_index * tok_rows, tok_rows, 0)
    matches = (my_ids[:, :, None] == expert_range[None, None, :]).astype(jnp.float32)
    return (send_table, arrival_places, matches)


def pair_gates(logits, matches):
    selected = jnp.sum(matches * logits[:, None, :], axis=2)
    largest = jnp.max(selected, axis=1, keepdims=True)
    exponent = jnp.exp(selected - largest)
    weights = exponent / jnp.sum(exponent, axis=1, keepdims=True)
    return (weights, jnp.sum(weights[:, :, None] * matches, axis=1))


def gates_back(dgate, weights, matches):
    dweights = jnp.sum(dgate[:, None, :] * matches, axis=2)
    dselected = weights * (dweights - jnp.sum(weights * dweights, axis=1, keepdims=True))
    return jnp.sum(dselected[:, :, None] * matches, axis=1)


def merge_back(send_table, gate_table, returned):
    weighted = send_table * gate_table.T[:, None, :]
    return jnp.einsum("ect,ecd->td", weighted, returned.astype(jnp.float32), precision=HIGH)


def branch_cotangent(send_table, gate_table, returned, incoming):
    spread_grad = jnp.einsum("ect,td->ecd", send_table, incoming, precision=HIGH)
    slot_gate = jnp.sum(send_table * gate_table.T[:, None, :], axis=2)
    cotangent_rows = (spread_grad * slot_gate[:, :, None]).astype(jnp.bfloat16)
    slot_dgate = jnp.sum(spread_grad * returned.astype(jnp.float32), axis=2)
    dgate = jnp.einsum("ect,ec->te", send_table, slot_dgate, precision=HIGH)
    return (cotangent_rows, dgate)


def expert_matches(ids, group_size):
    expert_range = jnp.arange(group_size, dtype=jnp.int32)
    return (ids[:, :, None] == expert_range[None, None, :]).astype(jnp.float32)


def expert_table(ids, my_index, group_size, tok_rows, slot_count):
    blocks = ids.reshape(-1, tok_rows, 2)
    chosen = jnp.sum((blocks == my_index).astype(jnp.float32), axis=2)
    before = jnp.triu(jnp.ones((tok_rows, tok_rows), jnp.float32), 1)
    ranking = jnp.dot(chosen, before)
    slot_ids = jnp.arange(slot_count, dtype=jnp.float32)[None, :, None]
    taken = chosen[:, None, :] * (ranking[:, None, :] == slot_ids).astype(jnp.float32)
    other = jnp.sum(blocks, axis=2) - my_index
    slot_other = jnp.sum(taken * other[:, None, :].astype(jnp.float32), axis=2)
    return (taken.astype(jnp.bfloat16), slot_other.reshape(-1).astype(jnp.int32))


def own_gate(logits, other, my_index):
    expert_range = jnp.arange(logits.shape[1], dtype=jnp.int32)[None]
    mine = jnp.sum(jnp.where(expert_range == my_index, logits, 0.0), axis=1, keepdims=True)
    theirs = jnp.sum(jnp.where(expert_range == other[:, None], logits, 0.0), axis=1, keepdims=True)
    return jax.nn.sigmoid(mine - theirs)


def pick_rows(taken, rows):
    blocks, slots, tokens = taken.shape
    picked = jnp.einsum(
        "bct,btd->bcd",
        taken,
        rows.reshape(blocks, tokens, -1),
        preferred_element_type=jnp.float32,
    )
    return picked.astype(jnp.bfloat16).reshape(blocks * slots, -1)


def return_rows(taken, rows):
    blocks, slots, tokens = taken.shape
    placed = jnp.einsum(
        "bct,bcd->btd",
        taken,
        rows.reshape(blocks, slots, -1),
        preferred_element_type=jnp.float32,
    )
    return placed.astype(jnp.bfloat16).reshape(blocks * tokens, -1)


def gather_all(rows):
    return lax.all_gather(rows, ("dp", "expert"), axis=0, tiled=True)


def scatter_all(rows):
    return lax.psum_scatter(rows, ("dp", "expert"), scatter_dimension=0, tiled=True)


def dispatch(rows):
    return lax.all_to_all(rows, "expert", split_axis=0, concat_axis=0, tiled=True)


def collect(rows):
    return lax.all_to_all(rows, "expert", split_axis=0, concat_axis=0, tiled=True)


def spread_rows(rows):
    return lax.all_gather(rows, "dp", axis=0, tiled=True)


def sum_rows(terms):
    return lax.psum_scatter(
        terms.astype(jnp.bfloat16), "dp", scatter_dimension=0, tiled=True
    ).astype(jnp.float32)


def send_rows(send_table, rows):
    return jnp.einsum(
        "ect,td->ecd", send_table.astype(jnp.bfloat16), rows, preferred_element_type=jnp.float32
    ).astype(jnp.bfloat16)


def per_device(
    tokens,
    cotangent,
    attention_routes,
    feedforward_routes,
    prefix_length,
    gain_attention,
    gain_feedforward,
    keyvalue_weight,
    router_weight,
    query_weight,
    output_weight,
    gate_weight,
    up_weight,
    down_weight,
):
    my_index = lax.axis_index("expert")
    group_size = lax.axis_size("expert")
    inputs = tokens[0].astype(jnp.float32)
    tok_rows = inputs.shape[0]
    model_width = inputs.shape[1]
    seq_total = tok_rows * group_size
    slot_count = 5 * 2 * tok_rows // (4 * group_size)
    query_width = HEADS * HEAD_DIM
    scaling = HEAD_DIM ** (-0.5)
    keyvalue_full, router_full, query_full, output_full = (
        lax.all_gather(keyvalue_weight, "dp", axis=0, tiled=True),
        lax.all_gather(router_weight, "dp", axis=0, tiled=True),
        lax.all_gather(query_weight[0], "dp", axis=0, tiled=True),
        lax.all_gather(output_weight[0], "dp", axis=0, tiled=True),
    )
    every_route = lax.all_gather(feedforward_routes[0], "dp", axis=0, tiled=True)
    cot_everyone = gather_all(cotangent[0])
    attention_cols = router_full[:, :group_size]
    feedforward_cols = router_full[:, group_size:]
    normed_attention, unit_attention, factor_attention = norm_parts(inputs, gain_attention)
    attention_in = normed_attention.astype(jnp.bfloat16)
    keyvalue_rows = jnp.dot(attention_in, keyvalue_full, preferred_element_type=jnp.float32).astype(
        jnp.bfloat16
    )
    keyvalue_seq = lax.all_gather(keyvalue_rows, "expert", axis=0, tiled=True)
    key_rows = keyvalue_seq[:, :query_width].reshape(seq_total, HEADS, HEAD_DIM)
    value_rows = keyvalue_seq[:, query_width:].reshape(seq_total, HEADS, HEAD_DIM)
    attend_table, attend_places, attend_matches = route_plan(
        attention_routes[0], my_index, group_size, tok_rows, slot_count
    )
    attend_logits = jnp.dot(attention_in, attention_cols, preferred_element_type=jnp.float32)
    attend_weights, attend_gate = pair_gates(attend_logits, attend_matches)
    arrived = dispatch(send_rows(attend_table, attention_in)).reshape(-1, model_width)
    queries = jnp.dot(arrived, query_full, preferred_element_type=jnp.float32).astype(jnp.bfloat16)
    queries = queries.reshape(-1, HEADS, HEAD_DIM)
    key_places = jnp.arange(seq_total, dtype=jnp.int32)
    allowed = (key_places[None, :] <= attend_places[:, None]) | (
        key_places[None, :] < prefix_length[0]
    )
    scores = (
        jnp.einsum("rhd,khd->hrk", queries, key_rows, preferred_element_type=jnp.float32) * scaling
    )
    scores = jnp.where(allowed[None], scores, NEG)
    row_max = jnp.max(scores, axis=2, keepdims=True)
    exponent = jnp.exp(scores - row_max)
    row_total = jnp.sum(exponent, axis=2, keepdims=True)
    log_total = row_max + jnp.log(row_total)
    attention_low = (exponent / row_total).astype(jnp.bfloat16)
    mixture = jnp.einsum(
        "hrk,khd->rhd", attention_low, value_rows, preferred_element_type=jnp.float32
    )
    mixture = mixture.astype(jnp.bfloat16).reshape(-1, query_width)
    attend_branch = jnp.dot(mixture, output_full, preferred_element_type=jnp.float32).astype(
        jnp.bfloat16
    )
    attend_returned = collect(attend_branch.reshape(group_size, slot_count, model_width))
    hidden = inputs + merge_back(attend_table, attend_gate, attend_returned)
    normed_feed, unit_feed, factor_feed = norm_parts(hidden, gain_feedforward)
    feed_in = normed_feed.astype(jnp.bfloat16)
    feed_ids = lax.dynamic_slice_in_dim(
        feedforward_routes[0], my_index * tok_rows, tok_rows, 0
    )
    feed_matches = expert_matches(feed_ids, group_size)
    feed_logits = jnp.dot(feed_in, feedforward_cols, preferred_element_type=jnp.float32)
    feed_weights, feed_gate = pair_gates(feed_logits, feed_matches)
    everyone = gather_all(feed_in)
    feed_taken, feed_pairs = expert_table(every_route, my_index, group_size, tok_rows, slot_count)
    pick = functools.partial(pick_rows, feed_taken)
    feed_rows = pick(everyone)
    cot_rows = pick(cot_everyone)
    row_logits = jnp.dot(feed_rows, feedforward_cols, preferred_element_type=jnp.float32)
    row_gate = own_gate(row_logits, feed_pairs, my_index)
    pre_gate = lax.dot_general(feed_rows, gate_weight[0], ACROSS, preferred_element_type=jnp.float32)
    pre_up = lax.dot_general(feed_rows, up_weight[0], ACROSS, preferred_element_type=jnp.float32)
    sigmoid_gate = jax.nn.sigmoid(pre_gate)
    act = pre_gate * sigmoid_gate * pre_up
    act_low = act.astype(jnp.bfloat16)
    act_scaled = (act * row_gate).astype(jnp.bfloat16)
    act_grad = lax.dot_general(cot_rows, down_weight[0], ACROSS, preferred_element_type=jnp.float32)
    slot_dgate = jnp.sum(act_low.astype(jnp.float32) * act_grad, axis=1)
    act_grad = act_grad * row_gate
    dgate_low = (act_grad * pre_up * sigmoid_gate * (1.0 + pre_gate * (1.0 - sigmoid_gate))).astype(
        jnp.bfloat16
    )
    dup_low = (act_grad * pre_gate * sigmoid_gate).astype(jnp.bfloat16)
    feed_dx = (
        jnp.dot(dgate_low, gate_weight[0], preferred_element_type=jnp.float32)
        + jnp.dot(dup_low, up_weight[0], preferred_element_type=jnp.float32)
    ).astype(jnp.bfloat16)
    feed_branch = jnp.dot(act_scaled, down_weight[0], preferred_element_type=jnp.float32).astype(
        jnp.bfloat16
    )
    grad_gate = lax.dot_general(dgate_low, feed_rows, DOWNWARD, preferred_element_type=jnp.float32)
    grad_up = lax.dot_general(dup_low, feed_rows, DOWNWARD, preferred_element_type=jnp.float32)
    grad_down = lax.dot_general(act_scaled, cot_rows, DOWNWARD, preferred_element_type=jnp.float32)
    token_dgate = jnp.einsum(
        "bct,bc->bt",
        feed_taken.astype(jnp.float32),
        slot_dgate.reshape(-1, slot_count),
        precision=HIGH,
    ).reshape(-1, 1)
    own_column = (jnp.arange(group_size) == my_index).astype(jnp.float32)[None]
    feed_dgate = scatter_all(token_dgate * own_column)
    feed_home = scatter_all(return_rows(feed_taken, feed_dx)).astype(jnp.float32)
    feed_sum = scatter_all(return_rows(feed_taken, feed_branch)).astype(jnp.float32)
    layer_output = hidden + feed_sum
    gradient = cotangent[0].astype(jnp.float32)
    feed_dlogits = gates_back(feed_dgate, feed_weights, feed_matches)
    feed_dnorm = feed_home + jnp.dot(
        feed_dlogits, feedforward_cols.astype(jnp.float32).T, precision=HIGH
    )
    grad_gain_feed = jnp.sum(feed_dnorm * unit_feed, axis=0)
    hidden_grad = gradient + norm_back(feed_dnorm, gain_feedforward, unit_feed, factor_feed)
    attend_cot, attend_dgate = branch_cotangent(
        attend_table, attend_gate, attend_returned, hidden_grad
    )
    attend_dlogits = gates_back(attend_dgate, attend_weights, attend_matches)
    attend_cot_rows = dispatch(attend_cot).reshape(-1, model_width)
    dmixture = lax.dot_general(
        attend_cot_rows, output_full, ACROSS, preferred_element_type=jnp.float32
    )
    dmixture = dmixture.astype(jnp.bfloat16).reshape(-1, HEADS, HEAD_DIM)
    grad_projection = lax.dot_general(
        mixture, attend_cot_rows, DOWNWARD, preferred_element_type=jnp.float32
    )
    scores_again = (
        jnp.einsum("rhd,khd->hrk", queries, key_rows, preferred_element_type=jnp.float32) * scaling
    )
    attention = jnp.where(allowed[None], jnp.exp(scores_again - log_total), 0.0)
    attention_again = attention.astype(jnp.bfloat16)
    dattention = jnp.einsum(
        "rhd,khd->hrk", dmixture, value_rows, preferred_element_type=jnp.float32
    )
    row_dot = jnp.sum(attention * dattention, axis=2, keepdims=True)
    dscores = (attention * (dattention - row_dot)).astype(jnp.bfloat16)
    dqueries = (
        jnp.einsum("hrk,khd->rhd", dscores, key_rows, preferred_element_type=jnp.float32) * scaling
    )
    dqueries = dqueries.astype(jnp.bfloat16).reshape(-1, query_width)
    dkeys = (
        jnp.einsum("hrk,rhd->khd", dscores, queries, preferred_element_type=jnp.float32) * scaling
    )
    dvalues = jnp.einsum(
        "hrk,rhd->khd", attention_again, dmixture, preferred_element_type=jnp.float32
    )
    grad_query = lax.dot_general(arrived, dqueries, DOWNWARD, preferred_element_type=jnp.float32)
    attend_dx = lax.dot_general(dqueries, query_full, ACROSS, preferred_element_type=jnp.float32)
    keyvalue_terms = jnp.concatenate(
        [dkeys.reshape(seq_total, query_width), dvalues.reshape(seq_total, query_width)], axis=1
    ).reshape(group_size, tok_rows, 2 * query_width)
    attend_home, keyvalue_home = (
        lax.all_to_all(
            attend_dx.reshape(group_size, slot_count, model_width).astype(jnp.bfloat16),
            "expert",
            split_axis=0,
            concat_axis=0,
            tiled=True,
        ).astype(jnp.float32),
        lax.all_to_all(
            keyvalue_terms.astype(jnp.bfloat16), "expert", split_axis=0, concat_axis=0, tiled=True
        ).astype(keyvalue_terms.dtype),
    )
    dkeyvalue = jnp.sum(keyvalue_home, axis=0).astype(jnp.bfloat16)
    attend_dnorm = (
        jnp.einsum("ect,ecd->td", attend_table, attend_home, precision=HIGH)
        + lax.dot_general(dkeyvalue, keyvalue_full, ACROSS, preferred_element_type=jnp.float32)
        + jnp.dot(attend_dlogits, attention_cols.astype(jnp.float32).T, precision=HIGH)
    )
    grad_keyvalue = lax.dot_general(
        attention_in, dkeyvalue, DOWNWARD, preferred_element_type=jnp.float32
    )
    grad_router = jnp.concatenate(
        [
            jnp.dot(attention_in.astype(jnp.float32).T, attend_dlogits, precision=HIGH),
            jnp.dot(feed_in.astype(jnp.float32).T, feed_dlogits, precision=HIGH),
        ],
        axis=1,
    )
    grad_gain_attend = jnp.sum(attend_dnorm * unit_attention, axis=0)
    grad_tokens = hidden_grad + norm_back(
        attend_dnorm, gain_attention, unit_attention, factor_attention
    )
    reduced = (
        lax.psum_scatter(
            grad_keyvalue.astype(jnp.bfloat16), "dp", scatter_dimension=0, tiled=True
        ).astype(jnp.float32),
        lax.psum_scatter(
            grad_router.astype(jnp.bfloat16), "dp", scatter_dimension=0, tiled=True
        ).astype(jnp.float32),
        lax.psum_scatter(
            grad_query.astype(jnp.bfloat16), "dp", scatter_dimension=0, tiled=True
        ).astype(jnp.float32),
        lax.psum_scatter(
            grad_projection.astype(jnp.bfloat16), "dp", scatter_dimension=0, tiled=True
        ).astype(jnp.float32),
        lax.psum_scatter(
            grad_gain_attend.astype(jnp.bfloat16), "dp", scatter_dimension=0, tiled=True
        ).astype(jnp.float32),
        lax.psum_scatter(
            grad_gain_feed.astype(jnp.bfloat16), "dp", scatter_dimension=0, tiled=True
        ).astype(jnp.float32),
    )
    shared = (
        lax.psum(reduced[0].astype(jnp.bfloat16), "expert").astype(jnp.float32),
        lax.psum(reduced[1].astype(jnp.bfloat16), "expert").astype(jnp.float32),
        lax.psum(reduced[4].astype(jnp.bfloat16), "expert").astype(jnp.float32),
        lax.psum(reduced[5].astype(jnp.bfloat16), "expert").astype(jnp.float32),
    )
    return (
        layer_output.astype(jnp.bfloat16)[None],
        grad_tokens[None],
        shared[2],
        shared[3],
        shared[0],
        shared[1],
        reduced[2][None],
        reduced[3][None],
        grad_gate[None],
        grad_up[None],
        grad_down[None],
    )


MESH = pl.DeviceIdType.MESH
CHIPS_Z = 4
TURNS = ((3, 2, 1, 0), (3, 0, 2, 1), (0, 3, 1, 2), (0, 1, 2, 3))


class Place:
    def __init__(self):
        self.dp, self.expert = lax.axis_index("dp"), lax.axis_index("expert")
        self.at = {
            "z": self.dp // 2,
            "y": self.dp % 2,
            "x": self.expert // 2,
            "c": self.expert % 2,
        }

    def across(self, axis):
        back = 1 - 2 * self.at[axis]
        if axis == "c":
            return (self.dp, self.expert + back)
        if axis == "x":
            return (self.dp, self.expert + 2 * back)
        return (self.dp + back, self.expert)

    def along(self, step):
        return (self.dp + 2 * step, self.expert)

    def block(self, whose, z, flips):
        at = {a: self.at[a] + flips.get(a, 0) * (1 - 2 * self.at[a]) for a in "xyc"}
        dp, expert = z * 2 + at["y"], at["x"] * 2 + at["c"]
        return {"all": dp * 4 + expert, "dp": dp, "expert": expert}[whose]


def enter(place, axes, others=()):
    barrier, count = pltpu.get_barrier_semaphore(), 0
    for device, condition in others:

        def greet(device=device):
            pl.semaphore_signal(barrier, inc=1, device_id=device, device_id_type=MESH)

        on(condition, greet)
        count = count + (1 if condition is None else condition.astype(jnp.int32))
    for axis in axes:
        if axis != "z":
            pl.semaphore_signal(
                barrier, inc=1, device_id=place.across(axis), device_id_type=MESH
            )
            count += 1
    if "z" in axes:
        z = place.at["z"]
        for step, there in ((-1, z > 0), (1, z < CHIPS_Z - 1)):

            @pl.when(there)
            def _(step=step):
                pl.semaphore_signal(
                    barrier, inc=1, device_id=place.along(step), device_id_type=MESH
                )

            count = count + there.astype(jnp.int32)
    pl.semaphore_wait(barrier, count)


def on(condition, action):
    if condition is None:
        action()
    else:
        pl.when(condition)(action)


def both(a, b):
    return b if a is None else a if b is None else a & b


class Post:
    def __init__(self, sems, place):
        self.sems, self.place, self.sent = sems, place, []

    def send(self, source, target, arrival, device, condition=None):
        number = len(self.sent)

        def copy():
            return pltpu.make_async_remote_copy(
                src_ref=source,
                dst_ref=target,
                send_sem=self.sems.at[number],
                recv_sem=arrival,
                device_id=device,
                device_id_type=MESH,
            )

        self.sent.append((condition, copy))
        on(condition, lambda: copy().start())

    def arrived(self, target, arrival):
        pltpu.make_async_remote_copy(
            src_ref=target,
            dst_ref=target,
            send_sem=self.sems.at[0],
            recv_sem=arrival,
            device_id=self.place.across("c"),
            device_id_type=MESH,
        ).wait_recv()

    def close(self):
        for condition, copy in self.sent:
            on(condition, lambda copy=copy: copy().wait_send())


FLIPS = {"x": 4, "y": 2, "c": 1}


def gather_plan(jobs, place, post, sources, targets, arrive_sems, own_sems):
    z_here = place.at["z"]
    line = 0
    waves, owns, starts = {}, [], []
    for j, (whose, rows, pieces) in enumerate(jobs):
        own = pltpu.make_async_copy(
            sources[j],
            targets[j].at[pl.ds(place.block(whose, z_here, {}) * rows, rows)],
            own_sems.at[j],
        )
        owns.append(own)
        begin = [own.start]
        for first, length, order in pieces:
            def part(z, flips, j=j, whose=whose, rows=rows, first=first, length=length):
                at = place.block(whose, z, flips) * rows + first
                return targets[j].at[pl.ds(at, length)]

            def mark(z, flips, line=line):
                return arrive_sems.at[line, z * 8 + sum(FLIPS[a] * v for a, v in flips.items())]

            def hand_on(source, z, flips, depth, side, wave, condition, order=order, part=part, mark=mark):
                for axis in order[max(depth, 0) :]:
                    if axis == "z" and (depth < 0 or order[depth] != "z"):
                        for step in (1, -1):
                            there = (z_here < CHIPS_Z - 1) if step > 0 else (z_here > 0)
                            post.send(source, part(z, flips), mark(z, flips), place.along(step), both(condition, there))
                    elif axis == "z":
                        there = (z_here < CHIPS_Z - 1) if side > 0 else (z_here > 0)
                        post.send(source, part(z, flips), mark(z, flips), place.along(side), both(condition, there))
                    elif depth < 0 or axis != order[depth]:
                        seen = dict(flips)
                        seen[axis] = 1
                        post.send(source, part(z, flips), mark(z, seen), place.across(axis), condition)

            def come(z, flips, depth, side, hops, wave, condition, order=order, part=part, mark=mark, hand_on=hand_on):
                def act():
                    on(condition, lambda: post.arrived(part(z, flips), mark(z, flips)))
                    hand_on(part(z, flips), z, flips, depth, side, wave, condition)

                waves.setdefault(wave, []).append(act)
                spread(z, flips, depth, side, hops, wave, condition, order, come)

            begin.append(
                lambda hand_on=hand_on, j=j, first=first, length=length: hand_on(
                    sources[j].at[pl.ds(first, length)], z_here, {}, -1, 0, 0, None
                )
            )
            spread(z_here, {}, -1, 0, 0, 0, None, order, come)
            line += 1
        starts.append(begin)
    return starts, waves, owns


def gather_kernel(jobs, axes, *refs):
    count = len(jobs)
    sources, targets = refs[:count], refs[count : 2 * count]
    send_sems, arrive_sems, own_sems = refs[2 * count :]
    place = Place()
    enter(place, axes)
    post = Post(send_sems, place)
    starts, waves, owns = gather_plan(jobs, place, post, sources, targets, arrive_sems, own_sems)
    for act in sum(starts, []):
        act()
    for wave in sorted(waves):
        for act in waves[wave]:
            act()
    for own in owns:
        own.wait()
    post.close()


def spread(z, flips, depth, side, hops, wave, condition, order, come):
    z_here = lax.axis_index("dp") // 2
    for later in range(max(depth, 0), len(order)):
        axis = order[later]
        if axis == "z":
            if depth >= 0 and order[depth] == "z":
                if hops < CHIPS_Z - 1:
                    far = hops + 1
                    there = (z_here >= far) if side > 0 else (z_here + far < CHIPS_Z)
                    come(z_here - side * far, flips, later, side, far, wave + 1, there)
            else:
                for step in (1, -1):
                    there = (z_here >= 1) if step > 0 else (z_here + 1 < CHIPS_Z)
                    come(z_here - step, flips, later, step, 1, wave + 1, both(condition, there))
        elif later > depth:
            seen = dict(flips)
            seen[axis] = 1
            come(z, seen, later, 0, 0, wave + 1, condition)


def gather(jobs, collective_id, name):
    arrays = [rows for rows, _, _ in jobs]
    sizes = {"all": 32, "dp": 8, "expert": 4}
    plan = tuple((whose, rows.shape[0], pieces) for rows, whose, pieces in jobs)
    axes = "".join(a for a in "cxyz" if any(a in order for _, _, ps in plan for _, _, order in ps))
    lines = sum(len(ps) for _, _, ps in plan)
    any_spec = pl.BlockSpec(memory_space=pltpu.HBM)
    return pl.pallas_call(
        functools.partial(gather_kernel, plan, axes),
        out_shape=[
            jax.ShapeDtypeStruct((sizes[whose] * r.shape[0], r.shape[1]), r.dtype)
            for r, whose, _ in jobs
        ],
        in_specs=[any_spec] * len(jobs),
        out_specs=[any_spec] * len(jobs),
        scratch_shapes=[
            pltpu.SemaphoreType.DMA((110 * lines,)),
            pltpu.SemaphoreType.DMA((lines, 32)),
            pltpu.SemaphoreType.DMA((len(jobs),)),
        ],
        compiler_params=pltpu.CompilerParams(
            collective_id=collective_id, has_side_effects=True
        ),
        name=name,
    )(*arrays)


def add_into(target, terms, length):
    @pl.loop(0, length // 16)
    def _(r):
        at = pl.ds(pl.multiple_of(r * 16, 16), 16)
        total = target[at, :].astype(jnp.float32)
        for term in terms:
            total = total + term[at, :].astype(jnp.float32)
        target[at, :] = total.astype(jnp.bfloat16)


def scatter_rooms(rows, width, order):
    steps, turns = len(order.replace("z", "")), CHIPS_Z if "z" in order else 1
    blocks = [turns * 2 ** (steps - 1)]
    blocks += [turns * 2 ** (steps - 1 - stage) for stage in range(steps)]
    if "z" in order:
        blocks.append(CHIPS_Z + 1)
    return [pltpu.VMEM((n, rows, width), jnp.bfloat16) for n in blocks]


def scatter_sems(order, pieces):
    steps, turns = len(order.replace("z", "")), CHIPS_Z if "z" in order else 1
    return [
        pltpu.SemaphoreType.DMA((turns * 2 ** (steps - 1),)),
        pltpu.SemaphoreType.DMA((pieces, steps, turns * 2 ** (steps - 1))),
        pltpu.SemaphoreType.DMA((pieces, CHIPS_Z + 1)),
    ]


def scatter_plan(whose, rows, pieces, place, post, source, rooms, sems):
    flat = [order.replace("z", "") for _, _, order in pieces]
    steps = len(flat[0])
    lined = "z" in pieces[0][2]
    turns = CHIPS_Z if lined else 1
    acc, bins, line = rooms[0], rooms[1 : 1 + steps], rooms[-1]
    load_sems, bin_sems, line_sems = sems
    z_here = place.at["z"]
    if lined:
        turn = [
            sum((z_here == z).astype(jnp.int32) * seq[k] for z, seq in enumerate(TURNS))
            for k in range(CHIPS_Z)
        ]
    else:
        turn = [z_here]
    slot_z = lambda k: turn[k] if lined else 0
    keep = 2 ** (steps - 1)
    names = sorted(flat[0][1:])
    loads = {}
    for k in range(turns):
        for n in reversed(range(keep)):
            flips = {a: (n >> i) & 1 for i, a in enumerate(names)}
            at = slot_z(k) * keep + n
            loads[k, n] = pltpu.make_async_copy(
                source.at[pl.ds(place.block(whose, turn[k], flips) * rows, rows)],
                acc.at[at],
                load_sems.at[at],
            )
    loaded = set()

    def mine(p, ref):
        first, length, _ = pieces[p]
        return ref.at[pl.ds(first, length)]

    def code_after(p, stage, flips):
        return sum(flips.get(a, 0) << i for i, a in enumerate(flat[p][stage + 1 :]))

    def gathered(p, k, stage, flips):
        n = sum(flips.get(a, 0) << i for i, a in enumerate(names))
        if (k, n) not in loaded:
            loads[k, n].wait()
            loaded.add((k, n))
        terms = []
        for before in range(stage):
            at = slot_z(k) * 2 ** (steps - 1 - before) + code_after(p, before, flips)
            ref = mine(p, bins[before].at[at])
            post.arrived(ref, bin_sems.at[p, before, at])
            terms.append(ref)
        block = mine(p, acc.at[slot_z(k) * keep + n])
        add_into(block, terms, pieces[p][1])
        return block

    def leave(k, stage):
        for code in reversed(range(2 ** (steps - 1 - stage))):
            for p in range(len(pieces)):
                flips = {a: (code >> i) & 1 for i, a in enumerate(flat[p][stage + 1 :])}
                flips[flat[p][stage]] = 1
                if stage == 0:
                    at = place.block(whose, turn[k], flips) * rows + pieces[p][0]
                    block = source.at[pl.ds(at, pieces[p][1])]
                else:
                    block = gathered(p, k, stage, flips)
                at = slot_z(k) * 2 ** (steps - 1 - stage) + code
                post.send(
                    block,
                    mine(p, bins[stage].at[at]),
                    bin_sems.at[p, stage, at],
                    place.across(flat[p][stage]),
                )

    def settle(k):
        for p in range(len(pieces)):
            block = gathered(p, k, steps, {})
            if not lined or k == turns - 1:
                continue
            t = turn[k]
            right = t > z_here

            def pass_on(p=p, t=t, block=block):
                ref = mine(p, line.at[t])
                post.arrived(ref, line_sems.at[p, t])
                add_into(block, [ref], pieces[p][1])

            pl.when((right & (z_here > 0)) | (~right & (z_here < CHIPS_Z - 1)))(pass_on)
            slot = jnp.where(t == z_here - 1, CHIPS_Z, t)
            post.send(
                block,
                mine(p, line.at[slot]),
                line_sems.at[p, slot],
                place.along(jnp.where(right, 1, -1)),
            )

    def finish(p):
        block = mine(p, acc.at[z_here * keep if lined else 0])
        if lined:
            for slot, there in ((z_here, z_here > 0), (CHIPS_Z, z_here < CHIPS_Z - 1)):

                def last(slot=slot):
                    ref = mine(p, line.at[slot])
                    post.arrived(ref, line_sems.at[p, slot])
                    add_into(block, [ref], pieces[p][1])

                pl.when(there)(last)
        return block

    works = [(-1, lambda k=k: leave(k, 0)) for k in range(turns)]
    for time in range(turns + steps):
        for stage in range(1, steps + 1):
            k = time - stage + 1
            if 0 <= k < turns:
                act = settle if stage == steps else lambda k, stage=stage: leave(k, stage)
                works.append((time, lambda k=k, act=act: act(k)))
    return list(loads.values()), works, finish


def sends_of(order, pieces):
    steps, turns = len(order.replace("z", "")), CHIPS_Z if "z" in order else 1
    return pieces * (turns * 2**steps + 4)


def widen(target, block, length):
    @pl.loop(0, length // 16)
    def _(r):
        at = pl.ds(pl.multiple_of(r * 16, 16), 16)
        target[at, :] = block[at, :].astype(jnp.float32)


def scatter_kernel(whose, rows, pieces, columns, filler, source, *refs):
    source = source.at[:, pl.ds(*columns)]
    given, refs = refs[: filler.operands], refs[filler.operands :]
    result, made, refs = refs[0], refs[1 : 1 + filler.results], refs[1 + filler.results :]
    rooms, refs = refs[: len(refs) - 4 - filler.rooms], refs[len(refs) - 4 - filler.rooms :]
    send_sems, sems, own = refs[0], refs[1:4], refs[4:]
    place = Place()
    post = Post(send_sems, place)
    loads, works, finish = scatter_plan(whose, rows, pieces, place, post, source, rooms, sems)
    for load in loads:
        load.start()
    enter(place, "".join(a for a in "cxyz" if a in pieces[0][2]))
    steps = filler.start(given, made, own)
    slots = [number for number, (time, _) in enumerate(works) if time >= 0]
    slots = slots[:: -(-len(slots) // filler.turns)]
    done = 0
    for number, (_, act) in enumerate(works):
        act()
        if number in slots:
            share = steps * (slots.index(number) + 1) // len(slots)
            filler.run(given, made, own, done, share)
            done = share
    for p in range(len(pieces)):
        first, length, _ = pieces[p]
        widen(result.at[pl.ds(first, length)], finish(p), length)
    filler.end(given, made, own)
    post.close()


class Nothing:
    operands = results = rooms = 0
    turns = 12
    shapes, scratch = [], []

    def start(self, given, made, own):
        return 0

    def run(self, given, made, own, first, last):
        pass

    def end(self, given, made, own):
        pass


class WeightGrads(Nothing):
    operands, results, rooms = 4, 2, 6
    TILE, CHUNK = 256, 512

    def __init__(self, rows, wide, narrow, width):
        self.chunks = rows // self.CHUNK
        self.tiles = (wide // self.TILE, narrow // self.TILE)
        self.shapes = [
            jax.ShapeDtypeStruct((wide, width), jnp.float32),
            jax.ShapeDtypeStruct((narrow, width), jnp.float32),
        ]
        self.scratch = [
            pltpu.VMEM((2, self.CHUNK, self.TILE), jnp.bfloat16),
            pltpu.VMEM((2, self.CHUNK, width), jnp.bfloat16),
            pltpu.VMEM((self.TILE, width), jnp.float32),
            pltpu.VMEM((self.TILE, width), jnp.float32),
            pltpu.SemaphoreType.DMA((2, 2)),
            pltpu.SemaphoreType.DMA((2,)),
        ]

    def copies(self, given, own, step, second):
        tile, chunk = step // self.chunks - (self.tiles[0] if second else 0), step % self.chunks
        slot = step % 2
        rows = pl.ds(pl.multiple_of(chunk * self.CHUNK, self.CHUNK), self.CHUNK)
        cols = pl.ds(pl.multiple_of(tile * self.TILE, self.TILE), self.TILE)
        left, right = given[2 * second], given[2 * second + 1]
        return [
            pltpu.make_async_copy(left.at[rows, cols], own[0].at[slot], own[4].at[slot, 0]),
            pltpu.make_async_copy(right.at[rows], own[1].at[slot], own[4].at[slot, 1]),
        ]

    def fetch(self, given, own, step, start):
        edge = self.tiles[0] * self.chunks
        for second in (0, 1):

            @pl.when((step >= edge) if second else (step < edge))
            def _(second=second):
                for copy in self.copies(given, own, step, second):
                    copy.start() if start else copy.wait()

    def put(self, made, own, tile, parity, start):
        for second in (0, 1):

            @pl.when((tile >= self.tiles[0]) if second else (tile < self.tiles[0]))
            def _(second=second):
                at = tile - (self.tiles[0] if second else 0)
                rows = pl.ds(pl.multiple_of(at * self.TILE, self.TILE), self.TILE)
                copy = pltpu.make_async_copy(
                    own[2 + parity], made[second].at[rows], own[5].at[parity]
                )
                copy.start() if start else copy.wait()

    def start(self, given, made, own):
        self.fetch(given, own, jnp.int32(0), True)
        return sum(self.tiles) * self.chunks

    def run(self, given, made, own, first, last):
        total = sum(self.tiles) * self.chunks

        @pl.loop(first, last)
        def _(step):
            tile, chunk = step // self.chunks, step % self.chunks

            @pl.when(step + 1 < total)
            def _():
                self.fetch(given, own, step + 1, True)

            self.fetch(given, own, step, False)
            part = lax.dot_general(
                own[0][step % 2], own[1][step % 2], DOWNWARD, preferred_element_type=jnp.float32
            )
            for parity in (0, 1):

                @pl.when(tile % 2 == parity)
                def _(parity=parity):
                    acc = own[2 + parity]

                    @pl.when(chunk == 0)
                    def _():
                        @pl.when(tile >= 2)
                        def _():
                            self.put(made, own, tile - 2, parity, False)

                        acc[...] = part

                    @pl.when(chunk > 0)
                    def _():
                        acc[...] += part

                    @pl.when(chunk == self.chunks - 1)
                    def _():
                        self.put(made, own, tile, parity, True)

    def end(self, given, made, own):
        tiles = sum(self.tiles)
        for tile in (tiles - 2, tiles - 1):
            self.put(made, own, jnp.int32(tile), tile % 2, False)


class LowGrads(Nothing):
    operands, results, rooms = 4, 2, 6
    TILE, turns = 256, 6

    def __init__(self, rows, left, widths):
        self.rows, self.widths = rows, widths
        self.tiles = [n // self.TILE for n in left]
        low = jnp.bfloat16
        self.shapes = [jax.ShapeDtypeStruct((n, w), low) for n, w in zip(left, widths)]
        self.scratch = [
            pltpu.VMEM((2, rows, self.TILE), low),
            pltpu.VMEM((rows, widths[0]), low),
            pltpu.VMEM((rows, widths[1]), low),
            pltpu.VMEM((2, self.TILE, max(widths)), low),
            pltpu.SemaphoreType.DMA((4,)),
            pltpu.SemaphoreType.DMA((2,)),
        ]

    def left(self, given, own, tile, second):
        at = pl.ds(pl.multiple_of(tile * self.TILE, self.TILE), self.TILE)
        slot = tile % 2
        return pltpu.make_async_copy(
            given[2 * second].at[:, at], own[0].at[slot], own[4].at[slot]
        )

    def put(self, made, own, tile, second):
        rows = pl.ds(pl.multiple_of(tile * self.TILE, self.TILE), self.TILE)
        slot = tile % 2
        return pltpu.make_async_copy(
            own[3].at[slot, :, pl.ds(0, self.widths[second])],
            made[second].at[rows],
            own[5].at[slot],
        )

    def start(self, given, made, own):
        for second in (0, 1):
            pltpu.make_async_copy(given[2 * second + 1], own[1 + second], own[4].at[2 + second]).start()
        self.left(given, own, jnp.int32(0), 0).start()
        return sum(self.tiles)

    def run(self, given, made, own, first, last):
        for second in (0, 1):
            base = self.tiles[0] if second else 0
            begin, end = max(first, base), min(last, base + self.tiles[second])
            if begin >= end:
                continue
            if begin == base:
                pltpu.make_async_copy(
                    given[2 * second + 1], own[1 + second], own[4].at[2 + second]
                ).wait()
                if second:
                    self.left(given, own, jnp.int32(0), second).start()

            @pl.loop(begin - base, end - base)
            def _(tile, second=second):
                slot = tile % 2

                @pl.when(tile + 1 < self.tiles[second])
                def _():
                    self.left(given, own, tile + 1, second).start()

                self.left(given, own, tile, second).wait()

                @pl.when(tile >= 2)
                def _():
                    self.put(made, own, tile - 2, second).wait()

                half = self.widths[second] // 2
                for part in (0, 1):
                    cols = slice(part * half, (part + 1) * half)
                    own[3][slot, :, cols] = lax.dot_general(
                        own[0][slot],
                        own[1 + second][:, cols],
                        DOWNWARD,
                        preferred_element_type=jnp.float32,
                    ).astype(jnp.bfloat16)
                self.put(made, own, tile, second).start()

            if end == base + self.tiles[second]:
                for tile in (self.tiles[second] - 2, self.tiles[second] - 1):
                    self.put(made, own, jnp.int32(tile), second).wait()


def scatter(array, whose, pieces, collective_id, name, filler=Nothing(), operands=(), columns=None):
    size = {"all": 32, "dp": 8, "expert": 4}[whose]
    columns = columns or (0, array.shape[1])
    rows, width = array.shape[0] // size, columns[1]
    order, count = pieces[0][2], len(pieces)
    hbm = pl.BlockSpec(memory_space=pltpu.HBM)
    out = pl.pallas_call(
        functools.partial(scatter_kernel, whose, rows, pieces, columns, filler),
        out_shape=[jax.ShapeDtypeStruct((rows, width), jnp.float32)] + filler.shapes,
        in_specs=[hbm] * (1 + len(operands)),
        out_specs=[pl.BlockSpec(memory_space=pltpu.VMEM)] + [hbm] * filler.results,
        scratch_shapes=scatter_rooms(rows, width, order)
        + [pltpu.SemaphoreType.DMA((sends_of(order, count),))]
        + scatter_sems(order, count)
        + filler.scratch,
        compiler_params=pltpu.CompilerParams(
            collective_id=collective_id, has_side_effects=True, vmem_limit_bytes=63 * 2**20
        ),
        name=name,
    )(array, *operands)
    return out if filler.results else out[0]


def sum_weights_kernel(rows, pieces, in_grad, out_grad, query, keyvalue, output, *refs):
    count = len(scatter_rooms(rows, 128, pieces[0][2]))
    in_rooms, out_rooms = refs[:count], refs[count : 2 * count]
    dealt, shared, out_dealt = refs[2 * count : 2 * count + 3]
    send_sems, deal_sems = refs[2 * count + 3 : 2 * count + 5]
    in_sems, out_sems = refs[2 * count + 5 : 2 * count + 8], refs[2 * count + 8 :]
    place = Place()
    post = Post(send_sems, place)
    z, y, e = place.at["z"], place.at["y"], place.expert
    wide = query.shape[1]
    span = (in_grad.shape[1] - wide) // 2
    partner, moves = (e * 2 + y, z), z != e
    peers = []
    for flip_x, flip_c in ((1, 1), (1, 0), (0, 1)):
        x = place.at["x"] + flip_x * (1 - 2 * place.at["x"])
        core = place.at["c"] + flip_c * (1 - 2 * place.at["c"])
        peers.append((x * 2 + core, flip_x * 2 + flip_c))
    in_loads, in_works, in_finish = scatter_plan(
        "dp", rows, pieces, place, post, in_grad, in_rooms, in_sems
    )
    out_loads, out_works, out_finish = scatter_plan(
        "dp", rows, pieces, place, post, out_grad, out_rooms, out_sems
    )
    for load in in_loads + out_loads:
        load.start()
    enter(place, "cxyz", [((place.dp, peers[0][0]), None), (partner, moves)])
    for (_, one), (_, other) in zip(in_works, out_works):
        one()
        other()
    cols = lambda block: pl.ds(pl.multiple_of(block * span, span), span)
    keep = slice(wide, wide + 2 * span)
    for p in range(len(pieces)):
        first, length, _ = pieces[p]
        at = pl.ds(first, length)
        block = in_finish(p)
        for n, (peer, flips) in enumerate(peers):
            post.send(
                block.at[:, cols(peer)],
                dealt.at[at, cols(e)],
                deal_sems.at[p, flips],
                (place.dp, peer),
            )
        post.send(block.at[:, keep], shared.at[2, at], deal_sems.at[p, 4], place.across("x"))
        post.send(block.at[:, keep], shared.at[1, at], deal_sems.at[p, 5], place.across("c"))
        done = out_finish(p)
        post.send(done, out_dealt.at[at], deal_sems.at[p, 6], partner, moves)

    def place_keys(p, flips, block):
        first, length, _ = pieces[p]
        rows_at = pl.ds(first, length)
        x = place.at["x"] + (flips // 2) * (1 - 2 * place.at["x"])
        core = place.at["c"] + (flips % 2) * (1 - 2 * place.at["c"])
        owner = x * 2 + core
        widen(keyvalue.at[rows_at, cols(owner)], block.at[:, pl.ds(0, span)], length)
        widen(
            keyvalue.at[rows_at, cols(wide // span + owner)], block.at[:, pl.ds(span, span)], length
        )

    for p in range(len(pieces)):
        first, length, _ = pieces[p]
        at = pl.ds(first, length)
        post.arrived(shared.at[2, at], deal_sems.at[p, 4])
        post.send(shared.at[2, at], shared.at[3, at], deal_sems.at[p, 7], place.across("c"))
        block = in_rooms[0].at[z, at]
        widen(query.at[at, cols(e)], block.at[:, cols(e)], length)
        place_keys(p, 0, block.at[:, keep])
        place_keys(p, 2, shared.at[2, at])
        post.arrived(shared.at[1, at], deal_sems.at[p, 5])
        place_keys(p, 1, shared.at[1, at])
        for peer, flips in peers:
            post.arrived(dealt.at[at, cols(peer)], deal_sems.at[p, flips])
            widen(query.at[at, cols(peer)], dealt.at[at, cols(peer)], length)

        def came(p=p, at=at, length=length):
            post.arrived(out_dealt.at[at], deal_sems.at[p, 6])
            widen(output.at[at], out_dealt.at[at], length)

        pl.when(moves)(came)
        pl.when(~moves)(
            lambda at=at, length=length: widen(output.at[at], out_rooms[0].at[z, at], length)
        )
        post.arrived(shared.at[3, at], deal_sems.at[p, 7])
        place_keys(p, 3, shared.at[3, at])
    post.close()


def sum_weights(in_grad, out_grad, pieces, collective_id):
    rows, wide = out_grad.shape[0] // 8, out_grad.shape[1]
    order, count = pieces[0][2], len(pieces)
    total = in_grad.shape[1]
    hbm = pl.BlockSpec(memory_space=pltpu.HBM)
    vmem = pl.BlockSpec(memory_space=pltpu.VMEM)
    shape = jax.ShapeDtypeStruct
    return pl.pallas_call(
        functools.partial(sum_weights_kernel, rows, pieces),
        out_shape=[
            shape((rows, wide), jnp.float32),
            shape((rows, 2 * wide), jnp.float32),
            shape((rows, wide), jnp.float32),
        ],
        in_specs=[hbm] * 2,
        out_specs=[vmem] * 3,
        scratch_shapes=scatter_rooms(rows, total, order)
        + scatter_rooms(rows, wide, order)
        + [
            pltpu.VMEM((rows, wide), jnp.bfloat16),
            pltpu.VMEM((4, rows, total - wide), jnp.bfloat16),
            pltpu.VMEM((rows, wide), jnp.bfloat16),
            pltpu.SemaphoreType.DMA((2 * sends_of(order, count) + 8 * count,)),
            pltpu.SemaphoreType.DMA((count, 8)),
        ]
        + scatter_sems(order, count)
        + scatter_sems(order, count),
        compiler_params=pltpu.CompilerParams(
            collective_id=collective_id, has_side_effects=True, vmem_limit_bytes=63 * 2**20
        ),
        name="sum_weights",
    )(in_grad, out_grad)


def weights_kernel(jobs, *refs):
    ready = len(jobs) - 2
    sources, (query, keyvalue, output) = refs[:ready], refs[ready : ready + 3]
    in_shard, out_shard = refs[ready + 3 : ready + 5]
    targets = refs[ready + 5 : 2 * ready + 7]
    send_sems, arrive_sems, own_sems, deal_sems = refs[2 * ready + 7 :]
    place = Place()
    z, y, e = place.at["z"], place.at["y"], place.expert
    span = (in_shard.shape[1] - query.shape[1]) // 2
    wide = query.shape[1]
    partner, moves = (e * 2 + y, z), z != e
    peers = []
    for flip_x, flip_c in ((1, 1), (1, 0), (0, 1)):
        x = place.at["x"] + flip_x * (1 - 2 * place.at["x"])
        core = place.at["c"] + flip_c * (1 - 2 * place.at["c"])
        peers.append((x * 2 + core, flip_x * 2 + flip_c))
    enter(place, "cxyz", [((place.dp, peers[0][0]), None), (partner, moves)])
    post = Post(send_sems, place)
    starts, waves, owns = gather_plan(
        jobs, place, post, list(sources) + [in_shard, out_shard], targets, arrive_sems, own_sems
    )
    cols = lambda block: pl.ds(pl.multiple_of(block * span, span), span)
    for peer, flips in peers:
        post.send(
            query.at[:, cols(peer)], in_shard.at[:, cols(e)], deal_sems.at[flips], (place.dp, peer)
        )
    post.send(output, out_shard, deal_sems.at[4], partner, moves)
    local = [
        pltpu.make_async_copy(query.at[:, cols(e)], in_shard.at[:, cols(e)], deal_sems.at[0]),
        pltpu.make_async_copy(
            keyvalue.at[:, cols(e)], in_shard.at[:, pl.ds(wide, span)], deal_sems.at[5]
        ),
        pltpu.make_async_copy(
            keyvalue.at[:, cols(wide // span + e)],
            in_shard.at[:, pl.ds(wide + span, span)],
            deal_sems.at[6],
        ),
    ]
    for copy in local:
        copy.start()
    stay = pltpu.make_async_copy(output, out_shard, deal_sems.at[7])
    pl.when(~moves)(stay.start)
    for act in sum(starts[:ready], []):
        act()
    for copy in local:
        copy.wait()
    for peer, flips in peers:
        post.arrived(in_shard.at[:, cols(peer)], deal_sems.at[flips])
    for act in starts[ready]:
        act()
    pl.when(~moves)(stay.wait)
    pl.when(moves)(lambda: post.arrived(out_shard, deal_sems.at[4]))
    for act in starts[ready + 1]:
        act()
    for wave in sorted(waves):
        for act in waves[wave]:
            act()
    for own in owns:
        own.wait()
    post.close()


def gather_weights(jobs, query, keyvalue, output, pieces, collective_id):
    rows, wide = query.shape
    span = wide // lax.axis_size("expert")
    shards = [
        jax.ShapeDtypeStruct((rows, wide + 2 * span), query.dtype),
        jax.ShapeDtypeStruct(output.shape, output.dtype),
    ]
    sizes = {"all": 32, "dp": 8, "expert": 4}
    plan = tuple((whose, r.shape[0], ps) for r, whose, ps in jobs)
    plan += tuple(("dp", s.shape[0], pieces) for s in shards)
    lines = sum(len(ps) for _, _, ps in plan)
    hbm = pl.BlockSpec(memory_space=pltpu.HBM)
    gathered = [
        jax.ShapeDtypeStruct((sizes[whose] * r.shape[0], r.shape[1]), r.dtype)
        for r, (whose, _, _) in zip([r for r, _, _ in jobs] + shards, plan)
    ]
    out = pl.pallas_call(
        functools.partial(weights_kernel, plan),
        out_shape=shards + gathered,
        in_specs=[hbm] * (len(jobs) + 3),
        out_specs=[hbm] * (2 + len(gathered)),
        scratch_shapes=[
            pltpu.SemaphoreType.DMA((110 * lines,)),
            pltpu.SemaphoreType.DMA((lines, 32)),
            pltpu.SemaphoreType.DMA((len(plan),)),
            pltpu.SemaphoreType.DMA((8,)),
        ],
        compiler_params=pltpu.CompilerParams(collective_id=collective_id, has_side_effects=True),
        name="gather_weights",
    )(*[r for r, _, _ in jobs], query, keyvalue, output)
    return out[2:]


def attention_bias(bias, block, rows, width, prefix):
    query = block * rows + lax.broadcasted_iota(jnp.int32, (rows, width), 0)
    key = lax.broadcasted_iota(jnp.int32, (rows, width), 1)
    bias[:, :width] = jnp.where((key <= query) | (key < prefix), 0.0, NEG)


def pick_expert(ref, lane, experts, span, chosen):
    total = None
    for e in range(experts):
        cols = ref[:, pl.ds(pl.multiple_of(e * span + lane, HEAD_DIM), HEAD_DIM)]
        term = jnp.where(chosen == e, cols.astype(jnp.float32), 0.0)
        total = term if total is None else total + term
    return total.astype(jnp.bfloat16)


def key_limits(blocks, rows):
    return [max((i + 1) * rows, blocks * rows // 2) for i in range(blocks)]


def for_each_limit(blocks, rows, body):
    block = pl.program_id(0)
    limits = key_limits(blocks, rows)
    for width in sorted(set(limits)):
        members = [i for i, limit in enumerate(limits) if limit == width]
        pl.when((block >= members[0]) & (block <= members[-1]))(lambda width=width: body(width))


def attention_kernel(experts, prefix, q, k, v, side, mixed, log_total, bias):
    rows, span = q.shape[0], k.shape[1]
    heads = span // HEAD_DIM
    block = pl.program_id(0)
    chosen = [side[:, 0:1], side[:, 1:2]]
    gates = [side[:, 2:3], side[:, 3:4]]

    def body(width):
        attention_bias(bias, block, rows, width, prefix[0])

        @pl.loop(0, heads)
        def _(head):
            lane = head * HEAD_DIM
            lanes = pl.ds(pl.multiple_of(lane, HEAD_DIM), HEAD_DIM)
            weighted = []
            for j in range(2):
                query = pick_expert(q, lane, experts, span, chosen[j])
                scores = lax.dot_general(
                    query, k[:width, lanes], ACROSS, preferred_element_type=jnp.float32
                )
                scores = scores * (HEAD_DIM**-0.5) + bias[:, :width]
                largest = jnp.max(scores, axis=1, keepdims=True)
                exponent = jnp.exp(scores - largest)
                total = jnp.sum(exponent, axis=1, keepdims=True)
                low = (exponent * (1.0 / total)).astype(jnp.bfloat16)
                out = jnp.dot(low, v[:width, lanes], preferred_element_type=jnp.float32)
                weighted.append(out * gates[j])
                at = pl.ds(pl.multiple_of((2 * head + j) * HEAD_DIM, HEAD_DIM), HEAD_DIM)
                log_total[:, at] = jnp.broadcast_to(
                    largest + jnp.log(total), (rows, HEAD_DIM)
                )
            for e in range(experts):
                cols = jnp.where(chosen[0] == e, weighted[0], 0.0) + jnp.where(
                    chosen[1] == e, weighted[1], 0.0
                )
                at = pl.ds(pl.multiple_of(e * span + lane, HEAD_DIM), HEAD_DIM)
                mixed[:, at] = cols.astype(jnp.bfloat16)

    for_each_limit(k.shape[0] // rows, rows, body)


def attention(projected, side, prefix, experts, rows):
    length = projected.shape[0]
    span = projected.shape[1] // (experts + 2)
    wide = experts * span
    return pl.pallas_call(
        functools.partial(attention_kernel, experts),
        grid=(length // rows,),
        in_specs=[
            pl.BlockSpec(memory_space=pltpu.SMEM),
            pl.BlockSpec((rows, wide), lambda i: (i, 0)),
            pl.BlockSpec((length, span), lambda i: (0, experts)),
            pl.BlockSpec((length, span), lambda i: (0, experts + 1)),
            pl.BlockSpec((rows, 128), lambda i: (i, 0)),
        ],
        out_specs=[
            pl.BlockSpec((rows, wide), lambda i: (i, 0)),
            pl.BlockSpec((rows, 2 * span), lambda i: (i, 0)),
        ],
        out_shape=[
            jax.ShapeDtypeStruct((length, wide), jnp.bfloat16),
            jax.ShapeDtypeStruct((length, 2 * span), jnp.float32),
        ],
        scratch_shapes=[pltpu.VMEM((rows, length), jnp.float32)],
        compiler_params=pltpu.CompilerParams(vmem_limit_bytes=48 * 2**20),
        name="attention",
    )(prefix, projected, projected, projected, side)


class AttentionBack(Nothing):
    operands, results, rooms = 4, 2, 11
    turns = 4

    def __init__(self, length, total, experts, rows):
        self.length, self.experts, self.rows = length, experts, rows
        self.span = total // (experts + 2)
        low, f32 = jnp.bfloat16, jnp.float32
        self.heads = self.span // HEAD_DIM
        self.blocks = length // rows
        self.shapes = [
            jax.ShapeDtypeStruct((length, total), low),
            jax.ShapeDtypeStruct((length, 128), f32),
        ]
        self.scratch = [
            pltpu.VMEM((length, total), low),
            pltpu.VMEM((length, 128), f32),
            pltpu.VMEM((length, 2 * self.span), f32),
            pltpu.VMEM((length, experts * self.span), low),
            pltpu.VMEM((length, total), low),
            pltpu.VMEM((length, 128), f32),
            pltpu.VMEM((rows, length), f32),
            pltpu.VMEM((length, self.span), f32),
            pltpu.VMEM((length, self.span), f32),
            pltpu.SemaphoreType.DMA((4,)),
            pltpu.SemaphoreType.DMA((2,)),
        ]

    def loads(self, given, own):
        return [pltpu.make_async_copy(given[i], own[i], own[9].at[i]) for i in range(4)]

    def start(self, given, made, own):
        for load in self.loads(given, own):
            load.start()
        for ref in (own[5], own[7], own[8]):
            ref[...] = jnp.zeros_like(ref)
        return self.blocks * self.heads

    def run(self, given, made, own, first, last):
        if first == 0:
            for load in self.loads(given, own):
                load.wait()

        @pl.loop(first, last)
        def _(step):
            block = step // self.heads
            limits = key_limits(self.blocks, self.rows)
            for width in sorted(set(limits)):
                members = [i for i, limit in enumerate(limits) if limit == width]

                @pl.when((block >= members[0]) & (block <= members[-1]))
                def _(width=width):
                    self.step(own, block, step % self.heads, width)

    def step(self, own, block, head, width):
        qkv, side_ref, log_total, dmix, dprojected, dgate, bias, dk, dv = own[:9]
        experts, span, rows = self.experts, self.span, self.rows
        scaling = HEAD_DIM**-0.5
        row_at = pl.ds(pl.multiple_of(block * rows, rows), rows)
        side = side_ref[row_at, :]
        chosen = [side[:, 0:1], side[:, 1:2]]
        gates = [side[:, 2:3], side[:, 3:4]]
        column = lax.broadcasted_iota(jnp.int32, (rows, 128), 1)
        query_at = block * rows + lax.broadcasted_iota(jnp.int32, (rows, width), 0)
        key_at = lax.broadcasted_iota(jnp.int32, (rows, width), 1)
        reach = key_at.astype(jnp.float32) < side[:, 4:5]
        bias[:, :width] = jnp.where((key_at <= query_at) | reach, 0.0, NEG)
        lane = head * HEAD_DIM
        lanes = lambda base: pl.ds(pl.multiple_of(base + lane, HEAD_DIM), HEAD_DIM)
        keys = qkv[:width, lanes(experts * span)]
        values = qkv[:width, lanes((experts + 1) * span)]
        dqueries = []
        for j in range(2):
            query = pick_expert(qkv.at[row_at], lane, experts, span, chosen[j])
            dm = pick_expert(dmix.at[row_at], lane, experts, span, chosen[j])
            at = pl.ds(pl.multiple_of((2 * head + j) * HEAD_DIM, HEAD_DIM), HEAD_DIM)
            logs = jnp.tile(log_total[row_at, at], (1, width // HEAD_DIM))
            scores = lax.dot_general(query, keys, ACROSS, preferred_element_type=jnp.float32)
            probs = jnp.exp(scores * scaling + bias[:, :width] - logs)
            dprobs = lax.dot_general(dm, values, ACROSS, preferred_element_type=jnp.float32)
            inner = jnp.sum(probs * dprobs, axis=1, keepdims=True)
            dgate[row_at, :] += jnp.where(column == j, inner, 0.0)
            probs = probs * gates[j]
            dscores = (probs * (dprobs - inner)).astype(jnp.bfloat16)
            low = probs.astype(jnp.bfloat16)
            dqueries.append(jnp.dot(dscores, keys, preferred_element_type=jnp.float32) * scaling)
            dk[:width, lanes(0)] += lax.dot_general(
                dscores, query, DOWNWARD, preferred_element_type=jnp.float32
            )
            dv[:width, lanes(0)] += lax.dot_general(
                low, dm, DOWNWARD, preferred_element_type=jnp.float32
            )
        for e in range(experts):
            cols = jnp.where(chosen[0] == e, dqueries[0], 0.0) + jnp.where(
                chosen[1] == e, dqueries[1], 0.0
            )
            dprojected[row_at, lanes(e * span)] = cols.astype(jnp.bfloat16)

    def end(self, given, made, own):
        dprojected, dgate, dk, dv = own[4], own[5], own[7], own[8]
        wide = self.experts * self.span
        dprojected[:, wide : wide + self.span] = (dk[...] * HEAD_DIM**-0.5).astype(jnp.bfloat16)
        dprojected[:, wide + self.span :] = dv[...].astype(jnp.bfloat16)
        copies = [
            pltpu.make_async_copy(dprojected, made[0], own[10].at[0]),
            pltpu.make_async_copy(dgate, made[1], own[10].at[1]),
        ]
        for copy in copies:
            copy.start()
        for copy in copies:
            copy.wait()


def expert_slots(ids, my_index, tok_rows):
    blocks = ids.reshape(-1, tok_rows, 2)
    chosen = jnp.sum((blocks == my_index).astype(jnp.float32), axis=2)
    before = jnp.triu(jnp.ones((tok_rows, tok_rows), jnp.float32), 1)
    slots = jnp.where(chosen > 0, jnp.dot(chosen, before), -1.0).astype(jnp.int32)
    return slots, jnp.sum(blocks, axis=2) - my_index


def feed_kernel(
    tok,
    slot_count,
    own_rows,
    cots,
    gate_weight,
    up_weight,
    down_weight,
    router_rows,
    slots,
    others,
    everyone,
    dx_part,
    out_part,
    x_kept,
    g_kept,
    d_kept,
    a_kept,
    dgate,
    w_in,
    w_down,
    rows_buf,
    cots_buf,
    xs,
    gs,
    pre,
    back,
    ds,
    acts,
    dx_buf,
    out_buf,
    dxs,
    outs,
    send_sems,
    arrive_sems,
    own_sem,
    weight_sems,
    load_sems,
    keep_sems,
):
    place = Place()
    z_here = place.at["z"]
    hidden = gate_weight.shape[0]
    padded = w_down.shape[0]
    width = own_rows.shape[1]
    half = tok // 2
    chips = 4 * CHIPS_Z
    pair = 2 * slot_count
    f32, low = jnp.float32, jnp.bfloat16

    loads = [
        pltpu.make_async_copy(gate_weight, w_in.at[pl.ds(0, hidden)], weight_sems.at[0]),
        pltpu.make_async_copy(
            router_rows, w_in.at[pl.ds(hidden, padded - hidden)], weight_sems.at[1]
        ),
        pltpu.make_async_copy(up_weight, w_in.at[pl.ds(padded, hidden)], weight_sems.at[2]),
        pltpu.make_async_copy(down_weight, w_down.at[pl.ds(0, hidden)], weight_sems.at[3]),
        pltpu.make_async_copy(
            own_rows, everyone.at[pl.ds(place.block("all", z_here, {}) * tok, tok)], own_sem
        ),
    ]
    for load in loads:
        load.start()
    w_in[padded + hidden :, :] = jnp.zeros((padded - hidden, width), low)
    w_down[hidden:, :] = jnp.zeros((padded - hidden, width), low)
    enter(place, "cxyz")

    def chip(u):
        u = jnp.asarray(u, jnp.int32)
        turn, q = u // 4, u % 4
        flip = lambda *at: ((q == at[0]) | (q == at[1])).astype(jnp.int32)
        k, xr, yr = turn + (q == 3) - (q == 0), flip(0, 1), flip(0, 2)
        k = jnp.where(u == 0, 0, jnp.minimum(k, CHIPS_Z - 1))
        xr = jnp.where(u == 0, 0, jnp.where(u == chips - 1, 1, xr))
        yr = jnp.where(u == 0, 0, jnp.where(u == chips - 1, 1, yr))
        inner = (z_here == 1) | (z_here == 2)
        near = jnp.where(inner, jnp.where(k == 3, 3, jnp.where(k == 2, 0, k + 1)), k)
        return jnp.where(z_here < 2, near, CHIPS_Z - 1 - near), xr, yr

    def first_block(u):
        z, xr, yr = chip(u)
        x = place.at["x"] + xr * (1 - 2 * place.at["x"])
        y = place.at["y"] + yr * (1 - 2 * place.at["y"])
        return (z * 2 + y) * 4 + x * 2

    def part(p, u, core):
        return everyone.at[pl.ds((first_block(u) + core) * tok + p * half, half)]

    def remote(source, target, number, mark, device):
        return pltpu.make_async_remote_copy(
            src_ref=source,
            dst_ref=target,
            send_sem=send_sems.at[number],
            recv_sem=arrive_sems.at[mark],
            device_id=device,
            device_id_type=MESH,
        )

    def routes(u, p):
        z, xr, yr = chip(u)
        plain = (xr + yr) == 0
        mark = (p * CHIPS_Z + z) * 8
        here = xr * 4 + yr * 2
        base = (u * 2 + p) * 5
        own = z == z_here
        right = plain & (z <= z_here) & (z_here < CHIPS_Z - 1)
        left = plain & (z >= z_here) & (z_here > 0)
        over_x = plain if p == 0 else xr == 0
        over_y = yr == 0 if p == 0 else plain
        return [
            (right, base, mark, place.along(1)),
            (left, base + 1, mark, place.along(-1)),
            (over_x, base + 2, mark + 4 + yr * 2, place.across("x")),
            (over_y, base + 3, mark + xr * 4 + 2, place.across("y")),
            (None, base + 4, mark + here + 1, place.across("c")),
        ]

    def hand_on(u, sources, pieces=(0, 1)):
        for p in pieces:
            for condition, number, mark, device in routes(u, p):
                target = part(p, u, place.at["c"])
                source = target if sources is None else sources[p]
                on(
                    condition,
                    lambda source=source, target=target, number=number, mark=mark, device=device: remote(
                        source, target, number, mark, device
                    ).start(),
                )

    def sibling_came(u):
        z, xr, yr = chip(u)
        for p in range(2):
            ref = part(p, u, 1 - place.at["c"])
            mark = (p * CHIPS_Z + z) * 8 + xr * 4 + yr * 2 + 1
            remote(ref, ref, 0, mark, place.across("c")).wait_recv()

    def take_in(u, p):
        z, xr, yr = chip(u)
        ref = part(p, u, place.at["c"])
        mark = (p * CHIPS_Z + z) * 8 + xr * 4 + yr * 2
        remote(ref, ref, 0, mark, place.across("c")).wait_recv()
        hand_on(u, None, (p,))

    def fetch(u):
        at = pl.ds(first_block(u) * tok, 2 * tok)
        return [
            pltpu.make_async_copy(everyone.at[at], rows_buf.at[u % 2], load_sems.at[u % 2, 0]),
            pltpu.make_async_copy(cots.at[at], cots_buf.at[u % 2], load_sems.at[u % 2, 1]),
        ]

    def keep(u):
        rows = pl.ds(u * pair, pair)
        blocks = pl.ds(first_block(u) * tok, 2 * tok)
        s = u % 2
        return [
            pltpu.make_async_copy(xs.at[s], x_kept.at[rows], keep_sems.at[s, 0]),
            pltpu.make_async_copy(gs.at[s], g_kept.at[rows], keep_sems.at[s, 1]),
            pltpu.make_async_copy(ds.at[s], d_kept.at[rows], keep_sems.at[s, 2]),
            pltpu.make_async_copy(acts.at[s], a_kept.at[rows], keep_sems.at[s, 3]),
            pltpu.make_async_copy(dx_buf.at[s], dx_part.at[blocks], keep_sems.at[s, 4]),
            pltpu.make_async_copy(out_buf.at[s], out_part.at[blocks], keep_sems.at[s, 5]),
        ]

    hand_on(0, [own_rows.at[pl.ds(0, half)], own_rows.at[pl.ds(half, half)]])
    loads[4].wait()
    sibling_came(0)
    for copy in fetch(0):
        copy.start()
    for p in range(2):
        take_in(1, p)
    for load in loads[:4]:
        load.wait()

    def compute(u):
        s = u % 2
        block = first_block(u)
        spread = []
        for b in range(2):
            row = slots[pl.ds(block + b, 1), :]
            table = lax.broadcasted_iota(jnp.int32, (slot_count, tok), 0) == row
            table = table.astype(f32)
            spread.append(table)
            at = pl.ds(b * slot_count, slot_count)
            from_rows = pl.ds(b * tok, tok)
            xs[s, at, :] = jnp.dot(
                table.astype(low), rows_buf[s, from_rows, :], preferred_element_type=f32
            ).astype(low)
            gs[s, at, :] = jnp.dot(
                table.astype(low), cots_buf[s, from_rows, :], preferred_element_type=f32
            ).astype(low)

        @pl.loop(0, 2 * padded // 256)
        def _(n):
            at = pl.ds(pl.multiple_of(n * 256, 256), 256)
            pre[:, at] = lax.dot_general(xs[s], w_in[at, :], ACROSS, preferred_element_type=f32)

        @pl.when(u + 2 < chips)
        def _():
            take_in(u + 2, 1)

        @pl.loop(0, padded // 256)
        def _(n):
            at = pl.ds(pl.multiple_of(n * 256, 256), 256)
            back[:, at] = lax.dot_general(gs[s], w_down[at, :], ACROSS, preferred_element_type=f32)

        for b in range(2):
            at = pl.ds(b * slot_count, slot_count)
            last = pre[at, padded - 128 : padded]
            column = lax.broadcasted_iota(jnp.int32, (slot_count, 128), 1) - (
                hidden - (padded - 128)
            )
            other = jnp.sum(
                spread[b] * others[pl.ds(block + b, 1), :].astype(f32), axis=1, keepdims=True
            )
            mine = jnp.sum(jnp.where(column == place.expert, last, 0.0), axis=1, keepdims=True)
            theirs = jnp.sum(
                jnp.where(column == other.astype(jnp.int32), last, 0.0), axis=1, keepdims=True
            )
            gate = 1.0 / (1.0 + jnp.exp(theirs - mine))
            inner = jnp.zeros((slot_count, 1), f32)
            for n in range(padded // 256):
                cols = pl.ds(n * 256, 256)
                pre_gate, pre_up = pre[at, cols], pre[at, pl.ds(padded + n * 256, 256)]
                dact = back[at, cols]
                sig = 1.0 / (1.0 + jnp.exp(-pre_gate))
                silu = pre_gate * sig
                act = silu * pre_up
                acts[s, at, cols] = (act * gate).astype(low)
                inner += jnp.sum(act * dact, axis=1, keepdims=True)
                dact = dact * gate
                ds[s, at, cols] = (dact * pre_up * sig * (1.0 + pre_gate * (1.0 - sig))).astype(low)
                ds[s, at, pl.ds(padded + n * 256, 256)] = (dact * silu).astype(low)
            dgate[pl.ds(block + b, 1), :] = jnp.sum(spread[b] * inner, axis=0, keepdims=True)

        @pl.loop(0, width // 256)
        def _(n):
            cols = pl.ds(pl.multiple_of(n * 256, 256), 256)
            dxs[:, cols] = jnp.dot(ds[s], w_in[:, cols], preferred_element_type=f32).astype(low)
            outs[:, cols] = jnp.dot(acts[s], w_down[:, cols], preferred_element_type=f32).astype(
                low
            )

        for b in range(2):
            at = pl.ds(b * slot_count, slot_count)
            back_table = spread[b].T.astype(low)
            to = pl.ds(b * tok, tok)
            dx_buf[s, to, :] = jnp.dot(
                back_table, dxs[at, :], preferred_element_type=f32
            ).astype(low)
            out_buf[s, to, :] = jnp.dot(
                back_table, outs[at, :], preferred_element_type=f32
            ).astype(low)

    @pl.loop(0, chips)
    def _(u):
        @pl.when(u + 1 < chips)
        def _():
            sibling_came(u + 1)
            for copy in fetch(u + 1):
                copy.start()

        @pl.when(u + 2 < chips)
        def _():
            take_in(u + 2, 0)

        for copy in fetch(u):
            copy.wait()

        @pl.when(u >= 2)
        def _():
            for copy in keep(u - 2):
                copy.wait()

        compute(u)
        for copy in keep(u):
            copy.start()

    for u in (chips - 2, chips - 1):
        for copy in keep(jnp.int32(u)):
            copy.wait()

    @pl.loop(0, chips)
    def _(u):
        for p in range(2):
            for condition, number, mark, device in routes(u, p):
                ref = part(p, u, place.at["c"])
                on(
                    condition,
                    lambda ref=ref, number=number, mark=mark, device=device: remote(
                        ref, ref, number, mark, device
                    ).wait_send(),
                )


def feed(own_rows, cots, gate_weight, up_weight, down_weight, router_rows, slots, others, slot_count):
    tok, width = own_rows.shape
    hidden = gate_weight.shape[0]
    padded = hidden + router_rows.shape[0]
    total = cots.shape[0]
    kept = total // tok * slot_count
    low = jnp.bfloat16
    hbm = pl.BlockSpec(memory_space=pltpu.HBM)
    vmem = pl.BlockSpec(memory_space=pltpu.VMEM)
    shape = jax.ShapeDtypeStruct
    pair = 2 * slot_count
    chips = 4 * CHIPS_Z
    return pl.pallas_call(
        functools.partial(feed_kernel, tok, slot_count),
        in_specs=[hbm] * 6 + [vmem] * 2,
        out_specs=[hbm] * 7 + [vmem],
        out_shape=[
            shape((total, width), low),
            shape((total, width), low),
            shape((total, width), low),
            shape((kept, width), low),
            shape((kept, width), low),
            shape((kept, 2 * padded), low),
            shape((kept, padded), low),
            shape(slots.shape, jnp.float32),
        ],
        scratch_shapes=[
            pltpu.VMEM((2 * padded, width), low),
            pltpu.VMEM((padded, width), low),
            pltpu.VMEM((2, 2 * tok, width), low),
            pltpu.VMEM((2, 2 * tok, width), low),
            pltpu.VMEM((2, pair, width), low),
            pltpu.VMEM((2, pair, width), low),
            pltpu.VMEM((pair, 2 * padded), jnp.float32),
            pltpu.VMEM((pair, padded), jnp.float32),
            pltpu.VMEM((2, pair, 2 * padded), low),
            pltpu.VMEM((2, pair, padded), low),
            pltpu.VMEM((2, 2 * tok, width), low),
            pltpu.VMEM((2, 2 * tok, width), low),
            pltpu.VMEM((pair, width), low),
            pltpu.VMEM((pair, width), low),
            pltpu.SemaphoreType.DMA((10 * chips,)),
            pltpu.SemaphoreType.DMA((16 * CHIPS_Z,)),
            pltpu.SemaphoreType.DMA,
            pltpu.SemaphoreType.DMA((4,)),
            pltpu.SemaphoreType.DMA((2, 2)),
            pltpu.SemaphoreType.DMA((2, 6)),
        ],
        compiler_params=pltpu.CompilerParams(
            collective_id=3, has_side_effects=True, vmem_limit_bytes=60 * 2**20
        ),
        name="feed_forward",
    )(own_rows, cots, gate_weight, up_weight, down_weight, router_rows, slots, others)


def per_device_torus(
    tokens,
    cotangent,
    attention_routes,
    feedforward_routes,
    prefix_length,
    gain_attention,
    gain_feedforward,
    keyvalue_weight,
    router_weight,
    query_weight,
    output_weight,
    gate_weight,
    up_weight,
    down_weight,
):
    my_index = lax.axis_index("expert")
    group_size = lax.axis_size("expert")
    dp_size = lax.axis_size("dp")
    inputs = tokens[0].astype(jnp.float32)
    tok_rows, model_width = inputs.shape
    slot_count = 5 * 2 * tok_rows // (4 * group_size)
    query_width = HEADS * HEAD_DIM
    span = query_width // group_size
    low = jnp.bfloat16
    f32 = jnp.float32

    normed_attention, unit_attention, factor_attention = norm_parts(inputs, gain_attention)
    attention_in = normed_attention.astype(low)
    quarters = lambda order: tuple(
        (i * tok_rows // 4, tok_rows // 4, order) for i in range(4)
    )
    rows_in = keyvalue_weight.shape[0]
    route_shard = feedforward_routes[0].astype(low).reshape(-1, 128)
    router_shard = router_weight.T.reshape(-1, 128)
    whole = lambda a: ((0, a.shape[0], "zy"),)
    cut = rows_in * 12 // 16
    sequence_in, cot_everyone, every_route, router_full, in_weight, out_weight = gather_weights(
        [
            (attention_in, "expert", quarters("xc")),
            (cotangent[0], "all", quarters("zyxc")),
            (route_shard, "dp", whole(route_shard)),
            (router_shard, "dp", whole(router_shard)),
        ],
        query_weight[0],
        keyvalue_weight,
        output_weight[0],
        ((0, cut, "zy"), (cut, rows_in - cut, "yz")),
        1,
    )
    every_route = every_route.reshape(-1, 2).astype(jnp.int32)
    router_full = (
        router_full.reshape(dp_size, 2 * group_size, rows_in)
        .transpose(0, 2, 1)
        .reshape(-1, 2 * group_size)
    )
    attention_cols = router_full[:, :group_size]
    feedforward_cols = router_full[:, group_size:]
    projected = jnp.dot(sequence_in, in_weight, preferred_element_type=f32).astype(low)
    attend_matches_all = expert_matches(attention_routes[0], group_size)
    attend_logits = jnp.dot(sequence_in, attention_cols, preferred_element_type=f32)
    attend_weights_all, _ = pair_gates(attend_logits, attend_matches_all)
    reach = jnp.broadcast_to(prefix_length.astype(f32)[None], (attend_logits.shape[0], 1))
    side = jnp.concatenate([attention_routes[0].astype(f32), attend_weights_all, reach], axis=1)
    side = jnp.pad(side, ((0, 0), (0, 128 - side.shape[1])))
    mixed, log_total = attention(projected, side, prefix_length, group_size, tok_rows)
    attend_part = jnp.dot(mixed, out_weight, preferred_element_type=f32).astype(low)
    attended = scatter(attend_part, "expert", quarters("cx"), 2, "sum_attention")
    hidden = inputs + attended
    normed_feed, unit_feed, factor_feed = norm_parts(hidden, gain_feedforward)
    feed_in = normed_feed.astype(low)
    everywhere = lambda a, b: ((0, tok_rows // 2, a), (tok_rows // 2, tok_rows // 2, b))
    mine = lambda a: lax.dynamic_slice_in_dim(a, my_index * tok_rows, tok_rows, 0)
    feed_matches = expert_matches(mine(feedforward_routes[0]), group_size)
    feed_logits = jnp.dot(feed_in, feedforward_cols, preferred_element_type=f32)
    feed_weights, _ = pair_gates(feed_logits, feed_matches)
    slots, others = expert_slots(every_route, my_index, tok_rows)
    hidden_rows = gate_weight.shape[1]
    padded = -(-hidden_rows // 256) * 256
    router_rows = jnp.pad(
        feedforward_cols.T, ((0, padded - hidden_rows - group_size), (0, 0))
    )
    _, dx_part, out_part, kept_rows, kept_cots, kept_back, kept_act, token_dgate = feed(
        feed_in,
        cot_everyone,
        gate_weight[0],
        up_weight[0],
        down_weight[0],
        router_rows,
        slots,
        others,
        slot_count,
    )
    own_row = (jnp.arange(group_size) == my_index).astype(f32)[None, :, None]
    feed_dgate = lax.psum_scatter(
        (token_dgate[:, None, :] * own_row).reshape(-1, tok_rows),
        ("dp", "expert"),
        scatter_dimension=0,
        tiled=True,
    ).T
    feed_home, grad_in_feed, grad_down = scatter(
        dx_part,
        "all",
        everywhere("cxyz", "cyxz"),
        4,
        "sum_rows",
        WeightGrads(kept_rows.shape[0], 2 * padded, padded, model_width),
        (kept_back, kept_rows, kept_act, kept_cots),
    )
    grad_gate = grad_in_feed[:hidden_rows]
    grad_up = grad_in_feed[padded : padded + hidden_rows]
    grad_down = grad_down[:hidden_rows]
    gradient = cotangent[0].astype(f32)
    feed_dlogits = gates_back(feed_dgate, feed_weights, feed_matches)
    feed_dnorm = feed_home + jnp.dot(feed_dlogits, feedforward_cols.astype(f32).T, precision=HIGH)
    grad_gain_feed = jnp.sum(feed_dnorm * unit_feed, axis=0)
    hidden_grad = gradient + norm_back(feed_dnorm, gain_feedforward, unit_feed, factor_feed)

    (sequence_grad,) = gather(
        [(hidden_grad.astype(low), "expert", quarters("xc"))], 5, "gather_cotangents"
    )
    dmix = lax.dot_general(sequence_grad, out_weight, ACROSS, preferred_element_type=f32).astype(low)
    length, total = projected.shape
    columns = model_width // 2
    first_sum, dprojected, gate_parts = scatter(
        out_part,
        "all",
        everywhere("cxyz", "cyxz"),
        7,
        "sum_output_left",
        AttentionBack(length, total, group_size, tok_rows),
        (projected, side, log_total, dmix),
        (0, columns),
    )
    attend_dx = lax.dot_general(dprojected, in_weight, ACROSS, preferred_element_type=f32)
    attend_home = scatter(attend_dx.astype(low), "expert", quarters("cx"), 2, "sum_attention")
    second_sum, grad_in, grad_out = scatter(
        out_part,
        "all",
        everywhere("cxyz", "cyxz"),
        8,
        "sum_output_right",
        LowGrads(length, (model_width, query_width), (total, model_width)),
        (sequence_in, dprojected, mixed, sequence_grad),
        (columns, model_width - columns),
    )
    layer_output = hidden + jnp.concatenate([first_sum, second_sum], axis=1)
    pair_dgate = lax.psum_scatter(
        gate_parts[:, :2].reshape(group_size, tok_rows, 2).transpose(0, 2, 1).reshape(-1, tok_rows),
        "expert",
        scatter_dimension=0,
        tiled=True,
    ).T
    matches = mine(attend_matches_all)
    weights = mine(attend_weights_all)
    dselected = weights * (pair_dgate - jnp.sum(weights * pair_dgate, axis=1, keepdims=True))
    attend_dlogits = jnp.sum(dselected[:, :, None] * matches, axis=1)
    attend_dnorm = attend_home + jnp.dot(
        attend_dlogits, attention_cols.astype(f32).T, precision=HIGH
    )
    grad_gain_attend = jnp.sum(attend_dnorm * unit_attention, axis=0)
    grad_tokens = hidden_grad + norm_back(
        attend_dnorm, gain_attention, unit_attention, factor_attention
    )
    small = jnp.concatenate(
        [
            lax.dot_general(attend_dlogits, attention_in.astype(f32), DOWNWARD, precision=HIGH),
            lax.dot_general(feed_dlogits, feed_in.astype(f32), DOWNWARD, precision=HIGH),
            grad_gain_attend[None],
            grad_gain_feed[None],
        ],
        axis=0,
    )
    small = lax.psum(small.astype(f32), ("dp", "expert"))
    small = lax.dynamic_slice_in_dim(small, lax.axis_index("dp") * rows_in, rows_in, 1)

    grad_query, grad_keyvalue, grad_projection = sum_weights(
        grad_in, grad_out, ((0, rows_in, "yz"),), 6
    )
    return (
        layer_output.astype(low)[None],
        grad_tokens[None],
        small[2 * group_size],
        small[2 * group_size + 1],
        grad_keyvalue,
        small[: 2 * group_size].T,
        grad_query[None],
        grad_projection[None],
        grad_gate[None],
        grad_up[None],
        grad_down[None],
    )


def solution(mesh):
    in_specs = (
        P("dp", "expert", None),
        P("dp", "expert", None),
        P("dp", None, None),
        P("dp", None, None),
        P("dp"),
        P(),
        P(),
        P("dp", None),
        P("dp", None),
        P("expert", "dp", None),
        P("expert", "dp", None),
        P("expert", "dp", None),
        P("expert", "dp", None),
        P("expert", "dp", None),
    )
    out_specs = (
        P("dp", "expert", None),
        P("dp", "expert", None),
        P("dp"),
        P("dp"),
        P("dp", None),
        P("dp", None),
        P("expert", "dp", None),
        P("expert", "dp", None),
        P("expert", "dp", None),
        P("expert", "dp", None),
        P("expert", "dp", None),
    )
    torus = (mesh.shape["dp"], mesh.shape["expert"]) == (8, 4)
    body = per_device_torus if torus else per_device
    return jax.shard_map(
        body, mesh=mesh, in_specs=in_specs, out_specs=out_specs, check_vma=False
    )
```

```python
import functools

import jax
import jax.numpy as jnp
from jax import lax
from jax.experimental import pallas as pl
from jax.experimental.pallas import tpu as pltpu
from jax.sharding import PartitionSpec as P

HEADS = 16
HEAD_DIM = 128


EPS = 1e-06
NEG = -1e30
HIGH = lax.Precision.HIGHEST
ACROSS = (((1,), (1,)), ((), ()))
DOWNWARD = (((0,), (0,)), ((), ()))


def norm_parts(vector, gain_vector):
    factor = lax.rsqrt(jnp.mean(vector * vector, axis=-1, keepdims=True) + EPS)
    normed = vector * factor
    return (normed * gain_vector, normed, factor)


def norm_back(incoming, gain_vector, normed, factor):
    dnormed = incoming * gain_vector
    return factor * (dnormed - normed * jnp.mean(dnormed * normed, axis=-1, keepdims=True))


def route_plan(sequence_ids, my_index, group_size, tok_rows, slot_count):
    expert_range = jnp.arange(group_size, dtype=jnp.int32)
    matches_all = (sequence_ids[:, :, None] == expert_range[None, None, :]).astype(jnp.int32)
    chosen = jnp.sum(matches_all, axis=1).reshape(group_size, tok_rows, group_size)
    ranking = jnp.cumsum(chosen, axis=1) - chosen
    slot_ids = jnp.arange(slot_count, dtype=jnp.int32)[None, :, None]
    block_pick = (expert_range == my_index).astype(jnp.int32)
    my_chosen = jnp.sum(chosen * block_pick[:, None, None], axis=0).T
    my_ranking = jnp.sum(ranking * block_pick[:, None, None], axis=0).T
    send_table = (
        my_chosen[:, None, :] * (my_ranking[:, None, :] == slot_ids).astype(jnp.int32)
    ).astype(jnp.float32)
    column_chosen = jnp.sum(chosen * block_pick[None, None, :], axis=2)
    column_ranking = jnp.sum(ranking * block_pick[None, None, :], axis=2)
    taken = column_chosen[:, None, :] * (column_ranking[:, None, :] == slot_ids).astype(jnp.int32)
    positions = (
        expert_range[:, None, None] * tok_rows
        + jnp.arange(tok_rows, dtype=jnp.int32)[None, None, :]
    )
    arrival_places = jnp.sum(taken * positions, axis=2).reshape(-1)
    my_ids = lax.dynamic_slice_in_dim(sequence_ids, my_index * tok_rows, tok_rows, 0)
    matches = (my_ids[:, :, None] == expert_range[None, None, :]).astype(jnp.float32)
    return (send_table, arrival_places, matches)


def pair_gates(logits, matches):
    selected = jnp.sum(matches * logits[:, None, :], axis=2)
    largest = jnp.max(selected, axis=1, keepdims=True)
    exponent = jnp.exp(selected - largest)
    weights = exponent / jnp.sum(exponent, axis=1, keepdims=True)
    return (weights, jnp.sum(weights[:, :, None] * matches, axis=1))


def gates_back(dgate, weights, matches):
    dweights = jnp.sum(dgate[:, None, :] * matches, axis=2)
    dselected = weights * (dweights - jnp.sum(weights * dweights, axis=1, keepdims=True))
    return jnp.sum(dselected[:, :, None] * matches, axis=1)


def merge_back(send_table, gate_table, returned):
    weighted = send_table * gate_table.T[:, None, :]
    return jnp.einsum("ect,ecd->td", weighted, returned.astype(jnp.float32), precision=HIGH)


def branch_cotangent(send_table, gate_table, returned, incoming):
    spread_grad = jnp.einsum("ect,td->ecd", send_table, incoming, precision=HIGH)
    slot_gate = jnp.sum(send_table * gate_table.T[:, None, :], axis=2)
    cotangent_rows = (spread_grad * slot_gate[:, :, None]).astype(jnp.bfloat16)
    slot_dgate = jnp.sum(spread_grad * returned.astype(jnp.float32), axis=2)
    dgate = jnp.einsum("ect,ec->te", send_table, slot_dgate, precision=HIGH)
    return (cotangent_rows, dgate)


def expert_matches(ids, group_size):
    expert_range = jnp.arange(group_size, dtype=jnp.int32)
    return (ids[:, :, None] == expert_range[None, None, :]).astype(jnp.float32)


def expert_table(ids, my_index, group_size, tok_rows, slot_count):
    blocks = ids.reshape(-1, tok_rows, 2)
    chosen = jnp.sum((blocks == my_index).astype(jnp.float32), axis=2)
    before = jnp.triu(jnp.ones((tok_rows, tok_rows), jnp.float32), 1)
    ranking = jnp.dot(chosen, before)
    slot_ids = jnp.arange(slot_count, dtype=jnp.float32)[None, :, None]
    taken = chosen[:, None, :] * (ranking[:, None, :] == slot_ids).astype(jnp.float32)
    other = jnp.sum(blocks, axis=2) - my_index
    slot_other = jnp.sum(taken * other[:, None, :].astype(jnp.float32), axis=2)
    return (taken.astype(jnp.bfloat16), slot_other.reshape(-1).astype(jnp.int32))


def own_gate(logits, other, my_index):
    expert_range = jnp.arange(logits.shape[1], dtype=jnp.int32)[None]
    mine = jnp.sum(jnp.where(expert_range == my_index, logits, 0.0), axis=1, keepdims=True)
    theirs = jnp.sum(jnp.where(expert_range == other[:, None], logits, 0.0), axis=1, keepdims=True)
    return jax.nn.sigmoid(mine - theirs)


def pick_rows(taken, rows):
    blocks, slots, tokens = taken.shape
    picked = jnp.einsum(
        "bct,btd->bcd",
        taken,
        rows.reshape(blocks, tokens, -1),
        preferred_element_type=jnp.float32,
    )
    return picked.astype(jnp.bfloat16).reshape(blocks * slots, -1)


def return_rows(taken, rows):
    blocks, slots, tokens = taken.shape
    placed = jnp.einsum(
        "bct,bcd->btd",
        taken,
        rows.reshape(blocks, slots, -1),
        preferred_element_type=jnp.float32,
    )
    return placed.astype(jnp.bfloat16).reshape(blocks * tokens, -1)


def gather_all(rows):
    return lax.all_gather(rows, ("dp", "expert"), axis=0, tiled=True)


def scatter_all(rows):
    return lax.psum_scatter(rows, ("dp", "expert"), scatter_dimension=0, tiled=True)


def dispatch(rows):
    return lax.all_to_all(rows, "expert", split_axis=0, concat_axis=0, tiled=True)


def collect(rows):
    return lax.all_to_all(rows, "expert", split_axis=0, concat_axis=0, tiled=True)


def spread_rows(rows):
    return lax.all_gather(rows, "dp", axis=0, tiled=True)


def sum_rows(terms):
    return lax.psum_scatter(
        terms.astype(jnp.bfloat16), "dp", scatter_dimension=0, tiled=True
    ).astype(jnp.float32)


def send_rows(send_table, rows):
    return jnp.einsum(
        "ect,td->ecd", send_table.astype(jnp.bfloat16), rows, preferred_element_type=jnp.float32
    ).astype(jnp.bfloat16)


def per_device(
    tokens,
    cotangent,
    attention_routes,
    feedforward_routes,
    prefix_length,
    gain_attention,
    gain_feedforward,
    keyvalue_weight,
    router_weight,
    query_weight,
    output_weight,
    gate_weight,
    up_weight,
    down_weight,
):
    my_index = lax.axis_index("expert")
    group_size = lax.axis_size("expert")
    inputs = tokens[0].astype(jnp.float32)
    tok_rows = inputs.shape[0]
    model_width = inputs.shape[1]
    seq_total = tok_rows * group_size
    slot_count = 5 * 2 * tok_rows // (4 * group_size)
    query_width = HEADS * HEAD_DIM
    scaling = HEAD_DIM ** (-0.5)
    keyvalue_full, router_full, query_full, output_full = (
        lax.all_gather(keyvalue_weight, "dp", axis=0, tiled=True),
        lax.all_gather(router_weight, "dp", axis=0, tiled=True),
        lax.all_gather(query_weight[0], "dp", axis=0, tiled=True),
        lax.all_gather(output_weight[0], "dp", axis=0, tiled=True),
    )
    every_route = lax.all_gather(feedforward_routes[0], "dp", axis=0, tiled=True)
    cot_everyone = gather_all(cotangent[0])
    attention_cols = router_full[:, :group_size]
    feedforward_cols = router_full[:, group_size:]
    normed_attention, unit_attention, factor_attention = norm_parts(inputs, gain_attention)
    attention_in = normed_attention.astype(jnp.bfloat16)
    keyvalue_rows = jnp.dot(attention_in, keyvalue_full, preferred_element_type=jnp.float32).astype(
        jnp.bfloat16
    )
    keyvalue_seq = lax.all_gather(keyvalue_rows, "expert", axis=0, tiled=True)
    key_rows = keyvalue_seq[:, :query_width].reshape(seq_total, HEADS, HEAD_DIM)
    value_rows = keyvalue_seq[:, query_width:].reshape(seq_total, HEADS, HEAD_DIM)
    attend_table, attend_places, attend_matches = route_plan(
        attention_routes[0], my_index, group_size, tok_rows, slot_count
    )
    attend_logits = jnp.dot(attention_in, attention_cols, preferred_element_type=jnp.float32)
    attend_weights, attend_gate = pair_gates(attend_logits, attend_matches)
    arrived = dispatch(send_rows(attend_table, attention_in)).reshape(-1, model_width)
    queries = jnp.dot(arrived, query_full, preferred_element_type=jnp.float32).astype(jnp.bfloat16)
    queries = queries.reshape(-1, HEADS, HEAD_DIM)
    key_places = jnp.arange(seq_total, dtype=jnp.int32)
    allowed = (key_places[None, :] <= attend_places[:, None]) | (
        key_places[None, :] < prefix_length[0]
    )
    scores = (
        jnp.einsum("rhd,khd->hrk", queries, key_rows, preferred_element_type=jnp.float32) * scaling
    )
    scores = jnp.where(allowed[None], scores, NEG)
    row_max = jnp.max(scores, axis=2, keepdims=True)
    exponent = jnp.exp(scores - row_max)
    row_total = jnp.sum(exponent, axis=2, keepdims=True)
    log_total = row_max + jnp.log(row_total)
    attention_low = (exponent / row_total).astype(jnp.bfloat16)
    mixture = jnp.einsum(
        "hrk,khd->rhd", attention_low, value_rows, preferred_element_type=jnp.float32
    )
    mixture = mixture.astype(jnp.bfloat16).reshape(-1, query_width)
    attend_branch = jnp.dot(mixture, output_full, preferred_element_type=jnp.float32).astype(
        jnp.bfloat16
    )
    attend_returned = collect(attend_branch.reshape(group_size, slot_count, model_width))
    hidden = inputs + merge_back(attend_table, attend_gate, attend_returned)
    normed_feed, unit_feed, factor_feed = norm_parts(hidden, gain_feedforward)
    feed_in = normed_feed.astype(jnp.bfloat16)
    feed_ids = lax.dynamic_slice_in_dim(
        feedforward_routes[0], my_index * tok_rows, tok_rows, 0
    )
    feed_matches = expert_matches(feed_ids, group_size)
    feed_logits = jnp.dot(feed_in, feedforward_cols, preferred_element_type=jnp.float32)
    feed_weights, feed_gate = pair_gates(feed_logits, feed_matches)
    everyone = gather_all(feed_in)
    feed_taken, feed_pairs = expert_table(every_route, my_index, group_size, tok_rows, slot_count)
    pick = functools.partial(pick_rows, feed_taken)
    feed_rows = pick(everyone)
    cot_rows = pick(cot_everyone)
    row_logits = jnp.dot(feed_rows, feedforward_cols, preferred_element_type=jnp.float32)
    row_gate = own_gate(row_logits, feed_pairs, my_index)
    pre_gate = lax.dot_general(feed_rows, gate_weight[0], ACROSS, preferred_element_type=jnp.float32)
    pre_up = lax.dot_general(feed_rows, up_weight[0], ACROSS, preferred_element_type=jnp.float32)
    sigmoid_gate = jax.nn.sigmoid(pre_gate)
    act = pre_gate * sigmoid_gate * pre_up
    act_low = act.astype(jnp.bfloat16)
    act_scaled = (act * row_gate).astype(jnp.bfloat16)
    act_grad = lax.dot_general(cot_rows, down_weight[0], ACROSS, preferred_element_type=jnp.float32)
    slot_dgate = jnp.sum(act_low.astype(jnp.float32) * act_grad, axis=1)
    act_grad = act_grad * row_gate
    dgate_low = (act_grad * pre_up * sigmoid_gate * (1.0 + pre_gate * (1.0 - sigmoid_gate))).astype(
        jnp.bfloat16
    )
    dup_low = (act_grad * pre_gate * sigmoid_gate).astype(jnp.bfloat16)
    feed_dx = (
        jnp.dot(dgate_low, gate_weight[0], preferred_element_type=jnp.float32)
        + jnp.dot(dup_low, up_weight[0], preferred_element_type=jnp.float32)
    ).astype(jnp.bfloat16)
    feed_branch = jnp.dot(act_scaled, down_weight[0], preferred_element_type=jnp.float32).astype(
        jnp.bfloat16
    )
    grad_gate = lax.dot_general(dgate_low, feed_rows, DOWNWARD, preferred_element_type=jnp.float32)
    grad_up = lax.dot_general(dup_low, feed_rows, DOWNWARD, preferred_element_type=jnp.float32)
    grad_down = lax.dot_general(act_scaled, cot_rows, DOWNWARD, preferred_element_type=jnp.float32)
    token_dgate = jnp.einsum(
        "bct,bc->bt",
        feed_taken.astype(jnp.float32),
        slot_dgate.reshape(-1, slot_count),
        precision=HIGH,
    ).reshape(-1, 1)
    own_column = (jnp.arange(group_size) == my_index).astype(jnp.float32)[None]
    feed_dgate = scatter_all(token_dgate * own_column)
    feed_home = scatter_all(return_rows(feed_taken, feed_dx)).astype(jnp.float32)
    feed_sum = scatter_all(return_rows(feed_taken, feed_branch)).astype(jnp.float32)
    layer_output = hidden + feed_sum
    gradient = cotangent[0].astype(jnp.float32)
    feed_dlogits = gates_back(feed_dgate, feed_weights, feed_matches)
    feed_dnorm = feed_home + jnp.dot(
        feed_dlogits, feedforward_cols.astype(jnp.float32).T, precision=HIGH
    )
    grad_gain_feed = jnp.sum(feed_dnorm * unit_feed, axis=0)
    hidden_grad = gradient + norm_back(feed_dnorm, gain_feedforward, unit_feed, factor_feed)
    attend_cot, attend_dgate = branch_cotangent(
        attend_table, attend_gate, attend_returned, hidden_grad
    )
    attend_dlogits = gates_back(attend_dgate, attend_weights, attend_matches)
    attend_cot_rows = dispatch(attend_cot).reshape(-1, model_width)
    dmixture = lax.dot_general(
        attend_cot_rows, output_full, ACROSS, preferred_element_type=jnp.float32
    )
    dmixture = dmixture.astype(jnp.bfloat16).reshape(-1, HEADS, HEAD_DIM)
    grad_projection = lax.dot_general(
        mixture, attend_cot_rows, DOWNWARD, preferred_element_type=jnp.float32
    )
    scores_again = (
        jnp.einsum("rhd,khd->hrk", queries, key_rows, preferred_element_type=jnp.float32) * scaling
    )
    attention = jnp.where(allowed[None], jnp.exp(scores_again - log_total), 0.0)
    attention_again = attention.astype(jnp.bfloat16)
    dattention = jnp.einsum(
        "rhd,khd->hrk", dmixture, value_rows, preferred_element_type=jnp.float32
    )
    row_dot = jnp.sum(attention * dattention, axis=2, keepdims=True)
    dscores = (attention * (dattention - row_dot)).astype(jnp.bfloat16)
    dqueries = (
        jnp.einsum("hrk,khd->rhd", dscores, key_rows, preferred_element_type=jnp.float32) * scaling
    )
    dqueries = dqueries.astype(jnp.bfloat16).reshape(-1, query_width)
    dkeys = (
        jnp.einsum("hrk,rhd->khd", dscores, queries, preferred_element_type=jnp.float32) * scaling
    )
    dvalues = jnp.einsum(
        "hrk,rhd->khd", attention_again, dmixture, preferred_element_type=jnp.float32
    )
    grad_query = lax.dot_general(arrived, dqueries, DOWNWARD, preferred_element_type=jnp.float32)
    attend_dx = lax.dot_general(dqueries, query_full, ACROSS, preferred_element_type=jnp.float32)
    keyvalue_terms = jnp.concatenate(
        [dkeys.reshape(seq_total, query_width), dvalues.reshape(seq_total, query_width)], axis=1
    ).reshape(group_size, tok_rows, 2 * query_width)
    attend_home, keyvalue_home = (
        lax.all_to_all(
            attend_dx.reshape(group_size, slot_count, model_width).astype(jnp.bfloat16),
            "expert",
            split_axis=0,
            concat_axis=0,
            tiled=True,
        ).astype(jnp.float32),
        lax.all_to_all(
            keyvalue_terms.astype(jnp.bfloat16), "expert", split_axis=0, concat_axis=0, tiled=True
        ).astype(keyvalue_terms.dtype),
    )
    dkeyvalue = jnp.sum(keyvalue_home, axis=0).astype(jnp.bfloat16)
    attend_dnorm = (
        jnp.einsum("ect,ecd->td", attend_table, attend_home, precision=HIGH)
        + lax.dot_general(dkeyvalue, keyvalue_full, ACROSS, preferred_element_type=jnp.float32)
        + jnp.dot(attend_dlogits, attention_cols.astype(jnp.float32).T, precision=HIGH)
    )
    grad_keyvalue = lax.dot_general(
        attention_in, dkeyvalue, DOWNWARD, preferred_element_type=jnp.float32
    )
    grad_router = jnp.concatenate(
        [
            jnp.dot(attention_in.astype(jnp.float32).T, attend_dlogits, precision=HIGH),
            jnp.dot(feed_in.astype(jnp.float32).T, feed_dlogits, precision=HIGH),
        ],
        axis=1,
    )
    grad_gain_attend = jnp.sum(attend_dnorm * unit_attention, axis=0)
    grad_tokens = hidden_grad + norm_back(
        attend_dnorm, gain_attention, unit_attention, factor_attention
    )
    reduced = (
        lax.psum_scatter(
            grad_keyvalue.astype(jnp.bfloat16), "dp", scatter_dimension=0, tiled=True
        ).astype(jnp.float32),
        lax.psum_scatter(
            grad_router.astype(jnp.bfloat16), "dp", scatter_dimension=0, tiled=True
        ).astype(jnp.float32),
        lax.psum_scatter(
            grad_query.astype(jnp.bfloat16), "dp", scatter_dimension=0, tiled=True
        ).astype(jnp.float32),
        lax.psum_scatter(
            grad_projection.astype(jnp.bfloat16), "dp", scatter_dimension=0, tiled=True
        ).astype(jnp.float32),
        lax.psum_scatter(
            grad_gain_attend.astype(jnp.bfloat16), "dp", scatter_dimension=0, tiled=True
        ).astype(jnp.float32),
        lax.psum_scatter(
            grad_gain_feed.astype(jnp.bfloat16), "dp", scatter_dimension=0, tiled=True
        ).astype(jnp.float32),
    )
    shared = (
        lax.psum(reduced[0].astype(jnp.bfloat16), "expert").astype(jnp.float32),
        lax.psum(reduced[1].astype(jnp.bfloat16), "expert").astype(jnp.float32),
        lax.psum(reduced[4].astype(jnp.bfloat16), "expert").astype(jnp.float32),
        lax.psum(reduced[5].astype(jnp.bfloat16), "expert").astype(jnp.float32),
    )
    return (
        layer_output.astype(jnp.bfloat16)[None],
        grad_tokens[None],
        shared[2],
        shared[3],
        shared[0],
        shared[1],
        reduced[2][None],
        reduced[3][None],
        grad_gate[None],
        grad_up[None],
        grad_down[None],
    )


MESH = pl.DeviceIdType.MESH
CHIPS_Z = 4
TURNS = ((3, 2, 1, 0), (3, 0, 2, 1), (0, 3, 1, 2), (0, 1, 2, 3))


class Place:
    def __init__(self):
        self.dp, self.expert = lax.axis_index("dp"), lax.axis_index("expert")
        self.at = {
            "z": self.dp // 2,
            "y": self.dp % 2,
            "x": self.expert // 2,
            "c": self.expert % 2,
        }

    def across(self, axis):
        back = 1 - 2 * self.at[axis]
        if axis == "c":
            return (self.dp, self.expert + back)
        if axis == "x":
            return (self.dp, self.expert + 2 * back)
        return (self.dp + back, self.expert)

    def along(self, step):
        return (self.dp + 2 * step, self.expert)

    def block(self, whose, z, flips):
        at = {a: self.at[a] + flips.get(a, 0) * (1 - 2 * self.at[a]) for a in "xyc"}
        dp, expert = z * 2 + at["y"], at["x"] * 2 + at["c"]
        return {"all": dp * 4 + expert, "dp": dp, "expert": expert}[whose]


def enter(place, axes, others=()):
    barrier, count = pltpu.get_barrier_semaphore(), 0
    for device, condition in others:

        def greet(device=device):
            pl.semaphore_signal(barrier, inc=1, device_id=device, device_id_type=MESH)

        on(condition, greet)
        count = count + (1 if condition is None else condition.astype(jnp.int32))
    for axis in axes:
        if axis != "z":
            pl.semaphore_signal(
                barrier, inc=1, device_id=place.across(axis), device_id_type=MESH
            )
            count += 1
    if "z" in axes:
        z = place.at["z"]
        for step, there in ((-1, z > 0), (1, z < CHIPS_Z - 1)):

            @pl.when(there)
            def _(step=step):
                pl.semaphore_signal(
                    barrier, inc=1, device_id=place.along(step), device_id_type=MESH
                )

            count = count + there.astype(jnp.int32)
    pl.semaphore_wait(barrier, count)


def on(condition, action):
    if condition is None:
        action()
    else:
        pl.when(condition)(action)


def both(a, b):
    return b if a is None else a if b is None else a & b


class Post:
    def __init__(self, sems, place):
        self.sems, self.place, self.sent = sems, place, []

    def send(self, source, target, arrival, device, condition=None):
        number = len(self.sent)

        def copy():
            return pltpu.make_async_remote_copy(
                src_ref=source,
                dst_ref=target,
                send_sem=self.sems.at[number],
                recv_sem=arrival,
                device_id=device,
                device_id_type=MESH,
            )

        self.sent.append((condition, copy))
        on(condition, lambda: copy().start())

    def arrived(self, target, arrival):
        pltpu.make_async_remote_copy(
            src_ref=target,
            dst_ref=target,
            send_sem=self.sems.at[0],
            recv_sem=arrival,
            device_id=self.place.across("c"),
            device_id_type=MESH,
        ).wait_recv()

    def close(self):
        for condition, copy in self.sent:
            on(condition, lambda copy=copy: copy().wait_send())


FLIPS = {"x": 4, "y": 2, "c": 1}


def gather_plan(jobs, place, post, sources, targets, arrive_sems, own_sems):
    z_here = place.at["z"]
    line = 0
    waves, owns, starts = {}, [], []
    for j, (whose, rows, pieces) in enumerate(jobs):
        own = pltpu.make_async_copy(
            sources[j],
            targets[j].at[pl.ds(place.block(whose, z_here, {}) * rows, rows)],
            own_sems.at[j],
        )
        owns.append(own)
        begin = [own.start]
        for first, length, order in pieces:
            def part(z, flips, j=j, whose=whose, rows=rows, first=first, length=length):
                at = place.block(whose, z, flips) * rows + first
                return targets[j].at[pl.ds(at, length)]

            def mark(z, flips, line=line):
                return arrive_sems.at[line, z * 8 + sum(FLIPS[a] * v for a, v in flips.items())]

            def hand_on(source, z, flips, depth, side, wave, condition, order=order, part=part, mark=mark):
                for axis in order[max(depth, 0) :]:
                    if axis == "z" and (depth < 0 or order[depth] != "z"):
                        for step in (1, -1):
                            there = (z_here < CHIPS_Z - 1) if step > 0 else (z_here > 0)
                            post.send(source, part(z, flips), mark(z, flips), place.along(step), both(condition, there))
                    elif axis == "z":
                        there = (z_here < CHIPS_Z - 1) if side > 0 else (z_here > 0)
                        post.send(source, part(z, flips), mark(z, flips), place.along(side), both(condition, there))
                    elif depth < 0 or axis != order[depth]:
                        seen = dict(flips)
                        seen[axis] = 1
                        post.send(source, part(z, flips), mark(z, seen), place.across(axis), condition)

            def come(z, flips, depth, side, hops, wave, condition, order=order, part=part, mark=mark, hand_on=hand_on):
                def act():
                    on(condition, lambda: post.arrived(part(z, flips), mark(z, flips)))
                    hand_on(part(z, flips), z, flips, depth, side, wave, condition)

                waves.setdefault(wave, []).append(act)
                spread(z, flips, depth, side, hops, wave, condition, order, come)

            begin.append(
                lambda hand_on=hand_on, j=j, first=first, length=length: hand_on(
                    sources[j].at[pl.ds(first, length)], z_here, {}, -1, 0, 0, None
                )
            )
            spread(z_here, {}, -1, 0, 0, 0, None, order, come)
            line += 1
        starts.append(begin)
    return starts, waves, owns


def gather_kernel(jobs, axes, *refs):
    count = len(jobs)
    sources, targets = refs[:count], refs[count : 2 * count]
    send_sems, arrive_sems, own_sems = refs[2 * count :]
    place = Place()
    enter(place, axes)
    post = Post(send_sems, place)
    starts, waves, owns = gather_plan(jobs, place, post, sources, targets, arrive_sems, own_sems)
    for act in sum(starts, []):
        act()
    for wave in sorted(waves):
        for act in waves[wave]:
            act()
    for own in owns:
        own.wait()
    post.close()


def spread(z, flips, depth, side, hops, wave, condition, order, come):
    z_here = lax.axis_index("dp") // 2
    for later in range(max(depth, 0), len(order)):
        axis = order[later]
        if axis == "z":
            if depth >= 0 and order[depth] == "z":
                if hops < CHIPS_Z - 1:
                    far = hops + 1
                    there = (z_here >= far) if side > 0 else (z_here + far < CHIPS_Z)
                    come(z_here - side * far, flips, later, side, far, wave + 1, there)
            else:
                for step in (1, -1):
                    there = (z_here >= 1) if step > 0 else (z_here + 1 < CHIPS_Z)
                    come(z_here - step, flips, later, step, 1, wave + 1, both(condition, there))
        elif later > depth:
            seen = dict(flips)
            seen[axis] = 1
            come(z, seen, later, 0, 0, wave + 1, condition)


def gather(jobs, collective_id, name):
    arrays = [rows for rows, _, _ in jobs]
    sizes = {"all": 32, "dp": 8, "expert": 4}
    plan = tuple((whose, rows.shape[0], pieces) for rows, whose, pieces in jobs)
    axes = "".join(a for a in "cxyz" if any(a in order for _, _, ps in plan for _, _, order in ps))
    lines = sum(len(ps) for _, _, ps in plan)
    any_spec = pl.BlockSpec(memory_space=pltpu.HBM)
    return pl.pallas_call(
        functools.partial(gather_kernel, plan, axes),
        out_shape=[
            jax.ShapeDtypeStruct((sizes[whose] * r.shape[0], r.shape[1]), r.dtype)
            for r, whose, _ in jobs
        ],
        in_specs=[any_spec] * len(jobs),
        out_specs=[any_spec] * len(jobs),
        scratch_shapes=[
            pltpu.SemaphoreType.DMA((110 * lines,)),
            pltpu.SemaphoreType.DMA((lines, 32)),
            pltpu.SemaphoreType.DMA((len(jobs),)),
        ],
        compiler_params=pltpu.CompilerParams(
            collective_id=collective_id, has_side_effects=True
        ),
        name=name,
    )(*arrays)


def add_into(target, terms, length):
    @pl.loop(0, length // 16)
    def _(r):
        at = pl.ds(pl.multiple_of(r * 16, 16), 16)
        total = target[at, :].astype(jnp.float32)
        for term in terms:
            total = total + term[at, :].astype(jnp.float32)
        target[at, :] = total.astype(jnp.bfloat16)


def scatter_rooms(rows, width, order):
    steps, turns = len(order.replace("z", "")), CHIPS_Z if "z" in order else 1
    blocks = [turns * 2 ** (steps - 1)]
    blocks += [turns * 2 ** (steps - 1 - stage) for stage in range(steps)]
    if "z" in order:
        blocks.append(CHIPS_Z + 1)
    return [pltpu.VMEM((n, rows, width), jnp.bfloat16) for n in blocks]


def scatter_sems(order, pieces):
    steps, turns = len(order.replace("z", "")), CHIPS_Z if "z" in order else 1
    return [
        pltpu.SemaphoreType.DMA((turns * 2 ** (steps - 1),)),
        pltpu.SemaphoreType.DMA((pieces, steps, turns * 2 ** (steps - 1))),
        pltpu.SemaphoreType.DMA((pieces, CHIPS_Z + 1)),
    ]


def scatter_plan(whose, rows, pieces, place, post, source, rooms, sems):
    flat = [order.replace("z", "") for _, _, order in pieces]
    steps = len(flat[0])
    lined = "z" in pieces[0][2]
    turns = CHIPS_Z if lined else 1
    acc, bins, line = rooms[0], rooms[1 : 1 + steps], rooms[-1]
    load_sems, bin_sems, line_sems = sems
    z_here = place.at["z"]
    if lined:
        turn = [
            sum((z_here == z).astype(jnp.int32) * seq[k] for z, seq in enumerate(TURNS))
            for k in range(CHIPS_Z)
        ]
    else:
        turn = [z_here]
    slot_z = lambda k: turn[k] if lined else 0
    keep = 2 ** (steps - 1)
    names = sorted(flat[0][1:])
    loads = {}
    for k in range(turns):
        for n in reversed(range(keep)):
            flips = {a: (n >> i) & 1 for i, a in enumerate(names)}
            at = slot_z(k) * keep + n
            loads[k, n] = pltpu.make_async_copy(
                source.at[pl.ds(place.block(whose, turn[k], flips) * rows, rows)],
                acc.at[at],
                load_sems.at[at],
            )
    loaded = set()

    def mine(p, ref):
        first, length, _ = pieces[p]
        return ref.at[pl.ds(first, length)]

    def code_after(p, stage, flips):
        return sum(flips.get(a, 0) << i for i, a in enumerate(flat[p][stage + 1 :]))

    def gathered(p, k, stage, flips):
        n = sum(flips.get(a, 0) << i for i, a in enumerate(names))
        if (k, n) not in loaded:
            loads[k, n].wait()
            loaded.add((k, n))
        terms = []
        for before in range(stage):
            at = slot_z(k) * 2 ** (steps - 1 - before) + code_after(p, before, flips)
            ref = mine(p, bins[before].at[at])
            post.arrived(ref, bin_sems.at[p, before, at])
            terms.append(ref)
        block = mine(p, acc.at[slot_z(k) * keep + n])
        add_into(block, terms, pieces[p][1])
        return block

    def leave(k, stage):
        for code in reversed(range(2 ** (steps - 1 - stage))):
            for p in range(len(pieces)):
                flips = {a: (code >> i) & 1 for i, a in enumerate(flat[p][stage + 1 :])}
                flips[flat[p][stage]] = 1
                if stage == 0:
                    at = place.block(whose, turn[k], flips) * rows + pieces[p][0]
                    block = source.at[pl.ds(at, pieces[p][1])]
                else:
                    block = gathered(p, k, stage, flips)
                at = slot_z(k) * 2 ** (steps - 1 - stage) + code
                post.send(
                    block,
                    mine(p, bins[stage].at[at]),
                    bin_sems.at[p, stage, at],
                    place.across(flat[p][stage]),
                )

    def settle(k):
        for p in range(len(pieces)):
            block = gathered(p, k, steps, {})
            if not lined or k == turns - 1:
                continue
            t = turn[k]
            right = t > z_here

            def pass_on(p=p, t=t, block=block):
                ref = mine(p, line.at[t])
                post.arrived(ref, line_sems.at[p, t])
                add_into(block, [ref], pieces[p][1])

            pl.when((right & (z_here > 0)) | (~right & (z_here < CHIPS_Z - 1)))(pass_on)
            slot = jnp.where(t == z_here - 1, CHIPS_Z, t)
            post.send(
                block,
                mine(p, line.at[slot]),
                line_sems.at[p, slot],
                place.along(jnp.where(right, 1, -1)),
            )

    def finish(p):
        block = mine(p, acc.at[z_here * keep if lined else 0])
        if lined:
            for slot, there in ((z_here, z_here > 0), (CHIPS_Z, z_here < CHIPS_Z - 1)):

                def last(slot=slot):
                    ref = mine(p, line.at[slot])
                    post.arrived(ref, line_sems.at[p, slot])
                    add_into(block, [ref], pieces[p][1])

                pl.when(there)(last)
        return block

    works = [(-1, lambda k=k: leave(k, 0)) for k in range(turns)]
    for time in range(turns + steps):
        for stage in range(1, steps + 1):
            k = time - stage + 1
            if 0 <= k < turns:
                act = settle if stage == steps else lambda k, stage=stage: leave(k, stage)
                works.append((time, lambda k=k, act=act: act(k)))
    return list(loads.values()), works, finish


def sends_of(order, pieces):
    steps, turns = len(order.replace("z", "")), CHIPS_Z if "z" in order else 1
    return pieces * (turns * 2**steps + 4)


def widen(target, block, length):
    @pl.loop(0, length // 16)
    def _(r):
        at = pl.ds(pl.multiple_of(r * 16, 16), 16)
        target[at, :] = block[at, :].astype(jnp.float32)


def scatter_kernel(whose, rows, pieces, columns, filler, source, *refs):
    source = source.at[:, pl.ds(*columns)]
    given, refs = refs[: filler.operands], refs[filler.operands :]
    result, made, refs = refs[0], refs[1 : 1 + filler.results], refs[1 + filler.results :]
    rooms, refs = refs[: len(refs) - 4 - filler.rooms], refs[len(refs) - 4 - filler.rooms :]
    send_sems, sems, own = refs[0], refs[1:4], refs[4:]
    place = Place()
    post = Post(send_sems, place)
    loads, works, finish = scatter_plan(whose, rows, pieces, place, post, source, rooms, sems)
    for load in loads:
        load.start()
    enter(place, "".join(a for a in "cxyz" if a in pieces[0][2]))
    steps = filler.start(given, made, own)
    slots = [number for number, (time, _) in enumerate(works) if time >= 0]
    slots = slots[:: -(-len(slots) // filler.turns)]
    done = 0
    for number, (_, act) in enumerate(works):
        act()
        if number in slots:
            share = steps * (slots.index(number) + 1) // len(slots)
            filler.run(given, made, own, done, share)
            done = share
    for p in range(len(pieces)):
        first, length, _ = pieces[p]
        widen(result.at[pl.ds(first, length)], finish(p), length)
    filler.end(given, made, own)
    post.close()


class Nothing:
    operands = results = rooms = 0
    turns = 12
    shapes, scratch = [], []

    def start(self, given, made, own):
        return 0

    def run(self, given, made, own, first, last):
        pass

    def end(self, given, made, own):
        pass


class WeightGrads(Nothing):
    operands, results, rooms = 4, 3, 6
    TILE, CHUNK = 256, 512

    def __init__(self, rows, padded, hidden, width):
        self.chunks = rows // self.CHUNK
        self.each = padded // self.TILE
        self.short = hidden - (self.each - 1) * self.TILE
        self.tiles = (2 * self.each, self.each)
        self.shapes = [jax.ShapeDtypeStruct((hidden, width), jnp.float32)] * 3
        self.scratch = [
            pltpu.VMEM((2, self.CHUNK, self.TILE), jnp.bfloat16),
            pltpu.VMEM((2, self.CHUNK, width), jnp.bfloat16),
            pltpu.VMEM((self.TILE, width), jnp.float32),
            pltpu.VMEM((self.TILE, width), jnp.float32),
            pltpu.SemaphoreType.DMA((2, 2)),
            pltpu.SemaphoreType.DMA((2,)),
        ]

    def copies(self, given, own, step, second):
        tile, chunk = step // self.chunks - (self.tiles[0] if second else 0), step % self.chunks
        slot = step % 2
        rows = pl.ds(pl.multiple_of(chunk * self.CHUNK, self.CHUNK), self.CHUNK)
        cols = pl.ds(pl.multiple_of(tile * self.TILE, self.TILE), self.TILE)
        left, right = given[2 * second], given[2 * second + 1]
        return [
            pltpu.make_async_copy(left.at[rows, cols], own[0].at[slot], own[4].at[slot, 0]),
            pltpu.make_async_copy(right.at[rows], own[1].at[slot], own[4].at[slot, 1]),
        ]

    def fetch(self, given, own, step, start):
        edge = self.tiles[0] * self.chunks
        for second in (0, 1):

            @pl.when((step >= edge) if second else (step < edge))
            def _(second=second):
                for copy in self.copies(given, own, step, second):
                    copy.start() if start else copy.wait()

    def put(self, made, own, tile, parity, start):
        row = (tile % self.each) * self.TILE
        for result in range(3):
            for last in (0, 1):
                length = self.short if last else self.TILE
                at_end = (tile % self.each) == self.each - 1

                @pl.when((tile // self.each == result) & (at_end if last else ~at_end))
                def _(result=result, length=length):
                    copy = pltpu.make_async_copy(
                        own[2 + parity].at[pl.ds(0, length)],
                        made[result].at[pl.ds(pl.multiple_of(row, self.TILE), length)],
                        own[5].at[parity],
                    )
                    copy.start() if start else copy.wait()

    def start(self, given, made, own):
        self.fetch(given, own, jnp.int32(0), True)
        return sum(self.tiles) * self.chunks

    def run(self, given, made, own, first, last):
        total = sum(self.tiles) * self.chunks

        @pl.loop(first, last)
        def _(step):
            tile, chunk = step // self.chunks, step % self.chunks

            @pl.when(step + 1 < total)
            def _():
                self.fetch(given, own, step + 1, True)

            self.fetch(given, own, step, False)
            part = lax.dot_general(
                own[0][step % 2], own[1][step % 2], DOWNWARD, preferred_element_type=jnp.float32
            )
            for parity in (0, 1):

                @pl.when(tile % 2 == parity)
                def _(parity=parity):
                    acc = own[2 + parity]

                    @pl.when(chunk == 0)
                    def _():
                        @pl.when(tile >= 2)
                        def _():
                            self.put(made, own, tile - 2, parity, False)

                        acc[...] = part

                    @pl.when(chunk > 0)
                    def _():
                        acc[...] += part

                    @pl.when(chunk == self.chunks - 1)
                    def _():
                        self.put(made, own, tile, parity, True)

    def end(self, given, made, own):
        tiles = sum(self.tiles)
        for tile in (tiles - 2, tiles - 1):
            self.put(made, own, jnp.int32(tile), tile % 2, False)


class LowGrad(Nothing):
    operands, results, rooms = 2, 1, 5
    TILE, turns = 256, 4

    def __init__(self, rows, left, width):
        self.tiles, self.width = left // self.TILE, width
        low = jnp.bfloat16
        self.shapes = [jax.ShapeDtypeStruct((left, width), low)]
        self.scratch = [
            pltpu.VMEM((2, rows, self.TILE), low),
            pltpu.VMEM((rows, width), low),
            pltpu.VMEM((2, self.TILE, width), low),
            pltpu.SemaphoreType.DMA((3,)),
            pltpu.SemaphoreType.DMA((2,)),
        ]

    def left(self, given, own, tile):
        at = pl.ds(pl.multiple_of(tile * self.TILE, self.TILE), self.TILE)
        return pltpu.make_async_copy(given[0].at[:, at], own[0].at[tile % 2], own[3].at[tile % 2])

    def right(self, given, own):
        return pltpu.make_async_copy(given[1], own[1], own[3].at[2])

    def put(self, made, own, tile):
        rows = pl.ds(pl.multiple_of(tile * self.TILE, self.TILE), self.TILE)
        return pltpu.make_async_copy(own[2].at[tile % 2], made[0].at[rows], own[4].at[tile % 2])

    def start(self, given, made, own):
        self.right(given, own).start()
        self.left(given, own, jnp.int32(0)).start()
        return self.tiles

    def run(self, given, made, own, first, last):
        if first == last:
            return
        if first == 0:
            self.right(given, own).wait()

        @pl.loop(first, last)
        def _(tile):
            slot = tile % 2

            @pl.when(tile + 1 < self.tiles)
            def _():
                self.left(given, own, tile + 1).start()

            self.left(given, own, tile).wait()

            @pl.when(tile >= 2)
            def _():
                self.put(made, own, tile - 2).wait()

            half = self.width // 2
            for part in (0, 1):
                cols = slice(part * half, (part + 1) * half)
                own[2][slot, :, cols] = lax.dot_general(
                    own[0][slot], own[1][:, cols], DOWNWARD, preferred_element_type=jnp.float32
                ).astype(jnp.bfloat16)
            self.put(made, own, tile).start()

    def end(self, given, made, own):
        for tile in (self.tiles - 2, self.tiles - 1):
            self.put(made, own, jnp.int32(tile)).wait()


class InTurn(Nothing):
    def __init__(self, one, other):
        self.parts = (one, other)
        self.operands = one.operands + other.operands
        self.results = one.results + other.results
        self.rooms = one.rooms + other.rooms
        self.turns = one.turns + other.turns
        self.shapes, self.scratch = one.shapes + other.shapes, one.scratch + other.scratch

    def split(self, given, made, own):
        one = self.parts[0]
        return (
            (given[: one.operands], made[: one.results], own[: one.rooms]),
            (given[one.operands :], made[one.results :], own[one.rooms :]),
        )

    def start(self, *refs):
        self.steps = [part.start(*own) for part, own in zip(self.parts, self.split(*refs))]
        return self.parts[0].turns + self.parts[1].turns

    def run(self, given, made, own, first, last):
        edge = self.parts[0].turns
        for n, (part, refs) in enumerate(zip(self.parts, self.split(given, made, own))):
            low, high = (0, edge) if n == 0 else (edge, edge + part.turns)
            begin, end = max(first, low) - low, min(last, high) - low
            if begin < end:
                steps = self.steps[n]
                part.run(*refs, steps * begin // part.turns, steps * end // part.turns)

    def end(self, *refs):
        for part, own in zip(self.parts, self.split(*refs)):
            part.end(*own)


def scatter(array, whose, pieces, collective_id, name, filler=Nothing(), operands=(), columns=None):
    size = {"all": 32, "dp": 8, "expert": 4}[whose]
    columns = columns or (0, array.shape[1])
    rows, width = array.shape[0] // size, columns[1]
    order, count = pieces[0][2], len(pieces)
    hbm = pl.BlockSpec(memory_space=pltpu.HBM)
    out = pl.pallas_call(
        functools.partial(scatter_kernel, whose, rows, pieces, columns, filler),
        out_shape=[jax.ShapeDtypeStruct((rows, width), jnp.float32)] + filler.shapes,
        in_specs=[hbm] * (1 + len(operands)),
        out_specs=[pl.BlockSpec(memory_space=pltpu.VMEM)] + [hbm] * filler.results,
        scratch_shapes=scatter_rooms(rows, width, order)
        + [pltpu.SemaphoreType.DMA((sends_of(order, count),))]
        + scatter_sems(order, count)
        + filler.scratch,
        compiler_params=pltpu.CompilerParams(
            collective_id=collective_id, has_side_effects=True, vmem_limit_bytes=63 * 2**20
        ),
        name=name,
    )(array, *operands)
    return out if filler.results else out[0]


def sum_right_kernel(rows, pieces, columns, out_rows, out_pieces, filler, source, out_grad, *refs):
    source = source.at[:, pl.ds(*columns)]
    given, refs = refs[: filler.operands], refs[filler.operands :]
    result, output, refs = refs[0], refs[1], refs[2:]
    made, refs = refs[: filler.results], refs[filler.results :]
    count = len(scatter_rooms(rows, 128, pieces[0][2]))
    rooms, refs = refs[:count], refs[count:]
    count = len(scatter_rooms(rows, 128, out_pieces[0][2]))
    out_rooms, refs = refs[:count], refs[count:]
    dealt, send_sems, deal_sems = refs[:3]
    sems, out_sems, own = refs[3:6], refs[6:9], refs[9:]
    place = Place()
    post = Post(send_sems, place)
    z, e = place.at["z"], place.expert
    partner, moves = (e * 2 + place.at["y"], z), z != e
    loads, works, finish = scatter_plan(
        "all", rows, pieces, place, post, source, rooms, sems
    )
    out_loads, out_works, out_finish = scatter_plan(
        "dp", out_rows, out_pieces, place, post, out_grad, out_rooms, out_sems
    )
    for load in loads + out_loads:
        load.start()
    enter(place, "cxyz", [(partner, moves)])
    steps = filler.start(given, made, own)
    times = sorted({time for time, _ in works + out_works})
    turns = [time for time in times if time >= 0]
    done = 0
    for time in times:
        for plan in (out_works, works):
            for at, act in plan:
                if at == time:
                    act()
        if time >= 0:
            share = steps * (turns.index(time) + 1) // len(turns)
            filler.run(given, made, own, done, share)
            done = share
    for p in range(len(out_pieces)):
        first, length, _ = out_pieces[p]
        at = pl.ds(first, length)
        post.send(out_finish(p), dealt.at[at], deal_sems.at[p], partner, moves)
    for p in range(len(pieces)):
        first, length, _ = pieces[p]
        widen(result.at[pl.ds(first, length)], finish(p), length)
    filler.end(given, made, own)
    for p in range(len(out_pieces)):
        first, length, _ = out_pieces[p]
        at = pl.ds(first, length)

        def came(p=p, at=at, length=length):
            post.arrived(dealt.at[at], deal_sems.at[p])
            widen(output.at[at], dealt.at[at], length)

        pl.when(moves)(came)
        pl.when(~moves)(
            lambda at=at, length=length: widen(output.at[at], out_rooms[0].at[z, at], length)
        )
    post.close()


def sum_right(array, columns, pieces, out_grad, out_pieces, collective_id, filler, operands):
    rows, width = array.shape[0] // 32, columns[1]
    out_rows, out_width = out_grad.shape[0] // 8, out_grad.shape[1]
    order, out_order = pieces[0][2], out_pieces[0][2]
    hbm = pl.BlockSpec(memory_space=pltpu.HBM)
    vmem = pl.BlockSpec(memory_space=pltpu.VMEM)
    shape = jax.ShapeDtypeStruct
    sends = sends_of(order, len(pieces)) + sends_of(out_order, len(out_pieces)) + len(out_pieces)
    return pl.pallas_call(
        functools.partial(
            sum_right_kernel, rows, pieces, columns, out_rows, out_pieces, filler
        ),
        out_shape=[
            shape((rows, width), jnp.float32),
            shape((out_rows, out_width), jnp.float32),
        ]
        + filler.shapes,
        in_specs=[hbm] * (2 + len(operands)),
        out_specs=[vmem] * 2 + [hbm] * filler.results,
        scratch_shapes=scatter_rooms(rows, width, order)
        + scatter_rooms(out_rows, out_width, out_order)
        + [
            pltpu.VMEM((out_rows, out_width), jnp.bfloat16),
            pltpu.SemaphoreType.DMA((sends,)),
            pltpu.SemaphoreType.DMA((len(out_pieces),)),
        ]
        + scatter_sems(order, len(pieces))
        + scatter_sems(out_order, len(out_pieces))
        + filler.scratch,
        compiler_params=pltpu.CompilerParams(
            collective_id=collective_id, has_side_effects=True, vmem_limit_bytes=63 * 2**20
        ),
        name="sum_output_right",
    )(array, out_grad, *operands)


def sum_weights_kernel(rows, pieces, in_grad, query, keyvalue, *refs):
    count = len(scatter_rooms(rows, 128, pieces[0][2]))
    rooms = refs[:count]
    dealt, shared, send_sems, deal_sems = refs[count : count + 4]
    place = Place()
    post = Post(send_sems, place)
    z, e = place.at["z"], place.expert
    wide = query.shape[1]
    span = (in_grad.shape[1] - wide) // 2
    peers = []
    for flip_x, flip_c in ((1, 1), (1, 0), (0, 1)):
        x = place.at["x"] + flip_x * (1 - 2 * place.at["x"])
        core = place.at["c"] + flip_c * (1 - 2 * place.at["c"])
        peers.append((x * 2 + core, flip_x * 2 + flip_c))
    loads, works, finish = scatter_plan(
        "dp", rows, pieces, place, post, in_grad, rooms, refs[count + 4 :]
    )
    for load in loads:
        load.start()
    enter(place, "cxyz", [((place.dp, peers[0][0]), None)])
    for _, act in works:
        act()
    cols = lambda block: pl.ds(pl.multiple_of(block * span, span), span)
    keep = slice(wide, wide + 2 * span)
    for p in range(len(pieces)):
        first, length, _ = pieces[p]
        at = pl.ds(first, length)
        block = finish(p)
        post.send(block.at[:, keep], shared.at[2, at], deal_sems.at[p, 4], place.across("x"))
        for peer, flips in peers:
            post.send(
                block.at[:, cols(peer)],
                dealt.at[at, cols(e)],
                deal_sems.at[p, flips],
                (place.dp, peer),
            )
        post.send(block.at[:, keep], shared.at[1, at], deal_sems.at[p, 5], place.across("c"))

    def place_keys(p, flips, block):
        first, length, _ = pieces[p]
        rows_at = pl.ds(first, length)
        x = place.at["x"] + (flips // 2) * (1 - 2 * place.at["x"])
        core = place.at["c"] + (flips % 2) * (1 - 2 * place.at["c"])
        owner = x * 2 + core
        widen(keyvalue.at[rows_at, cols(owner)], block.at[:, pl.ds(0, span)], length)
        widen(
            keyvalue.at[rows_at, cols(wide // span + owner)], block.at[:, pl.ds(span, span)], length
        )

    for p in range(len(pieces)):
        first, length, _ = pieces[p]
        at = pl.ds(first, length)
        block = rooms[0].at[z, at]
        widen(query.at[at, cols(e)], block.at[:, cols(e)], length)
        place_keys(p, 0, block.at[:, keep])
        post.arrived(shared.at[1, at], deal_sems.at[p, 5])
        place_keys(p, 1, shared.at[1, at])
        post.arrived(shared.at[2, at], deal_sems.at[p, 4])
        post.send(shared.at[2, at], shared.at[3, at], deal_sems.at[p, 6], place.across("c"))
        place_keys(p, 2, shared.at[2, at])
        for peer, flips in reversed(peers):
            post.arrived(dealt.at[at, cols(peer)], deal_sems.at[p, flips])
            widen(query.at[at, cols(peer)], dealt.at[at, cols(peer)], length)
        post.arrived(shared.at[3, at], deal_sems.at[p, 6])
        place_keys(p, 3, shared.at[3, at])
    post.close()


def sum_weights(in_grad, wide, pieces, collective_id):
    rows, total = in_grad.shape[0] // 8, in_grad.shape[1]
    order, count = pieces[0][2], len(pieces)
    vmem = pl.BlockSpec(memory_space=pltpu.VMEM)
    shape = jax.ShapeDtypeStruct
    return pl.pallas_call(
        functools.partial(sum_weights_kernel, rows, pieces),
        out_shape=[
            shape((rows, wide), jnp.float32),
            shape((rows, 2 * wide), jnp.float32),
        ],
        in_specs=[pl.BlockSpec(memory_space=pltpu.HBM)],
        out_specs=[vmem] * 2,
        scratch_shapes=scatter_rooms(rows, total, order)
        + [
            pltpu.VMEM((rows, wide), jnp.bfloat16),
            pltpu.VMEM((4, rows, total - wide), jnp.bfloat16),
            pltpu.SemaphoreType.DMA((sends_of(order, count) + 7 * count,)),
            pltpu.SemaphoreType.DMA((count, 7)),
        ]
        + scatter_sems(order, count),
        compiler_params=pltpu.CompilerParams(
            collective_id=collective_id, has_side_effects=True, vmem_limit_bytes=63 * 2**20
        ),
        name="sum_weights",
    )(in_grad)


def weights_kernel(jobs, *refs):
    ready = len(jobs) - 2
    sources, (query, keyvalue, output) = refs[:ready], refs[ready : ready + 3]
    in_shard, out_shard = refs[ready + 3 : ready + 5]
    targets = refs[ready + 5 : 2 * ready + 7]
    send_sems, arrive_sems, own_sems, deal_sems = refs[2 * ready + 7 :]
    place = Place()
    z, y, e = place.at["z"], place.at["y"], place.expert
    span = (in_shard.shape[1] - query.shape[1]) // 2
    wide = query.shape[1]
    partner, moves = (e * 2 + y, z), z != e
    peers = []
    for flip_x, flip_c in ((1, 1), (1, 0), (0, 1)):
        x = place.at["x"] + flip_x * (1 - 2 * place.at["x"])
        core = place.at["c"] + flip_c * (1 - 2 * place.at["c"])
        peers.append((x * 2 + core, flip_x * 2 + flip_c))
    enter(place, "cxyz", [((place.dp, peers[0][0]), None), (partner, moves)])
    post = Post(send_sems, place)
    starts, waves, owns = gather_plan(
        jobs, place, post, list(sources) + [in_shard, out_shard], targets, arrive_sems, own_sems
    )
    cols = lambda block: pl.ds(pl.multiple_of(block * span, span), span)
    for peer, flips in peers:
        post.send(
            query.at[:, cols(peer)], in_shard.at[:, cols(e)], deal_sems.at[flips], (place.dp, peer)
        )
    post.send(output, out_shard, deal_sems.at[4], partner, moves)
    local = [
        pltpu.make_async_copy(query.at[:, cols(e)], in_shard.at[:, cols(e)], deal_sems.at[0]),
        pltpu.make_async_copy(
            keyvalue.at[:, cols(e)], in_shard.at[:, pl.ds(wide, span)], deal_sems.at[5]
        ),
        pltpu.make_async_copy(
            keyvalue.at[:, cols(wide // span + e)],
            in_shard.at[:, pl.ds(wide + span, span)],
            deal_sems.at[6],
        ),
    ]
    for copy in local:
        copy.start()
    stay = pltpu.make_async_copy(output, out_shard, deal_sems.at[7])
    pl.when(~moves)(stay.start)
    for act in sum(starts[:ready], []):
        act()
    for copy in local:
        copy.wait()
    for peer, flips in peers:
        post.arrived(in_shard.at[:, cols(peer)], deal_sems.at[flips])
    for act in starts[ready]:
        act()
    pl.when(~moves)(stay.wait)
    pl.when(moves)(lambda: post.arrived(out_shard, deal_sems.at[4]))
    for act in starts[ready + 1]:
        act()
    for wave in sorted(waves):
        for act in waves[wave]:
            act()
    for own in owns:
        own.wait()
    post.close()


def gather_weights(jobs, query, keyvalue, output, pieces, collective_id):
    rows, wide = query.shape
    span = wide // lax.axis_size("expert")
    shards = [
        jax.ShapeDtypeStruct((rows, wide + 2 * span), query.dtype),
        jax.ShapeDtypeStruct(output.shape, output.dtype),
    ]
    sizes = {"all": 32, "dp": 8, "expert": 4}
    plan = tuple((whose, r.shape[0], ps) for r, whose, ps in jobs)
    plan += tuple(("dp", s.shape[0], pieces) for s in shards)
    lines = sum(len(ps) for _, _, ps in plan)
    hbm = pl.BlockSpec(memory_space=pltpu.HBM)
    gathered = [
        jax.ShapeDtypeStruct((sizes[whose] * r.shape[0], r.shape[1]), r.dtype)
        for r, (whose, _, _) in zip([r for r, _, _ in jobs] + shards, plan)
    ]
    out = pl.pallas_call(
        functools.partial(weights_kernel, plan),
        out_shape=shards + gathered,
        in_specs=[hbm] * (len(jobs) + 3),
        out_specs=[hbm] * (2 + len(gathered)),
        scratch_shapes=[
            pltpu.SemaphoreType.DMA((110 * lines,)),
            pltpu.SemaphoreType.DMA((lines, 32)),
            pltpu.SemaphoreType.DMA((len(plan),)),
            pltpu.SemaphoreType.DMA((8,)),
        ],
        compiler_params=pltpu.CompilerParams(collective_id=collective_id, has_side_effects=True),
        name="gather_weights",
    )(*[r for r, _, _ in jobs], query, keyvalue, output)
    return out[2:]


def attention_bias(bias, block, rows, width, prefix):
    query = block * rows + lax.broadcasted_iota(jnp.int32, (rows, width), 0)
    key = lax.broadcasted_iota(jnp.int32, (rows, width), 1)
    bias[:, :width] = jnp.where((key <= query) | (key < prefix), 0.0, NEG)


def pick_expert(ref, lane, experts, span, chosen):
    total = None
    for e in range(experts):
        cols = ref[:, pl.ds(pl.multiple_of(e * span + lane, HEAD_DIM), HEAD_DIM)]
        term = jnp.where(chosen == e, cols.astype(jnp.float32), 0.0)
        total = term if total is None else total + term
    return total.astype(jnp.bfloat16)


def key_limits(blocks, rows):
    return [max((i + 1) * rows, blocks * rows // 2) for i in range(blocks)]


def for_each_limit(blocks, rows, body):
    block = pl.program_id(0)
    limits = key_limits(blocks, rows)
    for width in sorted(set(limits)):
        members = [i for i, limit in enumerate(limits) if limit == width]
        pl.when((block >= members[0]) & (block <= members[-1]))(lambda width=width: body(width))


def attention_kernel(experts, prefix, q, k, v, side, mixed, log_total, bias):
    rows, span = q.shape[0], k.shape[1]
    heads = span // HEAD_DIM
    block = pl.program_id(0)
    chosen = [side[:, 0:1], side[:, 1:2]]
    gates = [side[:, 2:3], side[:, 3:4]]

    def body(width):
        attention_bias(bias, block, rows, width, prefix[0])

        @pl.loop(0, heads)
        def _(head):
            lane = head * HEAD_DIM
            lanes = pl.ds(pl.multiple_of(lane, HEAD_DIM), HEAD_DIM)
            weighted = []
            for j in range(2):
                query = pick_expert(q, lane, experts, span, chosen[j])
                scores = lax.dot_general(
                    query, k[:width, lanes], ACROSS, preferred_element_type=jnp.float32
                )
                scores = scores * (HEAD_DIM**-0.5) + bias[:, :width]
                largest = jnp.max(scores, axis=1, keepdims=True)
                exponent = jnp.exp(scores - largest)
                total = jnp.sum(exponent, axis=1, keepdims=True)
                low = (exponent * (1.0 / total)).astype(jnp.bfloat16)
                out = jnp.dot(low, v[:width, lanes], preferred_element_type=jnp.float32)
                weighted.append(out * gates[j])
                at = pl.ds(pl.multiple_of((2 * head + j) * HEAD_DIM, HEAD_DIM), HEAD_DIM)
                log_total[:, at] = jnp.broadcast_to(
                    largest + jnp.log(total), (rows, HEAD_DIM)
                )
            for e in range(experts):
                cols = jnp.where(chosen[0] == e, weighted[0], 0.0) + jnp.where(
                    chosen[1] == e, weighted[1], 0.0
                )
                at = pl.ds(pl.multiple_of(e * span + lane, HEAD_DIM), HEAD_DIM)
                mixed[:, at] = cols.astype(jnp.bfloat16)

    for_each_limit(k.shape[0] // rows, rows, body)


def attention(projected, side, prefix, experts, rows):
    length = projected.shape[0]
    span = projected.shape[1] // (experts + 2)
    wide = experts * span
    return pl.pallas_call(
        functools.partial(attention_kernel, experts),
        grid=(length // rows,),
        in_specs=[
            pl.BlockSpec(memory_space=pltpu.SMEM),
            pl.BlockSpec((rows, wide), lambda i: (i, 0)),
            pl.BlockSpec((length, span), lambda i: (0, experts)),
            pl.BlockSpec((length, span), lambda i: (0, experts + 1)),
            pl.BlockSpec((rows, 128), lambda i: (i, 0)),
        ],
        out_specs=[
            pl.BlockSpec((rows, wide), lambda i: (i, 0)),
            pl.BlockSpec((rows, 2 * span), lambda i: (i, 0)),
        ],
        out_shape=[
            jax.ShapeDtypeStruct((length, wide), jnp.bfloat16),
            jax.ShapeDtypeStruct((length, 2 * span), jnp.float32),
        ],
        scratch_shapes=[pltpu.VMEM((rows, length), jnp.float32)],
        compiler_params=pltpu.CompilerParams(vmem_limit_bytes=48 * 2**20),
        name="attention",
    )(prefix, projected, projected, projected, side)


class AttentionBack(Nothing):
    operands, results, rooms = 4, 2, 11
    turns = 4

    def __init__(self, length, total, experts, rows):
        self.length, self.experts, self.rows = length, experts, rows
        self.span = total // (experts + 2)
        low, f32 = jnp.bfloat16, jnp.float32
        self.heads = self.span // HEAD_DIM
        self.blocks = length // rows
        self.shapes = [
            jax.ShapeDtypeStruct((length, total), low),
            jax.ShapeDtypeStruct((length, 128), f32),
        ]
        self.scratch = [
            pltpu.VMEM((length, total), low),
            pltpu.VMEM((length, 128), f32),
            pltpu.VMEM((length, 2 * self.span), f32),
            pltpu.VMEM((length, experts * self.span), low),
            pltpu.VMEM((length, total), low),
            pltpu.VMEM((length, 128), f32),
            pltpu.VMEM((rows, length), f32),
            pltpu.VMEM((length, self.span), f32),
            pltpu.VMEM((length, self.span), f32),
            pltpu.SemaphoreType.DMA((4,)),
            pltpu.SemaphoreType.DMA((2,)),
        ]

    def loads(self, given, own):
        return [pltpu.make_async_copy(given[i], own[i], own[9].at[i]) for i in range(4)]

    def start(self, given, made, own):
        for load in self.loads(given, own):
            load.start()
        for ref in (own[5], own[7], own[8]):
            ref[...] = jnp.zeros_like(ref)
        return self.blocks * self.heads

    def run(self, given, made, own, first, last):
        if first == 0:
            for load in self.loads(given, own):
                load.wait()

        @pl.loop(first, last)
        def _(step):
            block = step // self.heads
            limits = key_limits(self.blocks, self.rows)
            for width in sorted(set(limits)):
                members = [i for i, limit in enumerate(limits) if limit == width]

                @pl.when((block >= members[0]) & (block <= members[-1]))
                def _(width=width):
                    self.step(own, block, step % self.heads, width)

    def step(self, own, block, head, width):
        qkv, side_ref, log_total, dmix, dprojected, dgate, bias, dk, dv = own[:9]
        experts, span, rows = self.experts, self.span, self.rows
        scaling = HEAD_DIM**-0.5
        row_at = pl.ds(pl.multiple_of(block * rows, rows), rows)
        side = side_ref[row_at, :]
        chosen = [side[:, 0:1], side[:, 1:2]]
        gates = [side[:, 2:3], side[:, 3:4]]
        column = lax.broadcasted_iota(jnp.int32, (rows, 128), 1)
        query_at = block * rows + lax.broadcasted_iota(jnp.int32, (rows, width), 0)
        key_at = lax.broadcasted_iota(jnp.int32, (rows, width), 1)
        reach = key_at.astype(jnp.float32) < side[:, 4:5]
        bias[:, :width] = jnp.where((key_at <= query_at) | reach, 0.0, NEG)
        lane = head * HEAD_DIM
        lanes = lambda base: pl.ds(pl.multiple_of(base + lane, HEAD_DIM), HEAD_DIM)
        keys = qkv[:width, lanes(experts * span)]
        values = qkv[:width, lanes((experts + 1) * span)]
        dqueries = []
        for j in range(2):
            query = pick_expert(qkv.at[row_at], lane, experts, span, chosen[j])
            dm = pick_expert(dmix.at[row_at], lane, experts, span, chosen[j])
            at = pl.ds(pl.multiple_of((2 * head + j) * HEAD_DIM, HEAD_DIM), HEAD_DIM)
            logs = jnp.tile(log_total[row_at, at], (1, width // HEAD_DIM))
            scores = lax.dot_general(query, keys, ACROSS, preferred_element_type=jnp.float32)
            probs = jnp.exp(scores * scaling + bias[:, :width] - logs)
            dprobs = lax.dot_general(dm, values, ACROSS, preferred_element_type=jnp.float32)
            inner = jnp.sum(probs * dprobs, axis=1, keepdims=True)
            dgate[row_at, :] += jnp.where(column == j, inner, 0.0)
            probs = probs * gates[j]
            dscores = (probs * (dprobs - inner)).astype(jnp.bfloat16)
            low = probs.astype(jnp.bfloat16)
            dqueries.append(jnp.dot(dscores, keys, preferred_element_type=jnp.float32) * scaling)
            dk[:width, lanes(0)] += lax.dot_general(
                dscores, query, DOWNWARD, preferred_element_type=jnp.float32
            )
            dv[:width, lanes(0)] += lax.dot_general(
                low, dm, DOWNWARD, preferred_element_type=jnp.float32
            )
        for e in range(experts):
            cols = jnp.where(chosen[0] == e, dqueries[0], 0.0) + jnp.where(
                chosen[1] == e, dqueries[1], 0.0
            )
            dprojected[row_at, lanes(e * span)] = cols.astype(jnp.bfloat16)

    def end(self, given, made, own):
        dprojected, dgate, dk, dv = own[4], own[5], own[7], own[8]
        wide = self.experts * self.span
        dprojected[:, wide : wide + self.span] = (dk[...] * HEAD_DIM**-0.5).astype(jnp.bfloat16)
        dprojected[:, wide + self.span :] = dv[...].astype(jnp.bfloat16)
        copies = [
            pltpu.make_async_copy(dprojected, made[0], own[10].at[0]),
            pltpu.make_async_copy(dgate, made[1], own[10].at[1]),
        ]
        for copy in copies:
            copy.start()
        for copy in copies:
            copy.wait()


def expert_slots(first, second, my_index):
    tok_rows = first.shape[1]
    chosen = ((first == my_index) | (second == my_index)).astype(jnp.float32)
    before = jnp.triu(jnp.ones((tok_rows, tok_rows), jnp.float32), 1)
    slots = jnp.where(chosen > 0, jnp.dot(chosen, before), -1.0).astype(jnp.int32)
    return slots, first + second - my_index


def feed_kernel(
    tok,
    slot_count,
    own_rows,
    cots_left,
    cots_right,
    gate_weight,
    up_weight,
    down_weight,
    router_rows,
    slots,
    others,
    everyone,
    dx_part,
    out_part,
    x_kept,
    g_kept,
    d_kept,
    a_kept,
    dgate,
    w_in,
    w_down,
    rows_buf,
    cots_buf,
    xs,
    gs,
    pre,
    back,
    ds,
    acts,
    dx_buf,
    out_buf,
    dxs,
    outs,
    send_sems,
    arrive_sems,
    own_sem,
    weight_sems,
    load_sems,
    keep_sems,
):
    place = Place()
    z_here = place.at["z"]
    hidden = gate_weight.shape[0]
    padded = w_down.shape[0]
    width = own_rows.shape[1]
    half = tok // 2
    chips = 4 * CHIPS_Z
    pair = 2 * slot_count
    f32, low = jnp.float32, jnp.bfloat16

    loads = [
        pltpu.make_async_copy(gate_weight, w_in.at[pl.ds(0, hidden)], weight_sems.at[0]),
        pltpu.make_async_copy(
            router_rows, w_in.at[pl.ds(hidden, padded - hidden)], weight_sems.at[1]
        ),
        pltpu.make_async_copy(up_weight, w_in.at[pl.ds(padded, hidden)], weight_sems.at[2]),
        pltpu.make_async_copy(down_weight, w_down.at[pl.ds(0, hidden)], weight_sems.at[3]),
        pltpu.make_async_copy(
            own_rows, everyone.at[pl.ds(place.block("all", z_here, {}) * tok, tok)], own_sem
        ),
    ]
    for load in loads:
        load.start()
    w_in[padded + hidden :, :] = jnp.zeros((padded - hidden, width), low)
    w_down[hidden:, :] = jnp.zeros((padded - hidden, width), low)
    enter(place, "cxyz")

    def chip(u):
        u = jnp.asarray(u, jnp.int32)
        turn, q = u // 4, u % 4
        flip = lambda *at: ((q == at[0]) | (q == at[1])).astype(jnp.int32)
        k, xr, yr = turn + (q == 3) - (q == 0), flip(0, 1), flip(0, 2)
        k = jnp.where(u == 0, 0, jnp.minimum(k, CHIPS_Z - 1))
        xr = jnp.where(u == 0, 0, jnp.where(u == chips - 1, 1, xr))
        yr = jnp.where(u == 0, 0, jnp.where(u == chips - 1, 1, yr))
        inner = (z_here == 1) | (z_here == 2)
        near = jnp.where(inner, jnp.where(k == 3, 3, jnp.where(k == 2, 0, k + 1)), k)
        return jnp.where(z_here < 2, near, CHIPS_Z - 1 - near), xr, yr

    def first_block(u):
        z, xr, yr = chip(u)
        x = place.at["x"] + xr * (1 - 2 * place.at["x"])
        y = place.at["y"] + yr * (1 - 2 * place.at["y"])
        return (z * 2 + y) * 4 + x * 2

    def part(p, u, core):
        return everyone.at[pl.ds((first_block(u) + core) * tok + p * half, half)]

    def remote(source, target, number, mark, device):
        return pltpu.make_async_remote_copy(
            src_ref=source,
            dst_ref=target,
            send_sem=send_sems.at[number],
            recv_sem=arrive_sems.at[mark],
            device_id=device,
            device_id_type=MESH,
        )

    def routes(u, p):
        z, xr, yr = chip(u)
        plain = (xr + yr) == 0
        mark = (p * CHIPS_Z + z) * 8
        here = xr * 4 + yr * 2
        base = (u * 2 + p) * 5
        own = z == z_here
        right = plain & (z <= z_here) & (z_here < CHIPS_Z - 1)
        left = plain & (z >= z_here) & (z_here > 0)
        over_x = plain if p == 0 else xr == 0
        over_y = yr == 0 if p == 0 else plain
        return [
            (right, base, mark, place.along(1)),
            (left, base + 1, mark, place.along(-1)),
            (over_x, base + 2, mark + 4 + yr * 2, place.across("x")),
            (over_y, base + 3, mark + xr * 4 + 2, place.across("y")),
            (None, base + 4, mark + here + 1, place.across("c")),
        ]

    def hand_on(u, sources, pieces=(0, 1)):
        for p in pieces:
            for condition, number, mark, device in routes(u, p):
                target = part(p, u, place.at["c"])
                source = target if sources is None else sources[p]
                on(
                    condition,
                    lambda source=source, target=target, number=number, mark=mark, device=device: remote(
                        source, target, number, mark, device
                    ).start(),
                )

    def sibling_came(u):
        z, xr, yr = chip(u)
        for p in range(2):
            ref = part(p, u, 1 - place.at["c"])
            mark = (p * CHIPS_Z + z) * 8 + xr * 4 + yr * 2 + 1
            remote(ref, ref, 0, mark, place.across("c")).wait_recv()

    def take_in(u, p):
        z, xr, yr = chip(u)
        ref = part(p, u, place.at["c"])
        mark = (p * CHIPS_Z + z) * 8 + xr * 4 + yr * 2
        remote(ref, ref, 0, mark, place.across("c")).wait_recv()
        hand_on(u, None, (p,))

    def fetch(u):
        at = pl.ds(first_block(u) * tok, 2 * tok)
        return [
            pltpu.make_async_copy(everyone.at[at], rows_buf.at[u % 2], load_sems.at[u % 2, 0]),
            pltpu.make_async_copy(
                cots_left.at[at], cots_buf.at[u % 2, :, pl.ds(0, width // 2)], load_sems.at[u % 2, 1]
            ),
            pltpu.make_async_copy(
                cots_right.at[at],
                cots_buf.at[u % 2, :, pl.ds(width // 2, width // 2)],
                load_sems.at[u % 2, 2],
            ),
        ]

    def keep(u):
        rows = pl.ds(u * pair, pair)
        blocks = pl.ds(first_block(u) * tok, 2 * tok)
        s = u % 2
        return [
            pltpu.make_async_copy(xs.at[s], x_kept.at[rows], keep_sems.at[s, 0]),
            pltpu.make_async_copy(gs.at[s], g_kept.at[rows], keep_sems.at[s, 1]),
            pltpu.make_async_copy(ds.at[s], d_kept.at[rows], keep_sems.at[s, 2]),
            pltpu.make_async_copy(acts.at[s], a_kept.at[rows], keep_sems.at[s, 3]),
            pltpu.make_async_copy(dx_buf.at[s], dx_part.at[blocks], keep_sems.at[s, 4]),
            pltpu.make_async_copy(out_buf.at[s], out_part.at[blocks], keep_sems.at[s, 5]),
        ]

    hand_on(0, [own_rows.at[pl.ds(0, half)], own_rows.at[pl.ds(half, half)]])
    loads[4].wait()
    sibling_came(0)
    for copy in fetch(0):
        copy.start()
    for p in range(2):
        take_in(1, p)
    for load in loads[:4]:
        load.wait()

    def compute(u):
        s = u % 2
        block = first_block(u)
        spread = []
        for b in range(2):
            row = slots[pl.ds(block + b, 1), :]
            table = lax.broadcasted_iota(jnp.int32, (slot_count, tok), 0) == row
            table = table.astype(f32)
            spread.append(table)
            at = pl.ds(b * slot_count, slot_count)
            from_rows = pl.ds(b * tok, tok)
            xs[s, at, :] = jnp.dot(
                table.astype(low), rows_buf[s, from_rows, :], preferred_element_type=f32
            ).astype(low)
            gs[s, at, :] = jnp.dot(
                table.astype(low), cots_buf[s, from_rows, :], preferred_element_type=f32
            ).astype(low)

        @pl.loop(0, 2 * padded // 256)
        def _(n):
            at = pl.ds(pl.multiple_of(n * 256, 256), 256)
            pre[:, at] = lax.dot_general(xs[s], w_in[at, :], ACROSS, preferred_element_type=f32)

        @pl.when(u + 2 < chips)
        def _():
            take_in(u + 2, 1)

        @pl.loop(0, padded // 256)
        def _(n):
            at = pl.ds(pl.multiple_of(n * 256, 256), 256)
            back[:, at] = lax.dot_general(gs[s], w_down[at, :], ACROSS, preferred_element_type=f32)

        for b in range(2):
            at = pl.ds(b * slot_count, slot_count)
            last = pre[at, padded - 128 : padded]
            column = lax.broadcasted_iota(jnp.int32, (slot_count, 128), 1) - (
                hidden - (padded - 128)
            )
            other = jnp.sum(
                spread[b] * others[pl.ds(block + b, 1), :].astype(f32), axis=1, keepdims=True
            )
            mine = jnp.sum(jnp.where(column == place.expert, last, 0.0), axis=1, keepdims=True)
            theirs = jnp.sum(
                jnp.where(column == other.astype(jnp.int32), last, 0.0), axis=1, keepdims=True
            )
            gate = 1.0 / (1.0 + jnp.exp(theirs - mine))
            inner = jnp.zeros((slot_count, 1), f32)
            for n in range(padded // 256):
                cols = pl.ds(n * 256, 256)
                pre_gate, pre_up = pre[at, cols], pre[at, pl.ds(padded + n * 256, 256)]
                dact = back[at, cols]
                sig = 1.0 / (1.0 + jnp.exp(-pre_gate))
                silu = pre_gate * sig
                act = silu * pre_up
                acts[s, at, cols] = (act * gate).astype(low)
                inner += jnp.sum(act * dact, axis=1, keepdims=True)
                dact = dact * gate
                ds[s, at, cols] = (dact * pre_up * sig * (1.0 + pre_gate * (1.0 - sig))).astype(low)
                ds[s, at, pl.ds(padded + n * 256, 256)] = (dact * silu).astype(low)
            dgate[pl.ds(block + b, 1), :] = jnp.sum(spread[b] * inner, axis=0, keepdims=True)

        @pl.loop(0, width // 256)
        def _(n):
            cols = pl.ds(pl.multiple_of(n * 256, 256), 256)
            dxs[:, cols] = jnp.dot(ds[s], w_in[:, cols], preferred_element_type=f32).astype(low)
            outs[:, cols] = jnp.dot(acts[s], w_down[:, cols], preferred_element_type=f32).astype(
                low
            )

        for b in range(2):
            at = pl.ds(b * slot_count, slot_count)
            back_table = spread[b].T.astype(low)
            to = pl.ds(b * tok, tok)
            dx_buf[s, to, :] = jnp.dot(
                back_table, dxs[at, :], preferred_element_type=f32
            ).astype(low)
            out_buf[s, to, :] = jnp.dot(
                back_table, outs[at, :], preferred_element_type=f32
            ).astype(low)

    @pl.loop(0, chips)
    def _(u):
        @pl.when(u + 1 < chips)
        def _():
            sibling_came(u + 1)
            for copy in fetch(u + 1):
                copy.start()

        @pl.when(u + 2 < chips)
        def _():
            take_in(u + 2, 0)

        for copy in fetch(u):
            copy.wait()

        @pl.when(u >= 2)
        def _():
            for copy in keep(u - 2):
                copy.wait()

        compute(u)
        for copy in keep(u):
            copy.start()

    for u in (chips - 2, chips - 1):
        for copy in keep(jnp.int32(u)):
            copy.wait()

    @pl.loop(0, chips)
    def _(u):
        for p in range(2):
            for condition, number, mark, device in routes(u, p):
                ref = part(p, u, place.at["c"])
                on(
                    condition,
                    lambda ref=ref, number=number, mark=mark, device=device: remote(
                        ref, ref, number, mark, device
                    ).wait_send(),
                )


def feed(
    own_rows,
    cots_left,
    cots_right,
    gate_weight,
    up_weight,
    down_weight,
    router_rows,
    slots,
    others,
    slot_count,
):
    tok, width = own_rows.shape
    hidden = gate_weight.shape[0]
    padded = hidden + router_rows.shape[0]
    total = cots_left.shape[0]
    kept = total // tok * slot_count
    low = jnp.bfloat16
    hbm = pl.BlockSpec(memory_space=pltpu.HBM)
    vmem = pl.BlockSpec(memory_space=pltpu.VMEM)
    shape = jax.ShapeDtypeStruct
    pair = 2 * slot_count
    chips = 4 * CHIPS_Z
    return pl.pallas_call(
        functools.partial(feed_kernel, tok, slot_count),
        in_specs=[hbm] * 7 + [vmem] * 2,
        out_specs=[hbm] * 7 + [vmem],
        out_shape=[
            shape((total, width), low),
            shape((total, width), low),
            shape((total, width), low),
            shape((kept, width), low),
            shape((kept, width), low),
            shape((kept, 2 * padded), low),
            shape((kept, padded), low),
            shape(slots.shape, jnp.float32),
        ],
        scratch_shapes=[
            pltpu.VMEM((2 * padded, width), low),
            pltpu.VMEM((padded, width), low),
            pltpu.VMEM((2, 2 * tok, width), low),
            pltpu.VMEM((2, 2 * tok, width), low),
            pltpu.VMEM((2, pair, width), low),
            pltpu.VMEM((2, pair, width), low),
            pltpu.VMEM((pair, 2 * padded), jnp.float32),
            pltpu.VMEM((pair, padded), jnp.float32),
            pltpu.VMEM((2, pair, 2 * padded), low),
            pltpu.VMEM((2, pair, padded), low),
            pltpu.VMEM((2, 2 * tok, width), low),
            pltpu.VMEM((2, 2 * tok, width), low),
            pltpu.VMEM((pair, width), low),
            pltpu.VMEM((pair, width), low),
            pltpu.SemaphoreType.DMA((10 * chips,)),
            pltpu.SemaphoreType.DMA((16 * CHIPS_Z,)),
            pltpu.SemaphoreType.DMA,
            pltpu.SemaphoreType.DMA((4,)),
            pltpu.SemaphoreType.DMA((2, 3)),
            pltpu.SemaphoreType.DMA((2, 6)),
        ],
        compiler_params=pltpu.CompilerParams(
            collective_id=3, has_side_effects=True, vmem_limit_bytes=60 * 2**20
        ),
        name="feed_forward",
    )(
        own_rows,
        cots_left,
        cots_right,
        gate_weight,
        up_weight,
        down_weight,
        router_rows,
        slots,
        others,
    )


def per_device_torus(
    tokens,
    cotangent,
    attention_routes,
    feedforward_routes,
    prefix_length,
    gain_attention,
    gain_feedforward,
    keyvalue_weight,
    router_weight,
    query_weight,
    output_weight,
    gate_weight,
    up_weight,
    down_weight,
):
    my_index = lax.axis_index("expert")
    group_size = lax.axis_size("expert")
    dp_size = lax.axis_size("dp")
    inputs = tokens[0].astype(jnp.float32)
    tok_rows, model_width = inputs.shape
    slot_count = 5 * 2 * tok_rows // (4 * group_size)
    query_width = HEADS * HEAD_DIM
    span = query_width // group_size
    low = jnp.bfloat16
    f32 = jnp.float32

    normed_attention, unit_attention, factor_attention = norm_parts(inputs, gain_attention)
    attention_in = normed_attention.astype(low)
    quarters = lambda order: tuple(
        (i * tok_rows // 4, tok_rows // 4, order) for i in range(4)
    )
    rows_in = keyvalue_weight.shape[0]
    route_shard = feedforward_routes[0].T.astype(low).reshape(-1, 128)
    half_model = model_width // 2
    router_shard = router_weight.T.reshape(-1, 128)
    whole = lambda a: ((0, a.shape[0], "zy"),)
    cut = rows_in * 13 // 16
    sequence_in, cots_left, every_route, router_full, in_weight, out_weight = gather_weights(
        [
            (attention_in, "expert", quarters("xc")),
            (cotangent[0, :, :half_model], "all", quarters("zyxc")),
            (route_shard, "dp", whole(route_shard)),
            (router_shard, "dp", whole(router_shard)),
        ],
        query_weight[0],
        keyvalue_weight,
        output_weight[0],
        ((0, cut, "zy"), (cut, rows_in - cut, "yz")),
        1,
    )
    cots_late, sequence_in = lax.optimization_barrier((cotangent[0, :, half_model:], sequence_in))
    cots_right = lax.all_gather(cots_late, ("dp", "expert"), axis=0, tiled=True)
    every_route = every_route.reshape(dp_size, 2, group_size, tok_rows).astype(jnp.int32)
    router_full = (
        router_full.reshape(dp_size, 2 * group_size, rows_in)
        .transpose(0, 2, 1)
        .reshape(-1, 2 * group_size)
    )
    attention_cols = router_full[:, :group_size]
    feedforward_cols = router_full[:, group_size:]
    projected = jnp.dot(sequence_in, in_weight, preferred_element_type=f32).astype(low)
    attend_matches_all = expert_matches(attention_routes[0], group_size)
    attend_logits = jnp.dot(sequence_in, attention_cols, preferred_element_type=f32)
    attend_weights_all, _ = pair_gates(attend_logits, attend_matches_all)
    reach = jnp.broadcast_to(prefix_length.astype(f32)[None], (attend_logits.shape[0], 1))
    side = jnp.concatenate([attention_routes[0].astype(f32), attend_weights_all, reach], axis=1)
    side = jnp.pad(side, ((0, 0), (0, 128 - side.shape[1])))
    mixed, log_total = attention(projected, side, prefix_length, group_size, tok_rows)
    attend_part = jnp.dot(mixed, out_weight, preferred_element_type=f32).astype(low)
    attended = scatter(attend_part, "expert", quarters("cx"), 2, "sum_attention")
    hidden = inputs + attended
    normed_feed, unit_feed, factor_feed = norm_parts(hidden, gain_feedforward)
    feed_in = normed_feed.astype(low)
    everywhere = lambda a, b: ((0, tok_rows // 2, a), (tok_rows // 2, tok_rows // 2, b))
    mine = lambda a: lax.dynamic_slice_in_dim(a, my_index * tok_rows, tok_rows, 0)
    feed_matches = expert_matches(mine(feedforward_routes[0]), group_size)
    feed_logits = jnp.dot(feed_in, feedforward_cols, preferred_element_type=f32)
    feed_weights, _ = pair_gates(feed_logits, feed_matches)
    slots, others = expert_slots(
        every_route[:, 0].reshape(-1, tok_rows), every_route[:, 1].reshape(-1, tok_rows), my_index
    )
    hidden_rows = gate_weight.shape[1]
    padded = -(-hidden_rows // 256) * 256
    router_rows = jnp.pad(
        feedforward_cols.T, ((0, padded - hidden_rows - group_size), (0, 0))
    )
    _, dx_part, out_part, kept_rows, kept_cots, kept_back, kept_act, token_dgate = feed(
        feed_in,
        cots_left,
        cots_right,
        gate_weight[0],
        up_weight[0],
        down_weight[0],
        router_rows,
        slots,
        others,
        slot_count,
    )
    own_row = (jnp.arange(group_size) == my_index).astype(f32)[None, :, None]
    feed_dgate = lax.psum_scatter(
        (token_dgate[:, None, :] * own_row).reshape(-1, tok_rows),
        ("dp", "expert"),
        scatter_dimension=0,
        tiled=True,
    ).T
    feed_home, grad_gate, grad_up, grad_down = scatter(
        dx_part,
        "all",
        everywhere("cxyz", "cyxz"),
        4,
        "sum_rows",
        WeightGrads(kept_rows.shape[0], padded, hidden_rows, model_width),
        (kept_back, kept_rows, kept_act, kept_cots),
    )
    gradient = cotangent[0].astype(f32)
    feed_dlogits = gates_back(feed_dgate, feed_weights, feed_matches)
    feed_dnorm = feed_home + jnp.dot(feed_dlogits, feedforward_cols.astype(f32).T, precision=HIGH)
    grad_gain_feed = jnp.sum(feed_dnorm * unit_feed, axis=0)
    hidden_grad = gradient + norm_back(feed_dnorm, gain_feedforward, unit_feed, factor_feed)

    (sequence_grad,) = gather(
        [(hidden_grad.astype(low), "expert", quarters("xc"))], 5, "gather_cotangents"
    )
    dmix = lax.dot_general(sequence_grad, out_weight, ACROSS, preferred_element_type=f32).astype(low)
    length, total = projected.shape
    columns = model_width // 2
    first_sum, dprojected, gate_parts, grad_out = scatter(
        out_part,
        "all",
        everywhere("cxyz", "cyxz"),
        7,
        "sum_output_left",
        InTurn(
            AttentionBack(length, total, group_size, tok_rows),
            LowGrad(length, query_width, model_width),
        ),
        (projected, side, log_total, dmix, mixed, sequence_grad),
        (0, columns),
    )
    attend_dx = lax.dot_general(dprojected, in_weight, ACROSS, preferred_element_type=f32)
    attend_dx = jnp.concatenate([attend_dx.astype(low), gate_parts.astype(low)], axis=1)
    attend_home = scatter(attend_dx, "expert", quarters("cx"), 9, "sum_attention_back")
    pair_dgate = attend_home[:, model_width : model_width + 2]
    attend_home = attend_home[:, :model_width]
    second_sum, grad_projection, grad_in = sum_right(
        out_part,
        (columns, model_width - columns),
        everywhere("cxyz", "cxyz"),
        grad_out,
        ((0, rows_in, "yz"),),
        8,
        LowGrad(length, model_width, total),
        (sequence_in, dprojected),
    )
    layer_output = hidden + jnp.concatenate([first_sum, second_sum], axis=1)
    matches = mine(attend_matches_all)
    weights = mine(attend_weights_all)
    dselected = weights * (pair_dgate - jnp.sum(weights * pair_dgate, axis=1, keepdims=True))
    attend_dlogits = jnp.sum(dselected[:, :, None] * matches, axis=1)
    attend_dnorm = attend_home + jnp.dot(
        attend_dlogits, attention_cols.astype(f32).T, precision=HIGH
    )
    grad_gain_attend = jnp.sum(attend_dnorm * unit_attention, axis=0)
    grad_tokens = hidden_grad + norm_back(
        attend_dnorm, gain_attention, unit_attention, factor_attention
    )
    small = jnp.concatenate(
        [
            lax.dot_general(attend_dlogits, attention_in.astype(f32), DOWNWARD, precision=HIGH),
            lax.dot_general(feed_dlogits, feed_in.astype(f32), DOWNWARD, precision=HIGH),
            grad_gain_attend[None],
            grad_gain_feed[None],
        ],
        axis=0,
    )
    small = lax.psum(small.astype(f32), ("dp", "expert"))
    small = lax.dynamic_slice_in_dim(small, lax.axis_index("dp") * rows_in, rows_in, 1)

    grad_query, grad_keyvalue = sum_weights(grad_in, query_width, ((0, rows_in, "yz"),), 6)
    return (
        layer_output.astype(low)[None],
        grad_tokens[None],
        small[2 * group_size],
        small[2 * group_size + 1],
        grad_keyvalue,
        small[: 2 * group_size].T,
        grad_query[None],
        grad_projection[None],
        grad_gate[None],
        grad_up[None],
        grad_down[None],
    )


def solution(mesh):
    in_specs = (
        P("dp", "expert", None),
        P("dp", "expert", None),
        P("dp", None, None),
        P("dp", None, None),
        P("dp"),
        P(),
        P(),
        P("dp", None),
        P("dp", None),
        P("expert", "dp", None),
        P("expert", "dp", None),
        P("expert", "dp", None),
        P("expert", "dp", None),
        P("expert", "dp", None),
    )
    out_specs = (
        P("dp", "expert", None),
        P("dp", "expert", None),
        P("dp"),
        P("dp"),
        P("dp", None),
        P("dp", None),
        P("expert", "dp", None),
        P("expert", "dp", None),
        P("expert", "dp", None),
        P("expert", "dp", None),
        P("expert", "dp", None),
    )
    torus = (mesh.shape["dp"], mesh.shape["expert"]) == (8, 4)
    body = per_device_torus if torus else per_device
    return jax.shard_map(
        body, mesh=mesh, in_specs=in_specs, out_specs=out_specs, check_vma=False
    )
```

```python
import functools

import jax
import jax.numpy as jnp
from jax import lax
from jax.experimental import pallas as pl
from jax.experimental.pallas import tpu as pltpu
from jax.sharding import PartitionSpec as P

HEADS = 16
HEAD_DIM = 128


EPS = 1e-06
NEG = -1e30
HIGH = lax.Precision.HIGHEST
ACROSS = (((1,), (1,)), ((), ()))
DOWNWARD = (((0,), (0,)), ((), ()))


def norm_parts(vector, gain_vector):
    factor = lax.rsqrt(jnp.mean(vector * vector, axis=-1, keepdims=True) + EPS)
    normed = vector * factor
    return (normed * gain_vector, normed, factor)


def norm_back(incoming, gain_vector, normed, factor):
    dnormed = incoming * gain_vector
    return factor * (dnormed - normed * jnp.mean(dnormed * normed, axis=-1, keepdims=True))


def route_plan(sequence_ids, my_index, group_size, tok_rows, slot_count):
    expert_range = jnp.arange(group_size, dtype=jnp.int32)
    matches_all = (sequence_ids[:, :, None] == expert_range[None, None, :]).astype(jnp.int32)
    chosen = jnp.sum(matches_all, axis=1).reshape(group_size, tok_rows, group_size)
    ranking = jnp.cumsum(chosen, axis=1) - chosen
    slot_ids = jnp.arange(slot_count, dtype=jnp.int32)[None, :, None]
    block_pick = (expert_range == my_index).astype(jnp.int32)
    my_chosen = jnp.sum(chosen * block_pick[:, None, None], axis=0).T
    my_ranking = jnp.sum(ranking * block_pick[:, None, None], axis=0).T
    send_table = (
        my_chosen[:, None, :] * (my_ranking[:, None, :] == slot_ids).astype(jnp.int32)
    ).astype(jnp.float32)
    column_chosen = jnp.sum(chosen * block_pick[None, None, :], axis=2)
    column_ranking = jnp.sum(ranking * block_pick[None, None, :], axis=2)
    taken = column_chosen[:, None, :] * (column_ranking[:, None, :] == slot_ids).astype(jnp.int32)
    positions = (
        expert_range[:, None, None] * tok_rows
        + jnp.arange(tok_rows, dtype=jnp.int32)[None, None, :]
    )
    arrival_places = jnp.sum(taken * positions, axis=2).reshape(-1)
    my_ids = lax.dynamic_slice_in_dim(sequence_ids, my_index * tok_rows, tok_rows, 0)
    matches = (my_ids[:, :, None] == expert_range[None, None, :]).astype(jnp.float32)
    return (send_table, arrival_places, matches)


def pair_gates(logits, matches):
    selected = jnp.sum(matches * logits[:, None, :], axis=2)
    largest = jnp.max(selected, axis=1, keepdims=True)
    exponent = jnp.exp(selected - largest)
    weights = exponent / jnp.sum(exponent, axis=1, keepdims=True)
    return (weights, jnp.sum(weights[:, :, None] * matches, axis=1))


def gates_back(dgate, weights, matches):
    dweights = jnp.sum(dgate[:, None, :] * matches, axis=2)
    dselected = weights * (dweights - jnp.sum(weights * dweights, axis=1, keepdims=True))
    return jnp.sum(dselected[:, :, None] * matches, axis=1)


def merge_back(send_table, gate_table, returned):
    weighted = send_table * gate_table.T[:, None, :]
    return jnp.einsum("ect,ecd->td", weighted, returned.astype(jnp.float32), precision=HIGH)


def branch_cotangent(send_table, gate_table, returned, incoming):
    spread_grad = jnp.einsum("ect,td->ecd", send_table, incoming, precision=HIGH)
    slot_gate = jnp.sum(send_table * gate_table.T[:, None, :], axis=2)
    cotangent_rows = (spread_grad * slot_gate[:, :, None]).astype(jnp.bfloat16)
    slot_dgate = jnp.sum(spread_grad * returned.astype(jnp.float32), axis=2)
    dgate = jnp.einsum("ect,ec->te", send_table, slot_dgate, precision=HIGH)
    return (cotangent_rows, dgate)


def expert_matches(ids, group_size):
    expert_range = jnp.arange(group_size, dtype=jnp.int32)
    return (ids[:, :, None] == expert_range[None, None, :]).astype(jnp.float32)


def expert_table(ids, my_index, group_size, tok_rows, slot_count):
    blocks = ids.reshape(-1, tok_rows, 2)
    chosen = jnp.sum((blocks == my_index).astype(jnp.float32), axis=2)
    before = jnp.triu(jnp.ones((tok_rows, tok_rows), jnp.float32), 1)
    ranking = jnp.dot(chosen, before)
    slot_ids = jnp.arange(slot_count, dtype=jnp.float32)[None, :, None]
    taken = chosen[:, None, :] * (ranking[:, None, :] == slot_ids).astype(jnp.float32)
    other = jnp.sum(blocks, axis=2) - my_index
    slot_other = jnp.sum(taken * other[:, None, :].astype(jnp.float32), axis=2)
    return (taken.astype(jnp.bfloat16), slot_other.reshape(-1).astype(jnp.int32))


def own_gate(logits, other, my_index):
    expert_range = jnp.arange(logits.shape[1], dtype=jnp.int32)[None]
    mine = jnp.sum(jnp.where(expert_range == my_index, logits, 0.0), axis=1, keepdims=True)
    theirs = jnp.sum(jnp.where(expert_range == other[:, None], logits, 0.0), axis=1, keepdims=True)
    return jax.nn.sigmoid(mine - theirs)


def pick_rows(taken, rows):
    blocks, slots, tokens = taken.shape
    picked = jnp.einsum(
        "bct,btd->bcd",
        taken,
        rows.reshape(blocks, tokens, -1),
        preferred_element_type=jnp.float32,
    )
    return picked.astype(jnp.bfloat16).reshape(blocks * slots, -1)


def return_rows(taken, rows):
    blocks, slots, tokens = taken.shape
    placed = jnp.einsum(
        "bct,bcd->btd",
        taken,
        rows.reshape(blocks, slots, -1),
        preferred_element_type=jnp.float32,
    )
    return placed.astype(jnp.bfloat16).reshape(blocks * tokens, -1)


def gather_all(rows):
    return lax.all_gather(rows, ("dp", "expert"), axis=0, tiled=True)


def scatter_all(rows):
    return lax.psum_scatter(rows, ("dp", "expert"), scatter_dimension=0, tiled=True)


def dispatch(rows):
    return lax.all_to_all(rows, "expert", split_axis=0, concat_axis=0, tiled=True)


def collect(rows):
    return lax.all_to_all(rows, "expert", split_axis=0, concat_axis=0, tiled=True)


def spread_rows(rows):
    return lax.all_gather(rows, "dp", axis=0, tiled=True)


def sum_rows(terms):
    return lax.psum_scatter(
        terms.astype(jnp.bfloat16), "dp", scatter_dimension=0, tiled=True
    ).astype(jnp.float32)


def send_rows(send_table, rows):
    return jnp.einsum(
        "ect,td->ecd", send_table.astype(jnp.bfloat16), rows, preferred_element_type=jnp.float32
    ).astype(jnp.bfloat16)


def per_device(
    tokens,
    cotangent,
    attention_routes,
    feedforward_routes,
    prefix_length,
    gain_attention,
    gain_feedforward,
    keyvalue_weight,
    router_weight,
    query_weight,
    output_weight,
    gate_weight,
    up_weight,
    down_weight,
):
    my_index = lax.axis_index("expert")
    group_size = lax.axis_size("expert")
    inputs = tokens[0].astype(jnp.float32)
    tok_rows = inputs.shape[0]
    model_width = inputs.shape[1]
    seq_total = tok_rows * group_size
    slot_count = 5 * 2 * tok_rows // (4 * group_size)
    query_width = HEADS * HEAD_DIM
    scaling = HEAD_DIM ** (-0.5)
    keyvalue_full, router_full, query_full, output_full = (
        lax.all_gather(keyvalue_weight, "dp", axis=0, tiled=True),
        lax.all_gather(router_weight, "dp", axis=0, tiled=True),
        lax.all_gather(query_weight[0], "dp", axis=0, tiled=True),
        lax.all_gather(output_weight[0], "dp", axis=0, tiled=True),
    )
    every_route = lax.all_gather(feedforward_routes[0], "dp", axis=0, tiled=True)
    cot_everyone = gather_all(cotangent[0])
    attention_cols = router_full[:, :group_size]
    feedforward_cols = router_full[:, group_size:]
    normed_attention, unit_attention, factor_attention = norm_parts(inputs, gain_attention)
    attention_in = normed_attention.astype(jnp.bfloat16)
    keyvalue_rows = jnp.dot(attention_in, keyvalue_full, preferred_element_type=jnp.float32).astype(
        jnp.bfloat16
    )
    keyvalue_seq = lax.all_gather(keyvalue_rows, "expert", axis=0, tiled=True)
    key_rows = keyvalue_seq[:, :query_width].reshape(seq_total, HEADS, HEAD_DIM)
    value_rows = keyvalue_seq[:, query_width:].reshape(seq_total, HEADS, HEAD_DIM)
    attend_table, attend_places, attend_matches = route_plan(
        attention_routes[0], my_index, group_size, tok_rows, slot_count
    )
    attend_logits = jnp.dot(attention_in, attention_cols, preferred_element_type=jnp.float32)
    attend_weights, attend_gate = pair_gates(attend_logits, attend_matches)
    arrived = dispatch(send_rows(attend_table, attention_in)).reshape(-1, model_width)
    queries = jnp.dot(arrived, query_full, preferred_element_type=jnp.float32).astype(jnp.bfloat16)
    queries = queries.reshape(-1, HEADS, HEAD_DIM)
    key_places = jnp.arange(seq_total, dtype=jnp.int32)
    allowed = (key_places[None, :] <= attend_places[:, None]) | (
        key_places[None, :] < prefix_length[0]
    )
    scores = (
        jnp.einsum("rhd,khd->hrk", queries, key_rows, preferred_element_type=jnp.float32) * scaling
    )
    scores = jnp.where(allowed[None], scores, NEG)
    row_max = jnp.max(scores, axis=2, keepdims=True)
    exponent = jnp.exp(scores - row_max)
    row_total = jnp.sum(exponent, axis=2, keepdims=True)
    log_total = row_max + jnp.log(row_total)
    attention_low = (exponent / row_total).astype(jnp.bfloat16)
    mixture = jnp.einsum(
        "hrk,khd->rhd", attention_low, value_rows, preferred_element_type=jnp.float32
    )
    mixture = mixture.astype(jnp.bfloat16).reshape(-1, query_width)
    attend_branch = jnp.dot(mixture, output_full, preferred_element_type=jnp.float32).astype(
        jnp.bfloat16
    )
    attend_returned = collect(attend_branch.reshape(group_size, slot_count, model_width))
    hidden = inputs + merge_back(attend_table, attend_gate, attend_returned)
    normed_feed, unit_feed, factor_feed = norm_parts(hidden, gain_feedforward)
    feed_in = normed_feed.astype(jnp.bfloat16)
    feed_ids = lax.dynamic_slice_in_dim(
        feedforward_routes[0], my_index * tok_rows, tok_rows, 0
    )
    feed_matches = expert_matches(feed_ids, group_size)
    feed_logits = jnp.dot(feed_in, feedforward_cols, preferred_element_type=jnp.float32)
    feed_weights, feed_gate = pair_gates(feed_logits, feed_matches)
    everyone = gather_all(feed_in)
    feed_taken, feed_pairs = expert_table(every_route, my_index, group_size, tok_rows, slot_count)
    pick = functools.partial(pick_rows, feed_taken)
    feed_rows = pick(everyone)
    cot_rows = pick(cot_everyone)
    row_logits = jnp.dot(feed_rows, feedforward_cols, preferred_element_type=jnp.float32)
    row_gate = own_gate(row_logits, feed_pairs, my_index)
    pre_gate = lax.dot_general(feed_rows, gate_weight[0], ACROSS, preferred_element_type=jnp.float32)
    pre_up = lax.dot_general(feed_rows, up_weight[0], ACROSS, preferred_element_type=jnp.float32)
    sigmoid_gate = jax.nn.sigmoid(pre_gate)
    act = pre_gate * sigmoid_gate * pre_up
    act_low = act.astype(jnp.bfloat16)
    act_scaled = (act * row_gate).astype(jnp.bfloat16)
    act_grad = lax.dot_general(cot_rows, down_weight[0], ACROSS, preferred_element_type=jnp.float32)
    slot_dgate = jnp.sum(act_low.astype(jnp.float32) * act_grad, axis=1)
    act_grad = act_grad * row_gate
    dgate_low = (act_grad * pre_up * sigmoid_gate * (1.0 + pre_gate * (1.0 - sigmoid_gate))).astype(
        jnp.bfloat16
    )
    dup_low = (act_grad * pre_gate * sigmoid_gate).astype(jnp.bfloat16)
    feed_dx = (
        jnp.dot(dgate_low, gate_weight[0], preferred_element_type=jnp.float32)
        + jnp.dot(dup_low, up_weight[0], preferred_element_type=jnp.float32)
    ).astype(jnp.bfloat16)
    feed_branch = jnp.dot(act_scaled, down_weight[0], preferred_element_type=jnp.float32).astype(
        jnp.bfloat16
    )
    grad_gate = lax.dot_general(dgate_low, feed_rows, DOWNWARD, preferred_element_type=jnp.float32)
    grad_up = lax.dot_general(dup_low, feed_rows, DOWNWARD, preferred_element_type=jnp.float32)
    grad_down = lax.dot_general(act_scaled, cot_rows, DOWNWARD, preferred_element_type=jnp.float32)
    token_dgate = jnp.einsum(
        "bct,bc->bt",
        feed_taken.astype(jnp.float32),
        slot_dgate.reshape(-1, slot_count),
        precision=HIGH,
    ).reshape(-1, 1)
    own_column = (jnp.arange(group_size) == my_index).astype(jnp.float32)[None]
    feed_dgate = scatter_all(token_dgate * own_column)
    feed_home = scatter_all(return_rows(feed_taken, feed_dx)).astype(jnp.float32)
    feed_sum = scatter_all(return_rows(feed_taken, feed_branch)).astype(jnp.float32)
    layer_output = hidden + feed_sum
    gradient = cotangent[0].astype(jnp.float32)
    feed_dlogits = gates_back(feed_dgate, feed_weights, feed_matches)
    feed_dnorm = feed_home + jnp.dot(
        feed_dlogits, feedforward_cols.astype(jnp.float32).T, precision=HIGH
    )
    grad_gain_feed = jnp.sum(feed_dnorm * unit_feed, axis=0)
    hidden_grad = gradient + norm_back(feed_dnorm, gain_feedforward, unit_feed, factor_feed)
    attend_cot, attend_dgate = branch_cotangent(
        attend_table, attend_gate, attend_returned, hidden_grad
    )
    attend_dlogits = gates_back(attend_dgate, attend_weights, attend_matches)
    attend_cot_rows = dispatch(attend_cot).reshape(-1, model_width)
    dmixture = lax.dot_general(
        attend_cot_rows, output_full, ACROSS, preferred_element_type=jnp.float32
    )
    dmixture = dmixture.astype(jnp.bfloat16).reshape(-1, HEADS, HEAD_DIM)
    grad_projection = lax.dot_general(
        mixture, attend_cot_rows, DOWNWARD, preferred_element_type=jnp.float32
    )
    scores_again = (
        jnp.einsum("rhd,khd->hrk", queries, key_rows, preferred_element_type=jnp.float32) * scaling
    )
    attention = jnp.where(allowed[None], jnp.exp(scores_again - log_total), 0.0)
    attention_again = attention.astype(jnp.bfloat16)
    dattention = jnp.einsum(
        "rhd,khd->hrk", dmixture, value_rows, preferred_element_type=jnp.float32
    )
    row_dot = jnp.sum(attention * dattention, axis=2, keepdims=True)
    dscores = (attention * (dattention - row_dot)).astype(jnp.bfloat16)
    dqueries = (
        jnp.einsum("hrk,khd->rhd", dscores, key_rows, preferred_element_type=jnp.float32) * scaling
    )
    dqueries = dqueries.astype(jnp.bfloat16).reshape(-1, query_width)
    dkeys = (
        jnp.einsum("hrk,rhd->khd", dscores, queries, preferred_element_type=jnp.float32) * scaling
    )
    dvalues = jnp.einsum(
        "hrk,rhd->khd", attention_again, dmixture, preferred_element_type=jnp.float32
    )
    grad_query = lax.dot_general(arrived, dqueries, DOWNWARD, preferred_element_type=jnp.float32)
    attend_dx = lax.dot_general(dqueries, query_full, ACROSS, preferred_element_type=jnp.float32)
    keyvalue_terms = jnp.concatenate(
        [dkeys.reshape(seq_total, query_width), dvalues.reshape(seq_total, query_width)], axis=1
    ).reshape(group_size, tok_rows, 2 * query_width)
    attend_home, keyvalue_home = (
        lax.all_to_all(
            attend_dx.reshape(group_size, slot_count, model_width).astype(jnp.bfloat16),
            "expert",
            split_axis=0,
            concat_axis=0,
            tiled=True,
        ).astype(jnp.float32),
        lax.all_to_all(
            keyvalue_terms.astype(jnp.bfloat16), "expert", split_axis=0, concat_axis=0, tiled=True
        ).astype(keyvalue_terms.dtype),
    )
    dkeyvalue = jnp.sum(keyvalue_home, axis=0).astype(jnp.bfloat16)
    attend_dnorm = (
        jnp.einsum("ect,ecd->td", attend_table, attend_home, precision=HIGH)
        + lax.dot_general(dkeyvalue, keyvalue_full, ACROSS, preferred_element_type=jnp.float32)
        + jnp.dot(attend_dlogits, attention_cols.astype(jnp.float32).T, precision=HIGH)
    )
    grad_keyvalue = lax.dot_general(
        attention_in, dkeyvalue, DOWNWARD, preferred_element_type=jnp.float32
    )
    grad_router = jnp.concatenate(
        [
            jnp.dot(attention_in.astype(jnp.float32).T, attend_dlogits, precision=HIGH),
            jnp.dot(feed_in.astype(jnp.float32).T, feed_dlogits, precision=HIGH),
        ],
        axis=1,
    )
    grad_gain_attend = jnp.sum(attend_dnorm * unit_attention, axis=0)
    grad_tokens = hidden_grad + norm_back(
        attend_dnorm, gain_attention, unit_attention, factor_attention
    )
    reduced = (
        lax.psum_scatter(
            grad_keyvalue.astype(jnp.bfloat16), "dp", scatter_dimension=0, tiled=True
        ).astype(jnp.float32),
        lax.psum_scatter(
            grad_router.astype(jnp.bfloat16), "dp", scatter_dimension=0, tiled=True
        ).astype(jnp.float32),
        lax.psum_scatter(
            grad_query.astype(jnp.bfloat16), "dp", scatter_dimension=0, tiled=True
        ).astype(jnp.float32),
        lax.psum_scatter(
            grad_projection.astype(jnp.bfloat16), "dp", scatter_dimension=0, tiled=True
        ).astype(jnp.float32),
        lax.psum_scatter(
            grad_gain_attend.astype(jnp.bfloat16), "dp", scatter_dimension=0, tiled=True
        ).astype(jnp.float32),
        lax.psum_scatter(
            grad_gain_feed.astype(jnp.bfloat16), "dp", scatter_dimension=0, tiled=True
        ).astype(jnp.float32),
    )
    shared = (
        lax.psum(reduced[0].astype(jnp.bfloat16), "expert").astype(jnp.float32),
        lax.psum(reduced[1].astype(jnp.bfloat16), "expert").astype(jnp.float32),
        lax.psum(reduced[4].astype(jnp.bfloat16), "expert").astype(jnp.float32),
        lax.psum(reduced[5].astype(jnp.bfloat16), "expert").astype(jnp.float32),
    )
    return (
        layer_output.astype(jnp.bfloat16)[None],
        grad_tokens[None],
        shared[2],
        shared[3],
        shared[0],
        shared[1],
        reduced[2][None],
        reduced[3][None],
        grad_gate[None],
        grad_up[None],
        grad_down[None],
    )


MESH = pl.DeviceIdType.MESH
CHIPS_Z = 4
TURNS = ((3, 2, 1, 0), (3, 0, 2, 1), (0, 3, 1, 2), (0, 1, 2, 3))


class Place:
    def __init__(self):
        self.dp, self.expert = lax.axis_index("dp"), lax.axis_index("expert")
        self.at = {
            "z": self.dp // 2,
            "y": self.dp % 2,
            "x": self.expert // 2,
            "c": self.expert % 2,
        }

    def across(self, axis):
        back = 1 - 2 * self.at[axis]
        if axis == "c":
            return (self.dp, self.expert + back)
        if axis == "x":
            return (self.dp, self.expert + 2 * back)
        return (self.dp + back, self.expert)

    def along(self, step):
        return (self.dp + 2 * step, self.expert)

    def block(self, whose, z, flips):
        at = {a: self.at[a] + flips.get(a, 0) * (1 - 2 * self.at[a]) for a in "xyc"}
        dp, expert = z * 2 + at["y"], at["x"] * 2 + at["c"]
        return {"all": dp * 4 + expert, "dp": dp, "expert": expert}[whose]


def enter(place, axes, others=()):
    barrier, count = pltpu.get_barrier_semaphore(), 0
    for device, condition in others:

        def greet(device=device):
            pl.semaphore_signal(barrier, inc=1, device_id=device, device_id_type=MESH)

        on(condition, greet)
        count = count + (1 if condition is None else condition.astype(jnp.int32))
    for axis in axes:
        if axis != "z":
            pl.semaphore_signal(
                barrier, inc=1, device_id=place.across(axis), device_id_type=MESH
            )
            count += 1
    if "z" in axes:
        z = place.at["z"]
        for step, there in ((-1, z > 0), (1, z < CHIPS_Z - 1)):

            @pl.when(there)
            def _(step=step):
                pl.semaphore_signal(
                    barrier, inc=1, device_id=place.along(step), device_id_type=MESH
                )

            count = count + there.astype(jnp.int32)
    pl.semaphore_wait(barrier, count)


def on(condition, action):
    if condition is None:
        action()
    else:
        pl.when(condition)(action)


def both(a, b):
    return b if a is None else a if b is None else a & b


class Post:
    def __init__(self, sems, place):
        self.sems, self.place, self.sent = sems, place, []

    def send(self, source, target, arrival, device, condition=None):
        number = len(self.sent)

        def copy():
            return pltpu.make_async_remote_copy(
                src_ref=source,
                dst_ref=target,
                send_sem=self.sems.at[number],
                recv_sem=arrival,
                device_id=device,
                device_id_type=MESH,
            )

        self.sent.append((condition, copy))
        on(condition, lambda: copy().start())

    def arrived(self, target, arrival):
        pltpu.make_async_remote_copy(
            src_ref=target,
            dst_ref=target,
            send_sem=self.sems.at[0],
            recv_sem=arrival,
            device_id=self.place.across("c"),
            device_id_type=MESH,
        ).wait_recv()

    def close(self):
        for condition, copy in self.sent:
            on(condition, lambda copy=copy: copy().wait_send())


FLIPS = {"x": 4, "y": 2, "c": 1}


def gather_plan(jobs, place, post, sources, targets, arrive_sems, own_sems):
    z_here = place.at["z"]
    line = 0
    waves, owns, starts = {}, [], []
    for j, (whose, rows, pieces) in enumerate(jobs):
        own = pltpu.make_async_copy(
            sources[j],
            targets[j].at[pl.ds(place.block(whose, z_here, {}) * rows, rows)],
            own_sems.at[j],
        )
        owns.append(own)
        begin = [own.start]
        for first, length, order in pieces:
            def part(z, flips, j=j, whose=whose, rows=rows, first=first, length=length):
                at = place.block(whose, z, flips) * rows + first
                return targets[j].at[pl.ds(at, length)]

            def mark(z, flips, line=line):
                return arrive_sems.at[line, z * 8 + sum(FLIPS[a] * v for a, v in flips.items())]

            def hand_on(source, z, flips, depth, side, wave, condition, order=order, part=part, mark=mark):
                for axis in order[max(depth, 0) :]:
                    if axis == "z" and (depth < 0 or order[depth] != "z"):
                        for step in (1, -1):
                            there = (z_here < CHIPS_Z - 1) if step > 0 else (z_here > 0)
                            post.send(source, part(z, flips), mark(z, flips), place.along(step), both(condition, there))
                    elif axis == "z":
                        there = (z_here < CHIPS_Z - 1) if side > 0 else (z_here > 0)
                        post.send(source, part(z, flips), mark(z, flips), place.along(side), both(condition, there))
                    elif depth < 0 or axis != order[depth]:
                        seen = dict(flips)
                        seen[axis] = 1
                        post.send(source, part(z, flips), mark(z, seen), place.across(axis), condition)

            def come(z, flips, depth, side, hops, wave, condition, order=order, part=part, mark=mark, hand_on=hand_on):
                def act():
                    on(condition, lambda: post.arrived(part(z, flips), mark(z, flips)))
                    hand_on(part(z, flips), z, flips, depth, side, wave, condition)

                waves.setdefault(wave, []).append(act)
                spread(z, flips, depth, side, hops, wave, condition, order, come)

            begin.append(
                lambda hand_on=hand_on, j=j, first=first, length=length: hand_on(
                    sources[j].at[pl.ds(first, length)], z_here, {}, -1, 0, 0, None
                )
            )
            spread(z_here, {}, -1, 0, 0, 0, None, order, come)
            line += 1
        starts.append(begin)
    return starts, waves, owns


def gather_kernel(jobs, axes, filler, *refs):
    count = len(jobs)
    sources, given, refs = refs[:count], refs[count : count + filler.operands], refs[count + filler.operands :]
    targets, made, refs = refs[:count], refs[count : count + filler.results], refs[count + filler.results :]
    send_sems, arrive_sems, own_sems = refs[:3]
    own = refs[3:]
    place = Place()
    enter(place, axes)
    post = Post(send_sems, place)
    starts, waves, owns = gather_plan(jobs, place, post, sources, targets, arrive_sems, own_sems)
    for act in sum(starts, []):
        act()
    steps, done = filler.start(given, made, own), 0
    for number, wave in enumerate(sorted(waves)):
        share = steps * (number + 1) // len(waves)
        filler.run(given, made, own, done, share)
        done = share
        for act in waves[wave]:
            act()
    for copy in owns:
        copy.wait()
    filler.end(given, made, own)
    post.close()


def spread(z, flips, depth, side, hops, wave, condition, order, come):
    z_here = lax.axis_index("dp") // 2
    for later in range(max(depth, 0), len(order)):
        axis = order[later]
        if axis == "z":
            if depth >= 0 and order[depth] == "z":
                if hops < CHIPS_Z - 1:
                    far = hops + 1
                    there = (z_here >= far) if side > 0 else (z_here + far < CHIPS_Z)
                    come(z_here - side * far, flips, later, side, far, wave + 1, there)
            else:
                for step in (1, -1):
                    there = (z_here >= 1) if step > 0 else (z_here + 1 < CHIPS_Z)
                    come(z_here - step, flips, later, step, 1, wave + 1, both(condition, there))
        elif later > depth:
            seen = dict(flips)
            seen[axis] = 1
            come(z, seen, later, 0, 0, wave + 1, condition)


class Nothing:
    operands = results = rooms = 0
    turns = 12
    shapes, scratch = [], []

    def start(self, given, made, own):
        return 0

    def run(self, given, made, own, first, last):
        pass

    def end(self, given, made, own):
        pass


def gather(jobs, collective_id, name, filler=Nothing(), operands=()):
    arrays = [rows for rows, _, _ in jobs]
    sizes = {"all": 32, "dp": 8, "expert": 4}
    plan = tuple((whose, rows.shape[0], pieces) for rows, whose, pieces in jobs)
    axes = "".join(a for a in "cxyz" if any(a in order for _, _, ps in plan for _, _, order in ps))
    lines = sum(len(ps) for _, _, ps in plan)
    hbm = pl.BlockSpec(memory_space=pltpu.HBM)
    return pl.pallas_call(
        functools.partial(gather_kernel, plan, axes, filler),
        out_shape=[
            jax.ShapeDtypeStruct((sizes[whose] * r.shape[0], r.shape[1]), r.dtype)
            for r, whose, _ in jobs
        ]
        + filler.shapes,
        in_specs=[hbm] * (len(jobs) + len(operands)),
        out_specs=[hbm] * (len(jobs) + filler.results),
        scratch_shapes=[
            pltpu.SemaphoreType.DMA((110 * lines,)),
            pltpu.SemaphoreType.DMA((lines, 32)),
            pltpu.SemaphoreType.DMA((len(jobs),)),
        ]
        + filler.scratch,
        compiler_params=pltpu.CompilerParams(
            collective_id=collective_id, has_side_effects=True, vmem_limit_bytes=48 * 2**20
        ),
        name=name,
    )(*arrays, *operands)


def add_into(target, terms, length):
    @pl.loop(0, length // 16)
    def _(r):
        at = pl.ds(pl.multiple_of(r * 16, 16), 16)
        total = target[at, :].astype(jnp.float32)
        for term in terms:
            total = total + term[at, :].astype(jnp.float32)
        target[at, :] = total.astype(jnp.bfloat16)


def scatter_rooms(rows, width, order):
    steps, turns = len(order.replace("z", "")), CHIPS_Z if "z" in order else 1
    blocks = [turns * 2 ** (steps - 1)]
    blocks += [turns * 2 ** (steps - 1 - stage) for stage in range(steps)]
    if "z" in order:
        blocks.append(CHIPS_Z + 1)
    return [pltpu.VMEM((n, rows, width), jnp.bfloat16) for n in blocks]


def scatter_sems(order, pieces):
    steps, turns = len(order.replace("z", "")), CHIPS_Z if "z" in order else 1
    return [
        pltpu.SemaphoreType.DMA((turns * 2 ** (steps - 1),)),
        pltpu.SemaphoreType.DMA((pieces, steps, turns * 2 ** (steps - 1))),
        pltpu.SemaphoreType.DMA((pieces, CHIPS_Z + 1)),
    ]


def scatter_plan(whose, rows, pieces, place, post, source, rooms, sems):
    flat = [order.replace("z", "") for _, _, order in pieces]
    steps = len(flat[0])
    lined = "z" in pieces[0][2]
    turns = CHIPS_Z if lined else 1
    acc, bins, line = rooms[0], rooms[1 : 1 + steps], rooms[-1]
    load_sems, bin_sems, line_sems = sems
    z_here = place.at["z"]
    if lined:
        turn = [
            sum((z_here == z).astype(jnp.int32) * seq[k] for z, seq in enumerate(TURNS))
            for k in range(CHIPS_Z)
        ]
    else:
        turn = [z_here]
    slot_z = lambda k: turn[k] if lined else 0
    keep = 2 ** (steps - 1)
    names = sorted(flat[0][1:])
    loads = {}
    for k in range(turns):
        for n in reversed(range(keep)):
            flips = {a: (n >> i) & 1 for i, a in enumerate(names)}
            at = slot_z(k) * keep + n
            loads[k, n] = pltpu.make_async_copy(
                source.at[pl.ds(place.block(whose, turn[k], flips) * rows, rows)],
                acc.at[at],
                load_sems.at[at],
            )
    loaded = set()

    def mine(p, ref):
        first, length, _ = pieces[p]
        return ref.at[pl.ds(first, length)]

    def code_after(p, stage, flips):
        return sum(flips.get(a, 0) << i for i, a in enumerate(flat[p][stage + 1 :]))

    def gathered(p, k, stage, flips):
        n = sum(flips.get(a, 0) << i for i, a in enumerate(names))
        if (k, n) not in loaded:
            loads[k, n].wait()
            loaded.add((k, n))
        terms = []
        for before in range(stage):
            at = slot_z(k) * 2 ** (steps - 1 - before) + code_after(p, before, flips)
            ref = mine(p, bins[before].at[at])
            post.arrived(ref, bin_sems.at[p, before, at])
            terms.append(ref)
        block = mine(p, acc.at[slot_z(k) * keep + n])
        add_into(block, terms, pieces[p][1])
        return block

    def leave(k, stage):
        for code in reversed(range(2 ** (steps - 1 - stage))):
            for p in range(len(pieces)):
                flips = {a: (code >> i) & 1 for i, a in enumerate(flat[p][stage + 1 :])}
                flips[flat[p][stage]] = 1
                if stage == 0:
                    at = place.block(whose, turn[k], flips) * rows + pieces[p][0]
                    block = source.at[pl.ds(at, pieces[p][1])]
                else:
                    block = gathered(p, k, stage, flips)
                at = slot_z(k) * 2 ** (steps - 1 - stage) + code
                post.send(
                    block,
                    mine(p, bins[stage].at[at]),
                    bin_sems.at[p, stage, at],
                    place.across(flat[p][stage]),
                )

    def settle(k):
        for p in range(len(pieces)):
            block = gathered(p, k, steps, {})
            if not lined or k == turns - 1:
                continue
            t = turn[k]
            right = t > z_here

            def pass_on(p=p, t=t, block=block):
                ref = mine(p, line.at[t])
                post.arrived(ref, line_sems.at[p, t])
                add_into(block, [ref], pieces[p][1])

            pl.when((right & (z_here > 0)) | (~right & (z_here < CHIPS_Z - 1)))(pass_on)
            slot = jnp.where(t == z_here - 1, CHIPS_Z, t)
            post.send(
                block,
                mine(p, line.at[slot]),
                line_sems.at[p, slot],
                place.along(jnp.where(right, 1, -1)),
            )

    def finish(p):
        block = mine(p, acc.at[z_here * keep if lined else 0])
        if lined:
            for slot, there in ((z_here, z_here > 0), (CHIPS_Z, z_here < CHIPS_Z - 1)):

                def last(slot=slot):
                    ref = mine(p, line.at[slot])
                    post.arrived(ref, line_sems.at[p, slot])
                    add_into(block, [ref], pieces[p][1])

                pl.when(there)(last)
        return block

    works = [(-1, lambda k=k: leave(k, 0)) for k in range(turns)]
    for time in range(turns + steps):
        for stage in range(1, steps + 1):
            k = time - stage + 1
            if 0 <= k < turns:
                act = settle if stage == steps else lambda k, stage=stage: leave(k, stage)
                works.append((time, lambda k=k, act=act: act(k)))
    return list(loads.values()), works, finish


def sends_of(order, pieces):
    steps, turns = len(order.replace("z", "")), CHIPS_Z if "z" in order else 1
    return pieces * (turns * 2**steps + 4)


def widen(target, block, length):
    @pl.loop(0, length // 16)
    def _(r):
        at = pl.ds(pl.multiple_of(r * 16, 16), 16)
        target[at, :] = block[at, :].astype(jnp.float32)


def scatter_kernel(whose, rows, pieces, columns, filler, source, *refs):
    source = source.at[:, pl.ds(*columns)]
    given, refs = refs[: filler.operands], refs[filler.operands :]
    result, made, refs = refs[0], refs[1 : 1 + filler.results], refs[1 + filler.results :]
    rooms, refs = refs[: len(refs) - 4 - filler.rooms], refs[len(refs) - 4 - filler.rooms :]
    send_sems, sems, own = refs[0], refs[1:4], refs[4:]
    place = Place()
    post = Post(send_sems, place)
    loads, works, finish = scatter_plan(whose, rows, pieces, place, post, source, rooms, sems)
    for load in loads:
        load.start()
    enter(place, "".join(a for a in "cxyz" if a in pieces[0][2]))
    steps = filler.start(given, made, own)
    slots = [number for number, (time, _) in enumerate(works) if time >= 0]
    slots = slots[:: -(-len(slots) // filler.turns)]
    done = 0
    for number, (_, act) in enumerate(works):
        act()
        if number in slots:
            share = steps * (slots.index(number) + 1) // len(slots)
            filler.run(given, made, own, done, share)
            done = share
    for p in range(len(pieces)):
        first, length, _ = pieces[p]
        widen(result.at[pl.ds(first, length)], finish(p), length)
    filler.end(given, made, own)
    post.close()


class WeightGrads(Nothing):
    operands, results, rooms = 4, 3, 6
    TILE, CHUNK = 256, 512

    def __init__(self, rows, padded, hidden, width):
        self.chunks = rows // self.CHUNK
        self.each = padded // self.TILE
        self.short = hidden - (self.each - 1) * self.TILE
        self.tiles = (2 * self.each, self.each)
        self.shapes = [jax.ShapeDtypeStruct((hidden, width), jnp.float32)] * 3
        self.scratch = [
            pltpu.VMEM((2, self.CHUNK, self.TILE), jnp.bfloat16),
            pltpu.VMEM((2, self.CHUNK, width), jnp.bfloat16),
            pltpu.VMEM((self.TILE, width), jnp.float32),
            pltpu.VMEM((self.TILE, width), jnp.float32),
            pltpu.SemaphoreType.DMA((2, 2)),
            pltpu.SemaphoreType.DMA((2,)),
        ]

    def copies(self, given, own, step, second):
        tile, chunk = step // self.chunks - (self.tiles[0] if second else 0), step % self.chunks
        slot = step % 2
        rows = pl.ds(pl.multiple_of(chunk * self.CHUNK, self.CHUNK), self.CHUNK)
        cols = pl.ds(pl.multiple_of(tile * self.TILE, self.TILE), self.TILE)
        left, right = given[2 * second], given[2 * second + 1]
        return [
            pltpu.make_async_copy(left.at[rows, cols], own[0].at[slot], own[4].at[slot, 0]),
            pltpu.make_async_copy(right.at[rows], own[1].at[slot], own[4].at[slot, 1]),
        ]

    def fetch(self, given, own, step, start):
        edge = self.tiles[0] * self.chunks
        for second in (0, 1):

            @pl.when((step >= edge) if second else (step < edge))
            def _(second=second):
                for copy in self.copies(given, own, step, second):
                    copy.start() if start else copy.wait()

    def put(self, made, own, tile, parity, start):
        row = (tile % self.each) * self.TILE
        for result in range(3):
            for last in (0, 1):
                length = self.short if last else self.TILE
                at_end = (tile % self.each) == self.each - 1

                @pl.when((tile // self.each == result) & (at_end if last else ~at_end))
                def _(result=result, length=length):
                    copy = pltpu.make_async_copy(
                        own[2 + parity].at[pl.ds(0, length)],
                        made[result].at[pl.ds(pl.multiple_of(row, self.TILE), length)],
                        own[5].at[parity],
                    )
                    copy.start() if start else copy.wait()

    def start(self, given, made, own):
        self.fetch(given, own, jnp.int32(0), True)
        return sum(self.tiles) * self.chunks

    def run(self, given, made, own, first, last):
        total = sum(self.tiles) * self.chunks

        @pl.loop(first, last)
        def _(step):
            tile, chunk = step // self.chunks, step % self.chunks

            @pl.when(step + 1 < total)
            def _():
                self.fetch(given, own, step + 1, True)

            self.fetch(given, own, step, False)
            part = lax.dot_general(
                own[0][step % 2], own[1][step % 2], DOWNWARD, preferred_element_type=jnp.float32
            )
            for parity in (0, 1):

                @pl.when(tile % 2 == parity)
                def _(parity=parity):
                    acc = own[2 + parity]

                    @pl.when(chunk == 0)
                    def _():
                        @pl.when(tile >= 2)
                        def _():
                            self.put(made, own, tile - 2, parity, False)

                        acc[...] = part

                    @pl.when(chunk > 0)
                    def _():
                        acc[...] += part

                    @pl.when(chunk == self.chunks - 1)
                    def _():
                        self.put(made, own, tile, parity, True)

    def end(self, given, made, own):
        tiles = sum(self.tiles)
        for tile in (tiles - 2, tiles - 1):
            self.put(made, own, jnp.int32(tile), tile % 2, False)


class LowGrad(Nothing):
    operands, results, rooms = 2, 1, 5
    TILE = 256

    def __init__(self, rows, left, width, turns):
        self.tiles, self.width, self.turns = left // self.TILE, width, turns
        low = jnp.bfloat16
        self.shapes = [jax.ShapeDtypeStruct((left, width), low)]
        self.scratch = [
            pltpu.VMEM((2, rows, self.TILE), low),
            pltpu.VMEM((rows, width), low),
            pltpu.VMEM((2, self.TILE, width), low),
            pltpu.SemaphoreType.DMA((3,)),
            pltpu.SemaphoreType.DMA((2,)),
        ]

    def left(self, given, own, tile):
        at = pl.ds(pl.multiple_of(tile * self.TILE, self.TILE), self.TILE)
        return pltpu.make_async_copy(given[0].at[:, at], own[0].at[tile % 2], own[3].at[tile % 2])

    def right(self, given, own):
        return pltpu.make_async_copy(given[1], own[1], own[3].at[2])

    def put(self, made, own, tile):
        rows = pl.ds(pl.multiple_of(tile * self.TILE, self.TILE), self.TILE)
        return pltpu.make_async_copy(own[2].at[tile % 2], made[0].at[rows], own[4].at[tile % 2])

    def start(self, given, made, own):
        self.right(given, own).start()
        self.left(given, own, jnp.int32(0)).start()
        return self.tiles

    def run(self, given, made, own, first, last):
        if first == last:
            return
        if first == 0:
            self.right(given, own).wait()

        @pl.loop(first, last)
        def _(tile):
            slot = tile % 2

            @pl.when(tile + 1 < self.tiles)
            def _():
                self.left(given, own, tile + 1).start()

            self.left(given, own, tile).wait()

            @pl.when(tile >= 2)
            def _():
                self.put(made, own, tile - 2).wait()

            half = self.width // 2
            for part in (0, 1):
                cols = slice(part * half, (part + 1) * half)
                own[2][slot, :, cols] = lax.dot_general(
                    own[0][slot], own[1][:, cols], DOWNWARD, preferred_element_type=jnp.float32
                ).astype(jnp.bfloat16)
            self.put(made, own, tile).start()

    def end(self, given, made, own):
        for tile in (self.tiles - 2, self.tiles - 1):
            self.put(made, own, jnp.int32(tile)).wait()


class RowGrads(Nothing):
    operands, results, rooms = 3, 1, 7
    TILE, turns = 256, 4

    def __init__(self, rows, depth, width):
        self.tiles, self.width = width // self.TILE, width
        low = jnp.bfloat16
        self.shapes = [jax.ShapeDtypeStruct((rows, width + 128), low)]
        self.scratch = [
            pltpu.VMEM((rows, depth), low),
            pltpu.VMEM((2, self.TILE, depth), low),
            pltpu.VMEM((2, rows, self.TILE), low),
            pltpu.VMEM((rows, 128), jnp.float32),
            pltpu.VMEM((rows, 128), low),
            pltpu.SemaphoreType.DMA((4,)),
            pltpu.SemaphoreType.DMA((3,)),
        ]

    def whole(self, given, own):
        return [
            pltpu.make_async_copy(given[0], own[0], own[5].at[2]),
            pltpu.make_async_copy(given[2], own[3], own[5].at[3]),
        ]

    def right(self, given, own, tile):
        at = pl.ds(pl.multiple_of(tile * self.TILE, self.TILE), self.TILE)
        return pltpu.make_async_copy(given[1].at[at], own[1].at[tile % 2], own[5].at[tile % 2])

    def put(self, made, own, tile):
        at = pl.ds(pl.multiple_of(tile * self.TILE, self.TILE), self.TILE)
        return pltpu.make_async_copy(own[2].at[tile % 2], made[0].at[:, at], own[6].at[tile % 2])

    def extra(self, made, own):
        return pltpu.make_async_copy(own[4], made[0].at[:, pl.ds(self.width, 128)], own[6].at[2])

    def start(self, given, made, own):
        for copy in self.whole(given, own):
            copy.start()
        self.right(given, own, jnp.int32(0)).start()
        return self.tiles

    def run(self, given, made, own, first, last):
        if first == last:
            return
        if first == 0:
            for copy in self.whole(given, own):
                copy.wait()
            own[4][...] = own[3][...].astype(jnp.bfloat16)
            self.extra(made, own).start()

        @pl.loop(first, last)
        def _(tile):
            slot = tile % 2

            @pl.when(tile + 1 < self.tiles)
            def _():
                self.right(given, own, tile + 1).start()

            self.right(given, own, tile).wait()

            @pl.when(tile >= 2)
            def _():
                self.put(made, own, tile - 2).wait()

            own[2][slot] = lax.dot_general(
                own[0][...], own[1][slot], ACROSS, preferred_element_type=jnp.float32
            ).astype(jnp.bfloat16)
            self.put(made, own, tile).start()

    def end(self, given, made, own):
        self.extra(made, own).wait()
        for tile in (self.tiles - 2, self.tiles - 1):
            self.put(made, own, jnp.int32(tile)).wait()


class InTurn(Nothing):
    def __init__(self, one, other):
        self.parts = (one, other)
        self.operands = one.operands + other.operands
        self.results = one.results + other.results
        self.rooms = one.rooms + other.rooms
        self.turns = one.turns + other.turns
        self.shapes, self.scratch = one.shapes + other.shapes, one.scratch + other.scratch

    def split(self, given, made, own):
        one = self.parts[0]
        return (
            (given[: one.operands], made[: one.results], own[: one.rooms]),
            (given[one.operands :], made[one.results :], own[one.rooms :]),
        )

    def start(self, *refs):
        self.steps = [part.start(*own) for part, own in zip(self.parts, self.split(*refs))]
        return self.parts[0].turns + self.parts[1].turns

    def run(self, given, made, own, first, last):
        edge = self.parts[0].turns
        for n, (part, refs) in enumerate(zip(self.parts, self.split(given, made, own))):
            low, high = (0, edge) if n == 0 else (edge, edge + part.turns)
            begin, end = max(first, low) - low, min(last, high) - low
            if begin < end:
                steps = self.steps[n]
                part.run(*refs, steps * begin // part.turns, steps * end // part.turns)

    def end(self, *refs):
        for part, own in zip(self.parts, self.split(*refs)):
            part.end(*own)


def scatter(array, whose, pieces, collective_id, name, filler=Nothing(), operands=(), columns=None):
    size = {"all": 32, "dp": 8, "expert": 4}[whose]
    columns = columns or (0, array.shape[1])
    rows, width = array.shape[0] // size, columns[1]
    order, count = pieces[0][2], len(pieces)
    hbm = pl.BlockSpec(memory_space=pltpu.HBM)
    out = pl.pallas_call(
        functools.partial(scatter_kernel, whose, rows, pieces, columns, filler),
        out_shape=[jax.ShapeDtypeStruct((rows, width), jnp.float32)] + filler.shapes,
        in_specs=[hbm] * (1 + len(operands)),
        out_specs=[pl.BlockSpec(memory_space=pltpu.VMEM)] + [hbm] * filler.results,
        scratch_shapes=scatter_rooms(rows, width, order)
        + [pltpu.SemaphoreType.DMA((sends_of(order, count),))]
        + scatter_sems(order, count)
        + filler.scratch,
        compiler_params=pltpu.CompilerParams(
            collective_id=collective_id, has_side_effects=True, vmem_limit_bytes=63 * 2**20
        ),
        name=name,
    )(array, *operands)
    return out if filler.results else out[0]


def sum_right_kernel(rows, pieces, columns, out_rows, out_pieces, filler, source, out_grad, *refs):
    source = source.at[:, pl.ds(*columns)]
    given, refs = refs[: filler.operands], refs[filler.operands :]
    result, output, refs = refs[0], refs[1], refs[2:]
    made, refs = refs[: filler.results], refs[filler.results :]
    count = len(scatter_rooms(rows, 128, pieces[0][2]))
    rooms, refs = refs[:count], refs[count:]
    count = len(scatter_rooms(rows, 128, out_pieces[0][2]))
    out_rooms, refs = refs[:count], refs[count:]
    dealt, send_sems, deal_sems = refs[:3]
    sems, out_sems, own = refs[3:6], refs[6:9], refs[9:]
    place = Place()
    post = Post(send_sems, place)
    z, e = place.at["z"], place.expert
    partner, moves = (e * 2 + place.at["y"], z), z != e
    loads, works, finish = scatter_plan(
        "all", rows, pieces, place, post, source, rooms, sems
    )
    out_loads, out_works, out_finish = scatter_plan(
        "dp", out_rows, out_pieces, place, post, out_grad, out_rooms, out_sems
    )
    for load in loads + out_loads:
        load.start()
    enter(place, "cxyz", [(partner, moves)])
    steps = filler.start(given, made, own)
    times = sorted({time for time, _ in works + out_works})
    turns = [time for time in times if time >= 0]
    done = 0
    for time in times:
        for plan in (out_works, works):
            for at, act in plan:
                if at == time:
                    act()
        if time >= 0:
            share = steps * (turns.index(time) + 1) // len(turns)
            filler.run(given, made, own, done, share)
            done = share
    for p in range(len(out_pieces)):
        first, length, _ = out_pieces[p]
        at = pl.ds(first, length)
        post.send(out_finish(p), dealt.at[at], deal_sems.at[p], partner, moves)
    for p in range(len(pieces)):
        first, length, _ = pieces[p]
        widen(result.at[pl.ds(first, length)], finish(p), length)
    filler.end(given, made, own)
    for p in range(len(out_pieces)):
        first, length, _ = out_pieces[p]
        at = pl.ds(first, length)

        def came(p=p, at=at, length=length):
            post.arrived(dealt.at[at], deal_sems.at[p])
            widen(output.at[at], dealt.at[at], length)

        pl.when(moves)(came)
        pl.when(~moves)(
            lambda at=at, length=length: widen(output.at[at], out_rooms[0].at[z, at], length)
        )
    post.close()


def sum_right(array, columns, pieces, out_grad, out_pieces, collective_id, filler, operands):
    rows, width = array.shape[0] // 32, columns[1]
    out_rows, out_width = out_grad.shape[0] // 8, out_grad.shape[1]
    order, out_order = pieces[0][2], out_pieces[0][2]
    hbm = pl.BlockSpec(memory_space=pltpu.HBM)
    vmem = pl.BlockSpec(memory_space=pltpu.VMEM)
    shape = jax.ShapeDtypeStruct
    sends = sends_of(order, len(pieces)) + sends_of(out_order, len(out_pieces)) + len(out_pieces)
    return pl.pallas_call(
        functools.partial(
            sum_right_kernel, rows, pieces, columns, out_rows, out_pieces, filler
        ),
        out_shape=[
            shape((rows, width), jnp.float32),
            shape((out_rows, out_width), jnp.float32),
        ]
        + filler.shapes,
        in_specs=[hbm] * (2 + len(operands)),
        out_specs=[vmem] * 2 + [hbm] * filler.results,
        scratch_shapes=scatter_rooms(rows, width, order)
        + scatter_rooms(out_rows, out_width, out_order)
        + [
            pltpu.VMEM((out_rows, out_width), jnp.bfloat16),
            pltpu.SemaphoreType.DMA((sends,)),
            pltpu.SemaphoreType.DMA((len(out_pieces),)),
        ]
        + scatter_sems(order, len(pieces))
        + scatter_sems(out_order, len(out_pieces))
        + filler.scratch,
        compiler_params=pltpu.CompilerParams(
            collective_id=collective_id, has_side_effects=True, vmem_limit_bytes=63 * 2**20
        ),
        name="sum_output_right",
    )(array, out_grad, *operands)


def sum_weights_kernel(rows, pieces, in_grad, query, keyvalue, *refs):
    count = len(scatter_rooms(rows, 128, pieces[0][2]))
    rooms = refs[:count]
    dealt, shared, send_sems, deal_sems = refs[count : count + 4]
    place = Place()
    post = Post(send_sems, place)
    z, e = place.at["z"], place.expert
    wide = query.shape[1]
    span = (in_grad.shape[1] - wide) // 2
    peers = []
    for flip_x, flip_c in ((1, 1), (1, 0), (0, 1)):
        x = place.at["x"] + flip_x * (1 - 2 * place.at["x"])
        core = place.at["c"] + flip_c * (1 - 2 * place.at["c"])
        peers.append((x * 2 + core, flip_x * 2 + flip_c))
    loads, works, finish = scatter_plan(
        "dp", rows, pieces, place, post, in_grad, rooms, refs[count + 4 :]
    )
    for load in loads:
        load.start()
    enter(place, "cxyz", [((place.dp, peers[0][0]), None)])
    for _, act in works:
        act()
    cols = lambda block: pl.ds(pl.multiple_of(block * span, span), span)
    keep = slice(wide, wide + 2 * span)
    for p in range(len(pieces)):
        first, length, _ = pieces[p]
        at = pl.ds(first, length)
        block = finish(p)
        post.send(block.at[:, keep], shared.at[2, at], deal_sems.at[p, 4], place.across("x"))
        for peer, flips in peers:
            post.send(
                block.at[:, cols(peer)],
                dealt.at[at, cols(e)],
                deal_sems.at[p, flips],
                (place.dp, peer),
            )
        post.send(block.at[:, keep], shared.at[1, at], deal_sems.at[p, 5], place.across("c"))

    def place_keys(p, flips, block):
        first, length, _ = pieces[p]
        rows_at = pl.ds(first, length)
        x = place.at["x"] + (flips // 2) * (1 - 2 * place.at["x"])
        core = place.at["c"] + (flips % 2) * (1 - 2 * place.at["c"])
        owner = x * 2 + core
        widen(keyvalue.at[rows_at, cols(owner)], block.at[:, pl.ds(0, span)], length)
        widen(
            keyvalue.at[rows_at, cols(wide // span + owner)], block.at[:, pl.ds(span, span)], length
        )

    for p in range(len(pieces)):
        first, length, _ = pieces[p]
        at = pl.ds(first, length)
        block = rooms[0].at[z, at]
        widen(query.at[at, cols(e)], block.at[:, cols(e)], length)
        place_keys(p, 0, block.at[:, keep])
        post.arrived(shared.at[1, at], deal_sems.at[p, 5])
        place_keys(p, 1, shared.at[1, at])
        post.arrived(shared.at[2, at], deal_sems.at[p, 4])
        post.send(shared.at[2, at], shared.at[3, at], deal_sems.at[p, 6], place.across("c"))
        place_keys(p, 2, shared.at[2, at])
        for peer, flips in reversed(peers):
            post.arrived(dealt.at[at, cols(peer)], deal_sems.at[p, flips])
            widen(query.at[at, cols(peer)], dealt.at[at, cols(peer)], length)
        post.arrived(shared.at[3, at], deal_sems.at[p, 6])
        place_keys(p, 3, shared.at[3, at])
    post.close()


def sum_weights(in_grad, wide, pieces, collective_id):
    rows, total = in_grad.shape[0] // 8, in_grad.shape[1]
    order, count = pieces[0][2], len(pieces)
    vmem = pl.BlockSpec(memory_space=pltpu.VMEM)
    shape = jax.ShapeDtypeStruct
    return pl.pallas_call(
        functools.partial(sum_weights_kernel, rows, pieces),
        out_shape=[
            shape((rows, wide), jnp.float32),
            shape((rows, 2 * wide), jnp.float32),
        ],
        in_specs=[pl.BlockSpec(memory_space=pltpu.HBM)],
        out_specs=[vmem] * 2,
        scratch_shapes=scatter_rooms(rows, total, order)
        + [
            pltpu.VMEM((rows, wide), jnp.bfloat16),
            pltpu.VMEM((4, rows, total - wide), jnp.bfloat16),
            pltpu.SemaphoreType.DMA((sends_of(order, count) + 7 * count,)),
            pltpu.SemaphoreType.DMA((count, 7)),
        ]
        + scatter_sems(order, count),
        compiler_params=pltpu.CompilerParams(
            collective_id=collective_id, has_side_effects=True, vmem_limit_bytes=63 * 2**20
        ),
        name="sum_weights",
    )(in_grad)


def weights_kernel(jobs, *refs):
    ready = len(jobs) - 2
    sources, (query, keyvalue, output) = refs[:ready], refs[ready : ready + 3]
    in_shard, out_shard = refs[ready + 3 : ready + 5]
    targets = refs[ready + 5 : 2 * ready + 7]
    send_sems, arrive_sems, own_sems, deal_sems = refs[2 * ready + 7 :]
    place = Place()
    z, y, e = place.at["z"], place.at["y"], place.expert
    span = (in_shard.shape[1] - query.shape[1]) // 2
    wide = query.shape[1]
    partner, moves = (e * 2 + y, z), z != e
    peers = []
    for flip_x, flip_c in ((1, 1), (1, 0), (0, 1)):
        x = place.at["x"] + flip_x * (1 - 2 * place.at["x"])
        core = place.at["c"] + flip_c * (1 - 2 * place.at["c"])
        peers.append((x * 2 + core, flip_x * 2 + flip_c))
    enter(place, "cxyz", [((place.dp, peers[0][0]), None), (partner, moves)])
    post = Post(send_sems, place)
    starts, waves, owns = gather_plan(
        jobs, place, post, list(sources) + [in_shard, out_shard], targets, arrive_sems, own_sems
    )
    cols = lambda block: pl.ds(pl.multiple_of(block * span, span), span)
    for peer, flips in peers:
        post.send(
            query.at[:, cols(peer)], in_shard.at[:, cols(e)], deal_sems.at[flips], (place.dp, peer)
        )
    post.send(output, out_shard, deal_sems.at[4], partner, moves)
    local = [
        pltpu.make_async_copy(query.at[:, cols(e)], in_shard.at[:, cols(e)], deal_sems.at[0]),
        pltpu.make_async_copy(
            keyvalue.at[:, cols(e)], in_shard.at[:, pl.ds(wide, span)], deal_sems.at[5]
        ),
        pltpu.make_async_copy(
            keyvalue.at[:, cols(wide // span + e)],
            in_shard.at[:, pl.ds(wide + span, span)],
            deal_sems.at[6],
        ),
    ]
    for copy in local:
        copy.start()
    stay = pltpu.make_async_copy(output, out_shard, deal_sems.at[7])
    pl.when(~moves)(stay.start)
    for act in sum(starts[:ready], []):
        act()
    for copy in local:
        copy.wait()
    for peer, flips in peers:
        post.arrived(in_shard.at[:, cols(peer)], deal_sems.at[flips])
    for act in starts[ready]:
        act()
    pl.when(~moves)(stay.wait)
    pl.when(moves)(lambda: post.arrived(out_shard, deal_sems.at[4]))
    for act in starts[ready + 1]:
        act()
    for wave in sorted(waves):
        for act in waves[wave]:
            act()
    for own in owns:
        own.wait()
    post.close()


def gather_weights(jobs, query, keyvalue, output, pieces, collective_id):
    rows, wide = query.shape
    span = wide // lax.axis_size("expert")
    shards = [
        jax.ShapeDtypeStruct((rows, wide + 2 * span), query.dtype),
        jax.ShapeDtypeStruct(output.shape, output.dtype),
    ]
    sizes = {"all": 32, "dp": 8, "expert": 4}
    plan = tuple((whose, r.shape[0], ps) for r, whose, ps in jobs)
    plan += tuple(("dp", s.shape[0], pieces) for s in shards)
    lines = sum(len(ps) for _, _, ps in plan)
    hbm = pl.BlockSpec(memory_space=pltpu.HBM)
    gathered = [
        jax.ShapeDtypeStruct((sizes[whose] * r.shape[0], r.shape[1]), r.dtype)
        for r, (whose, _, _) in zip([r for r, _, _ in jobs] + shards, plan)
    ]
    out = pl.pallas_call(
        functools.partial(weights_kernel, plan),
        out_shape=shards + gathered,
        in_specs=[hbm] * (len(jobs) + 3),
        out_specs=[hbm] * (2 + len(gathered)),
        scratch_shapes=[
            pltpu.SemaphoreType.DMA((110 * lines,)),
            pltpu.SemaphoreType.DMA((lines, 32)),
            pltpu.SemaphoreType.DMA((len(plan),)),
            pltpu.SemaphoreType.DMA((8,)),
        ],
        compiler_params=pltpu.CompilerParams(collective_id=collective_id, has_side_effects=True),
        name="gather_weights",
    )(*[r for r, _, _ in jobs], query, keyvalue, output)
    return out[2:]


def attention_bias(bias, block, rows, width, prefix):
    query = block * rows + lax.broadcasted_iota(jnp.int32, (rows, width), 0)
    key = lax.broadcasted_iota(jnp.int32, (rows, width), 1)
    bias[:, :width] = jnp.where((key <= query) | (key < prefix), 0.0, NEG)


def pick_expert(ref, lane, experts, span, chosen):
    total = None
    for e in range(experts):
        cols = ref[:, pl.ds(pl.multiple_of(e * span + lane, HEAD_DIM), HEAD_DIM)]
        term = jnp.where(chosen == e, cols.astype(jnp.float32), 0.0)
        total = term if total is None else total + term
    return total.astype(jnp.bfloat16)


def key_limits(blocks, rows):
    return [max((i + 1) * rows, blocks * rows // 2) for i in range(blocks)]


def for_each_limit(blocks, rows, body):
    block = pl.program_id(0)
    limits = key_limits(blocks, rows)
    for width in sorted(set(limits)):
        members = [i for i, limit in enumerate(limits) if limit == width]
        pl.when((block >= members[0]) & (block <= members[-1]))(lambda width=width: body(width))


def attention_kernel(experts, prefix, q, k, v, side, mixed, log_total, bias):
    rows, span = q.shape[0], k.shape[1]
    heads = span // HEAD_DIM
    block = pl.program_id(0)
    chosen = [side[:, 0:1], side[:, 1:2]]
    gates = [side[:, 2:3], side[:, 3:4]]

    def body(width):
        attention_bias(bias, block, rows, width, prefix[0])

        @pl.loop(0, heads)
        def _(head):
            lane = head * HEAD_DIM
            lanes = pl.ds(pl.multiple_of(lane, HEAD_DIM), HEAD_DIM)
            weighted = []
            for j in range(2):
                query = pick_expert(q, lane, experts, span, chosen[j])
                scores = lax.dot_general(
                    query, k[:width, lanes], ACROSS, preferred_element_type=jnp.float32
                )
                scores = scores * (HEAD_DIM**-0.5) + bias[:, :width]
                largest = jnp.max(scores, axis=1, keepdims=True)
                exponent = jnp.exp(scores - largest)
                total = jnp.sum(exponent, axis=1, keepdims=True)
                low = (exponent * (1.0 / total)).astype(jnp.bfloat16)
                out = jnp.dot(low, v[:width, lanes], preferred_element_type=jnp.float32)
                weighted.append(out * gates[j])
                at = pl.ds(pl.multiple_of((2 * head + j) * HEAD_DIM, HEAD_DIM), HEAD_DIM)
                log_total[:, at] = jnp.broadcast_to(
                    largest + jnp.log(total), (rows, HEAD_DIM)
                )
            for e in range(experts):
                cols = jnp.where(chosen[0] == e, weighted[0], 0.0) + jnp.where(
                    chosen[1] == e, weighted[1], 0.0
                )
                at = pl.ds(pl.multiple_of(e * span + lane, HEAD_DIM), HEAD_DIM)
                mixed[:, at] = cols.astype(jnp.bfloat16)

    for_each_limit(k.shape[0] // rows, rows, body)


def attention(projected, side, prefix, experts, rows):
    length = projected.shape[0]
    span = projected.shape[1] // (experts + 2)
    wide = experts * span
    return pl.pallas_call(
        functools.partial(attention_kernel, experts),
        grid=(length // rows,),
        in_specs=[
            pl.BlockSpec(memory_space=pltpu.SMEM),
            pl.BlockSpec((rows, wide), lambda i: (i, 0)),
            pl.BlockSpec((length, span), lambda i: (0, experts)),
            pl.BlockSpec((length, span), lambda i: (0, experts + 1)),
            pl.BlockSpec((rows, 128), lambda i: (i, 0)),
        ],
        out_specs=[
            pl.BlockSpec((rows, wide), lambda i: (i, 0)),
            pl.BlockSpec((rows, 2 * span), lambda i: (i, 0)),
        ],
        out_shape=[
            jax.ShapeDtypeStruct((length, wide), jnp.bfloat16),
            jax.ShapeDtypeStruct((length, 2 * span), jnp.float32),
        ],
        scratch_shapes=[pltpu.VMEM((rows, length), jnp.float32)],
        compiler_params=pltpu.CompilerParams(vmem_limit_bytes=48 * 2**20),
        name="attention",
    )(prefix, projected, projected, projected, side)


class AttentionBack(Nothing):
    operands, results, rooms = 4, 2, 11
    turns = 4

    def __init__(self, length, total, experts, rows):
        self.length, self.experts, self.rows = length, experts, rows
        self.span = total // (experts + 2)
        low, f32 = jnp.bfloat16, jnp.float32
        self.heads = self.span // HEAD_DIM
        self.blocks = length // rows
        self.shapes = [
            jax.ShapeDtypeStruct((length, total), low),
            jax.ShapeDtypeStruct((length, 128), f32),
        ]
        self.scratch = [
            pltpu.VMEM((length, total), low),
            pltpu.VMEM((length, 128), f32),
            pltpu.VMEM((length, 2 * self.span), f32),
            pltpu.VMEM((length, experts * self.span), low),
            pltpu.VMEM((length, total), low),
            pltpu.VMEM((length, 128), f32),
            pltpu.VMEM((rows, length), f32),
            pltpu.VMEM((length, self.span), f32),
            pltpu.VMEM((length, self.span), f32),
            pltpu.SemaphoreType.DMA((4,)),
            pltpu.SemaphoreType.DMA((2,)),
        ]

    def loads(self, given, own):
        return [pltpu.make_async_copy(given[i], own[i], own[9].at[i]) for i in range(4)]

    def start(self, given, made, own):
        for load in self.loads(given, own):
            load.start()
        for ref in (own[5], own[7], own[8]):
            ref[...] = jnp.zeros_like(ref)
        return self.blocks * self.heads

    def run(self, given, made, own, first, last):
        if first == 0:
            for load in self.loads(given, own):
                load.wait()

        @pl.loop(first, last)
        def _(step):
            block = step // self.heads
            limits = key_limits(self.blocks, self.rows)
            for width in sorted(set(limits)):
                members = [i for i, limit in enumerate(limits) if limit == width]

                @pl.when((block >= members[0]) & (block <= members[-1]))
                def _(width=width):
                    self.step(own, block, step % self.heads, width)

    def step(self, own, block, head, width):
        qkv, side_ref, log_total, dmix, dprojected, dgate, bias, dk, dv = own[:9]
        experts, span, rows = self.experts, self.span, self.rows
        scaling = HEAD_DIM**-0.5
        row_at = pl.ds(pl.multiple_of(block * rows, rows), rows)
        side = side_ref[row_at, :]
        chosen = [side[:, 0:1], side[:, 1:2]]
        gates = [side[:, 2:3], side[:, 3:4]]
        column = lax.broadcasted_iota(jnp.int32, (rows, 128), 1)
        query_at = block * rows + lax.broadcasted_iota(jnp.int32, (rows, width), 0)
        key_at = lax.broadcasted_iota(jnp.int32, (rows, width), 1)
        reach = key_at.astype(jnp.float32) < side[:, 4:5]
        bias[:, :width] = jnp.where((key_at <= query_at) | reach, 0.0, NEG)
        lane = head * HEAD_DIM
        lanes = lambda base: pl.ds(pl.multiple_of(base + lane, HEAD_DIM), HEAD_DIM)
        keys = qkv[:width, lanes(experts * span)]
        values = qkv[:width, lanes((experts + 1) * span)]
        dqueries = []
        for j in range(2):
            query = pick_expert(qkv.at[row_at], lane, experts, span, chosen[j])
            dm = pick_expert(dmix.at[row_at], lane, experts, span, chosen[j])
            at = pl.ds(pl.multiple_of((2 * head + j) * HEAD_DIM, HEAD_DIM), HEAD_DIM)
            logs = jnp.tile(log_total[row_at, at], (1, width // HEAD_DIM))
            scores = lax.dot_general(query, keys, ACROSS, preferred_element_type=jnp.float32)
            probs = jnp.exp(scores * scaling + bias[:, :width] - logs)
            dprobs = lax.dot_general(dm, values, ACROSS, preferred_element_type=jnp.float32)
            inner = jnp.sum(probs * dprobs, axis=1, keepdims=True)
            dgate[row_at, :] += jnp.where(column == j, inner, 0.0)
            probs = probs * gates[j]
            dscores = (probs * (dprobs - inner)).astype(jnp.bfloat16)
            low = probs.astype(jnp.bfloat16)
            dqueries.append(jnp.dot(dscores, keys, preferred_element_type=jnp.float32) * scaling)
            dk[:width, lanes(0)] += lax.dot_general(
                dscores, query, DOWNWARD, preferred_element_type=jnp.float32
            )
            dv[:width, lanes(0)] += lax.dot_general(
                low, dm, DOWNWARD, preferred_element_type=jnp.float32
            )
        for e in range(experts):
            cols = jnp.where(chosen[0] == e, dqueries[0], 0.0) + jnp.where(
                chosen[1] == e, dqueries[1], 0.0
            )
            dprojected[row_at, lanes(e * span)] = cols.astype(jnp.bfloat16)

    def end(self, given, made, own):
        dprojected, dgate, dk, dv = own[4], own[5], own[7], own[8]
        wide = self.experts * self.span
        dprojected[:, wide : wide + self.span] = (dk[...] * HEAD_DIM**-0.5).astype(jnp.bfloat16)
        dprojected[:, wide + self.span :] = dv[...].astype(jnp.bfloat16)
        copies = [
            pltpu.make_async_copy(dprojected, made[0], own[10].at[0]),
            pltpu.make_async_copy(dgate, made[1], own[10].at[1]),
        ]
        for copy in copies:
            copy.start()
        for copy in copies:
            copy.wait()


def chip_in_turn(u, z_here):
    u = jnp.asarray(u, jnp.int32)
    turn, q = u // 4, u % 4
    flip = lambda *at: ((q == at[0]) | (q == at[1])).astype(jnp.int32)
    k, xr, yr = turn + (q == 3) - (q == 0), flip(0, 1), flip(0, 2)
    k = jnp.where(u == 0, 0, jnp.minimum(k, CHIPS_Z - 1))
    last = 4 * CHIPS_Z - 1
    xr = jnp.where(u == 0, 0, jnp.where(u == last, 1, xr))
    yr = jnp.where(u == 0, 0, jnp.where(u == last, 1, yr))
    inner = (z_here == 1) | (z_here == 2)
    near = jnp.where(inner, jnp.where(k == 3, 3, jnp.where(k == 2, 0, k + 1)), k)
    return jnp.where(z_here < 2, near, CHIPS_Z - 1 - near), xr, yr


def block_in_turn(u, place):
    z, xr, yr = chip_in_turn(u, place.at["z"])
    x = place.at["x"] + xr * (1 - 2 * place.at["x"])
    y = place.at["y"] + yr * (1 - 2 * place.at["y"])
    return (z * 2 + y) * 4 + x * 2


class BranchRows(Nothing):
    operands, results, rooms = 3, 1, 8

    def __init__(self, tok, slot_count, blocks, hidden, padded, width):
        self.tok, self.slot_count, self.hidden = tok, slot_count, hidden
        low = jnp.bfloat16
        self.chips = blocks // 2
        self.shapes = [jax.ShapeDtypeStruct((blocks * tok, width), low)]
        self.scratch = [
            pltpu.VMEM((padded, width), low),
            pltpu.VMEM((blocks, tok), jnp.int32),
            pltpu.VMEM((2, 2 * slot_count, padded), low),
            pltpu.VMEM((2 * slot_count, width), low),
            pltpu.VMEM((2, 2 * tok, width), low),
            pltpu.SemaphoreType.DMA((2,)),
            pltpu.SemaphoreType.DMA((2,)),
            pltpu.SemaphoreType.DMA((2,)),
        ]

    def whole(self, given, own):
        return [
            pltpu.make_async_copy(given[1], own[0].at[pl.ds(0, self.hidden)], own[5].at[0]),
            pltpu.make_async_copy(given[2], own[1], own[5].at[1]),
        ]

    def take(self, given, own, u):
        rows = pl.ds(pl.multiple_of(u * 2 * self.slot_count, 64), 2 * self.slot_count)
        return pltpu.make_async_copy(given[0].at[rows], own[2].at[u % 2], own[6].at[u % 2])

    def put(self, made, own, u):
        rows = pl.ds(block_in_turn(u, Place()) * self.tok, 2 * self.tok)
        return pltpu.make_async_copy(own[4].at[u % 2], made[0].at[rows], own[7].at[u % 2])

    def start(self, given, made, own):
        for copy in self.whole(given, own):
            copy.start()
        self.take(given, own, jnp.int32(0)).start()
        own[0][self.hidden :, :] = jnp.zeros_like(own[0][self.hidden :, :])
        return self.chips

    def run(self, given, made, own, first, last):
        if first == last:
            return
        if first == 0:
            for copy in self.whole(given, own):
                copy.wait()
        w_down, slots, acts, outs, placed = own[:5]

        @pl.loop(first, last)
        def _(u):
            s = u % 2

            @pl.when(u + 1 < self.chips)
            def _():
                self.take(given, own, u + 1).start()

            self.take(given, own, u).wait()

            @pl.when(u >= 2)
            def _():
                self.put(made, own, u - 2).wait()

            @pl.loop(0, outs.shape[1] // 256)
            def _(n):
                cols = pl.ds(pl.multiple_of(n * 256, 256), 256)
                outs[:, cols] = jnp.dot(
                    acts[s], w_down[:, cols], preferred_element_type=jnp.float32
                ).astype(jnp.bfloat16)

            block = block_in_turn(u, Place())
            for b in range(2):
                row = slots[pl.ds(block + b, 1), :]
                number = lax.broadcasted_iota(jnp.int32, (self.slot_count, self.tok), 0)
                table = (number == row).astype(jnp.float32).T.astype(jnp.bfloat16)
                placed[s, pl.ds(b * self.tok, self.tok), :] = jnp.dot(
                    table,
                    outs[pl.ds(b * self.slot_count, self.slot_count), :],
                    preferred_element_type=jnp.float32,
                ).astype(jnp.bfloat16)
            self.put(made, own, u).start()

    def end(self, given, made, own):
        for u in (self.chips - 2, self.chips - 1):
            self.put(made, own, jnp.int32(u)).wait()


def expert_slots(first, second, my_index):
    tok_rows = first.shape[1]
    chosen = ((first == my_index) | (second == my_index)).astype(jnp.float32)
    before = jnp.triu(jnp.ones((tok_rows, tok_rows), jnp.float32), 1)
    slots = jnp.where(chosen > 0, jnp.dot(chosen, before), -1.0).astype(jnp.int32)
    return slots, first + second - my_index


def feed_kernel(
    tok,
    slot_count,
    own_rows,
    cots_left,
    cots_right,
    gate_weight,
    up_weight,
    down_weight,
    router_rows,
    slots,
    others,
    everyone,
    dx_part,
    x_kept,
    g_kept,
    d_kept,
    a_kept,
    dgate,
    w_in,
    w_down,
    rows_buf,
    cots_buf,
    xs,
    gs,
    pre,
    back,
    ds,
    acts,
    dx_buf,
    dxs,
    send_sems,
    arrive_sems,
    own_sem,
    weight_sems,
    load_sems,
    keep_sems,
):
    place = Place()
    z_here = place.at["z"]
    hidden = gate_weight.shape[0]
    padded = w_down.shape[0]
    width = own_rows.shape[1]
    half = tok // 2
    chips = 4 * CHIPS_Z
    pair = 2 * slot_count
    f32, low = jnp.float32, jnp.bfloat16

    loads = [
        pltpu.make_async_copy(gate_weight, w_in.at[pl.ds(0, hidden)], weight_sems.at[0]),
        pltpu.make_async_copy(
            router_rows, w_in.at[pl.ds(hidden, padded - hidden)], weight_sems.at[1]
        ),
        pltpu.make_async_copy(up_weight, w_in.at[pl.ds(padded, hidden)], weight_sems.at[2]),
        pltpu.make_async_copy(down_weight, w_down.at[pl.ds(0, hidden)], weight_sems.at[3]),
        pltpu.make_async_copy(
            own_rows, everyone.at[pl.ds(place.block("all", z_here, {}) * tok, tok)], own_sem
        ),
    ]
    for load in loads:
        load.start()
    w_in[padded + hidden :, :] = jnp.zeros((padded - hidden, width), low)
    w_down[hidden:, :] = jnp.zeros((padded - hidden, width), low)
    enter(place, "cxyz")

    def chip(u):
        return chip_in_turn(u, z_here)

    def first_block(u):
        return block_in_turn(u, place)

    def part(p, u, core):
        return everyone.at[pl.ds((first_block(u) + core) * tok + p * half, half)]

    def remote(source, target, number, mark, device):
        return pltpu.make_async_remote_copy(
            src_ref=source,
            dst_ref=target,
            send_sem=send_sems.at[number],
            recv_sem=arrive_sems.at[mark],
            device_id=device,
            device_id_type=MESH,
        )

    def routes(u, p):
        z, xr, yr = chip(u)
        plain = (xr + yr) == 0
        mark = (p * CHIPS_Z + z) * 8
        here = xr * 4 + yr * 2
        base = (u * 2 + p) * 5
        own = z == z_here
        right = plain & (z <= z_here) & (z_here < CHIPS_Z - 1)
        left = plain & (z >= z_here) & (z_here > 0)
        over_x = plain if p == 0 else xr == 0
        over_y = yr == 0 if p == 0 else plain
        return [
            (right, base, mark, place.along(1)),
            (left, base + 1, mark, place.along(-1)),
            (over_x, base + 2, mark + 4 + yr * 2, place.across("x")),
            (over_y, base + 3, mark + xr * 4 + 2, place.across("y")),
            (None, base + 4, mark + here + 1, place.across("c")),
        ]

    def hand_on(u, sources, pieces=(0, 1)):
        for p in pieces:
            for condition, number, mark, device in routes(u, p):
                target = part(p, u, place.at["c"])
                source = target if sources is None else sources[p]
                on(
                    condition,
                    lambda source=source, target=target, number=number, mark=mark, device=device: remote(
                        source, target, number, mark, device
                    ).start(),
                )

    def sibling_came(u):
        z, xr, yr = chip(u)
        for p in range(2):
            ref = part(p, u, 1 - place.at["c"])
            mark = (p * CHIPS_Z + z) * 8 + xr * 4 + yr * 2 + 1
            remote(ref, ref, 0, mark, place.across("c")).wait_recv()

    def take_in(u, p):
        z, xr, yr = chip(u)
        ref = part(p, u, place.at["c"])
        mark = (p * CHIPS_Z + z) * 8 + xr * 4 + yr * 2
        remote(ref, ref, 0, mark, place.across("c")).wait_recv()
        hand_on(u, None, (p,))

    def fetch(u):
        at = pl.ds(first_block(u) * tok, 2 * tok)
        return [
            pltpu.make_async_copy(everyone.at[at], rows_buf.at[u % 2], load_sems.at[u % 2, 0]),
            pltpu.make_async_copy(
                cots_left.at[at], cots_buf.at[u % 2, :, pl.ds(0, width // 2)], load_sems.at[u % 2, 1]
            ),
            pltpu.make_async_copy(
                cots_right.at[at],
                cots_buf.at[u % 2, :, pl.ds(width // 2, width // 2)],
                load_sems.at[u % 2, 2],
            ),
        ]

    def keep(u):
        rows = pl.ds(u * pair, pair)
        blocks = pl.ds(first_block(u) * tok, 2 * tok)
        s = u % 2
        return [
            pltpu.make_async_copy(xs.at[s], x_kept.at[rows], keep_sems.at[s, 0]),
            pltpu.make_async_copy(gs.at[s], g_kept.at[rows], keep_sems.at[s, 1]),
            pltpu.make_async_copy(ds.at[s], d_kept.at[rows], keep_sems.at[s, 2]),
            pltpu.make_async_copy(acts.at[s], a_kept.at[rows], keep_sems.at[s, 3]),
            pltpu.make_async_copy(dx_buf.at[s], dx_part.at[blocks], keep_sems.at[s, 4]),
        ]

    hand_on(0, [own_rows.at[pl.ds(0, half)], own_rows.at[pl.ds(half, half)]])
    loads[4].wait()
    sibling_came(0)
    for copy in fetch(0):
        copy.start()
    for p in range(2):
        take_in(1, p)
    for load in loads[:4]:
        load.wait()

    def compute(u):
        s = u % 2
        block = first_block(u)
        spread = []
        for b in range(2):
            row = slots[pl.ds(block + b, 1), :]
            table = lax.broadcasted_iota(jnp.int32, (slot_count, tok), 0) == row
            table = table.astype(f32)
            spread.append(table)
            at = pl.ds(b * slot_count, slot_count)
            from_rows = pl.ds(b * tok, tok)
            xs[s, at, :] = jnp.dot(
                table.astype(low), rows_buf[s, from_rows, :], preferred_element_type=f32
            ).astype(low)
            gs[s, at, :] = jnp.dot(
                table.astype(low), cots_buf[s, from_rows, :], preferred_element_type=f32
            ).astype(low)

        @pl.loop(0, 2 * padded // 256)
        def _(n):
            at = pl.ds(pl.multiple_of(n * 256, 256), 256)
            pre[:, at] = lax.dot_general(xs[s], w_in[at, :], ACROSS, preferred_element_type=f32)

        @pl.when(u + 2 < chips)
        def _():
            take_in(u + 2, 1)

        @pl.loop(0, padded // 256)
        def _(n):
            at = pl.ds(pl.multiple_of(n * 256, 256), 256)
            back[:, at] = lax.dot_general(gs[s], w_down[at, :], ACROSS, preferred_element_type=f32)

        for b in range(2):
            at = pl.ds(b * slot_count, slot_count)
            last = pre[at, padded - 128 : padded]
            column = lax.broadcasted_iota(jnp.int32, (slot_count, 128), 1) - (
                hidden - (padded - 128)
            )
            other = jnp.sum(
                spread[b] * others[pl.ds(block + b, 1), :].astype(f32), axis=1, keepdims=True
            )
            mine = jnp.sum(jnp.where(column == place.expert, last, 0.0), axis=1, keepdims=True)
            theirs = jnp.sum(
                jnp.where(column == other.astype(jnp.int32), last, 0.0), axis=1, keepdims=True
            )
            gate = 1.0 / (1.0 + jnp.exp(theirs - mine))
            inner = jnp.zeros((slot_count, 1), f32)
            for n in range(padded // 256):
                cols = pl.ds(n * 256, 256)
                pre_gate, pre_up = pre[at, cols], pre[at, pl.ds(padded + n * 256, 256)]
                dact = back[at, cols]
                sig = 1.0 / (1.0 + jnp.exp(-pre_gate))
                silu = pre_gate * sig
                act = silu * pre_up
                acts[s, at, cols] = (act * gate).astype(low)
                inner += jnp.sum(act * dact, axis=1, keepdims=True)
                dact = dact * gate
                ds[s, at, cols] = (dact * pre_up * sig * (1.0 + pre_gate * (1.0 - sig))).astype(low)
                ds[s, at, pl.ds(padded + n * 256, 256)] = (dact * silu).astype(low)
            dgate[pl.ds(block + b, 1), :] = jnp.sum(spread[b] * inner, axis=0, keepdims=True)

        @pl.loop(0, width // 256)
        def _(n):
            cols = pl.ds(pl.multiple_of(n * 256, 256), 256)
            dxs[:, cols] = jnp.dot(ds[s], w_in[:, cols], preferred_element_type=f32).astype(low)

        for b in range(2):
            at = pl.ds(b * slot_count, slot_count)
            back_table = spread[b].T.astype(low)
            to = pl.ds(b * tok, tok)
            dx_buf[s, to, :] = jnp.dot(
                back_table, dxs[at, :], preferred_element_type=f32
            ).astype(low)

    @pl.loop(0, chips)
    def _(u):
        @pl.when(u + 1 < chips)
        def _():
            sibling_came(u + 1)
            for copy in fetch(u + 1):
                copy.start()

        @pl.when(u + 2 < chips)
        def _():
            take_in(u + 2, 0)

        for copy in fetch(u):
            copy.wait()

        @pl.when(u >= 2)
        def _():
            for copy in keep(u - 2):
                copy.wait()

        compute(u)
        for copy in keep(u):
            copy.start()

    for u in (chips - 2, chips - 1):
        for copy in keep(jnp.int32(u)):
            copy.wait()

    @pl.loop(0, chips)
    def _(u):
        for p in range(2):
            for condition, number, mark, device in routes(u, p):
                ref = part(p, u, place.at["c"])
                on(
                    condition,
                    lambda ref=ref, number=number, mark=mark, device=device: remote(
                        ref, ref, number, mark, device
                    ).wait_send(),
                )


def feed(
    own_rows,
    cots_left,
    cots_right,
    gate_weight,
    up_weight,
    down_weight,
    router_rows,
    slots,
    others,
    slot_count,
):
    tok, width = own_rows.shape
    hidden = gate_weight.shape[0]
    padded = hidden + router_rows.shape[0]
    total = cots_left.shape[0]
    kept = total // tok * slot_count
    low = jnp.bfloat16
    hbm = pl.BlockSpec(memory_space=pltpu.HBM)
    vmem = pl.BlockSpec(memory_space=pltpu.VMEM)
    shape = jax.ShapeDtypeStruct
    pair = 2 * slot_count
    chips = 4 * CHIPS_Z
    return pl.pallas_call(
        functools.partial(feed_kernel, tok, slot_count),
        in_specs=[hbm] * 7 + [vmem] * 2,
        out_specs=[hbm] * 6 + [vmem],
        out_shape=[
            shape((total, width), low),
            shape((total, width), low),
            shape((kept, width), low),
            shape((kept, width), low),
            shape((kept, 2 * padded), low),
            shape((kept, padded), low),
            shape(slots.shape, jnp.float32),
        ],
        scratch_shapes=[
            pltpu.VMEM((2 * padded, width), low),
            pltpu.VMEM((padded, width), low),
            pltpu.VMEM((2, 2 * tok, width), low),
            pltpu.VMEM((2, 2 * tok, width), low),
            pltpu.VMEM((2, pair, width), low),
            pltpu.VMEM((2, pair, width), low),
            pltpu.VMEM((pair, 2 * padded), jnp.float32),
            pltpu.VMEM((pair, padded), jnp.float32),
            pltpu.VMEM((2, pair, 2 * padded), low),
            pltpu.VMEM((2, pair, padded), low),
            pltpu.VMEM((2, 2 * tok, width), low),
            pltpu.VMEM((pair, width), low),
            pltpu.SemaphoreType.DMA((10 * chips,)),
            pltpu.SemaphoreType.DMA((16 * CHIPS_Z,)),
            pltpu.SemaphoreType.DMA,
            pltpu.SemaphoreType.DMA((4,)),
            pltpu.SemaphoreType.DMA((2, 3)),
            pltpu.SemaphoreType.DMA((2, 6)),
        ],
        compiler_params=pltpu.CompilerParams(
            collective_id=3, has_side_effects=True, vmem_limit_bytes=60 * 2**20
        ),
        name="feed_forward",
    )(
        own_rows,
        cots_left,
        cots_right,
        gate_weight,
        up_weight,
        down_weight,
        router_rows,
        slots,
        others,
    )


def per_device_torus(
    tokens,
    cotangent,
    attention_routes,
    feedforward_routes,
    prefix_length,
    gain_attention,
    gain_feedforward,
    keyvalue_weight,
    router_weight,
    query_weight,
    output_weight,
    gate_weight,
    up_weight,
    down_weight,
):
    my_index = lax.axis_index("expert")
    group_size = lax.axis_size("expert")
    dp_size = lax.axis_size("dp")
    inputs = tokens[0].astype(jnp.float32)
    tok_rows, model_width = inputs.shape
    slot_count = 5 * 2 * tok_rows // (4 * group_size)
    query_width = HEADS * HEAD_DIM
    span = query_width // group_size
    low = jnp.bfloat16
    f32 = jnp.float32

    normed_attention, unit_attention, factor_attention = norm_parts(inputs, gain_attention)
    attention_in = normed_attention.astype(low)
    quarters = lambda order: tuple(
        (i * tok_rows // 4, tok_rows // 4, order) for i in range(4)
    )
    rows_in = keyvalue_weight.shape[0]
    route_shard = feedforward_routes[0].T.astype(low).reshape(-1, 128)
    half_model = model_width // 2
    router_shard = router_weight.T.reshape(-1, 128)
    whole = lambda a: ((0, a.shape[0], "zy"),)
    cut = rows_in * 13 // 16
    sequence_in, cots_left, every_route, router_full, in_weight, out_weight = gather_weights(
        [
            (attention_in, "expert", quarters("xc")),
            (cotangent[0, :, :half_model], "all", quarters("zyxc")),
            (route_shard, "dp", whole(route_shard)),
            (router_shard, "dp", whole(router_shard)),
        ],
        query_weight[0],
        keyvalue_weight,
        output_weight[0],
        ((0, cut, "zy"), (cut, rows_in - cut, "yz")),
        1,
    )
    cots_late, sequence_in = lax.optimization_barrier((cotangent[0, :, half_model:], sequence_in))
    cots_right = lax.all_gather(cots_late, ("dp", "expert"), axis=0, tiled=True)
    every_route = every_route.reshape(dp_size, 2, group_size, tok_rows).astype(jnp.int32)
    router_full = (
        router_full.reshape(dp_size, 2 * group_size, rows_in)
        .transpose(0, 2, 1)
        .reshape(-1, 2 * group_size)
    )
    attention_cols = router_full[:, :group_size]
    feedforward_cols = router_full[:, group_size:]
    projected = jnp.dot(sequence_in, in_weight, preferred_element_type=f32).astype(low)
    attend_matches_all = expert_matches(attention_routes[0], group_size)
    attend_logits = jnp.dot(sequence_in, attention_cols, preferred_element_type=f32)
    attend_weights_all, _ = pair_gates(attend_logits, attend_matches_all)
    reach = jnp.broadcast_to(prefix_length.astype(f32)[None], (attend_logits.shape[0], 1))
    side = jnp.concatenate([attention_routes[0].astype(f32), attend_weights_all, reach], axis=1)
    side = jnp.pad(side, ((0, 0), (0, 128 - side.shape[1])))
    mixed, log_total = attention(projected, side, prefix_length, group_size, tok_rows)
    attend_part = jnp.dot(mixed, out_weight, preferred_element_type=f32).astype(low)
    attended = scatter(attend_part, "expert", quarters("cx"), 2, "sum_attention")
    hidden = inputs + attended
    normed_feed, unit_feed, factor_feed = norm_parts(hidden, gain_feedforward)
    feed_in = normed_feed.astype(low)
    everywhere = lambda a, b: ((0, tok_rows // 2, a), (tok_rows // 2, tok_rows // 2, b))
    mine = lambda a: lax.dynamic_slice_in_dim(a, my_index * tok_rows, tok_rows, 0)
    feed_matches = expert_matches(mine(feedforward_routes[0]), group_size)
    feed_logits = jnp.dot(feed_in, feedforward_cols, preferred_element_type=f32)
    feed_weights, _ = pair_gates(feed_logits, feed_matches)
    slots, others = expert_slots(
        every_route[:, 0].reshape(-1, tok_rows), every_route[:, 1].reshape(-1, tok_rows), my_index
    )
    hidden_rows = gate_weight.shape[1]
    padded = -(-hidden_rows // 256) * 256
    router_rows = jnp.pad(
        feedforward_cols.T, ((0, padded - hidden_rows - group_size), (0, 0))
    )
    _, dx_part, kept_rows, kept_cots, kept_back, kept_act, token_dgate = feed(
        feed_in,
        cots_left,
        cots_right,
        gate_weight[0],
        up_weight[0],
        down_weight[0],
        router_rows,
        slots,
        others,
        slot_count,
    )
    own_row = (jnp.arange(group_size) == my_index).astype(f32)[None, :, None]
    feed_dgate = lax.psum_scatter(
        (token_dgate[:, None, :] * own_row).reshape(-1, tok_rows),
        ("dp", "expert"),
        scatter_dimension=0,
        tiled=True,
    ).T
    feed_home, grad_gate, grad_up, grad_down = scatter(
        dx_part,
        "all",
        everywhere("cxyz", "cyxz"),
        4,
        "sum_rows",
        WeightGrads(kept_rows.shape[0], padded, hidden_rows, model_width),
        (kept_back, kept_rows, kept_act, kept_cots),
    )
    gradient = cotangent[0].astype(f32)
    feed_dlogits = gates_back(feed_dgate, feed_weights, feed_matches)
    feed_dnorm = feed_home + jnp.dot(feed_dlogits, feedforward_cols.astype(f32).T, precision=HIGH)
    grad_gain_feed = jnp.sum(feed_dnorm * unit_feed, axis=0)
    hidden_grad = gradient + norm_back(feed_dnorm, gain_feedforward, unit_feed, factor_feed)

    sequence_grad, out_part = gather(
        [(hidden_grad.astype(low), "expert", quarters("xc"))],
        5,
        "gather_cotangents",
        BranchRows(tok_rows, slot_count, slots.shape[0], hidden_rows, padded, model_width),
        (kept_act, down_weight[0], slots),
    )
    dmix = lax.dot_general(sequence_grad, out_weight, ACROSS, preferred_element_type=f32).astype(low)
    length, total = projected.shape
    columns = model_width // 2
    first_sum, dprojected, gate_parts, grad_out = scatter(
        out_part,
        "all",
        everywhere("cxyz", "cyxz"),
        7,
        "sum_output_left",
        InTurn(
            AttentionBack(length, total, group_size, tok_rows),
            LowGrad(length, query_width, model_width, 4),
        ),
        (projected, side, log_total, dmix, mixed, sequence_grad),
        (0, columns),
    )
    second_sum, grad_projection, attend_dx = sum_right(
        out_part,
        (columns, model_width - columns),
        everywhere("cxyz", "cxyz"),
        grad_out,
        ((0, rows_in, "yz"),),
        8,
        RowGrads(length, total, model_width),
        (dprojected, in_weight, gate_parts),
    )
    attend_home, grad_in = scatter(
        attend_dx,
        "expert",
        quarters("cx"),
        9,
        "sum_attention_back",
        LowGrad(length, model_width, total, 1),
        (sequence_in, dprojected),
    )
    pair_dgate = attend_home[:, model_width : model_width + 2]
    attend_home = attend_home[:, :model_width]
    layer_output = hidden + jnp.concatenate([first_sum, second_sum], axis=1)
    matches = mine(attend_matches_all)
    weights = mine(attend_weights_all)
    dselected = weights * (pair_dgate - jnp.sum(weights * pair_dgate, axis=1, keepdims=True))
    attend_dlogits = jnp.sum(dselected[:, :, None] * matches, axis=1)
    attend_dnorm = attend_home + jnp.dot(
        attend_dlogits, attention_cols.astype(f32).T, precision=HIGH
    )
    grad_gain_attend = jnp.sum(attend_dnorm * unit_attention, axis=0)
    grad_tokens = hidden_grad + norm_back(
        attend_dnorm, gain_attention, unit_attention, factor_attention
    )
    small = jnp.concatenate(
        [
            lax.dot_general(attend_dlogits, attention_in.astype(f32), DOWNWARD, precision=HIGH),
            lax.dot_general(feed_dlogits, feed_in.astype(f32), DOWNWARD, precision=HIGH),
            grad_gain_attend[None],
            grad_gain_feed[None],
        ],
        axis=0,
    )
    small = lax.psum(small.astype(f32), ("dp", "expert"))
    small = lax.dynamic_slice_in_dim(small, lax.axis_index("dp") * rows_in, rows_in, 1)

    grad_query, grad_keyvalue = sum_weights(grad_in, query_width, ((0, rows_in, "yz"),), 6)
    return (
        layer_output.astype(low)[None],
        grad_tokens[None],
        small[2 * group_size],
        small[2 * group_size + 1],
        grad_keyvalue,
        small[: 2 * group_size].T,
        grad_query[None],
        grad_projection[None],
        grad_gate[None],
        grad_up[None],
        grad_down[None],
    )


def solution(mesh):
    in_specs = (
        P("dp", "expert", None),
        P("dp", "expert", None),
        P("dp", None, None),
        P("dp", None, None),
        P("dp"),
        P(),
        P(),
        P("dp", None),
        P("dp", None),
        P("expert", "dp", None),
        P("expert", "dp", None),
        P("expert", "dp", None),
        P("expert", "dp", None),
        P("expert", "dp", None),
    )
    out_specs = (
        P("dp", "expert", None),
        P("dp", "expert", None),
        P("dp"),
        P("dp"),
        P("dp", None),
        P("dp", None),
        P("expert", "dp", None),
        P("expert", "dp", None),
        P("expert", "dp", None),
        P("expert", "dp", None),
        P("expert", "dp", None),
    )
    torus = (mesh.shape["dp"], mesh.shape["expert"]) == (8, 4)
    body = per_device_torus if torus else per_device
    return jax.shard_map(
        body, mesh=mesh, in_specs=in_specs, out_specs=out_specs, check_vma=False
    )
```

```python
import functools

import jax
import jax.numpy as jnp
from jax import lax
from jax.experimental import pallas as pl
from jax.experimental.pallas import tpu as pltpu
from jax.sharding import PartitionSpec as P

HEADS = 16
HEAD_DIM = 128


EPS = 1e-06
NEG = -1e30
HIGH = lax.Precision.HIGHEST
ACROSS = (((1,), (1,)), ((), ()))
DOWNWARD = (((0,), (0,)), ((), ()))


def norm_parts(vector, gain_vector):
    factor = lax.rsqrt(jnp.mean(vector * vector, axis=-1, keepdims=True) + EPS)
    normed = vector * factor
    return (normed * gain_vector, normed, factor)


def norm_back(incoming, gain_vector, normed, factor):
    dnormed = incoming * gain_vector
    return factor * (dnormed - normed * jnp.mean(dnormed * normed, axis=-1, keepdims=True))


def route_plan(sequence_ids, my_index, group_size, tok_rows, slot_count):
    expert_range = jnp.arange(group_size, dtype=jnp.int32)
    matches_all = (sequence_ids[:, :, None] == expert_range[None, None, :]).astype(jnp.int32)
    chosen = jnp.sum(matches_all, axis=1).reshape(group_size, tok_rows, group_size)
    ranking = jnp.cumsum(chosen, axis=1) - chosen
    slot_ids = jnp.arange(slot_count, dtype=jnp.int32)[None, :, None]
    block_pick = (expert_range == my_index).astype(jnp.int32)
    my_chosen = jnp.sum(chosen * block_pick[:, None, None], axis=0).T
    my_ranking = jnp.sum(ranking * block_pick[:, None, None], axis=0).T
    send_table = (
        my_chosen[:, None, :] * (my_ranking[:, None, :] == slot_ids).astype(jnp.int32)
    ).astype(jnp.float32)
    column_chosen = jnp.sum(chosen * block_pick[None, None, :], axis=2)
    column_ranking = jnp.sum(ranking * block_pick[None, None, :], axis=2)
    taken = column_chosen[:, None, :] * (column_ranking[:, None, :] == slot_ids).astype(jnp.int32)
    positions = (
        expert_range[:, None, None] * tok_rows
        + jnp.arange(tok_rows, dtype=jnp.int32)[None, None, :]
    )
    arrival_places = jnp.sum(taken * positions, axis=2).reshape(-1)
    my_ids = lax.dynamic_slice_in_dim(sequence_ids, my_index * tok_rows, tok_rows, 0)
    matches = (my_ids[:, :, None] == expert_range[None, None, :]).astype(jnp.float32)
    return (send_table, arrival_places, matches)


def pair_gates(logits, matches):
    selected = jnp.sum(matches * logits[:, None, :], axis=2)
    largest = jnp.max(selected, axis=1, keepdims=True)
    exponent = jnp.exp(selected - largest)
    weights = exponent / jnp.sum(exponent, axis=1, keepdims=True)
    return (weights, jnp.sum(weights[:, :, None] * matches, axis=1))


def gates_back(dgate, weights, matches):
    dweights = jnp.sum(dgate[:, None, :] * matches, axis=2)
    dselected = weights * (dweights - jnp.sum(weights * dweights, axis=1, keepdims=True))
    return jnp.sum(dselected[:, :, None] * matches, axis=1)


def merge_back(send_table, gate_table, returned):
    weighted = send_table * gate_table.T[:, None, :]
    return jnp.einsum("ect,ecd->td", weighted, returned.astype(jnp.float32), precision=HIGH)


def branch_cotangent(send_table, gate_table, returned, incoming):
    spread_grad = jnp.einsum("ect,td->ecd", send_table, incoming, precision=HIGH)
    slot_gate = jnp.sum(send_table * gate_table.T[:, None, :], axis=2)
    cotangent_rows = (spread_grad * slot_gate[:, :, None]).astype(jnp.bfloat16)
    slot_dgate = jnp.sum(spread_grad * returned.astype(jnp.float32), axis=2)
    dgate = jnp.einsum("ect,ec->te", send_table, slot_dgate, precision=HIGH)
    return (cotangent_rows, dgate)


def expert_matches(ids, group_size):
    expert_range = jnp.arange(group_size, dtype=jnp.int32)
    return (ids[:, :, None] == expert_range[None, None, :]).astype(jnp.float32)


def expert_table(ids, my_index, group_size, tok_rows, slot_count):
    blocks = ids.reshape(-1, tok_rows, 2)
    chosen = jnp.sum((blocks == my_index).astype(jnp.float32), axis=2)
    before = jnp.triu(jnp.ones((tok_rows, tok_rows), jnp.float32), 1)
    ranking = jnp.dot(chosen, before)
    slot_ids = jnp.arange(slot_count, dtype=jnp.float32)[None, :, None]
    taken = chosen[:, None, :] * (ranking[:, None, :] == slot_ids).astype(jnp.float32)
    other = jnp.sum(blocks, axis=2) - my_index
    slot_other = jnp.sum(taken * other[:, None, :].astype(jnp.float32), axis=2)
    return (taken.astype(jnp.bfloat16), slot_other.reshape(-1).astype(jnp.int32))


def own_gate(logits, other, my_index):
    expert_range = jnp.arange(logits.shape[1], dtype=jnp.int32)[None]
    mine = jnp.sum(jnp.where(expert_range == my_index, logits, 0.0), axis=1, keepdims=True)
    theirs = jnp.sum(jnp.where(expert_range == other[:, None], logits, 0.0), axis=1, keepdims=True)
    return jax.nn.sigmoid(mine - theirs)


def pick_rows(taken, rows):
    blocks, slots, tokens = taken.shape
    picked = jnp.einsum(
        "bct,btd->bcd",
        taken,
        rows.reshape(blocks, tokens, -1),
        preferred_element_type=jnp.float32,
    )
    return picked.astype(jnp.bfloat16).reshape(blocks * slots, -1)


def return_rows(taken, rows):
    blocks, slots, tokens = taken.shape
    placed = jnp.einsum(
        "bct,bcd->btd",
        taken,
        rows.reshape(blocks, slots, -1),
        preferred_element_type=jnp.float32,
    )
    return placed.astype(jnp.bfloat16).reshape(blocks * tokens, -1)


def gather_all(rows):
    return lax.all_gather(rows, ("dp", "expert"), axis=0, tiled=True)


def scatter_all(rows):
    return lax.psum_scatter(rows, ("dp", "expert"), scatter_dimension=0, tiled=True)


def dispatch(rows):
    return lax.all_to_all(rows, "expert", split_axis=0, concat_axis=0, tiled=True)


def collect(rows):
    return lax.all_to_all(rows, "expert", split_axis=0, concat_axis=0, tiled=True)


def spread_rows(rows):
    return lax.all_gather(rows, "dp", axis=0, tiled=True)


def sum_rows(terms):
    return lax.psum_scatter(
        terms.astype(jnp.bfloat16), "dp", scatter_dimension=0, tiled=True
    ).astype(jnp.float32)


def send_rows(send_table, rows):
    return jnp.einsum(
        "ect,td->ecd", send_table.astype(jnp.bfloat16), rows, preferred_element_type=jnp.float32
    ).astype(jnp.bfloat16)


def per_device(
    tokens,
    cotangent,
    attention_routes,
    feedforward_routes,
    prefix_length,
    gain_attention,
    gain_feedforward,
    keyvalue_weight,
    router_weight,
    query_weight,
    output_weight,
    gate_weight,
    up_weight,
    down_weight,
):
    my_index = lax.axis_index("expert")
    group_size = lax.axis_size("expert")
    inputs = tokens[0].astype(jnp.float32)
    tok_rows = inputs.shape[0]
    model_width = inputs.shape[1]
    seq_total = tok_rows * group_size
    slot_count = 5 * 2 * tok_rows // (4 * group_size)
    query_width = HEADS * HEAD_DIM
    scaling = HEAD_DIM ** (-0.5)
    keyvalue_full, router_full, query_full, output_full = (
        lax.all_gather(keyvalue_weight, "dp", axis=0, tiled=True),
        lax.all_gather(router_weight, "dp", axis=0, tiled=True),
        lax.all_gather(query_weight[0], "dp", axis=0, tiled=True),
        lax.all_gather(output_weight[0], "dp", axis=0, tiled=True),
    )
    every_route = lax.all_gather(feedforward_routes[0], "dp", axis=0, tiled=True)
    cot_everyone = gather_all(cotangent[0])
    attention_cols = router_full[:, :group_size]
    feedforward_cols = router_full[:, group_size:]
    normed_attention, unit_attention, factor_attention = norm_parts(inputs, gain_attention)
    attention_in = normed_attention.astype(jnp.bfloat16)
    keyvalue_rows = jnp.dot(attention_in, keyvalue_full, preferred_element_type=jnp.float32).astype(
        jnp.bfloat16
    )
    keyvalue_seq = lax.all_gather(keyvalue_rows, "expert", axis=0, tiled=True)
    key_rows = keyvalue_seq[:, :query_width].reshape(seq_total, HEADS, HEAD_DIM)
    value_rows = keyvalue_seq[:, query_width:].reshape(seq_total, HEADS, HEAD_DIM)
    attend_table, attend_places, attend_matches = route_plan(
        attention_routes[0], my_index, group_size, tok_rows, slot_count
    )
    attend_logits = jnp.dot(attention_in, attention_cols, preferred_element_type=jnp.float32)
    attend_weights, attend_gate = pair_gates(attend_logits, attend_matches)
    arrived = dispatch(send_rows(attend_table, attention_in)).reshape(-1, model_width)
    queries = jnp.dot(arrived, query_full, preferred_element_type=jnp.float32).astype(jnp.bfloat16)
    queries = queries.reshape(-1, HEADS, HEAD_DIM)
    key_places = jnp.arange(seq_total, dtype=jnp.int32)
    allowed = (key_places[None, :] <= attend_places[:, None]) | (
        key_places[None, :] < prefix_length[0]
    )
    scores = (
        jnp.einsum("rhd,khd->hrk", queries, key_rows, preferred_element_type=jnp.float32) * scaling
    )
    scores = jnp.where(allowed[None], scores, NEG)
    row_max = jnp.max(scores, axis=2, keepdims=True)
    exponent = jnp.exp(scores - row_max)
    row_total = jnp.sum(exponent, axis=2, keepdims=True)
    log_total = row_max + jnp.log(row_total)
    attention_low = (exponent / row_total).astype(jnp.bfloat16)
    mixture = jnp.einsum(
        "hrk,khd->rhd", attention_low, value_rows, preferred_element_type=jnp.float32
    )
    mixture = mixture.astype(jnp.bfloat16).reshape(-1, query_width)
    attend_branch = jnp.dot(mixture, output_full, preferred_element_type=jnp.float32).astype(
        jnp.bfloat16
    )
    attend_returned = collect(attend_branch.reshape(group_size, slot_count, model_width))
    hidden = inputs + merge_back(attend_table, attend_gate, attend_returned)
    normed_feed, unit_feed, factor_feed = norm_parts(hidden, gain_feedforward)
    feed_in = normed_feed.astype(jnp.bfloat16)
    feed_ids = lax.dynamic_slice_in_dim(
        feedforward_routes[0], my_index * tok_rows, tok_rows, 0
    )
    feed_matches = expert_matches(feed_ids, group_size)
    feed_logits = jnp.dot(feed_in, feedforward_cols, preferred_element_type=jnp.float32)
    feed_weights, feed_gate = pair_gates(feed_logits, feed_matches)
    everyone = gather_all(feed_in)
    feed_taken, feed_pairs = expert_table(every_route, my_index, group_size, tok_rows, slot_count)
    pick = functools.partial(pick_rows, feed_taken)
    feed_rows = pick(everyone)
    cot_rows = pick(cot_everyone)
    row_logits = jnp.dot(feed_rows, feedforward_cols, preferred_element_type=jnp.float32)
    row_gate = own_gate(row_logits, feed_pairs, my_index)
    pre_gate = lax.dot_general(feed_rows, gate_weight[0], ACROSS, preferred_element_type=jnp.float32)
    pre_up = lax.dot_general(feed_rows, up_weight[0], ACROSS, preferred_element_type=jnp.float32)
    sigmoid_gate = jax.nn.sigmoid(pre_gate)
    act = pre_gate * sigmoid_gate * pre_up
    act_low = act.astype(jnp.bfloat16)
    act_scaled = (act * row_gate).astype(jnp.bfloat16)
    act_grad = lax.dot_general(cot_rows, down_weight[0], ACROSS, preferred_element_type=jnp.float32)
    slot_dgate = jnp.sum(act_low.astype(jnp.float32) * act_grad, axis=1)
    act_grad = act_grad * row_gate
    dgate_low = (act_grad * pre_up * sigmoid_gate * (1.0 + pre_gate * (1.0 - sigmoid_gate))).astype(
        jnp.bfloat16
    )
    dup_low = (act_grad * pre_gate * sigmoid_gate).astype(jnp.bfloat16)
    feed_dx = (
        jnp.dot(dgate_low, gate_weight[0], preferred_element_type=jnp.float32)
        + jnp.dot(dup_low, up_weight[0], preferred_element_type=jnp.float32)
    ).astype(jnp.bfloat16)
    feed_branch = jnp.dot(act_scaled, down_weight[0], preferred_element_type=jnp.float32).astype(
        jnp.bfloat16
    )
    grad_gate = lax.dot_general(dgate_low, feed_rows, DOWNWARD, preferred_element_type=jnp.float32)
    grad_up = lax.dot_general(dup_low, feed_rows, DOWNWARD, preferred_element_type=jnp.float32)
    grad_down = lax.dot_general(act_scaled, cot_rows, DOWNWARD, preferred_element_type=jnp.float32)
    token_dgate = jnp.einsum(
        "bct,bc->bt",
        feed_taken.astype(jnp.float32),
        slot_dgate.reshape(-1, slot_count),
        precision=HIGH,
    ).reshape(-1, 1)
    own_column = (jnp.arange(group_size) == my_index).astype(jnp.float32)[None]
    feed_dgate = scatter_all(token_dgate * own_column)
    feed_home = scatter_all(return_rows(feed_taken, feed_dx)).astype(jnp.float32)
    feed_sum = scatter_all(return_rows(feed_taken, feed_branch)).astype(jnp.float32)
    layer_output = hidden + feed_sum
    gradient = cotangent[0].astype(jnp.float32)
    feed_dlogits = gates_back(feed_dgate, feed_weights, feed_matches)
    feed_dnorm = feed_home + jnp.dot(
        feed_dlogits, feedforward_cols.astype(jnp.float32).T, precision=HIGH
    )
    grad_gain_feed = jnp.sum(feed_dnorm * unit_feed, axis=0)
    hidden_grad = gradient + norm_back(feed_dnorm, gain_feedforward, unit_feed, factor_feed)
    attend_cot, attend_dgate = branch_cotangent(
        attend_table, attend_gate, attend_returned, hidden_grad
    )
    attend_dlogits = gates_back(attend_dgate, attend_weights, attend_matches)
    attend_cot_rows = dispatch(attend_cot).reshape(-1, model_width)
    dmixture = lax.dot_general(
        attend_cot_rows, output_full, ACROSS, preferred_element_type=jnp.float32
    )
    dmixture = dmixture.astype(jnp.bfloat16).reshape(-1, HEADS, HEAD_DIM)
    grad_projection = lax.dot_general(
        mixture, attend_cot_rows, DOWNWARD, preferred_element_type=jnp.float32
    )
    scores_again = (
        jnp.einsum("rhd,khd->hrk", queries, key_rows, preferred_element_type=jnp.float32) * scaling
    )
    attention = jnp.where(allowed[None], jnp.exp(scores_again - log_total), 0.0)
    attention_again = attention.astype(jnp.bfloat16)
    dattention = jnp.einsum(
        "rhd,khd->hrk", dmixture, value_rows, preferred_element_type=jnp.float32
    )
    row_dot = jnp.sum(attention * dattention, axis=2, keepdims=True)
    dscores = (attention * (dattention - row_dot)).astype(jnp.bfloat16)
    dqueries = (
        jnp.einsum("hrk,khd->rhd", dscores, key_rows, preferred_element_type=jnp.float32) * scaling
    )
    dqueries = dqueries.astype(jnp.bfloat16).reshape(-1, query_width)
    dkeys = (
        jnp.einsum("hrk,rhd->khd", dscores, queries, preferred_element_type=jnp.float32) * scaling
    )
    dvalues = jnp.einsum(
        "hrk,rhd->khd", attention_again, dmixture, preferred_element_type=jnp.float32
    )
    grad_query = lax.dot_general(arrived, dqueries, DOWNWARD, preferred_element_type=jnp.float32)
    attend_dx = lax.dot_general(dqueries, query_full, ACROSS, preferred_element_type=jnp.float32)
    keyvalue_terms = jnp.concatenate(
        [dkeys.reshape(seq_total, query_width), dvalues.reshape(seq_total, query_width)], axis=1
    ).reshape(group_size, tok_rows, 2 * query_width)
    attend_home, keyvalue_home = (
        lax.all_to_all(
            attend_dx.reshape(group_size, slot_count, model_width).astype(jnp.bfloat16),
            "expert",
            split_axis=0,
            concat_axis=0,
            tiled=True,
        ).astype(jnp.float32),
        lax.all_to_all(
            keyvalue_terms.astype(jnp.bfloat16), "expert", split_axis=0, concat_axis=0, tiled=True
        ).astype(keyvalue_terms.dtype),
    )
    dkeyvalue = jnp.sum(keyvalue_home, axis=0).astype(jnp.bfloat16)
    attend_dnorm = (
        jnp.einsum("ect,ecd->td", attend_table, attend_home, precision=HIGH)
        + lax.dot_general(dkeyvalue, keyvalue_full, ACROSS, preferred_element_type=jnp.float32)
        + jnp.dot(attend_dlogits, attention_cols.astype(jnp.float32).T, precision=HIGH)
    )
    grad_keyvalue = lax.dot_general(
        attention_in, dkeyvalue, DOWNWARD, preferred_element_type=jnp.float32
    )
    grad_router = jnp.concatenate(
        [
            jnp.dot(attention_in.astype(jnp.float32).T, attend_dlogits, precision=HIGH),
            jnp.dot(feed_in.astype(jnp.float32).T, feed_dlogits, precision=HIGH),
        ],
        axis=1,
    )
    grad_gain_attend = jnp.sum(attend_dnorm * unit_attention, axis=0)
    grad_tokens = hidden_grad + norm_back(
        attend_dnorm, gain_attention, unit_attention, factor_attention
    )
    reduced = (
        lax.psum_scatter(
            grad_keyvalue.astype(jnp.bfloat16), "dp", scatter_dimension=0, tiled=True
        ).astype(jnp.float32),
        lax.psum_scatter(
            grad_router.astype(jnp.bfloat16), "dp", scatter_dimension=0, tiled=True
        ).astype(jnp.float32),
        lax.psum_scatter(
            grad_query.astype(jnp.bfloat16), "dp", scatter_dimension=0, tiled=True
        ).astype(jnp.float32),
        lax.psum_scatter(
            grad_projection.astype(jnp.bfloat16), "dp", scatter_dimension=0, tiled=True
        ).astype(jnp.float32),
        lax.psum_scatter(
            grad_gain_attend.astype(jnp.bfloat16), "dp", scatter_dimension=0, tiled=True
        ).astype(jnp.float32),
        lax.psum_scatter(
            grad_gain_feed.astype(jnp.bfloat16), "dp", scatter_dimension=0, tiled=True
        ).astype(jnp.float32),
    )
    shared = (
        lax.psum(reduced[0].astype(jnp.bfloat16), "expert").astype(jnp.float32),
        lax.psum(reduced[1].astype(jnp.bfloat16), "expert").astype(jnp.float32),
        lax.psum(reduced[4].astype(jnp.bfloat16), "expert").astype(jnp.float32),
        lax.psum(reduced[5].astype(jnp.bfloat16), "expert").astype(jnp.float32),
    )
    return (
        layer_output.astype(jnp.bfloat16)[None],
        grad_tokens[None],
        shared[2],
        shared[3],
        shared[0],
        shared[1],
        reduced[2][None],
        reduced[3][None],
        grad_gate[None],
        grad_up[None],
        grad_down[None],
    )


MESH = pl.DeviceIdType.MESH
CHIPS_Z = 4
TURNS = ((3, 2, 1, 0), (3, 0, 2, 1), (0, 3, 1, 2), (0, 1, 2, 3))


class Place:
    def __init__(self):
        self.dp, self.expert = lax.axis_index("dp"), lax.axis_index("expert")
        self.at = {
            "z": self.dp // 2,
            "y": self.dp % 2,
            "x": self.expert // 2,
            "c": self.expert % 2,
        }

    def across(self, axis):
        back = 1 - 2 * self.at[axis]
        if axis == "c":
            return (self.dp, self.expert + back)
        if axis == "x":
            return (self.dp, self.expert + 2 * back)
        return (self.dp + back, self.expert)

    def along(self, step):
        return (self.dp + 2 * step, self.expert)

    def block(self, whose, z, flips):
        at = {a: self.at[a] + flips.get(a, 0) * (1 - 2 * self.at[a]) for a in "xyc"}
        dp, expert = z * 2 + at["y"], at["x"] * 2 + at["c"]
        return {"all": dp * 4 + expert, "dp": dp, "expert": expert}[whose]


def enter(place, axes, others=()):
    barrier, count = pltpu.get_barrier_semaphore(), 0
    for device, condition in others:

        def greet(device=device):
            pl.semaphore_signal(barrier, inc=1, device_id=device, device_id_type=MESH)

        on(condition, greet)
        count = count + (1 if condition is None else condition.astype(jnp.int32))
    for axis in axes:
        if axis != "z":
            pl.semaphore_signal(
                barrier, inc=1, device_id=place.across(axis), device_id_type=MESH
            )
            count += 1
    if "z" in axes:
        z = place.at["z"]
        for step, there in ((-1, z > 0), (1, z < CHIPS_Z - 1)):

            @pl.when(there)
            def _(step=step):
                pl.semaphore_signal(
                    barrier, inc=1, device_id=place.along(step), device_id_type=MESH
                )

            count = count + there.astype(jnp.int32)
    pl.semaphore_wait(barrier, count)


def on(condition, action):
    if condition is None:
        action()
    else:
        pl.when(condition)(action)


def both(a, b):
    return b if a is None else a if b is None else a & b


class Post:
    def __init__(self, sems, place):
        self.sems, self.place, self.sent = sems, place, []

    def send(self, source, target, arrival, device, condition=None):
        number = len(self.sent)

        def copy():
            return pltpu.make_async_remote_copy(
                src_ref=source,
                dst_ref=target,
                send_sem=self.sems.at[number],
                recv_sem=arrival,
                device_id=device,
                device_id_type=MESH,
            )

        self.sent.append((condition, copy))
        on(condition, lambda: copy().start())

    def arrived(self, target, arrival):
        pltpu.make_async_remote_copy(
            src_ref=target,
            dst_ref=target,
            send_sem=self.sems.at[0],
            recv_sem=arrival,
            device_id=self.place.across("c"),
            device_id_type=MESH,
        ).wait_recv()

    def close(self):
        for condition, copy in self.sent:
            on(condition, lambda copy=copy: copy().wait_send())


FLIPS = {"x": 4, "y": 2, "c": 1}


def gather_plan(jobs, place, post, sources, targets, arrive_sems, own_sems):
    z_here = place.at["z"]
    line = 0
    waves, owns, starts = {}, [], []
    for j, (whose, rows, pieces) in enumerate(jobs):
        own = pltpu.make_async_copy(
            sources[j],
            targets[j].at[pl.ds(place.block(whose, z_here, {}) * rows, rows)],
            own_sems.at[j],
        )
        owns.append(own)
        begin = [own.start]
        for first, length, order in pieces:
            def part(z, flips, j=j, whose=whose, rows=rows, first=first, length=length):
                at = place.block(whose, z, flips) * rows + first
                return targets[j].at[pl.ds(at, length)]

            def mark(z, flips, line=line):
                return arrive_sems.at[line, z * 8 + sum(FLIPS[a] * v for a, v in flips.items())]

            def hand_on(source, z, flips, depth, side, wave, condition, order=order, part=part, mark=mark):
                for axis in order[max(depth, 0) :]:
                    if axis == "z" and (depth < 0 or order[depth] != "z"):
                        for step in (1, -1):
                            there = (z_here < CHIPS_Z - 1) if step > 0 else (z_here > 0)
                            post.send(source, part(z, flips), mark(z, flips), place.along(step), both(condition, there))
                    elif axis == "z":
                        there = (z_here < CHIPS_Z - 1) if side > 0 else (z_here > 0)
                        post.send(source, part(z, flips), mark(z, flips), place.along(side), both(condition, there))
                    elif depth < 0 or axis != order[depth]:
                        seen = dict(flips)
                        seen[axis] = 1
                        post.send(source, part(z, flips), mark(z, seen), place.across(axis), condition)

            def come(z, flips, depth, side, hops, wave, condition, order=order, part=part, mark=mark, hand_on=hand_on):
                def act():
                    on(condition, lambda: post.arrived(part(z, flips), mark(z, flips)))
                    hand_on(part(z, flips), z, flips, depth, side, wave, condition)

                waves.setdefault(wave, []).append(act)
                spread(z, flips, depth, side, hops, wave, condition, order, come)

            begin.append(
                lambda hand_on=hand_on, j=j, first=first, length=length: hand_on(
                    sources[j].at[pl.ds(first, length)], z_here, {}, -1, 0, 0, None
                )
            )
            spread(z_here, {}, -1, 0, 0, 0, None, order, come)
            line += 1
        starts.append(begin)
    return starts, waves, owns


def gather_kernel(jobs, axes, filler, *refs):
    count = len(jobs)
    sources, given, refs = refs[:count], refs[count : count + filler.operands], refs[count + filler.operands :]
    targets, made, refs = refs[:count], refs[count : count + filler.results], refs[count + filler.results :]
    send_sems, arrive_sems, own_sems = refs[:3]
    own = refs[3:]
    place = Place()
    enter(place, axes)
    post = Post(send_sems, place)
    starts, waves, owns = gather_plan(jobs, place, post, sources, targets, arrive_sems, own_sems)
    for act in sum(starts, []):
        act()
    steps, done = filler.start(given, made, own), 0
    for number, wave in enumerate(sorted(waves)):
        share = steps * (number + 1) // len(waves)
        filler.run(given, made, own, done, share)
        done = share
        for act in waves[wave]:
            act()
    for copy in owns:
        copy.wait()
    filler.end(given, made, own)
    post.close()


def spread(z, flips, depth, side, hops, wave, condition, order, come):
    z_here = lax.axis_index("dp") // 2
    for later in range(max(depth, 0), len(order)):
        axis = order[later]
        if axis == "z":
            if depth >= 0 and order[depth] == "z":
                if hops < CHIPS_Z - 1:
                    far = hops + 1
                    there = (z_here >= far) if side > 0 else (z_here + far < CHIPS_Z)
                    come(z_here - side * far, flips, later, side, far, wave + 1, there)
            else:
                for step in (1, -1):
                    there = (z_here >= 1) if step > 0 else (z_here + 1 < CHIPS_Z)
                    come(z_here - step, flips, later, step, 1, wave + 1, both(condition, there))
        elif later > depth:
            seen = dict(flips)
            seen[axis] = 1
            come(z, seen, later, 0, 0, wave + 1, condition)


class Nothing:
    operands = results = rooms = 0
    turns = 12
    shapes, scratch = [], []

    def start(self, given, made, own):
        return 0

    def run(self, given, made, own, first, last):
        pass

    def end(self, given, made, own):
        pass


def gather(jobs, collective_id, name, filler=Nothing(), operands=()):
    arrays = [rows for rows, _, _ in jobs]
    sizes = {"all": 32, "dp": 8, "expert": 4}
    plan = tuple((whose, rows.shape[0], pieces) for rows, whose, pieces in jobs)
    axes = "".join(a for a in "cxyz" if any(a in order for _, _, ps in plan for _, _, order in ps))
    lines = sum(len(ps) for _, _, ps in plan)
    hbm = pl.BlockSpec(memory_space=pltpu.HBM)
    return pl.pallas_call(
        functools.partial(gather_kernel, plan, axes, filler),
        out_shape=[
            jax.ShapeDtypeStruct((sizes[whose] * r.shape[0], r.shape[1]), r.dtype)
            for r, whose, _ in jobs
        ]
        + filler.shapes,
        in_specs=[hbm] * (len(jobs) + len(operands)),
        out_specs=[hbm] * (len(jobs) + filler.results),
        scratch_shapes=[
            pltpu.SemaphoreType.DMA((110 * lines,)),
            pltpu.SemaphoreType.DMA((lines, 32)),
            pltpu.SemaphoreType.DMA((len(jobs),)),
        ]
        + filler.scratch,
        compiler_params=pltpu.CompilerParams(
            collective_id=collective_id, has_side_effects=True, vmem_limit_bytes=48 * 2**20
        ),
        name=name,
    )(*arrays, *operands)


def add_into(target, terms, length):
    @pl.loop(0, length // 16)
    def _(r):
        at = pl.ds(pl.multiple_of(r * 16, 16), 16)
        total = target[at, :].astype(jnp.float32)
        for term in terms:
            total = total + term[at, :].astype(jnp.float32)
        target[at, :] = total.astype(jnp.bfloat16)


def scatter_rooms(rows, width, order):
    steps, turns = len(order.replace("z", "")), CHIPS_Z if "z" in order else 1
    blocks = [turns * 2 ** (steps - 1)]
    blocks += [turns * 2 ** (steps - 1 - stage) for stage in range(steps)]
    if "z" in order:
        blocks.append(CHIPS_Z + 1)
    return [pltpu.VMEM((n, rows, width), jnp.bfloat16) for n in blocks]


def scatter_sems(order, pieces):
    steps, turns = len(order.replace("z", "")), CHIPS_Z if "z" in order else 1
    return [
        pltpu.SemaphoreType.DMA((turns * 2 ** (steps - 1),)),
        pltpu.SemaphoreType.DMA((pieces, steps, turns * 2 ** (steps - 1))),
        pltpu.SemaphoreType.DMA((pieces, CHIPS_Z + 1)),
    ]


def scatter_plan(whose, rows, pieces, place, post, source, rooms, sems):
    flat = [order.replace("z", "") for _, _, order in pieces]
    steps = len(flat[0])
    lined = "z" in pieces[0][2]
    turns = CHIPS_Z if lined else 1
    acc, bins, line = rooms[0], rooms[1 : 1 + steps], rooms[-1]
    load_sems, bin_sems, line_sems = sems
    z_here = place.at["z"]
    if lined:
        turn = [
            sum((z_here == z).astype(jnp.int32) * seq[k] for z, seq in enumerate(TURNS))
            for k in range(CHIPS_Z)
        ]
    else:
        turn = [z_here]
    slot_z = lambda k: turn[k] if lined else 0
    keep = 2 ** (steps - 1)
    names = sorted(flat[0][1:])
    loads = {}
    for k in range(turns):
        for n in reversed(range(keep)):
            flips = {a: (n >> i) & 1 for i, a in enumerate(names)}
            at = slot_z(k) * keep + n
            loads[k, n] = pltpu.make_async_copy(
                source.at[pl.ds(place.block(whose, turn[k], flips) * rows, rows)],
                acc.at[at],
                load_sems.at[at],
            )
    loaded = set()

    def mine(p, ref):
        first, length, _ = pieces[p]
        return ref.at[pl.ds(first, length)]

    def code_after(p, stage, flips):
        return sum(flips.get(a, 0) << i for i, a in enumerate(flat[p][stage + 1 :]))

    def gathered(p, k, stage, flips):
        n = sum(flips.get(a, 0) << i for i, a in enumerate(names))
        if (k, n) not in loaded:
            loads[k, n].wait()
            loaded.add((k, n))
        terms = []
        for before in range(stage):
            at = slot_z(k) * 2 ** (steps - 1 - before) + code_after(p, before, flips)
            ref = mine(p, bins[before].at[at])
            post.arrived(ref, bin_sems.at[p, before, at])
            terms.append(ref)
        block = mine(p, acc.at[slot_z(k) * keep + n])
        add_into(block, terms, pieces[p][1])
        return block

    def leave(k, stage):
        for code in reversed(range(2 ** (steps - 1 - stage))):
            for p in range(len(pieces)):
                flips = {a: (code >> i) & 1 for i, a in enumerate(flat[p][stage + 1 :])}
                flips[flat[p][stage]] = 1
                if stage == 0:
                    at = place.block(whose, turn[k], flips) * rows + pieces[p][0]
                    block = source.at[pl.ds(at, pieces[p][1])]
                else:
                    block = gathered(p, k, stage, flips)
                at = slot_z(k) * 2 ** (steps - 1 - stage) + code
                post.send(
                    block,
                    mine(p, bins[stage].at[at]),
                    bin_sems.at[p, stage, at],
                    place.across(flat[p][stage]),
                )

    def settle(k):
        for p in range(len(pieces)):
            block = gathered(p, k, steps, {})
            if not lined or k == turns - 1:
                continue
            t = turn[k]
            right = t > z_here

            def pass_on(p=p, t=t, block=block):
                ref = mine(p, line.at[t])
                post.arrived(ref, line_sems.at[p, t])
                add_into(block, [ref], pieces[p][1])

            pl.when((right & (z_here > 0)) | (~right & (z_here < CHIPS_Z - 1)))(pass_on)
            slot = jnp.where(t == z_here - 1, CHIPS_Z, t)
            post.send(
                block,
                mine(p, line.at[slot]),
                line_sems.at[p, slot],
                place.along(jnp.where(right, 1, -1)),
            )

    def finish(p):
        block = mine(p, acc.at[z_here * keep if lined else 0])
        if lined:
            for slot, there in ((z_here, z_here > 0), (CHIPS_Z, z_here < CHIPS_Z - 1)):

                def last(slot=slot):
                    ref = mine(p, line.at[slot])
                    post.arrived(ref, line_sems.at[p, slot])
                    add_into(block, [ref], pieces[p][1])

                pl.when(there)(last)
        return block

    works = [(-1, lambda k=k: leave(k, 0)) for k in range(turns)]
    for time in range(turns + steps):
        for stage in range(1, steps + 1):
            k = time - stage + 1
            if 0 <= k < turns:
                act = settle if stage == steps else lambda k, stage=stage: leave(k, stage)
                works.append((time, lambda k=k, act=act: act(k)))
    return list(loads.values()), works, finish


def sends_of(order, pieces):
    steps, turns = len(order.replace("z", "")), CHIPS_Z if "z" in order else 1
    return pieces * (turns * 2**steps + 4)


def widen(target, block, length):
    @pl.loop(0, length // 16)
    def _(r):
        at = pl.ds(pl.multiple_of(r * 16, 16), 16)
        target[at, :] = block[at, :].astype(jnp.float32)


def scatter_kernel(whose, rows, pieces, columns, filler, source, *refs):
    source = source.at[:, pl.ds(*columns)]
    given, refs = refs[: filler.operands], refs[filler.operands :]
    result, made, refs = refs[0], refs[1 : 1 + filler.results], refs[1 + filler.results :]
    rooms, refs = refs[: len(refs) - 4 - filler.rooms], refs[len(refs) - 4 - filler.rooms :]
    send_sems, sems, own = refs[0], refs[1:4], refs[4:]
    place = Place()
    post = Post(send_sems, place)
    loads, works, finish = scatter_plan(whose, rows, pieces, place, post, source, rooms, sems)
    for load in loads:
        load.start()
    enter(place, "".join(a for a in "cxyz" if a in pieces[0][2]))
    steps = filler.start(given, made, own)
    slots = [number for number, (time, _) in enumerate(works) if time >= 0]
    slots = slots[:: -(-len(slots) // filler.turns)]
    done = 0
    for number, (_, act) in enumerate(works):
        act()
        if number in slots:
            share = steps * (slots.index(number) + 1) // len(slots)
            filler.run(given, made, own, done, share)
            done = share
    for p in range(len(pieces)):
        first, length, _ = pieces[p]
        widen(result.at[pl.ds(first, length)], finish(p), length)
    filler.end(given, made, own)
    post.close()


class WeightGrads(Nothing):
    operands, results, rooms = 4, 3, 6
    TILE, CHUNK = 256, 512

    def __init__(self, rows, padded, hidden, width):
        self.chunks = rows // self.CHUNK
        self.each = padded // self.TILE
        self.short = hidden - (self.each - 1) * self.TILE
        self.tiles = (2 * self.each, self.each)
        self.shapes = [jax.ShapeDtypeStruct((hidden, width), jnp.float32)] * 3
        self.scratch = [
            pltpu.VMEM((2, self.CHUNK, self.TILE), jnp.bfloat16),
            pltpu.VMEM((2, self.CHUNK, width), jnp.bfloat16),
            pltpu.VMEM((self.TILE, width), jnp.float32),
            pltpu.VMEM((self.TILE, width), jnp.float32),
            pltpu.SemaphoreType.DMA((2, 2)),
            pltpu.SemaphoreType.DMA((2,)),
        ]

    def copies(self, given, own, step, second):
        tile, chunk = step // self.chunks - (self.tiles[0] if second else 0), step % self.chunks
        slot = step % 2
        rows = pl.ds(pl.multiple_of(chunk * self.CHUNK, self.CHUNK), self.CHUNK)
        cols = pl.ds(pl.multiple_of(tile * self.TILE, self.TILE), self.TILE)
        left, right = given[2 * second], given[2 * second + 1]
        return [
            pltpu.make_async_copy(left.at[rows, cols], own[0].at[slot], own[4].at[slot, 0]),
            pltpu.make_async_copy(right.at[rows], own[1].at[slot], own[4].at[slot, 1]),
        ]

    def fetch(self, given, own, step, start):
        edge = self.tiles[0] * self.chunks
        for second in (0, 1):

            @pl.when((step >= edge) if second else (step < edge))
            def _(second=second):
                for copy in self.copies(given, own, step, second):
                    copy.start() if start else copy.wait()

    def put(self, made, own, tile, parity, start):
        row = (tile % self.each) * self.TILE
        for result in range(3):
            for last in (0, 1):
                length = self.short if last else self.TILE
                at_end = (tile % self.each) == self.each - 1

                @pl.when((tile // self.each == result) & (at_end if last else ~at_end))
                def _(result=result, length=length):
                    copy = pltpu.make_async_copy(
                        own[2 + parity].at[pl.ds(0, length)],
                        made[result].at[pl.ds(pl.multiple_of(row, self.TILE), length)],
                        own[5].at[parity],
                    )
                    copy.start() if start else copy.wait()

    def start(self, given, made, own):
        self.fetch(given, own, jnp.int32(0), True)
        return sum(self.tiles) * self.chunks

    def run(self, given, made, own, first, last):
        total = sum(self.tiles) * self.chunks

        @pl.loop(first, last)
        def _(step):
            tile, chunk = step // self.chunks, step % self.chunks

            @pl.when(step + 1 < total)
            def _():
                self.fetch(given, own, step + 1, True)

            self.fetch(given, own, step, False)
            part = lax.dot_general(
                own[0][step % 2], own[1][step % 2], DOWNWARD, preferred_element_type=jnp.float32
            )
            for parity in (0, 1):

                @pl.when(tile % 2 == parity)
                def _(parity=parity):
                    acc = own[2 + parity]

                    @pl.when(chunk == 0)
                    def _():
                        @pl.when(tile >= 2)
                        def _():
                            self.put(made, own, tile - 2, parity, False)

                        acc[...] = part

                    @pl.when(chunk > 0)
                    def _():
                        acc[...] += part

                    @pl.when(chunk == self.chunks - 1)
                    def _():
                        self.put(made, own, tile, parity, True)

    def end(self, given, made, own):
        tiles = sum(self.tiles)
        for tile in (tiles - 2, tiles - 1):
            self.put(made, own, jnp.int32(tile), tile % 2, False)


class LowGrad(Nothing):
    operands, results, rooms = 2, 1, 5
    TILE = 256

    def __init__(self, rows, left, width, turns):
        self.tiles, self.width, self.turns = left // self.TILE, width, turns
        low = jnp.bfloat16
        self.shapes = [jax.ShapeDtypeStruct((left, width), low)]
        self.scratch = [
            pltpu.VMEM((2, rows, self.TILE), low),
            pltpu.VMEM((rows, width), low),
            pltpu.VMEM((2, self.TILE, width), low),
            pltpu.SemaphoreType.DMA((3,)),
            pltpu.SemaphoreType.DMA((2,)),
        ]

    def left(self, given, own, tile):
        at = pl.ds(pl.multiple_of(tile * self.TILE, self.TILE), self.TILE)
        return pltpu.make_async_copy(given[0].at[:, at], own[0].at[tile % 2], own[3].at[tile % 2])

    def right(self, given, own):
        return pltpu.make_async_copy(given[1], own[1], own[3].at[2])

    def put(self, made, own, tile):
        rows = pl.ds(pl.multiple_of(tile * self.TILE, self.TILE), self.TILE)
        return pltpu.make_async_copy(own[2].at[tile % 2], made[0].at[rows], own[4].at[tile % 2])

    def start(self, given, made, own):
        self.right(given, own).start()
        self.left(given, own, jnp.int32(0)).start()
        return self.tiles

    def run(self, given, made, own, first, last):
        if first == last:
            return
        if first == 0:
            self.right(given, own).wait()

        @pl.loop(first, last)
        def _(tile):
            slot = tile % 2

            @pl.when(tile + 1 < self.tiles)
            def _():
                self.left(given, own, tile + 1).start()

            self.left(given, own, tile).wait()

            @pl.when(tile >= 2)
            def _():
                self.put(made, own, tile - 2).wait()

            half = self.width // 2
            for part in (0, 1):
                cols = slice(part * half, (part + 1) * half)
                own[2][slot, :, cols] = lax.dot_general(
                    own[0][slot], own[1][:, cols], DOWNWARD, preferred_element_type=jnp.float32
                ).astype(jnp.bfloat16)
            self.put(made, own, tile).start()

    def end(self, given, made, own):
        for tile in (self.tiles - 2, self.tiles - 1):
            self.put(made, own, jnp.int32(tile)).wait()


class RowGrads(Nothing):
    operands, results, rooms = 3, 1, 7
    TILE, turns = 256, 4

    def __init__(self, rows, depth, width):
        self.tiles, self.width = width // self.TILE, width
        low = jnp.bfloat16
        self.shapes = [jax.ShapeDtypeStruct((rows, width + 128), low)]
        self.scratch = [
            pltpu.VMEM((rows, depth), low),
            pltpu.VMEM((2, self.TILE, depth), low),
            pltpu.VMEM((2, rows, self.TILE), low),
            pltpu.VMEM((rows, 128), jnp.float32),
            pltpu.VMEM((rows, 128), low),
            pltpu.SemaphoreType.DMA((4,)),
            pltpu.SemaphoreType.DMA((3,)),
        ]

    def whole(self, given, own):
        return [
            pltpu.make_async_copy(given[0], own[0], own[5].at[2]),
            pltpu.make_async_copy(given[2], own[3], own[5].at[3]),
        ]

    def right(self, given, own, tile):
        at = pl.ds(pl.multiple_of(tile * self.TILE, self.TILE), self.TILE)
        return pltpu.make_async_copy(given[1].at[at], own[1].at[tile % 2], own[5].at[tile % 2])

    def put(self, made, own, tile):
        at = pl.ds(pl.multiple_of(tile * self.TILE, self.TILE), self.TILE)
        return pltpu.make_async_copy(own[2].at[tile % 2], made[0].at[:, at], own[6].at[tile % 2])

    def extra(self, made, own):
        return pltpu.make_async_copy(own[4], made[0].at[:, pl.ds(self.width, 128)], own[6].at[2])

    def start(self, given, made, own):
        for copy in self.whole(given, own):
            copy.start()
        self.right(given, own, jnp.int32(0)).start()
        return self.tiles

    def run(self, given, made, own, first, last):
        if first == last:
            return
        if first == 0:
            for copy in self.whole(given, own):
                copy.wait()
            own[4][...] = own[3][...].astype(jnp.bfloat16)
            self.extra(made, own).start()

        @pl.loop(first, last)
        def _(tile):
            slot = tile % 2

            @pl.when(tile + 1 < self.tiles)
            def _():
                self.right(given, own, tile + 1).start()

            self.right(given, own, tile).wait()

            @pl.when(tile >= 2)
            def _():
                self.put(made, own, tile - 2).wait()

            own[2][slot] = lax.dot_general(
                own[0][...], own[1][slot], ACROSS, preferred_element_type=jnp.float32
            ).astype(jnp.bfloat16)
            self.put(made, own, tile).start()

    def end(self, given, made, own):
        self.extra(made, own).wait()
        for tile in (self.tiles - 2, self.tiles - 1):
            self.put(made, own, jnp.int32(tile)).wait()


class InTurn(Nothing):
    def __init__(self, one, other):
        self.parts = (one, other)
        self.operands = one.operands + other.operands
        self.results = one.results + other.results
        self.rooms = one.rooms + other.rooms
        self.turns = one.turns + other.turns
        self.shapes, self.scratch = one.shapes + other.shapes, one.scratch + other.scratch

    def split(self, given, made, own):
        one = self.parts[0]
        return (
            (given[: one.operands], made[: one.results], own[: one.rooms]),
            (given[one.operands :], made[one.results :], own[one.rooms :]),
        )

    def start(self, *refs):
        self.steps = [part.start(*own) for part, own in zip(self.parts, self.split(*refs))]
        return self.parts[0].turns + self.parts[1].turns

    def run(self, given, made, own, first, last):
        edge = self.parts[0].turns
        for n, (part, refs) in enumerate(zip(self.parts, self.split(given, made, own))):
            low, high = (0, edge) if n == 0 else (edge, edge + part.turns)
            begin, end = max(first, low) - low, min(last, high) - low
            if begin < end:
                steps = self.steps[n]
                part.run(*refs, steps * begin // part.turns, steps * end // part.turns)

    def end(self, *refs):
        for part, own in zip(self.parts, self.split(*refs)):
            part.end(*own)


def scatter(array, whose, pieces, collective_id, name, filler=Nothing(), operands=(), columns=None):
    size = {"all": 32, "dp": 8, "expert": 4}[whose]
    columns = columns or (0, array.shape[1])
    rows, width = array.shape[0] // size, columns[1]
    order, count = pieces[0][2], len(pieces)
    hbm = pl.BlockSpec(memory_space=pltpu.HBM)
    out = pl.pallas_call(
        functools.partial(scatter_kernel, whose, rows, pieces, columns, filler),
        out_shape=[jax.ShapeDtypeStruct((rows, width), jnp.float32)] + filler.shapes,
        in_specs=[hbm] * (1 + len(operands)),
        out_specs=[pl.BlockSpec(memory_space=pltpu.VMEM)] + [hbm] * filler.results,
        scratch_shapes=scatter_rooms(rows, width, order)
        + [pltpu.SemaphoreType.DMA((sends_of(order, count),))]
        + scatter_sems(order, count)
        + filler.scratch,
        compiler_params=pltpu.CompilerParams(
            collective_id=collective_id, has_side_effects=True, vmem_limit_bytes=63 * 2**20
        ),
        name=name,
    )(array, *operands)
    return out if filler.results else out[0]


def sum_with_output_kernel(rows, pieces, out_rows, out_pieces, filler, source, out_grad, *refs):
    given, refs = refs[: filler.operands], refs[filler.operands :]
    result, output, refs = refs[0], refs[1], refs[2:]
    made, refs = refs[: filler.results], refs[filler.results :]
    count = len(scatter_rooms(rows, 128, pieces[0][2]))
    rooms, refs = refs[:count], refs[count:]
    count = len(scatter_rooms(rows, 128, out_pieces[0][2]))
    out_rooms, refs = refs[:count], refs[count:]
    dealt, send_sems, deal_sems = refs[:3]
    sems, out_sems, own = refs[3:6], refs[6:9], refs[9:]
    place = Place()
    post = Post(send_sems, place)
    z, e = place.at["z"], place.expert
    partner, moves = (e * 2 + place.at["y"], z), z != e
    loads, works, finish = scatter_plan(
        "expert", rows, pieces, place, post, source, rooms, sems
    )
    out_loads, out_works, out_finish = scatter_plan(
        "dp", out_rows, out_pieces, place, post, out_grad, out_rooms, out_sems
    )
    for load in loads + out_loads:
        load.start()
    enter(place, "cxyz", [(partner, moves)])
    steps = filler.start(given, made, own)
    times = sorted({time for time, _ in works + out_works})
    turns = [time for time in times if time >= 0]
    done = 0
    for time in times:
        for plan in (works, out_works):
            for at, act in plan:
                if at == time:
                    act()
        if time >= 0:
            share = steps * (turns.index(time) + 1) // len(turns)
            filler.run(given, made, own, done, share)
            done = share
    for p in range(len(out_pieces)):
        first, length, _ = out_pieces[p]
        at = pl.ds(first, length)
        post.send(out_finish(p), dealt.at[at], deal_sems.at[p], partner, moves)
    for p in range(len(pieces)):
        first, length, _ = pieces[p]
        widen(result.at[pl.ds(first, length)], finish(p), length)
    filler.end(given, made, own)
    for p in range(len(out_pieces)):
        first, length, _ = out_pieces[p]
        at = pl.ds(first, length)

        def came(p=p, at=at, length=length):
            post.arrived(dealt.at[at], deal_sems.at[p])
            widen(output.at[at], dealt.at[at], length)

        pl.when(moves)(came)
        pl.when(~moves)(
            lambda at=at, length=length: widen(output.at[at], out_rooms[0].at[z, at], length)
        )
    post.close()


def sum_with_output(array, pieces, out_grad, out_pieces, collective_id, filler, operands):
    rows, width = array.shape[0] // 4, array.shape[1]
    out_rows, out_width = out_grad.shape[0] // 8, out_grad.shape[1]
    order, out_order = pieces[0][2], out_pieces[0][2]
    hbm = pl.BlockSpec(memory_space=pltpu.HBM)
    vmem = pl.BlockSpec(memory_space=pltpu.VMEM)
    shape = jax.ShapeDtypeStruct
    sends = sends_of(order, len(pieces)) + sends_of(out_order, len(out_pieces)) + len(out_pieces)
    return pl.pallas_call(
        functools.partial(
            sum_with_output_kernel, rows, pieces, out_rows, out_pieces, filler
        ),
        out_shape=[
            shape((rows, width), jnp.float32),
            shape((out_rows, out_width), jnp.float32),
        ]
        + filler.shapes,
        in_specs=[hbm] * (2 + len(operands)),
        out_specs=[vmem] * 2 + [hbm] * filler.results,
        scratch_shapes=scatter_rooms(rows, width, order)
        + scatter_rooms(out_rows, out_width, out_order)
        + [
            pltpu.VMEM((out_rows, out_width), jnp.bfloat16),
            pltpu.SemaphoreType.DMA((sends,)),
            pltpu.SemaphoreType.DMA((len(out_pieces),)),
        ]
        + scatter_sems(order, len(pieces))
        + scatter_sems(out_order, len(out_pieces))
        + filler.scratch,
        compiler_params=pltpu.CompilerParams(
            collective_id=collective_id, has_side_effects=True, vmem_limit_bytes=63 * 2**20
        ),
        name="sum_attention_back",
    )(array, out_grad, *operands)


def sum_weights_kernel(rows, pieces, in_grad, query, keyvalue, *refs):
    count = len(scatter_rooms(rows, 128, pieces[0][2]))
    rooms = refs[:count]
    dealt, shared, send_sems, deal_sems = refs[count : count + 4]
    place = Place()
    post = Post(send_sems, place)
    z, e = place.at["z"], place.expert
    wide = query.shape[1]
    span = (in_grad.shape[1] - wide) // 2
    peers = []
    for flip_x, flip_c in ((1, 1), (1, 0), (0, 1)):
        x = place.at["x"] + flip_x * (1 - 2 * place.at["x"])
        core = place.at["c"] + flip_c * (1 - 2 * place.at["c"])
        peers.append((x * 2 + core, flip_x * 2 + flip_c))
    loads, works, finish = scatter_plan(
        "dp", rows, pieces, place, post, in_grad, rooms, refs[count + 4 :]
    )
    for load in loads:
        load.start()
    enter(place, "cxyz", [((place.dp, peers[0][0]), None)])
    for _, act in works:
        act()
    cols = lambda block: pl.ds(pl.multiple_of(block * span, span), span)
    keep = slice(wide, wide + 2 * span)
    for p in range(len(pieces)):
        first, length, _ = pieces[p]
        at = pl.ds(first, length)
        block = finish(p)
        post.send(block.at[:, keep], shared.at[2, at], deal_sems.at[p, 4], place.across("x"))
        for peer, flips in peers:
            post.send(
                block.at[:, cols(peer)],
                dealt.at[at, cols(e)],
                deal_sems.at[p, flips],
                (place.dp, peer),
            )
        post.send(block.at[:, keep], shared.at[1, at], deal_sems.at[p, 5], place.across("c"))

    def place_keys(p, flips, block):
        first, length, _ = pieces[p]
        rows_at = pl.ds(first, length)
        x = place.at["x"] + (flips // 2) * (1 - 2 * place.at["x"])
        core = place.at["c"] + (flips % 2) * (1 - 2 * place.at["c"])
        owner = x * 2 + core
        widen(keyvalue.at[rows_at, cols(owner)], block.at[:, pl.ds(0, span)], length)
        widen(
            keyvalue.at[rows_at, cols(wide // span + owner)], block.at[:, pl.ds(span, span)], length
        )

    for p in range(len(pieces)):
        first, length, _ = pieces[p]
        at = pl.ds(first, length)
        block = rooms[0].at[z, at]
        widen(query.at[at, cols(e)], block.at[:, cols(e)], length)
        place_keys(p, 0, block.at[:, keep])
        post.arrived(shared.at[1, at], deal_sems.at[p, 5])
        place_keys(p, 1, shared.at[1, at])
        post.arrived(shared.at[2, at], deal_sems.at[p, 4])
        post.send(shared.at[2, at], shared.at[3, at], deal_sems.at[p, 6], place.across("c"))
        place_keys(p, 2, shared.at[2, at])
        for peer, flips in reversed(peers):
            post.arrived(dealt.at[at, cols(peer)], deal_sems.at[p, flips])
            widen(query.at[at, cols(peer)], dealt.at[at, cols(peer)], length)
        post.arrived(shared.at[3, at], deal_sems.at[p, 6])
        place_keys(p, 3, shared.at[3, at])
    post.close()


def sum_weights(in_grad, wide, pieces, collective_id):
    rows, total = in_grad.shape[0] // 8, in_grad.shape[1]
    order, count = pieces[0][2], len(pieces)
    vmem = pl.BlockSpec(memory_space=pltpu.VMEM)
    shape = jax.ShapeDtypeStruct
    return pl.pallas_call(
        functools.partial(sum_weights_kernel, rows, pieces),
        out_shape=[
            shape((rows, wide), jnp.float32),
            shape((rows, 2 * wide), jnp.float32),
        ],
        in_specs=[pl.BlockSpec(memory_space=pltpu.HBM)],
        out_specs=[vmem] * 2,
        scratch_shapes=scatter_rooms(rows, total, order)
        + [
            pltpu.VMEM((rows, wide), jnp.bfloat16),
            pltpu.VMEM((4, rows, total - wide), jnp.bfloat16),
            pltpu.SemaphoreType.DMA((sends_of(order, count) + 7 * count,)),
            pltpu.SemaphoreType.DMA((count, 7)),
        ]
        + scatter_sems(order, count),
        compiler_params=pltpu.CompilerParams(
            collective_id=collective_id, has_side_effects=True, vmem_limit_bytes=63 * 2**20
        ),
        name="sum_weights",
    )(in_grad)


def weights_kernel(jobs, *refs):
    ready = len(jobs) - 2
    sources, (query, keyvalue, output) = refs[:ready], refs[ready : ready + 3]
    in_shard, out_shard = refs[ready + 3 : ready + 5]
    targets = refs[ready + 5 : 2 * ready + 7]
    send_sems, arrive_sems, own_sems, deal_sems = refs[2 * ready + 7 :]
    place = Place()
    z, y, e = place.at["z"], place.at["y"], place.expert
    span = (in_shard.shape[1] - query.shape[1]) // 2
    wide = query.shape[1]
    partner, moves = (e * 2 + y, z), z != e
    peers = []
    for flip_x, flip_c in ((1, 1), (1, 0), (0, 1)):
        x = place.at["x"] + flip_x * (1 - 2 * place.at["x"])
        core = place.at["c"] + flip_c * (1 - 2 * place.at["c"])
        peers.append((x * 2 + core, flip_x * 2 + flip_c))
    enter(place, "cxyz", [((place.dp, peers[0][0]), None), (partner, moves)])
    post = Post(send_sems, place)
    starts, waves, owns = gather_plan(
        jobs, place, post, list(sources) + [in_shard, out_shard], targets, arrive_sems, own_sems
    )
    cols = lambda block: pl.ds(pl.multiple_of(block * span, span), span)
    for peer, flips in peers:
        post.send(
            query.at[:, cols(peer)], in_shard.at[:, cols(e)], deal_sems.at[flips], (place.dp, peer)
        )
    post.send(output, out_shard, deal_sems.at[4], partner, moves)
    local = [
        pltpu.make_async_copy(query.at[:, cols(e)], in_shard.at[:, cols(e)], deal_sems.at[0]),
        pltpu.make_async_copy(
            keyvalue.at[:, cols(e)], in_shard.at[:, pl.ds(wide, span)], deal_sems.at[5]
        ),
        pltpu.make_async_copy(
            keyvalue.at[:, cols(wide // span + e)],
            in_shard.at[:, pl.ds(wide + span, span)],
            deal_sems.at[6],
        ),
    ]
    for copy in local:
        copy.start()
    stay = pltpu.make_async_copy(output, out_shard, deal_sems.at[7])
    pl.when(~moves)(stay.start)
    for act in sum(starts[:ready], []):
        act()
    for copy in local:
        copy.wait()
    for peer, flips in peers:
        post.arrived(in_shard.at[:, cols(peer)], deal_sems.at[flips])
    for act in starts[ready]:
        act()
    pl.when(~moves)(stay.wait)
    pl.when(moves)(lambda: post.arrived(out_shard, deal_sems.at[4]))
    for act in starts[ready + 1]:
        act()
    for wave in sorted(waves):
        for act in waves[wave]:
            act()
    for own in owns:
        own.wait()
    post.close()


def gather_weights(jobs, query, keyvalue, output, pieces, collective_id):
    rows, wide = query.shape
    span = wide // lax.axis_size("expert")
    shards = [
        jax.ShapeDtypeStruct((rows, wide + 2 * span), query.dtype),
        jax.ShapeDtypeStruct(output.shape, output.dtype),
    ]
    sizes = {"all": 32, "dp": 8, "expert": 4}
    plan = tuple((whose, r.shape[0], ps) for r, whose, ps in jobs)
    plan += tuple(("dp", s.shape[0], pieces) for s in shards)
    lines = sum(len(ps) for _, _, ps in plan)
    hbm = pl.BlockSpec(memory_space=pltpu.HBM)
    gathered = [
        jax.ShapeDtypeStruct((sizes[whose] * r.shape[0], r.shape[1]), r.dtype)
        for r, (whose, _, _) in zip([r for r, _, _ in jobs] + shards, plan)
    ]
    out = pl.pallas_call(
        functools.partial(weights_kernel, plan),
        out_shape=shards + gathered,
        in_specs=[hbm] * (len(jobs) + 3),
        out_specs=[hbm] * (2 + len(gathered)),
        scratch_shapes=[
            pltpu.SemaphoreType.DMA((110 * lines,)),
            pltpu.SemaphoreType.DMA((lines, 32)),
            pltpu.SemaphoreType.DMA((len(plan),)),
            pltpu.SemaphoreType.DMA((8,)),
        ],
        compiler_params=pltpu.CompilerParams(collective_id=collective_id, has_side_effects=True),
        name="gather_weights",
    )(*[r for r, _, _ in jobs], query, keyvalue, output)
    return out[2:]


def attention_bias(bias, block, rows, width, prefix):
    query = block * rows + lax.broadcasted_iota(jnp.int32, (rows, width), 0)
    key = lax.broadcasted_iota(jnp.int32, (rows, width), 1)
    bias[:, :width] = jnp.where((key <= query) | (key < prefix), 0.0, NEG)


def pick_expert(ref, lane, experts, span, chosen):
    total = None
    for e in range(experts):
        cols = ref[:, pl.ds(pl.multiple_of(e * span + lane, HEAD_DIM), HEAD_DIM)]
        term = jnp.where(chosen == e, cols.astype(jnp.float32), 0.0)
        total = term if total is None else total + term
    return total.astype(jnp.bfloat16)


def key_limits(blocks, rows):
    return [max((i + 1) * rows, blocks * rows // 2) for i in range(blocks)]


def for_each_limit(blocks, rows, body):
    block = pl.program_id(0)
    limits = key_limits(blocks, rows)
    for width in sorted(set(limits)):
        members = [i for i, limit in enumerate(limits) if limit == width]
        pl.when((block >= members[0]) & (block <= members[-1]))(lambda width=width: body(width))


def attention_kernel(experts, prefix, q, k, v, side, mixed, log_total, bias):
    rows, span = q.shape[0], k.shape[1]
    heads = span // HEAD_DIM
    block = pl.program_id(0)
    chosen = [side[:, 0:1], side[:, 1:2]]
    gates = [side[:, 2:3], side[:, 3:4]]

    def body(width):
        attention_bias(bias, block, rows, width, prefix[0])

        @pl.loop(0, heads)
        def _(head):
            lane = head * HEAD_DIM
            lanes = pl.ds(pl.multiple_of(lane, HEAD_DIM), HEAD_DIM)
            weighted = []
            for j in range(2):
                query = pick_expert(q, lane, experts, span, chosen[j])
                scores = lax.dot_general(
                    query, k[:width, lanes], ACROSS, preferred_element_type=jnp.float32
                )
                scores = scores * (HEAD_DIM**-0.5) + bias[:, :width]
                largest = jnp.max(scores, axis=1, keepdims=True)
                exponent = jnp.exp(scores - largest)
                total = jnp.sum(exponent, axis=1, keepdims=True)
                low = (exponent * (1.0 / total)).astype(jnp.bfloat16)
                out = jnp.dot(low, v[:width, lanes], preferred_element_type=jnp.float32)
                weighted.append(out * gates[j])
                at = pl.ds(pl.multiple_of((2 * head + j) * HEAD_DIM, HEAD_DIM), HEAD_DIM)
                log_total[:, at] = jnp.broadcast_to(
                    largest + jnp.log(total), (rows, HEAD_DIM)
                )
            for e in range(experts):
                cols = jnp.where(chosen[0] == e, weighted[0], 0.0) + jnp.where(
                    chosen[1] == e, weighted[1], 0.0
                )
                at = pl.ds(pl.multiple_of(e * span + lane, HEAD_DIM), HEAD_DIM)
                mixed[:, at] = cols.astype(jnp.bfloat16)

    for_each_limit(k.shape[0] // rows, rows, body)


def attention(projected, side, prefix, experts, rows):
    length = projected.shape[0]
    span = projected.shape[1] // (experts + 2)
    wide = experts * span
    return pl.pallas_call(
        functools.partial(attention_kernel, experts),
        grid=(length // rows,),
        in_specs=[
            pl.BlockSpec(memory_space=pltpu.SMEM),
            pl.BlockSpec((rows, wide), lambda i: (i, 0)),
            pl.BlockSpec((length, span), lambda i: (0, experts)),
            pl.BlockSpec((length, span), lambda i: (0, experts + 1)),
            pl.BlockSpec((rows, 128), lambda i: (i, 0)),
        ],
        out_specs=[
            pl.BlockSpec((rows, wide), lambda i: (i, 0)),
            pl.BlockSpec((rows, 2 * span), lambda i: (i, 0)),
        ],
        out_shape=[
            jax.ShapeDtypeStruct((length, wide), jnp.bfloat16),
            jax.ShapeDtypeStruct((length, 2 * span), jnp.float32),
        ],
        scratch_shapes=[pltpu.VMEM((rows, length), jnp.float32)],
        compiler_params=pltpu.CompilerParams(vmem_limit_bytes=48 * 2**20),
        name="attention",
    )(prefix, projected, projected, projected, side)


class AttentionBack(Nothing):
    operands, results, rooms = 4, 2, 11
    turns = 4

    def __init__(self, length, total, experts, rows):
        self.length, self.experts, self.rows = length, experts, rows
        self.span = total // (experts + 2)
        low, f32 = jnp.bfloat16, jnp.float32
        self.heads = self.span // HEAD_DIM
        self.blocks = length // rows
        self.shapes = [
            jax.ShapeDtypeStruct((length, total), low),
            jax.ShapeDtypeStruct((length, 128), f32),
        ]
        self.scratch = [
            pltpu.VMEM((length, total), low),
            pltpu.VMEM((length, 128), f32),
            pltpu.VMEM((length, 2 * self.span), f32),
            pltpu.VMEM((length, experts * self.span), low),
            pltpu.VMEM((length, total), low),
            pltpu.VMEM((length, 128), f32),
            pltpu.VMEM((rows, length), f32),
            pltpu.VMEM((length, self.span), f32),
            pltpu.VMEM((length, self.span), f32),
            pltpu.SemaphoreType.DMA((4,)),
            pltpu.SemaphoreType.DMA((2,)),
        ]

    def loads(self, given, own):
        return [pltpu.make_async_copy(given[i], own[i], own[9].at[i]) for i in range(4)]

    def start(self, given, made, own):
        for load in self.loads(given, own):
            load.start()
        for ref in (own[5], own[7], own[8]):
            ref[...] = jnp.zeros_like(ref)
        return self.blocks * self.heads

    def run(self, given, made, own, first, last):
        if first == 0:
            for load in self.loads(given, own):
                load.wait()

        @pl.loop(first, last)
        def _(step):
            block = step // self.heads
            limits = key_limits(self.blocks, self.rows)
            for width in sorted(set(limits)):
                members = [i for i, limit in enumerate(limits) if limit == width]

                @pl.when((block >= members[0]) & (block <= members[-1]))
                def _(width=width):
                    self.step(own, block, step % self.heads, width)

    def step(self, own, block, head, width):
        qkv, side_ref, log_total, dmix, dprojected, dgate, bias, dk, dv = own[:9]
        experts, span, rows = self.experts, self.span, self.rows
        scaling = HEAD_DIM**-0.5
        row_at = pl.ds(pl.multiple_of(block * rows, rows), rows)
        side = side_ref[row_at, :]
        chosen = [side[:, 0:1], side[:, 1:2]]
        gates = [side[:, 2:3], side[:, 3:4]]
        column = lax.broadcasted_iota(jnp.int32, (rows, 128), 1)
        query_at = block * rows + lax.broadcasted_iota(jnp.int32, (rows, width), 0)
        key_at = lax.broadcasted_iota(jnp.int32, (rows, width), 1)
        reach = key_at.astype(jnp.float32) < side[:, 4:5]
        bias[:, :width] = jnp.where((key_at <= query_at) | reach, 0.0, NEG)
        lane = head * HEAD_DIM
        lanes = lambda base: pl.ds(pl.multiple_of(base + lane, HEAD_DIM), HEAD_DIM)
        keys = qkv[:width, lanes(experts * span)]
        values = qkv[:width, lanes((experts + 1) * span)]
        dqueries = []
        for j in range(2):
            query = pick_expert(qkv.at[row_at], lane, experts, span, chosen[j])
            dm = pick_expert(dmix.at[row_at], lane, experts, span, chosen[j])
            at = pl.ds(pl.multiple_of((2 * head + j) * HEAD_DIM, HEAD_DIM), HEAD_DIM)
            logs = jnp.tile(log_total[row_at, at], (1, width // HEAD_DIM))
            scores = lax.dot_general(query, keys, ACROSS, preferred_element_type=jnp.float32)
            probs = jnp.exp(scores * scaling + bias[:, :width] - logs)
            dprobs = lax.dot_general(dm, values, ACROSS, preferred_element_type=jnp.float32)
            inner = jnp.sum(probs * dprobs, axis=1, keepdims=True)
            dgate[row_at, :] += jnp.where(column == j, inner, 0.0)
            probs = probs * gates[j]
            dscores = (probs * (dprobs - inner)).astype(jnp.bfloat16)
            low = probs.astype(jnp.bfloat16)
            dqueries.append(jnp.dot(dscores, keys, preferred_element_type=jnp.float32) * scaling)
            dk[:width, lanes(0)] += lax.dot_general(
                dscores, query, DOWNWARD, preferred_element_type=jnp.float32
            )
            dv[:width, lanes(0)] += lax.dot_general(
                low, dm, DOWNWARD, preferred_element_type=jnp.float32
            )
        for e in range(experts):
            cols = jnp.where(chosen[0] == e, dqueries[0], 0.0) + jnp.where(
                chosen[1] == e, dqueries[1], 0.0
            )
            dprojected[row_at, lanes(e * span)] = cols.astype(jnp.bfloat16)

    def end(self, given, made, own):
        dprojected, dgate, dk, dv = own[4], own[5], own[7], own[8]
        wide = self.experts * self.span
        dprojected[:, wide : wide + self.span] = (dk[...] * HEAD_DIM**-0.5).astype(jnp.bfloat16)
        dprojected[:, wide + self.span :] = dv[...].astype(jnp.bfloat16)
        copies = [
            pltpu.make_async_copy(dprojected, made[0], own[10].at[0]),
            pltpu.make_async_copy(dgate, made[1], own[10].at[1]),
        ]
        for copy in copies:
            copy.start()
        for copy in copies:
            copy.wait()


def chip_in_turn(u, z_here):
    u = jnp.asarray(u, jnp.int32)
    turn, q = u // 4, u % 4
    flip = lambda *at: ((q == at[0]) | (q == at[1])).astype(jnp.int32)
    k, xr, yr = turn + (q == 3) - (q == 0), flip(0, 1), flip(0, 2)
    k = jnp.where(u == 0, 0, jnp.minimum(k, CHIPS_Z - 1))
    last = 4 * CHIPS_Z - 1
    xr = jnp.where(u == 0, 0, jnp.where(u == last, 1, xr))
    yr = jnp.where(u == 0, 0, jnp.where(u == last, 1, yr))
    inner = (z_here == 1) | (z_here == 2)
    near = jnp.where(inner, jnp.where(k == 3, 3, jnp.where(k == 2, 0, k + 1)), k)
    return jnp.where(z_here < 2, near, CHIPS_Z - 1 - near), xr, yr


def block_in_turn(u, place):
    z, xr, yr = chip_in_turn(u, place.at["z"])
    x = place.at["x"] + xr * (1 - 2 * place.at["x"])
    y = place.at["y"] + yr * (1 - 2 * place.at["y"])
    return (z * 2 + y) * 4 + x * 2


class BranchRows(Nothing):
    operands, results, rooms = 3, 1, 8

    def __init__(self, tok, slot_count, blocks, hidden, padded, width):
        self.tok, self.slot_count, self.hidden = tok, slot_count, hidden
        low = jnp.bfloat16
        self.chips = blocks // 2
        self.shapes = [jax.ShapeDtypeStruct((blocks * tok, width), low)]
        self.scratch = [
            pltpu.VMEM((padded, width), low),
            pltpu.VMEM((blocks, tok), jnp.int32),
            pltpu.VMEM((2, 2 * slot_count, padded), low),
            pltpu.VMEM((2 * slot_count, width), low),
            pltpu.VMEM((2, 2 * tok, width), low),
            pltpu.SemaphoreType.DMA((2,)),
            pltpu.SemaphoreType.DMA((2,)),
            pltpu.SemaphoreType.DMA((2,)),
        ]

    def whole(self, given, own):
        return [
            pltpu.make_async_copy(given[1], own[0].at[pl.ds(0, self.hidden)], own[5].at[0]),
            pltpu.make_async_copy(given[2], own[1], own[5].at[1]),
        ]

    def take(self, given, own, u):
        rows = pl.ds(pl.multiple_of(u * 2 * self.slot_count, 64), 2 * self.slot_count)
        return pltpu.make_async_copy(given[0].at[rows], own[2].at[u % 2], own[6].at[u % 2])

    def put(self, made, own, u):
        rows = pl.ds(block_in_turn(u, Place()) * self.tok, 2 * self.tok)
        return pltpu.make_async_copy(own[4].at[u % 2], made[0].at[rows], own[7].at[u % 2])

    def start(self, given, made, own):
        for copy in self.whole(given, own):
            copy.start()
        self.take(given, own, jnp.int32(0)).start()
        own[0][self.hidden :, :] = jnp.zeros_like(own[0][self.hidden :, :])
        return self.chips

    def run(self, given, made, own, first, last):
        if first == last:
            return
        if first == 0:
            for copy in self.whole(given, own):
                copy.wait()
        w_down, slots, acts, outs, placed = own[:5]

        @pl.loop(first, last)
        def _(u):
            s = u % 2

            @pl.when(u + 1 < self.chips)
            def _():
                self.take(given, own, u + 1).start()

            self.take(given, own, u).wait()

            @pl.when(u >= 2)
            def _():
                self.put(made, own, u - 2).wait()

            @pl.loop(0, outs.shape[1] // 256)
            def _(n):
                cols = pl.ds(pl.multiple_of(n * 256, 256), 256)
                outs[:, cols] = jnp.dot(
                    acts[s], w_down[:, cols], preferred_element_type=jnp.float32
                ).astype(jnp.bfloat16)

            block = block_in_turn(u, Place())
            for b in range(2):
                row = slots[pl.ds(block + b, 1), :]
                number = lax.broadcasted_iota(jnp.int32, (self.slot_count, self.tok), 0)
                table = (number == row).astype(jnp.float32).T.astype(jnp.bfloat16)
                placed[s, pl.ds(b * self.tok, self.tok), :] = jnp.dot(
                    table,
                    outs[pl.ds(b * self.slot_count, self.slot_count), :],
                    preferred_element_type=jnp.float32,
                ).astype(jnp.bfloat16)
            self.put(made, own, u).start()

    def end(self, given, made, own):
        for u in (self.chips - 2, self.chips - 1):
            self.put(made, own, jnp.int32(u)).wait()


def expert_slots(first, second, my_index):
    tok_rows = first.shape[1]
    chosen = ((first == my_index) | (second == my_index)).astype(jnp.float32)
    before = jnp.triu(jnp.ones((tok_rows, tok_rows), jnp.float32), 1)
    slots = jnp.where(chosen > 0, jnp.dot(chosen, before), -1.0).astype(jnp.int32)
    return slots, first + second - my_index


def feed_kernel(
    tok,
    slot_count,
    own_rows,
    cots_left,
    cots_right,
    gate_weight,
    up_weight,
    down_weight,
    router_rows,
    slots,
    others,
    everyone,
    dx_part,
    x_kept,
    g_kept,
    d_kept,
    a_kept,
    dgate,
    w_in,
    w_down,
    rows_buf,
    cots_buf,
    xs,
    gs,
    pre,
    back,
    ds,
    acts,
    dx_buf,
    dxs,
    send_sems,
    arrive_sems,
    own_sem,
    weight_sems,
    load_sems,
    keep_sems,
):
    place = Place()
    z_here = place.at["z"]
    hidden = gate_weight.shape[0]
    padded = w_down.shape[0]
    width, cut = own_rows.shape[1], cots_left.shape[1]
    half = tok // 2
    chips = 4 * CHIPS_Z
    pair = 2 * slot_count
    f32, low = jnp.float32, jnp.bfloat16

    loads = [
        pltpu.make_async_copy(gate_weight, w_in.at[pl.ds(0, hidden)], weight_sems.at[0]),
        pltpu.make_async_copy(
            router_rows, w_in.at[pl.ds(hidden, padded - hidden)], weight_sems.at[1]
        ),
        pltpu.make_async_copy(up_weight, w_in.at[pl.ds(padded, hidden)], weight_sems.at[2]),
        pltpu.make_async_copy(down_weight, w_down.at[pl.ds(0, hidden)], weight_sems.at[3]),
        pltpu.make_async_copy(
            own_rows, everyone.at[pl.ds(place.block("all", z_here, {}) * tok, tok)], own_sem
        ),
    ]
    for load in loads:
        load.start()
    w_in[padded + hidden :, :] = jnp.zeros((padded - hidden, width), low)
    w_down[hidden:, :] = jnp.zeros((padded - hidden, width), low)
    enter(place, "cxyz")

    def chip(u):
        return chip_in_turn(u, z_here)

    def first_block(u):
        return block_in_turn(u, place)

    def part(p, u, core):
        return everyone.at[pl.ds((first_block(u) + core) * tok + p * half, half)]

    def remote(source, target, number, mark, device):
        return pltpu.make_async_remote_copy(
            src_ref=source,
            dst_ref=target,
            send_sem=send_sems.at[number],
            recv_sem=arrive_sems.at[mark],
            device_id=device,
            device_id_type=MESH,
        )

    def routes(u, p):
        z, xr, yr = chip(u)
        plain = (xr + yr) == 0
        mark = (p * CHIPS_Z + z) * 8
        here = xr * 4 + yr * 2
        base = (u * 2 + p) * 5
        own = z == z_here
        right = plain & (z <= z_here) & (z_here < CHIPS_Z - 1)
        left = plain & (z >= z_here) & (z_here > 0)
        over_x = plain if p == 0 else xr == 0
        over_y = yr == 0 if p == 0 else plain
        return [
            (right, base, mark, place.along(1)),
            (left, base + 1, mark, place.along(-1)),
            (over_x, base + 2, mark + 4 + yr * 2, place.across("x")),
            (over_y, base + 3, mark + xr * 4 + 2, place.across("y")),
            (None, base + 4, mark + here + 1, place.across("c")),
        ]

    def hand_on(u, sources, pieces=(0, 1)):
        for p in pieces:
            for condition, number, mark, device in routes(u, p):
                target = part(p, u, place.at["c"])
                source = target if sources is None else sources[p]
                on(
                    condition,
                    lambda source=source, target=target, number=number, mark=mark, device=device: remote(
                        source, target, number, mark, device
                    ).start(),
                )

    def sibling_came(u):
        z, xr, yr = chip(u)
        for p in range(2):
            ref = part(p, u, 1 - place.at["c"])
            mark = (p * CHIPS_Z + z) * 8 + xr * 4 + yr * 2 + 1
            remote(ref, ref, 0, mark, place.across("c")).wait_recv()

    def take_in(u, p):
        z, xr, yr = chip(u)
        ref = part(p, u, place.at["c"])
        mark = (p * CHIPS_Z + z) * 8 + xr * 4 + yr * 2
        remote(ref, ref, 0, mark, place.across("c")).wait_recv()
        hand_on(u, None, (p,))

    def fetch(u):
        at = pl.ds(first_block(u) * tok, 2 * tok)
        return [
            pltpu.make_async_copy(everyone.at[at], rows_buf.at[u % 2], load_sems.at[u % 2, 0]),
            pltpu.make_async_copy(
                cots_left.at[at], cots_buf.at[u % 2, :, pl.ds(0, cut)], load_sems.at[u % 2, 1]
            ),
            pltpu.make_async_copy(
                cots_right.at[at],
                cots_buf.at[u % 2, :, pl.ds(cut, width - cut)],
                load_sems.at[u % 2, 2],
            ),
        ]

    def keep(u):
        rows = pl.ds(u * pair, pair)
        blocks = pl.ds(first_block(u) * tok, 2 * tok)
        s = u % 2
        return [
            pltpu.make_async_copy(xs.at[s], x_kept.at[rows], keep_sems.at[s, 0]),
            pltpu.make_async_copy(gs.at[s], g_kept.at[rows], keep_sems.at[s, 1]),
            pltpu.make_async_copy(ds.at[s], d_kept.at[rows], keep_sems.at[s, 2]),
            pltpu.make_async_copy(acts.at[s], a_kept.at[rows], keep_sems.at[s, 3]),
            pltpu.make_async_copy(dx_buf.at[s], dx_part.at[blocks], keep_sems.at[s, 4]),
        ]

    hand_on(0, [own_rows.at[pl.ds(0, half)], own_rows.at[pl.ds(half, half)]])
    loads[4].wait()
    sibling_came(0)
    for copy in fetch(0):
        copy.start()
    for p in range(2):
        take_in(1, p)
    for load in loads[:4]:
        load.wait()

    def compute(u):
        s = u % 2
        block = first_block(u)
        spread = []
        for b in range(2):
            row = slots[pl.ds(block + b, 1), :]
            table = lax.broadcasted_iota(jnp.int32, (slot_count, tok), 0) == row
            table = table.astype(f32)
            spread.append(table)
            at = pl.ds(b * slot_count, slot_count)
            from_rows = pl.ds(b * tok, tok)
            xs[s, at, :] = jnp.dot(
                table.astype(low), rows_buf[s, from_rows, :], preferred_element_type=f32
            ).astype(low)
            gs[s, at, :] = jnp.dot(
                table.astype(low), cots_buf[s, from_rows, :], preferred_element_type=f32
            ).astype(low)

        @pl.loop(0, 2 * padded // 256)
        def _(n):
            at = pl.ds(pl.multiple_of(n * 256, 256), 256)
            pre[:, at] = lax.dot_general(xs[s], w_in[at, :], ACROSS, preferred_element_type=f32)

        @pl.when(u + 2 < chips)
        def _():
            take_in(u + 2, 1)

        @pl.loop(0, padded // 256)
        def _(n):
            at = pl.ds(pl.multiple_of(n * 256, 256), 256)
            back[:, at] = lax.dot_general(gs[s], w_down[at, :], ACROSS, preferred_element_type=f32)

        for b in range(2):
            at = pl.ds(b * slot_count, slot_count)
            last = pre[at, padded - 128 : padded]
            column = lax.broadcasted_iota(jnp.int32, (slot_count, 128), 1) - (
                hidden - (padded - 128)
            )
            other = jnp.sum(
                spread[b] * others[pl.ds(block + b, 1), :].astype(f32), axis=1, keepdims=True
            )
            mine = jnp.sum(jnp.where(column == place.expert, last, 0.0), axis=1, keepdims=True)
            theirs = jnp.sum(
                jnp.where(column == other.astype(jnp.int32), last, 0.0), axis=1, keepdims=True
            )
            gate = 1.0 / (1.0 + jnp.exp(theirs - mine))
            inner = jnp.zeros((slot_count, 1), f32)
            for n in range(padded // 256):
                cols = pl.ds(n * 256, 256)
                pre_gate, pre_up = pre[at, cols], pre[at, pl.ds(padded + n * 256, 256)]
                dact = back[at, cols]
                sig = 1.0 / (1.0 + jnp.exp(-pre_gate))
                silu = pre_gate * sig
                act = silu * pre_up
                acts[s, at, cols] = (act * gate).astype(low)
                inner += jnp.sum(act * dact, axis=1, keepdims=True)
                dact = dact * gate
                ds[s, at, cols] = (dact * pre_up * sig * (1.0 + pre_gate * (1.0 - sig))).astype(low)
                ds[s, at, pl.ds(padded + n * 256, 256)] = (dact * silu).astype(low)
            dgate[pl.ds(block + b, 1), :] = jnp.sum(spread[b] * inner, axis=0, keepdims=True)

        @pl.loop(0, width // 256)
        def _(n):
            cols = pl.ds(pl.multiple_of(n * 256, 256), 256)
            dxs[:, cols] = jnp.dot(ds[s], w_in[:, cols], preferred_element_type=f32).astype(low)

        for b in range(2):
            at = pl.ds(b * slot_count, slot_count)
            back_table = spread[b].T.astype(low)
            to = pl.ds(b * tok, tok)
            dx_buf[s, to, :] = jnp.dot(
                back_table, dxs[at, :], preferred_element_type=f32
            ).astype(low)

    @pl.loop(0, chips)
    def _(u):
        @pl.when(u + 1 < chips)
        def _():
            sibling_came(u + 1)
            for copy in fetch(u + 1):
                copy.start()

        @pl.when(u + 2 < chips)
        def _():
            take_in(u + 2, 0)

        for copy in fetch(u):
            copy.wait()

        @pl.when(u >= 2)
        def _():
            for copy in keep(u - 2):
                copy.wait()

        compute(u)
        for copy in keep(u):
            copy.start()

    for u in (chips - 2, chips - 1):
        for copy in keep(jnp.int32(u)):
            copy.wait()

    @pl.loop(0, chips)
    def _(u):
        for p in range(2):
            for condition, number, mark, device in routes(u, p):
                ref = part(p, u, place.at["c"])
                on(
                    condition,
                    lambda ref=ref, number=number, mark=mark, device=device: remote(
                        ref, ref, number, mark, device
                    ).wait_send(),
                )


def feed(
    own_rows,
    cots_left,
    cots_right,
    gate_weight,
    up_weight,
    down_weight,
    router_rows,
    slots,
    others,
    slot_count,
):
    tok, width = own_rows.shape
    hidden = gate_weight.shape[0]
    padded = hidden + router_rows.shape[0]
    total = cots_left.shape[0]
    kept = total // tok * slot_count
    low = jnp.bfloat16
    hbm = pl.BlockSpec(memory_space=pltpu.HBM)
    vmem = pl.BlockSpec(memory_space=pltpu.VMEM)
    shape = jax.ShapeDtypeStruct
    pair = 2 * slot_count
    chips = 4 * CHIPS_Z
    return pl.pallas_call(
        functools.partial(feed_kernel, tok, slot_count),
        in_specs=[hbm] * 7 + [vmem] * 2,
        out_specs=[hbm] * 6 + [vmem],
        out_shape=[
            shape((total, width), low),
            shape((total, width), low),
            shape((kept, width), low),
            shape((kept, width), low),
            shape((kept, 2 * padded), low),
            shape((kept, padded), low),
            shape(slots.shape, jnp.float32),
        ],
        scratch_shapes=[
            pltpu.VMEM((2 * padded, width), low),
            pltpu.VMEM((padded, width), low),
            pltpu.VMEM((2, 2 * tok, width), low),
            pltpu.VMEM((2, 2 * tok, width), low),
            pltpu.VMEM((2, pair, width), low),
            pltpu.VMEM((2, pair, width), low),
            pltpu.VMEM((pair, 2 * padded), jnp.float32),
            pltpu.VMEM((pair, padded), jnp.float32),
            pltpu.VMEM((2, pair, 2 * padded), low),
            pltpu.VMEM((2, pair, padded), low),
            pltpu.VMEM((2, 2 * tok, width), low),
            pltpu.VMEM((pair, width), low),
            pltpu.SemaphoreType.DMA((10 * chips,)),
            pltpu.SemaphoreType.DMA((16 * CHIPS_Z,)),
            pltpu.SemaphoreType.DMA,
            pltpu.SemaphoreType.DMA((4,)),
            pltpu.SemaphoreType.DMA((2, 3)),
            pltpu.SemaphoreType.DMA((2, 6)),
        ],
        compiler_params=pltpu.CompilerParams(
            collective_id=3, has_side_effects=True, vmem_limit_bytes=60 * 2**20
        ),
        name="feed_forward",
    )(
        own_rows,
        cots_left,
        cots_right,
        gate_weight,
        up_weight,
        down_weight,
        router_rows,
        slots,
        others,
    )


def per_device_torus(
    tokens,
    cotangent,
    attention_routes,
    feedforward_routes,
    prefix_length,
    gain_attention,
    gain_feedforward,
    keyvalue_weight,
    router_weight,
    query_weight,
    output_weight,
    gate_weight,
    up_weight,
    down_weight,
):
    my_index = lax.axis_index("expert")
    group_size = lax.axis_size("expert")
    dp_size = lax.axis_size("dp")
    inputs = tokens[0].astype(jnp.float32)
    tok_rows, model_width = inputs.shape
    slot_count = 5 * 2 * tok_rows // (4 * group_size)
    query_width = HEADS * HEAD_DIM
    span = query_width // group_size
    low = jnp.bfloat16
    f32 = jnp.float32

    normed_attention, unit_attention, factor_attention = norm_parts(inputs, gain_attention)
    attention_in = normed_attention.astype(low)
    quarters = lambda order: tuple(
        (i * tok_rows // 4, tok_rows // 4, order) for i in range(4)
    )
    rows_in = keyvalue_weight.shape[0]
    route_shard = feedforward_routes[0].T.astype(low).reshape(-1, 128)
    early = model_width * 5 // 8
    router_shard = router_weight.T.reshape(-1, 128)
    whole = lambda a: ((0, a.shape[0], "zy"),)
    cut = rows_in * 13 // 16
    sequence_in, cots_left, every_route, router_full, in_weight, out_weight = gather_weights(
        [
            (attention_in, "expert", quarters("xc")),
            (cotangent[0, :, :early], "all", quarters("zyxc")),
            (route_shard, "dp", whole(route_shard)),
            (router_shard, "dp", whole(router_shard)),
        ],
        query_weight[0],
        keyvalue_weight,
        output_weight[0],
        ((0, cut, "zy"), (cut, rows_in - cut, "yz")),
        1,
    )
    cots_late, sequence_in = lax.optimization_barrier((cotangent[0, :, early:], sequence_in))
    cots_right = lax.all_gather(cots_late, ("dp", "expert"), axis=0, tiled=True)
    every_route = every_route.reshape(dp_size, 2, group_size, tok_rows).astype(jnp.int32)
    router_full = (
        router_full.reshape(dp_size, 2 * group_size, rows_in)
        .transpose(0, 2, 1)
        .reshape(-1, 2 * group_size)
    )
    attention_cols = router_full[:, :group_size]
    feedforward_cols = router_full[:, group_size:]
    projected = jnp.dot(sequence_in, in_weight, preferred_element_type=f32).astype(low)
    attend_matches_all = expert_matches(attention_routes[0], group_size)
    attend_logits = jnp.dot(sequence_in, attention_cols, preferred_element_type=f32)
    attend_weights_all, _ = pair_gates(attend_logits, attend_matches_all)
    reach = jnp.broadcast_to(prefix_length.astype(f32)[None], (attend_logits.shape[0], 1))
    side = jnp.concatenate([attention_routes[0].astype(f32), attend_weights_all, reach], axis=1)
    side = jnp.pad(side, ((0, 0), (0, 128 - side.shape[1])))
    mixed, log_total = attention(projected, side, prefix_length, group_size, tok_rows)
    attend_part = jnp.dot(mixed, out_weight, preferred_element_type=f32).astype(low)
    attended = scatter(attend_part, "expert", quarters("cx"), 2, "sum_attention")
    hidden = inputs + attended
    normed_feed, unit_feed, factor_feed = norm_parts(hidden, gain_feedforward)
    feed_in = normed_feed.astype(low)
    everywhere = lambda a, b: ((0, tok_rows // 2, a), (tok_rows // 2, tok_rows // 2, b))
    mine = lambda a: lax.dynamic_slice_in_dim(a, my_index * tok_rows, tok_rows, 0)
    feed_matches = expert_matches(mine(feedforward_routes[0]), group_size)
    feed_logits = jnp.dot(feed_in, feedforward_cols, preferred_element_type=f32)
    feed_weights, _ = pair_gates(feed_logits, feed_matches)
    slots, others = expert_slots(
        every_route[:, 0].reshape(-1, tok_rows), every_route[:, 1].reshape(-1, tok_rows), my_index
    )
    hidden_rows = gate_weight.shape[1]
    padded = -(-hidden_rows // 256) * 256
    router_rows = jnp.pad(
        feedforward_cols.T, ((0, padded - hidden_rows - group_size), (0, 0))
    )
    _, dx_part, kept_rows, kept_cots, kept_back, kept_act, token_dgate = feed(
        feed_in,
        cots_left,
        cots_right,
        gate_weight[0],
        up_weight[0],
        down_weight[0],
        router_rows,
        slots,
        others,
        slot_count,
    )
    own_row = (jnp.arange(group_size) == my_index).astype(f32)[None, :, None]
    feed_dgate = lax.psum_scatter(
        (token_dgate[:, None, :] * own_row).reshape(-1, tok_rows),
        ("dp", "expert"),
        scatter_dimension=0,
        tiled=True,
    ).T
    feed_home, grad_gate, grad_up, grad_down = scatter(
        dx_part,
        "all",
        everywhere("cxyz", "cyxz"),
        4,
        "sum_rows",
        WeightGrads(kept_rows.shape[0], padded, hidden_rows, model_width),
        (kept_back, kept_rows, kept_act, kept_cots),
    )
    gradient = cotangent[0].astype(f32)
    feed_dlogits = gates_back(feed_dgate, feed_weights, feed_matches)
    feed_dnorm = feed_home + jnp.dot(feed_dlogits, feedforward_cols.astype(f32).T, precision=HIGH)
    grad_gain_feed = jnp.sum(feed_dnorm * unit_feed, axis=0)
    hidden_grad = gradient + norm_back(feed_dnorm, gain_feedforward, unit_feed, factor_feed)

    sequence_grad, out_part = gather(
        [(hidden_grad.astype(low), "expert", quarters("xc"))],
        5,
        "gather_cotangents",
        BranchRows(tok_rows, slot_count, slots.shape[0], hidden_rows, padded, model_width),
        (kept_act, down_weight[0], slots),
    )
    dmix = lax.dot_general(sequence_grad, out_weight, ACROSS, preferred_element_type=f32).astype(low)
    length, total = projected.shape
    columns = model_width // 2
    first_sum, dprojected, gate_parts, grad_out = scatter(
        out_part,
        "all",
        everywhere("cxyz", "cyxz"),
        7,
        "sum_output_left",
        InTurn(
            AttentionBack(length, total, group_size, tok_rows),
            LowGrad(length, query_width, model_width, 4),
        ),
        (projected, side, log_total, dmix, mixed, sequence_grad),
        (0, columns),
    )
    second_sum, attend_dx = scatter(
        out_part,
        "all",
        everywhere("cxyz", "cyxz"),
        8,
        "sum_output_right",
        RowGrads(length, total, model_width),
        (dprojected, in_weight, gate_parts),
        (columns, model_width - columns),
    )
    attend_home, grad_projection, grad_in = sum_with_output(
        attend_dx,
        quarters("cx"),
        grad_out,
        ((0, rows_in, "yz"),),
        9,
        LowGrad(length, model_width, total, 4),
        (sequence_in, dprojected),
    )
    pair_dgate = attend_home[:, model_width : model_width + 2]
    attend_home = attend_home[:, :model_width]
    layer_output = hidden + jnp.concatenate([first_sum, second_sum], axis=1)
    matches = mine(attend_matches_all)
    weights = mine(attend_weights_all)
    dselected = weights * (pair_dgate - jnp.sum(weights * pair_dgate, axis=1, keepdims=True))
    attend_dlogits = jnp.sum(dselected[:, :, None] * matches, axis=1)
    attend_dnorm = attend_home + jnp.dot(
        attend_dlogits, attention_cols.astype(f32).T, precision=HIGH
    )
    grad_gain_attend = jnp.sum(attend_dnorm * unit_attention, axis=0)
    grad_tokens = hidden_grad + norm_back(
        attend_dnorm, gain_attention, unit_attention, factor_attention
    )
    small = jnp.concatenate(
        [
            lax.dot_general(attend_dlogits, attention_in.astype(f32), DOWNWARD, precision=HIGH),
            lax.dot_general(feed_dlogits, feed_in.astype(f32), DOWNWARD, precision=HIGH),
            grad_gain_attend[None],
            grad_gain_feed[None],
        ],
        axis=0,
    )
    small = lax.psum(small.astype(f32), ("dp", "expert"))
    small = lax.dynamic_slice_in_dim(small, lax.axis_index("dp") * rows_in, rows_in, 1)

    grad_query, grad_keyvalue = sum_weights(grad_in, query_width, ((0, rows_in, "yz"),), 6)
    return (
        layer_output.astype(low)[None],
        grad_tokens[None],
        small[2 * group_size],
        small[2 * group_size + 1],
        grad_keyvalue,
        small[: 2 * group_size].T,
        grad_query[None],
        grad_projection[None],
        grad_gate[None],
        grad_up[None],
        grad_down[None],
    )


def solution(mesh):
    in_specs = (
        P("dp", "expert", None),
        P("dp", "expert", None),
        P("dp", None, None),
        P("dp", None, None),
        P("dp"),
        P(),
        P(),
        P("dp", None),
        P("dp", None),
        P("expert", "dp", None),
        P("expert", "dp", None),
        P("expert", "dp", None),
        P("expert", "dp", None),
        P("expert", "dp", None),
    )
    out_specs = (
        P("dp", "expert", None),
        P("dp", "expert", None),
        P("dp"),
        P("dp"),
        P("dp", None),
        P("dp", None),
        P("expert", "dp", None),
        P("expert", "dp", None),
        P("expert", "dp", None),
        P("expert", "dp", None),
        P("expert", "dp", None),
    )
    torus = (mesh.shape["dp"], mesh.shape["expert"]) == (8, 4)
    body = per_device_torus if torus else per_device
    return jax.shard_map(
        body, mesh=mesh, in_specs=in_specs, out_specs=out_specs, check_vma=False
    )
```

```python
import functools

import jax
import jax.numpy as jnp
from jax import lax
from jax.experimental import pallas as pl
from jax.experimental.pallas import tpu as pltpu
from jax.sharding import PartitionSpec as P

HEADS = 16
HEAD_DIM = 128


EPS = 1e-06
NEG = -1e30
HIGH = lax.Precision.HIGHEST
ACROSS = (((1,), (1,)), ((), ()))
DOWNWARD = (((0,), (0,)), ((), ()))


def norm_parts(vector, gain_vector):
    factor = lax.rsqrt(jnp.mean(vector * vector, axis=-1, keepdims=True) + EPS)
    normed = vector * factor
    return (normed * gain_vector, normed, factor)


def norm_back(incoming, gain_vector, normed, factor):
    dnormed = incoming * gain_vector
    return factor * (dnormed - normed * jnp.mean(dnormed * normed, axis=-1, keepdims=True))


def route_plan(sequence_ids, my_index, group_size, tok_rows, slot_count):
    expert_range = jnp.arange(group_size, dtype=jnp.int32)
    matches_all = (sequence_ids[:, :, None] == expert_range[None, None, :]).astype(jnp.int32)
    chosen = jnp.sum(matches_all, axis=1).reshape(group_size, tok_rows, group_size)
    ranking = jnp.cumsum(chosen, axis=1) - chosen
    slot_ids = jnp.arange(slot_count, dtype=jnp.int32)[None, :, None]
    block_pick = (expert_range == my_index).astype(jnp.int32)
    my_chosen = jnp.sum(chosen * block_pick[:, None, None], axis=0).T
    my_ranking = jnp.sum(ranking * block_pick[:, None, None], axis=0).T
    send_table = (
        my_chosen[:, None, :] * (my_ranking[:, None, :] == slot_ids).astype(jnp.int32)
    ).astype(jnp.float32)
    column_chosen = jnp.sum(chosen * block_pick[None, None, :], axis=2)
    column_ranking = jnp.sum(ranking * block_pick[None, None, :], axis=2)
    taken = column_chosen[:, None, :] * (column_ranking[:, None, :] == slot_ids).astype(jnp.int32)
    positions = (
        expert_range[:, None, None] * tok_rows
        + jnp.arange(tok_rows, dtype=jnp.int32)[None, None, :]
    )
    arrival_places = jnp.sum(taken * positions, axis=2).reshape(-1)
    my_ids = lax.dynamic_slice_in_dim(sequence_ids, my_index * tok_rows, tok_rows, 0)
    matches = (my_ids[:, :, None] == expert_range[None, None, :]).astype(jnp.float32)
    return (send_table, arrival_places, matches)


def pair_gates(logits, matches):
    selected = jnp.sum(matches * logits[:, None, :], axis=2)
    largest = jnp.max(selected, axis=1, keepdims=True)
    exponent = jnp.exp(selected - largest)
    weights = exponent / jnp.sum(exponent, axis=1, keepdims=True)
    return (weights, jnp.sum(weights[:, :, None] * matches, axis=1))


def gates_back(dgate, weights, matches):
    dweights = jnp.sum(dgate[:, None, :] * matches, axis=2)
    dselected = weights * (dweights - jnp.sum(weights * dweights, axis=1, keepdims=True))
    return jnp.sum(dselected[:, :, None] * matches, axis=1)


def merge_back(send_table, gate_table, returned):
    weighted = send_table * gate_table.T[:, None, :]
    return jnp.einsum("ect,ecd->td", weighted, returned.astype(jnp.float32), precision=HIGH)


def branch_cotangent(send_table, gate_table, returned, incoming):
    spread_grad = jnp.einsum("ect,td->ecd", send_table, incoming, precision=HIGH)
    slot_gate = jnp.sum(send_table * gate_table.T[:, None, :], axis=2)
    cotangent_rows = (spread_grad * slot_gate[:, :, None]).astype(jnp.bfloat16)
    slot_dgate = jnp.sum(spread_grad * returned.astype(jnp.float32), axis=2)
    dgate = jnp.einsum("ect,ec->te", send_table, slot_dgate, precision=HIGH)
    return (cotangent_rows, dgate)


def expert_matches(ids, group_size):
    expert_range = jnp.arange(group_size, dtype=jnp.int32)
    return (ids[:, :, None] == expert_range[None, None, :]).astype(jnp.float32)


def expert_table(ids, my_index, group_size, tok_rows, slot_count):
    blocks = ids.reshape(-1, tok_rows, 2)
    chosen = jnp.sum((blocks == my_index).astype(jnp.float32), axis=2)
    before = jnp.triu(jnp.ones((tok_rows, tok_rows), jnp.float32), 1)
    ranking = jnp.dot(chosen, before)
    slot_ids = jnp.arange(slot_count, dtype=jnp.float32)[None, :, None]
    taken = chosen[:, None, :] * (ranking[:, None, :] == slot_ids).astype(jnp.float32)
    other = jnp.sum(blocks, axis=2) - my_index
    slot_other = jnp.sum(taken * other[:, None, :].astype(jnp.float32), axis=2)
    return (taken.astype(jnp.bfloat16), slot_other.reshape(-1).astype(jnp.int32))


def own_gate(logits, other, my_index):
    expert_range = jnp.arange(logits.shape[1], dtype=jnp.int32)[None]
    mine = jnp.sum(jnp.where(expert_range == my_index, logits, 0.0), axis=1, keepdims=True)
    theirs = jnp.sum(jnp.where(expert_range == other[:, None], logits, 0.0), axis=1, keepdims=True)
    return jax.nn.sigmoid(mine - theirs)


def pick_rows(taken, rows):
    blocks, slots, tokens = taken.shape
    picked = jnp.einsum(
        "bct,btd->bcd",
        taken,
        rows.reshape(blocks, tokens, -1),
        preferred_element_type=jnp.float32,
    )
    return picked.astype(jnp.bfloat16).reshape(blocks * slots, -1)


def return_rows(taken, rows):
    blocks, slots, tokens = taken.shape
    placed = jnp.einsum(
        "bct,bcd->btd",
        taken,
        rows.reshape(blocks, slots, -1),
        preferred_element_type=jnp.float32,
    )
    return placed.astype(jnp.bfloat16).reshape(blocks * tokens, -1)


def gather_all(rows):
    return lax.all_gather(rows, ("dp", "expert"), axis=0, tiled=True)


def scatter_all(rows):
    return lax.psum_scatter(rows, ("dp", "expert"), scatter_dimension=0, tiled=True)


def dispatch(rows):
    return lax.all_to_all(rows, "expert", split_axis=0, concat_axis=0, tiled=True)


def collect(rows):
    return lax.all_to_all(rows, "expert", split_axis=0, concat_axis=0, tiled=True)


def spread_rows(rows):
    return lax.all_gather(rows, "dp", axis=0, tiled=True)


def sum_rows(terms):
    return lax.psum_scatter(
        terms.astype(jnp.bfloat16), "dp", scatter_dimension=0, tiled=True
    ).astype(jnp.float32)


def send_rows(send_table, rows):
    return jnp.einsum(
        "ect,td->ecd", send_table.astype(jnp.bfloat16), rows, preferred_element_type=jnp.float32
    ).astype(jnp.bfloat16)


def per_device(
    tokens,
    cotangent,
    attention_routes,
    feedforward_routes,
    prefix_length,
    gain_attention,
    gain_feedforward,
    keyvalue_weight,
    router_weight,
    query_weight,
    output_weight,
    gate_weight,
    up_weight,
    down_weight,
):
    my_index = lax.axis_index("expert")
    group_size = lax.axis_size("expert")
    inputs = tokens[0].astype(jnp.float32)
    tok_rows = inputs.shape[0]
    model_width = inputs.shape[1]
    seq_total = tok_rows * group_size
    slot_count = 5 * 2 * tok_rows // (4 * group_size)
    query_width = HEADS * HEAD_DIM
    scaling = HEAD_DIM ** (-0.5)
    keyvalue_full, router_full, query_full, output_full = (
        lax.all_gather(keyvalue_weight, "dp", axis=0, tiled=True),
        lax.all_gather(router_weight, "dp", axis=0, tiled=True),
        lax.all_gather(query_weight[0], "dp", axis=0, tiled=True),
        lax.all_gather(output_weight[0], "dp", axis=0, tiled=True),
    )
    every_route = lax.all_gather(feedforward_routes[0], "dp", axis=0, tiled=True)
    cot_everyone = gather_all(cotangent[0])
    attention_cols = router_full[:, :group_size]
    feedforward_cols = router_full[:, group_size:]
    normed_attention, unit_attention, factor_attention = norm_parts(inputs, gain_attention)
    attention_in = normed_attention.astype(jnp.bfloat16)
    keyvalue_rows = jnp.dot(attention_in, keyvalue_full, preferred_element_type=jnp.float32).astype(
        jnp.bfloat16
    )
    keyvalue_seq = lax.all_gather(keyvalue_rows, "expert", axis=0, tiled=True)
    key_rows = keyvalue_seq[:, :query_width].reshape(seq_total, HEADS, HEAD_DIM)
    value_rows = keyvalue_seq[:, query_width:].reshape(seq_total, HEADS, HEAD_DIM)
    attend_table, attend_places, attend_matches = route_plan(
        attention_routes[0], my_index, group_size, tok_rows, slot_count
    )
    attend_logits = jnp.dot(attention_in, attention_cols, preferred_element_type=jnp.float32)
    attend_weights, attend_gate = pair_gates(attend_logits, attend_matches)
    arrived = dispatch(send_rows(attend_table, attention_in)).reshape(-1, model_width)
    queries = jnp.dot(arrived, query_full, preferred_element_type=jnp.float32).astype(jnp.bfloat16)
    queries = queries.reshape(-1, HEADS, HEAD_DIM)
    key_places = jnp.arange(seq_total, dtype=jnp.int32)
    allowed = (key_places[None, :] <= attend_places[:, None]) | (
        key_places[None, :] < prefix_length[0]
    )
    scores = (
        jnp.einsum("rhd,khd->hrk", queries, key_rows, preferred_element_type=jnp.float32) * scaling
    )
    scores = jnp.where(allowed[None], scores, NEG)
    row_max = jnp.max(scores, axis=2, keepdims=True)
    exponent = jnp.exp(scores - row_max)
    row_total = jnp.sum(exponent, axis=2, keepdims=True)
    log_total = row_max + jnp.log(row_total)
    attention_low = (exponent / row_total).astype(jnp.bfloat16)
    mixture = jnp.einsum(
        "hrk,khd->rhd", attention_low, value_rows, preferred_element_type=jnp.float32
    )
    mixture = mixture.astype(jnp.bfloat16).reshape(-1, query_width)
    attend_branch = jnp.dot(mixture, output_full, preferred_element_type=jnp.float32).astype(
        jnp.bfloat16
    )
    attend_returned = collect(attend_branch.reshape(group_size, slot_count, model_width))
    hidden = inputs + merge_back(attend_table, attend_gate, attend_returned)
    normed_feed, unit_feed, factor_feed = norm_parts(hidden, gain_feedforward)
    feed_in = normed_feed.astype(jnp.bfloat16)
    feed_ids = lax.dynamic_slice_in_dim(
        feedforward_routes[0], my_index * tok_rows, tok_rows, 0
    )
    feed_matches = expert_matches(feed_ids, group_size)
    feed_logits = jnp.dot(feed_in, feedforward_cols, preferred_element_type=jnp.float32)
    feed_weights, feed_gate = pair_gates(feed_logits, feed_matches)
    everyone = gather_all(feed_in)
    feed_taken, feed_pairs = expert_table(every_route, my_index, group_size, tok_rows, slot_count)
    pick = functools.partial(pick_rows, feed_taken)
    feed_rows = pick(everyone)
    cot_rows = pick(cot_everyone)
    row_logits = jnp.dot(feed_rows, feedforward_cols, preferred_element_type=jnp.float32)
    row_gate = own_gate(row_logits, feed_pairs, my_index)
    pre_gate = lax.dot_general(feed_rows, gate_weight[0], ACROSS, preferred_element_type=jnp.float32)
    pre_up = lax.dot_general(feed_rows, up_weight[0], ACROSS, preferred_element_type=jnp.float32)
    sigmoid_gate = jax.nn.sigmoid(pre_gate)
    act = pre_gate * sigmoid_gate * pre_up
    act_low = act.astype(jnp.bfloat16)
    act_scaled = (act * row_gate).astype(jnp.bfloat16)
    act_grad = lax.dot_general(cot_rows, down_weight[0], ACROSS, preferred_element_type=jnp.float32)
    slot_dgate = jnp.sum(act_low.astype(jnp.float32) * act_grad, axis=1)
    act_grad = act_grad * row_gate
    dgate_low = (act_grad * pre_up * sigmoid_gate * (1.0 + pre_gate * (1.0 - sigmoid_gate))).astype(
        jnp.bfloat16
    )
    dup_low = (act_grad * pre_gate * sigmoid_gate).astype(jnp.bfloat16)
    feed_dx = (
        jnp.dot(dgate_low, gate_weight[0], preferred_element_type=jnp.float32)
        + jnp.dot(dup_low, up_weight[0], preferred_element_type=jnp.float32)
    ).astype(jnp.bfloat16)
    feed_branch = jnp.dot(act_scaled, down_weight[0], preferred_element_type=jnp.float32).astype(
        jnp.bfloat16
    )
    grad_gate = lax.dot_general(dgate_low, feed_rows, DOWNWARD, preferred_element_type=jnp.float32)
    grad_up = lax.dot_general(dup_low, feed_rows, DOWNWARD, preferred_element_type=jnp.float32)
    grad_down = lax.dot_general(act_scaled, cot_rows, DOWNWARD, preferred_element_type=jnp.float32)
    token_dgate = jnp.einsum(
        "bct,bc->bt",
        feed_taken.astype(jnp.float32),
        slot_dgate.reshape(-1, slot_count),
        precision=HIGH,
    ).reshape(-1, 1)
    own_column = (jnp.arange(group_size) == my_index).astype(jnp.float32)[None]
    feed_dgate = scatter_all(token_dgate * own_column)
    feed_home = scatter_all(return_rows(feed_taken, feed_dx)).astype(jnp.float32)
    feed_sum = scatter_all(return_rows(feed_taken, feed_branch)).astype(jnp.float32)
    layer_output = hidden + feed_sum
    gradient = cotangent[0].astype(jnp.float32)
    feed_dlogits = gates_back(feed_dgate, feed_weights, feed_matches)
    feed_dnorm = feed_home + jnp.dot(
        feed_dlogits, feedforward_cols.astype(jnp.float32).T, precision=HIGH
    )
    grad_gain_feed = jnp.sum(feed_dnorm * unit_feed, axis=0)
    hidden_grad = gradient + norm_back(feed_dnorm, gain_feedforward, unit_feed, factor_feed)
    attend_cot, attend_dgate = branch_cotangent(
        attend_table, attend_gate, attend_returned, hidden_grad
    )
    attend_dlogits = gates_back(attend_dgate, attend_weights, attend_matches)
    attend_cot_rows = dispatch(attend_cot).reshape(-1, model_width)
    dmixture = lax.dot_general(
        attend_cot_rows, output_full, ACROSS, preferred_element_type=jnp.float32
    )
    dmixture = dmixture.astype(jnp.bfloat16).reshape(-1, HEADS, HEAD_DIM)
    grad_projection = lax.dot_general(
        mixture, attend_cot_rows, DOWNWARD, preferred_element_type=jnp.float32
    )
    scores_again = (
        jnp.einsum("rhd,khd->hrk", queries, key_rows, preferred_element_type=jnp.float32) * scaling
    )
    attention = jnp.where(allowed[None], jnp.exp(scores_again - log_total), 0.0)
    attention_again = attention.astype(jnp.bfloat16)
    dattention = jnp.einsum(
        "rhd,khd->hrk", dmixture, value_rows, preferred_element_type=jnp.float32
    )
    row_dot = jnp.sum(attention * dattention, axis=2, keepdims=True)
    dscores = (attention * (dattention - row_dot)).astype(jnp.bfloat16)
    dqueries = (
        jnp.einsum("hrk,khd->rhd", dscores, key_rows, preferred_element_type=jnp.float32) * scaling
    )
    dqueries = dqueries.astype(jnp.bfloat16).reshape(-1, query_width)
    dkeys = (
        jnp.einsum("hrk,rhd->khd", dscores, queries, preferred_element_type=jnp.float32) * scaling
    )
    dvalues = jnp.einsum(
        "hrk,rhd->khd", attention_again, dmixture, preferred_element_type=jnp.float32
    )
    grad_query = lax.dot_general(arrived, dqueries, DOWNWARD, preferred_element_type=jnp.float32)
    attend_dx = lax.dot_general(dqueries, query_full, ACROSS, preferred_element_type=jnp.float32)
    keyvalue_terms = jnp.concatenate(
        [dkeys.reshape(seq_total, query_width), dvalues.reshape(seq_total, query_width)], axis=1
    ).reshape(group_size, tok_rows, 2 * query_width)
    attend_home, keyvalue_home = (
        lax.all_to_all(
            attend_dx.reshape(group_size, slot_count, model_width).astype(jnp.bfloat16),
            "expert",
            split_axis=0,
            concat_axis=0,
            tiled=True,
        ).astype(jnp.float32),
        lax.all_to_all(
            keyvalue_terms.astype(jnp.bfloat16), "expert", split_axis=0, concat_axis=0, tiled=True
        ).astype(keyvalue_terms.dtype),
    )
    dkeyvalue = jnp.sum(keyvalue_home, axis=0).astype(jnp.bfloat16)
    attend_dnorm = (
        jnp.einsum("ect,ecd->td", attend_table, attend_home, precision=HIGH)
        + lax.dot_general(dkeyvalue, keyvalue_full, ACROSS, preferred_element_type=jnp.float32)
        + jnp.dot(attend_dlogits, attention_cols.astype(jnp.float32).T, precision=HIGH)
    )
    grad_keyvalue = lax.dot_general(
        attention_in, dkeyvalue, DOWNWARD, preferred_element_type=jnp.float32
    )
    grad_router = jnp.concatenate(
        [
            jnp.dot(attention_in.astype(jnp.float32).T, attend_dlogits, precision=HIGH),
            jnp.dot(feed_in.astype(jnp.float32).T, feed_dlogits, precision=HIGH),
        ],
        axis=1,
    )
    grad_gain_attend = jnp.sum(attend_dnorm * unit_attention, axis=0)
    grad_tokens = hidden_grad + norm_back(
        attend_dnorm, gain_attention, unit_attention, factor_attention
    )
    reduced = (
        lax.psum_scatter(
            grad_keyvalue.astype(jnp.bfloat16), "dp", scatter_dimension=0, tiled=True
        ).astype(jnp.float32),
        lax.psum_scatter(
            grad_router.astype(jnp.bfloat16), "dp", scatter_dimension=0, tiled=True
        ).astype(jnp.float32),
        lax.psum_scatter(
            grad_query.astype(jnp.bfloat16), "dp", scatter_dimension=0, tiled=True
        ).astype(jnp.float32),
        lax.psum_scatter(
            grad_projection.astype(jnp.bfloat16), "dp", scatter_dimension=0, tiled=True
        ).astype(jnp.float32),
        lax.psum_scatter(
            grad_gain_attend.astype(jnp.bfloat16), "dp", scatter_dimension=0, tiled=True
        ).astype(jnp.float32),
        lax.psum_scatter(
            grad_gain_feed.astype(jnp.bfloat16), "dp", scatter_dimension=0, tiled=True
        ).astype(jnp.float32),
    )
    shared = (
        lax.psum(reduced[0].astype(jnp.bfloat16), "expert").astype(jnp.float32),
        lax.psum(reduced[1].astype(jnp.bfloat16), "expert").astype(jnp.float32),
        lax.psum(reduced[4].astype(jnp.bfloat16), "expert").astype(jnp.float32),
        lax.psum(reduced[5].astype(jnp.bfloat16), "expert").astype(jnp.float32),
    )
    return (
        layer_output.astype(jnp.bfloat16)[None],
        grad_tokens[None],
        shared[2],
        shared[3],
        shared[0],
        shared[1],
        reduced[2][None],
        reduced[3][None],
        grad_gate[None],
        grad_up[None],
        grad_down[None],
    )


MESH = pl.DeviceIdType.MESH
CHIPS_Z = 4
TURNS = ((3, 2, 1, 0), (3, 0, 2, 1), (0, 3, 1, 2), (0, 1, 2, 3))


class Place:
    def __init__(self):
        self.dp, self.expert = lax.axis_index("dp"), lax.axis_index("expert")
        self.at = {
            "z": self.dp // 2,
            "y": self.dp % 2,
            "x": self.expert // 2,
            "c": self.expert % 2,
        }

    def across(self, axis):
        back = 1 - 2 * self.at[axis]
        if axis == "c":
            return (self.dp, self.expert + back)
        if axis == "x":
            return (self.dp, self.expert + 2 * back)
        return (self.dp + back, self.expert)

    def along(self, step):
        return (self.dp + 2 * step, self.expert)

    def block(self, whose, z, flips):
        at = {a: self.at[a] + flips.get(a, 0) * (1 - 2 * self.at[a]) for a in "xyc"}
        dp, expert = z * 2 + at["y"], at["x"] * 2 + at["c"]
        return {"all": dp * 4 + expert, "dp": dp, "expert": expert}[whose]


def enter(place, axes, others=()):
    barrier, count = pltpu.get_barrier_semaphore(), 0
    for device, condition in others:

        def greet(device=device):
            pl.semaphore_signal(barrier, inc=1, device_id=device, device_id_type=MESH)

        on(condition, greet)
        count = count + (1 if condition is None else condition.astype(jnp.int32))
    for axis in axes:
        if axis != "z":
            pl.semaphore_signal(
                barrier, inc=1, device_id=place.across(axis), device_id_type=MESH
            )
            count += 1
    if "z" in axes:
        z = place.at["z"]
        for step, there in ((-1, z > 0), (1, z < CHIPS_Z - 1)):

            @pl.when(there)
            def _(step=step):
                pl.semaphore_signal(
                    barrier, inc=1, device_id=place.along(step), device_id_type=MESH
                )

            count = count + there.astype(jnp.int32)
    pl.semaphore_wait(barrier, count)


def on(condition, action):
    if condition is None:
        action()
    else:
        pl.when(condition)(action)


def both(a, b):
    return b if a is None else a if b is None else a & b


class Post:
    def __init__(self, sems, place):
        self.sems, self.place, self.sent = sems, place, []

    def send(self, source, target, arrival, device, condition=None):
        number = len(self.sent)

        def copy():
            return pltpu.make_async_remote_copy(
                src_ref=source,
                dst_ref=target,
                send_sem=self.sems.at[number],
                recv_sem=arrival,
                device_id=device,
                device_id_type=MESH,
            )

        self.sent.append((condition, copy))
        on(condition, lambda: copy().start())

    def arrived(self, target, arrival):
        pltpu.make_async_remote_copy(
            src_ref=target,
            dst_ref=target,
            send_sem=self.sems.at[0],
            recv_sem=arrival,
            device_id=self.place.across("c"),
            device_id_type=MESH,
        ).wait_recv()

    def close(self):
        for condition, copy in self.sent:
            on(condition, lambda copy=copy: copy().wait_send())


FLIPS = {"x": 4, "y": 2, "c": 1}


def gather_plan(jobs, place, post, sources, targets, arrive_sems, own_sems):
    z_here = place.at["z"]
    line = 0
    waves, owns, starts = {}, [], []
    for j, (whose, rows, pieces) in enumerate(jobs):
        own = pltpu.make_async_copy(
            sources[j],
            targets[j].at[pl.ds(place.block(whose, z_here, {}) * rows, rows)],
            own_sems.at[j],
        )
        owns.append(own)
        begin = [own.start]
        for first, length, order in pieces:
            def part(z, flips, j=j, whose=whose, rows=rows, first=first, length=length):
                at = place.block(whose, z, flips) * rows + first
                return targets[j].at[pl.ds(at, length)]

            def mark(z, flips, line=line):
                return arrive_sems.at[line, z * 8 + sum(FLIPS[a] * v for a, v in flips.items())]

            def hand_on(source, z, flips, depth, side, wave, condition, order=order, part=part, mark=mark):
                for axis in order[max(depth, 0) :]:
                    if axis == "z" and (depth < 0 or order[depth] != "z"):
                        for step in (1, -1):
                            there = (z_here < CHIPS_Z - 1) if step > 0 else (z_here > 0)
                            post.send(source, part(z, flips), mark(z, flips), place.along(step), both(condition, there))
                    elif axis == "z":
                        there = (z_here < CHIPS_Z - 1) if side > 0 else (z_here > 0)
                        post.send(source, part(z, flips), mark(z, flips), place.along(side), both(condition, there))
                    elif depth < 0 or axis != order[depth]:
                        seen = dict(flips)
                        seen[axis] = 1
                        post.send(source, part(z, flips), mark(z, seen), place.across(axis), condition)

            def come(z, flips, depth, side, hops, wave, condition, order=order, part=part, mark=mark, hand_on=hand_on):
                def act():
                    on(condition, lambda: post.arrived(part(z, flips), mark(z, flips)))
                    hand_on(part(z, flips), z, flips, depth, side, wave, condition)

                waves.setdefault(wave, []).append(act)
                spread(z, flips, depth, side, hops, wave, condition, order, come)

            begin.append(
                lambda hand_on=hand_on, j=j, first=first, length=length: hand_on(
                    sources[j].at[pl.ds(first, length)], z_here, {}, -1, 0, 0, None
                )
            )
            spread(z_here, {}, -1, 0, 0, 0, None, order, come)
            line += 1
        starts.append(begin)
    return starts, waves, owns


def gather_kernel(jobs, axes, filler, *refs):
    count = len(jobs)
    sources, given, refs = refs[:count], refs[count : count + filler.operands], refs[count + filler.operands :]
    targets, made, refs = refs[:count], refs[count : count + filler.results], refs[count + filler.results :]
    send_sems, arrive_sems, own_sems = refs[:3]
    own = refs[3:]
    place = Place()
    enter(place, axes)
    post = Post(send_sems, place)
    starts, waves, owns = gather_plan(jobs, place, post, sources, targets, arrive_sems, own_sems)
    for act in sum(starts, []):
        act()
    steps, done = filler.start(given, made, own), 0
    for number, wave in enumerate(sorted(waves)):
        share = steps * (number + 1) // len(waves)
        filler.run(given, made, own, done, share)
        done = share
        for act in waves[wave]:
            act()
    for copy in owns:
        copy.wait()
    filler.end(given, made, own)
    post.close()


def spread(z, flips, depth, side, hops, wave, condition, order, come):
    z_here = lax.axis_index("dp") // 2
    for later in range(max(depth, 0), len(order)):
        axis = order[later]
        if axis == "z":
            if depth >= 0 and order[depth] == "z":
                if hops < CHIPS_Z - 1:
                    far = hops + 1
                    there = (z_here >= far) if side > 0 else (z_here + far < CHIPS_Z)
                    come(z_here - side * far, flips, later, side, far, wave + 1, there)
            else:
                for step in (1, -1):
                    there = (z_here >= 1) if step > 0 else (z_here + 1 < CHIPS_Z)
                    come(z_here - step, flips, later, step, 1, wave + 1, both(condition, there))
        elif later > depth:
            seen = dict(flips)
            seen[axis] = 1
            come(z, seen, later, 0, 0, wave + 1, condition)


class Nothing:
    operands = results = rooms = 0
    turns = 12
    shapes, scratch = [], []

    def start(self, given, made, own):
        return 0

    def run(self, given, made, own, first, last):
        pass

    def end(self, given, made, own):
        pass


def gather(jobs, collective_id, name, filler=Nothing(), operands=()):
    arrays = [rows for rows, _, _ in jobs]
    sizes = {"all": 32, "dp": 8, "expert": 4}
    plan = tuple((whose, rows.shape[0], pieces) for rows, whose, pieces in jobs)
    axes = "".join(a for a in "cxyz" if any(a in order for _, _, ps in plan for _, _, order in ps))
    lines = sum(len(ps) for _, _, ps in plan)
    hbm = pl.BlockSpec(memory_space=pltpu.HBM)
    return pl.pallas_call(
        functools.partial(gather_kernel, plan, axes, filler),
        out_shape=[
            jax.ShapeDtypeStruct((sizes[whose] * r.shape[0], r.shape[1]), r.dtype)
            for r, whose, _ in jobs
        ]
        + filler.shapes,
        in_specs=[hbm] * (len(jobs) + len(operands)),
        out_specs=[hbm] * (len(jobs) + filler.results),
        scratch_shapes=[
            pltpu.SemaphoreType.DMA((110 * lines,)),
            pltpu.SemaphoreType.DMA((lines, 32)),
            pltpu.SemaphoreType.DMA((len(jobs),)),
        ]
        + filler.scratch,
        compiler_params=pltpu.CompilerParams(
            collective_id=collective_id, has_side_effects=True, vmem_limit_bytes=48 * 2**20
        ),
        name=name,
    )(*arrays, *operands)


def add_into(target, terms, length):
    @pl.loop(0, length // 16)
    def _(r):
        at = pl.ds(pl.multiple_of(r * 16, 16), 16)
        total = target[at, :].astype(jnp.float32)
        for term in terms:
            total = total + term[at, :].astype(jnp.float32)
        target[at, :] = total.astype(jnp.bfloat16)


def scatter_rooms(rows, width, order):
    steps, turns = len(order.replace("z", "")), CHIPS_Z if "z" in order else 1
    blocks = [turns * 2 ** (steps - 1)]
    blocks += [turns * 2 ** (steps - 1 - stage) for stage in range(steps)]
    if "z" in order:
        blocks.append(CHIPS_Z + 1)
    return [pltpu.VMEM((n, rows, width), jnp.bfloat16) for n in blocks]


def scatter_sems(order, pieces):
    steps, turns = len(order.replace("z", "")), CHIPS_Z if "z" in order else 1
    return [
        pltpu.SemaphoreType.DMA((turns * 2 ** (steps - 1),)),
        pltpu.SemaphoreType.DMA((pieces, steps, turns * 2 ** (steps - 1))),
        pltpu.SemaphoreType.DMA((pieces, CHIPS_Z + 1)),
    ]


def scatter_plan(whose, rows, pieces, place, post, source, rooms, sems):
    flat = [order.replace("z", "") for _, _, order in pieces]
    steps = len(flat[0])
    lined = "z" in pieces[0][2]
    turns = CHIPS_Z if lined else 1
    acc, bins, line = rooms[0], rooms[1 : 1 + steps], rooms[-1]
    load_sems, bin_sems, line_sems = sems
    z_here = place.at["z"]
    if lined:
        turn = [
            sum((z_here == z).astype(jnp.int32) * seq[k] for z, seq in enumerate(TURNS))
            for k in range(CHIPS_Z)
        ]
    else:
        turn = [z_here]
    slot_z = lambda k: turn[k] if lined else 0
    keep = 2 ** (steps - 1)
    names = sorted(flat[0][1:])
    loads = {}
    for k in range(turns):
        for n in reversed(range(keep)):
            flips = {a: (n >> i) & 1 for i, a in enumerate(names)}
            at = slot_z(k) * keep + n
            loads[k, n] = pltpu.make_async_copy(
                source.at[pl.ds(place.block(whose, turn[k], flips) * rows, rows)],
                acc.at[at],
                load_sems.at[at],
            )
    loaded = set()

    def mine(p, ref):
        first, length, _ = pieces[p]
        return ref.at[pl.ds(first, length)]

    def code_after(p, stage, flips):
        return sum(flips.get(a, 0) << i for i, a in enumerate(flat[p][stage + 1 :]))

    def gathered(p, k, stage, flips):
        n = sum(flips.get(a, 0) << i for i, a in enumerate(names))
        if (k, n) not in loaded:
            loads[k, n].wait()
            loaded.add((k, n))
        terms = []
        for before in range(stage):
            at = slot_z(k) * 2 ** (steps - 1 - before) + code_after(p, before, flips)
            ref = mine(p, bins[before].at[at])
            post.arrived(ref, bin_sems.at[p, before, at])
            terms.append(ref)
        block = mine(p, acc.at[slot_z(k) * keep + n])
        add_into(block, terms, pieces[p][1])
        return block

    def leave(k, stage):
        for code in reversed(range(2 ** (steps - 1 - stage))):
            for p in range(len(pieces)):
                flips = {a: (code >> i) & 1 for i, a in enumerate(flat[p][stage + 1 :])}
                flips[flat[p][stage]] = 1
                if stage == 0:
                    at = place.block(whose, turn[k], flips) * rows + pieces[p][0]
                    block = source.at[pl.ds(at, pieces[p][1])]
                else:
                    block = gathered(p, k, stage, flips)
                at = slot_z(k) * 2 ** (steps - 1 - stage) + code
                post.send(
                    block,
                    mine(p, bins[stage].at[at]),
                    bin_sems.at[p, stage, at],
                    place.across(flat[p][stage]),
                )

    def settle(k):
        for p in range(len(pieces)):
            block = gathered(p, k, steps, {})
            if not lined or k == turns - 1:
                continue
            t = turn[k]
            right = t > z_here

            def pass_on(p=p, t=t, block=block):
                ref = mine(p, line.at[t])
                post.arrived(ref, line_sems.at[p, t])
                add_into(block, [ref], pieces[p][1])

            pl.when((right & (z_here > 0)) | (~right & (z_here < CHIPS_Z - 1)))(pass_on)
            slot = jnp.where(t == z_here - 1, CHIPS_Z, t)
            post.send(
                block,
                mine(p, line.at[slot]),
                line_sems.at[p, slot],
                place.along(jnp.where(right, 1, -1)),
            )

    def finish(p):
        block = mine(p, acc.at[z_here * keep if lined else 0])
        if lined:
            for slot, there in ((z_here, z_here > 0), (CHIPS_Z, z_here < CHIPS_Z - 1)):

                def last(slot=slot):
                    ref = mine(p, line.at[slot])
                    post.arrived(ref, line_sems.at[p, slot])
                    add_into(block, [ref], pieces[p][1])

                pl.when(there)(last)
        return block

    works = [(-1, lambda k=k: leave(k, 0)) for k in range(turns)]
    for time in range(turns + steps):
        for stage in range(1, steps + 1):
            k = time - stage + 1
            if 0 <= k < turns:
                act = settle if stage == steps else lambda k, stage=stage: leave(k, stage)
                works.append((time, lambda k=k, act=act: act(k)))
    return list(loads.values()), works, finish


def sends_of(order, pieces):
    steps, turns = len(order.replace("z", "")), CHIPS_Z if "z" in order else 1
    return pieces * (turns * 2**steps + 4)


def widen(target, block, length):
    @pl.loop(0, length // 16)
    def _(r):
        at = pl.ds(pl.multiple_of(r * 16, 16), 16)
        target[at, :] = block[at, :].astype(jnp.float32)


def scatter_kernel(whose, rows, pieces, columns, filler, source, *refs):
    source = source.at[:, pl.ds(*columns)]
    given, refs = refs[: filler.operands], refs[filler.operands :]
    result, made, refs = refs[0], refs[1 : 1 + filler.results], refs[1 + filler.results :]
    rooms, refs = refs[: len(refs) - 4 - filler.rooms], refs[len(refs) - 4 - filler.rooms :]
    send_sems, sems, own = refs[0], refs[1:4], refs[4:]
    place = Place()
    post = Post(send_sems, place)
    loads, works, finish = scatter_plan(whose, rows, pieces, place, post, source, rooms, sems)
    for load in loads:
        load.start()
    enter(place, "".join(a for a in "cxyz" if a in pieces[0][2]))
    steps = filler.start(given, made, own)
    slots = [number for number, (time, _) in enumerate(works) if time >= 0]
    slots = slots[:: -(-len(slots) // filler.turns)]
    done = 0
    for number, (_, act) in enumerate(works):
        act()
        if number in slots:
            share = steps * (slots.index(number) + 1) // len(slots)
            filler.run(given, made, own, done, share)
            done = share
    for p in range(len(pieces)):
        first, length, _ = pieces[p]
        widen(result.at[pl.ds(first, length)], finish(p), length)
    filler.end(given, made, own)
    post.close()


class WeightGrads(Nothing):
    operands, results, rooms = 4, 3, 6
    TILE, CHUNK = 256, 512

    def __init__(self, rows, padded, hidden, width):
        self.chunks = rows // self.CHUNK
        self.each = padded // self.TILE
        self.short = hidden - (self.each - 1) * self.TILE
        self.tiles = (2 * self.each, self.each)
        self.shapes = [jax.ShapeDtypeStruct((hidden, width), jnp.float32)] * 3
        self.scratch = [
            pltpu.VMEM((2, self.CHUNK, self.TILE), jnp.bfloat16),
            pltpu.VMEM((2, self.CHUNK, width), jnp.bfloat16),
            pltpu.VMEM((self.TILE, width), jnp.float32),
            pltpu.VMEM((self.TILE, width), jnp.float32),
            pltpu.SemaphoreType.DMA((2, 2)),
            pltpu.SemaphoreType.DMA((2,)),
        ]

    def copies(self, given, own, step, second):
        tile, chunk = step // self.chunks - (self.tiles[0] if second else 0), step % self.chunks
        slot = step % 2
        rows = pl.ds(pl.multiple_of(chunk * self.CHUNK, self.CHUNK), self.CHUNK)
        cols = pl.ds(pl.multiple_of(tile * self.TILE, self.TILE), self.TILE)
        left, right = given[2 * second], given[2 * second + 1]
        return [
            pltpu.make_async_copy(left.at[rows, cols], own[0].at[slot], own[4].at[slot, 0]),
            pltpu.make_async_copy(right.at[rows], own[1].at[slot], own[4].at[slot, 1]),
        ]

    def fetch(self, given, own, step, start):
        edge = self.tiles[0] * self.chunks
        for second in (0, 1):

            @pl.when((step >= edge) if second else (step < edge))
            def _(second=second):
                for copy in self.copies(given, own, step, second):
                    copy.start() if start else copy.wait()

    def put(self, made, own, tile, parity, start):
        row = (tile % self.each) * self.TILE
        for result in range(3):
            for last in (0, 1):
                length = self.short if last else self.TILE
                at_end = (tile % self.each) == self.each - 1

                @pl.when((tile // self.each == result) & (at_end if last else ~at_end))
                def _(result=result, length=length):
                    copy = pltpu.make_async_copy(
                        own[2 + parity].at[pl.ds(0, length)],
                        made[result].at[pl.ds(pl.multiple_of(row, self.TILE), length)],
                        own[5].at[parity],
                    )
                    copy.start() if start else copy.wait()

    def start(self, given, made, own):
        self.fetch(given, own, jnp.int32(0), True)
        return sum(self.tiles) * self.chunks

    def run(self, given, made, own, first, last):
        total = sum(self.tiles) * self.chunks

        @pl.loop(first, last)
        def _(step):
            tile, chunk = step // self.chunks, step % self.chunks

            @pl.when(step + 1 < total)
            def _():
                self.fetch(given, own, step + 1, True)

            self.fetch(given, own, step, False)
            part = lax.dot_general(
                own[0][step % 2], own[1][step % 2], DOWNWARD, preferred_element_type=jnp.float32
            )
            for parity in (0, 1):

                @pl.when(tile % 2 == parity)
                def _(parity=parity):
                    acc = own[2 + parity]

                    @pl.when(chunk == 0)
                    def _():
                        @pl.when(tile >= 2)
                        def _():
                            self.put(made, own, tile - 2, parity, False)

                        acc[...] = part

                    @pl.when(chunk > 0)
                    def _():
                        acc[...] += part

                    @pl.when(chunk == self.chunks - 1)
                    def _():
                        self.put(made, own, tile, parity, True)

    def end(self, given, made, own):
        tiles = sum(self.tiles)
        for tile in (tiles - 2, tiles - 1):
            self.put(made, own, jnp.int32(tile), tile % 2, False)


class LowGrad(Nothing):
    operands, results, rooms = 2, 1, 5
    TILE = 256

    def __init__(self, rows, left, width, turns):
        self.tiles, self.width, self.turns = left // self.TILE, width, turns
        low = jnp.bfloat16
        self.shapes = [jax.ShapeDtypeStruct((left, width), low)]
        self.scratch = [
            pltpu.VMEM((2, rows, self.TILE), low),
            pltpu.VMEM((rows, width), low),
            pltpu.VMEM((2, self.TILE, width), low),
            pltpu.SemaphoreType.DMA((3,)),
            pltpu.SemaphoreType.DMA((2,)),
        ]

    def left(self, given, own, tile):
        at = pl.ds(pl.multiple_of(tile * self.TILE, self.TILE), self.TILE)
        return pltpu.make_async_copy(given[0].at[:, at], own[0].at[tile % 2], own[3].at[tile % 2])

    def right(self, given, own):
        return pltpu.make_async_copy(given[1], own[1], own[3].at[2])

    def put(self, made, own, tile):
        rows = pl.ds(pl.multiple_of(tile * self.TILE, self.TILE), self.TILE)
        return pltpu.make_async_copy(own[2].at[tile % 2], made[0].at[rows], own[4].at[tile % 2])

    def start(self, given, made, own):
        self.right(given, own).start()
        self.left(given, own, jnp.int32(0)).start()
        return self.tiles

    def run(self, given, made, own, first, last):
        if first == last:
            return
        if first == 0:
            self.right(given, own).wait()

        @pl.loop(first, last)
        def _(tile):
            slot = tile % 2

            @pl.when(tile + 1 < self.tiles)
            def _():
                self.left(given, own, tile + 1).start()

            self.left(given, own, tile).wait()

            @pl.when(tile >= 2)
            def _():
                self.put(made, own, tile - 2).wait()

            half = self.width // 2
            for part in (0, 1):
                cols = slice(part * half, (part + 1) * half)
                own[2][slot, :, cols] = lax.dot_general(
                    own[0][slot], own[1][:, cols], DOWNWARD, preferred_element_type=jnp.float32
                ).astype(jnp.bfloat16)
            self.put(made, own, tile).start()

    def end(self, given, made, own):
        for tile in (self.tiles - 2, self.tiles - 1):
            self.put(made, own, jnp.int32(tile)).wait()


class RowGrads(Nothing):
    operands, results, rooms = 3, 1, 7
    TILE, turns = 256, 4

    def __init__(self, rows, depth, width):
        self.tiles, self.width = width // self.TILE, width
        low = jnp.bfloat16
        self.shapes = [jax.ShapeDtypeStruct((rows, width + 128), low)]
        self.scratch = [
            pltpu.VMEM((rows, depth), low),
            pltpu.VMEM((2, self.TILE, depth), low),
            pltpu.VMEM((2, rows, self.TILE), low),
            pltpu.VMEM((rows, 128), jnp.float32),
            pltpu.VMEM((rows, 128), low),
            pltpu.SemaphoreType.DMA((4,)),
            pltpu.SemaphoreType.DMA((3,)),
        ]

    def whole(self, given, own):
        return [
            pltpu.make_async_copy(given[0], own[0], own[5].at[2]),
            pltpu.make_async_copy(given[2], own[3], own[5].at[3]),
        ]

    def right(self, given, own, tile):
        at = pl.ds(pl.multiple_of(tile * self.TILE, self.TILE), self.TILE)
        return pltpu.make_async_copy(given[1].at[at], own[1].at[tile % 2], own[5].at[tile % 2])

    def put(self, made, own, tile):
        at = pl.ds(pl.multiple_of(tile * self.TILE, self.TILE), self.TILE)
        return pltpu.make_async_copy(own[2].at[tile % 2], made[0].at[:, at], own[6].at[tile % 2])

    def extra(self, made, own):
        return pltpu.make_async_copy(own[4], made[0].at[:, pl.ds(self.width, 128)], own[6].at[2])

    def start(self, given, made, own):
        for copy in self.whole(given, own):
            copy.start()
        self.right(given, own, jnp.int32(0)).start()
        return self.tiles

    def run(self, given, made, own, first, last):
        if first == last:
            return
        if first == 0:
            for copy in self.whole(given, own):
                copy.wait()
            own[4][...] = own[3][...].astype(jnp.bfloat16)
            self.extra(made, own).start()

        @pl.loop(first, last)
        def _(tile):
            slot = tile % 2

            @pl.when(tile + 1 < self.tiles)
            def _():
                self.right(given, own, tile + 1).start()

            self.right(given, own, tile).wait()

            @pl.when(tile >= 2)
            def _():
                self.put(made, own, tile - 2).wait()

            own[2][slot] = lax.dot_general(
                own[0][...], own[1][slot], ACROSS, preferred_element_type=jnp.float32
            ).astype(jnp.bfloat16)
            self.put(made, own, tile).start()

    def end(self, given, made, own):
        self.extra(made, own).wait()
        for tile in (self.tiles - 2, self.tiles - 1):
            self.put(made, own, jnp.int32(tile)).wait()


class InTurn(Nothing):
    def __init__(self, one, other):
        self.parts = (one, other)
        self.operands = one.operands + other.operands
        self.results = one.results + other.results
        self.rooms = one.rooms + other.rooms
        self.turns = one.turns + other.turns
        self.shapes, self.scratch = one.shapes + other.shapes, one.scratch + other.scratch

    def split(self, given, made, own):
        one = self.parts[0]
        return (
            (given[: one.operands], made[: one.results], own[: one.rooms]),
            (given[one.operands :], made[one.results :], own[one.rooms :]),
        )

    def start(self, *refs):
        self.steps = [part.start(*own) for part, own in zip(self.parts, self.split(*refs))]
        return self.parts[0].turns + self.parts[1].turns

    def run(self, given, made, own, first, last):
        edge = self.parts[0].turns
        for n, (part, refs) in enumerate(zip(self.parts, self.split(given, made, own))):
            low, high = (0, edge) if n == 0 else (edge, edge + part.turns)
            begin, end = max(first, low) - low, min(last, high) - low
            if begin < end:
                steps = self.steps[n]
                part.run(*refs, steps * begin // part.turns, steps * end // part.turns)

    def end(self, *refs):
        for part, own in zip(self.parts, self.split(*refs)):
            part.end(*own)


def scatter(array, whose, pieces, collective_id, name, filler=Nothing(), operands=(), columns=None):
    size = {"all": 32, "dp": 8, "expert": 4}[whose]
    columns = columns or (0, array.shape[1])
    rows, width = array.shape[0] // size, columns[1]
    order, count = pieces[0][2], len(pieces)
    hbm = pl.BlockSpec(memory_space=pltpu.HBM)
    out = pl.pallas_call(
        functools.partial(scatter_kernel, whose, rows, pieces, columns, filler),
        out_shape=[jax.ShapeDtypeStruct((rows, width), jnp.float32)] + filler.shapes,
        in_specs=[hbm] * (1 + len(operands)),
        out_specs=[pl.BlockSpec(memory_space=pltpu.VMEM)] + [hbm] * filler.results,
        scratch_shapes=scatter_rooms(rows, width, order)
        + [pltpu.SemaphoreType.DMA((sends_of(order, count),))]
        + scatter_sems(order, count)
        + filler.scratch,
        compiler_params=pltpu.CompilerParams(
            collective_id=collective_id, has_side_effects=True, vmem_limit_bytes=63 * 2**20
        ),
        name=name,
    )(array, *operands)
    return out if filler.results else out[0]


def sum_with_output_kernel(rows, pieces, out_rows, out_pieces, filler, source, out_grad, *refs):
    given, refs = refs[: filler.operands], refs[filler.operands :]
    result, output, refs = refs[0], refs[1], refs[2:]
    made, refs = refs[: filler.results], refs[filler.results :]
    count = len(scatter_rooms(rows, 128, pieces[0][2]))
    rooms, refs = refs[:count], refs[count:]
    count = len(scatter_rooms(rows, 128, out_pieces[0][2]))
    out_rooms, refs = refs[:count], refs[count:]
    send_sems = refs[0]
    sems, out_sems, own = refs[1:4], refs[4:7], refs[7:]
    place = Place()
    post = Post(send_sems, place)
    loads, works, finish = scatter_plan(
        "expert", rows, pieces, place, post, source, rooms, sems
    )
    out_loads, out_works, out_finish = scatter_plan(
        "dp", out_rows, out_pieces, place, post, out_grad, out_rooms, out_sems
    )
    for load in loads + out_loads:
        load.start()
    enter(place, "cxyz")
    steps = filler.start(given, made, own)
    times = sorted({time for time, _ in works + out_works})
    turns = [time for time in times if time >= 0]
    done = 0
    for time in times:
        for plan in (works, out_works):
            for at, act in plan:
                if at == time:
                    act()
        if time >= 0:
            share = steps * (turns.index(time) + 1) // len(turns)
            filler.run(given, made, own, done, share)
            done = share
    for p in range(len(out_pieces)):
        first, length, _ = out_pieces[p]
        output[pl.ds(first, length), :] = out_finish(p)[...]
    for p in range(len(pieces)):
        first, length, _ = pieces[p]
        widen(result.at[pl.ds(first, length)], finish(p), length)
    filler.end(given, made, own)
    post.close()


def sum_with_output(array, pieces, out_grad, out_pieces, collective_id, filler, operands):
    rows, width = array.shape[0] // 4, array.shape[1]
    out_rows, out_width = out_grad.shape[0] // 8, out_grad.shape[1]
    order, out_order = pieces[0][2], out_pieces[0][2]
    hbm = pl.BlockSpec(memory_space=pltpu.HBM)
    vmem = pl.BlockSpec(memory_space=pltpu.VMEM)
    shape = jax.ShapeDtypeStruct
    sends = sends_of(order, len(pieces)) + sends_of(out_order, len(out_pieces))
    return pl.pallas_call(
        functools.partial(
            sum_with_output_kernel, rows, pieces, out_rows, out_pieces, filler
        ),
        out_shape=[
            shape((rows, width), jnp.float32),
            shape((out_rows, out_width), jnp.bfloat16),
        ]
        + filler.shapes,
        in_specs=[hbm] * (2 + len(operands)),
        out_specs=[vmem] * 2 + [hbm] * filler.results,
        scratch_shapes=scatter_rooms(rows, width, order)
        + scatter_rooms(out_rows, out_width, out_order)
        + [
            pltpu.SemaphoreType.DMA((sends,)),
        ]
        + scatter_sems(order, len(pieces))
        + scatter_sems(out_order, len(out_pieces))
        + filler.scratch,
        compiler_params=pltpu.CompilerParams(
            collective_id=collective_id, has_side_effects=True, vmem_limit_bytes=63 * 2**20
        ),
        name="sum_attention_back",
    )(array, out_grad, *operands)


def sum_weights_kernel(rows, pieces, in_grad, out_rows, query, keyvalue, output, *refs):
    count = len(scatter_rooms(rows, 128, pieces[0][2]))
    rooms = refs[:count]
    dealt, shared, out_dealt, send_sems, deal_sems = refs[count : count + 5]
    place = Place()
    post = Post(send_sems, place)
    z, e = place.at["z"], place.expert
    wide = query.shape[1]
    span = (in_grad.shape[1] - wide) // 2
    peers = []
    for flip_x, flip_c in ((1, 1), (1, 0), (0, 1)):
        x = place.at["x"] + flip_x * (1 - 2 * place.at["x"])
        core = place.at["c"] + flip_c * (1 - 2 * place.at["c"])
        peers.append((x * 2 + core, flip_x * 2 + flip_c))
    loads, works, finish = scatter_plan(
        "dp", rows, pieces, place, post, in_grad, rooms, refs[count + 5 :]
    )
    for load in loads:
        load.start()
    partner, moves = (e * 2 + place.at["y"], z), z != e
    enter(place, "cxyz", [((place.dp, peers[0][0]), None), (partner, moves)])
    stay = pltpu.make_async_copy(out_rows, out_dealt, deal_sems.at[0, 0])
    pl.when(~moves)(stay.start)
    for time, act in works:
        if time == 0:
            break
        act()
    post.send(out_rows, out_dealt, deal_sems.at[0, 7], partner, moves)
    for time, act in works:
        if time >= 0:
            act()
    cols = lambda block: pl.ds(pl.multiple_of(block * span, span), span)
    keep = slice(wide, wide + 2 * span)
    for p in range(len(pieces)):
        first, length, _ = pieces[p]
        at = pl.ds(first, length)
        block = finish(p)
        post.send(block.at[:, keep], shared.at[2, at], deal_sems.at[p, 4], place.across("x"))
        for peer, flips in peers:
            post.send(
                block.at[:, cols(peer)],
                dealt.at[at, cols(e)],
                deal_sems.at[p, flips],
                (place.dp, peer),
            )
        post.send(block.at[:, keep], shared.at[1, at], deal_sems.at[p, 5], place.across("c"))

    def place_keys(p, flips, block):
        first, length, _ = pieces[p]
        rows_at = pl.ds(first, length)
        x = place.at["x"] + (flips // 2) * (1 - 2 * place.at["x"])
        core = place.at["c"] + (flips % 2) * (1 - 2 * place.at["c"])
        owner = x * 2 + core
        widen(keyvalue.at[rows_at, cols(owner)], block.at[:, pl.ds(0, span)], length)
        widen(
            keyvalue.at[rows_at, cols(wide // span + owner)], block.at[:, pl.ds(span, span)], length
        )

    for p in range(len(pieces)):
        first, length, _ = pieces[p]
        at = pl.ds(first, length)
        block = rooms[0].at[z, at]
        widen(query.at[at, cols(e)], block.at[:, cols(e)], length)
        place_keys(p, 0, block.at[:, keep])
        post.arrived(shared.at[1, at], deal_sems.at[p, 5])
        place_keys(p, 1, shared.at[1, at])
        post.arrived(shared.at[2, at], deal_sems.at[p, 4])
        post.send(shared.at[2, at], shared.at[3, at], deal_sems.at[p, 6], place.across("c"))
        place_keys(p, 2, shared.at[2, at])
        for peer, flips in reversed(peers):
            post.arrived(dealt.at[at, cols(peer)], deal_sems.at[p, flips])
            widen(query.at[at, cols(peer)], dealt.at[at, cols(peer)], length)
        post.arrived(shared.at[3, at], deal_sems.at[p, 6])
        place_keys(p, 3, shared.at[3, at])
    pl.when(~moves)(stay.wait)
    pl.when(moves)(lambda: post.arrived(out_dealt, deal_sems.at[0, 7]))
    widen(output, out_dealt, rows)
    post.close()


def sum_weights(in_grad, out_rows, pieces, collective_id):
    wide = out_rows.shape[1]
    rows, total = in_grad.shape[0] // 8, in_grad.shape[1]
    order, count = pieces[0][2], len(pieces)
    vmem = pl.BlockSpec(memory_space=pltpu.VMEM)
    shape = jax.ShapeDtypeStruct
    return pl.pallas_call(
        functools.partial(sum_weights_kernel, rows, pieces),
        out_shape=[
            shape((rows, wide), jnp.float32),
            shape((rows, 2 * wide), jnp.float32),
            shape((rows, wide), jnp.float32),
        ],
        in_specs=[pl.BlockSpec(memory_space=pltpu.HBM)] * 2,
        out_specs=[vmem] * 3,
        scratch_shapes=scatter_rooms(rows, total, order)
        + [
            pltpu.VMEM((rows, wide), jnp.bfloat16),
            pltpu.VMEM((4, rows, total - wide), jnp.bfloat16),
            pltpu.VMEM((rows, wide), jnp.bfloat16),
            pltpu.SemaphoreType.DMA((sends_of(order, count) + 7 * count + 1,)),
            pltpu.SemaphoreType.DMA((count, 8)),
        ]
        + scatter_sems(order, count),
        compiler_params=pltpu.CompilerParams(
            collective_id=collective_id, has_side_effects=True, vmem_limit_bytes=63 * 2**20
        ),
        name="sum_weights",
    )(in_grad, out_rows)


def weights_kernel(jobs, *refs):
    ready = len(jobs) - 2
    sources, (query, keyvalue, output) = refs[:ready], refs[ready : ready + 3]
    in_shard, out_shard = refs[ready + 3 : ready + 5]
    targets = refs[ready + 5 : 2 * ready + 7]
    send_sems, arrive_sems, own_sems, deal_sems = refs[2 * ready + 7 :]
    place = Place()
    z, y, e = place.at["z"], place.at["y"], place.expert
    span = (in_shard.shape[1] - query.shape[1]) // 2
    wide = query.shape[1]
    partner, moves = (e * 2 + y, z), z != e
    peers = []
    for flip_x, flip_c in ((1, 1), (1, 0), (0, 1)):
        x = place.at["x"] + flip_x * (1 - 2 * place.at["x"])
        core = place.at["c"] + flip_c * (1 - 2 * place.at["c"])
        peers.append((x * 2 + core, flip_x * 2 + flip_c))
    enter(place, "cxyz", [((place.dp, peers[0][0]), None), (partner, moves)])
    post = Post(send_sems, place)
    starts, waves, owns = gather_plan(
        jobs, place, post, list(sources) + [in_shard, out_shard], targets, arrive_sems, own_sems
    )
    cols = lambda block: pl.ds(pl.multiple_of(block * span, span), span)
    for peer, flips in peers:
        post.send(
            query.at[:, cols(peer)], in_shard.at[:, cols(e)], deal_sems.at[flips], (place.dp, peer)
        )
    post.send(output, out_shard, deal_sems.at[4], partner, moves)
    local = [
        pltpu.make_async_copy(query.at[:, cols(e)], in_shard.at[:, cols(e)], deal_sems.at[0]),
        pltpu.make_async_copy(
            keyvalue.at[:, cols(e)], in_shard.at[:, pl.ds(wide, span)], deal_sems.at[5]
        ),
        pltpu.make_async_copy(
            keyvalue.at[:, cols(wide // span + e)],
            in_shard.at[:, pl.ds(wide + span, span)],
            deal_sems.at[6],
        ),
    ]
    for copy in local:
        copy.start()
    stay = pltpu.make_async_copy(output, out_shard, deal_sems.at[7])
    pl.when(~moves)(stay.start)
    for act in sum(starts[:ready], []):
        act()
    for copy in local:
        copy.wait()
    for peer, flips in peers:
        post.arrived(in_shard.at[:, cols(peer)], deal_sems.at[flips])
    for act in starts[ready]:
        act()
    pl.when(~moves)(stay.wait)
    pl.when(moves)(lambda: post.arrived(out_shard, deal_sems.at[4]))
    for act in starts[ready + 1]:
        act()
    for wave in sorted(waves):
        for act in waves[wave]:
            act()
    for own in owns:
        own.wait()
    post.close()


def gather_weights(jobs, query, keyvalue, output, pieces, collective_id):
    rows, wide = query.shape
    span = wide // lax.axis_size("expert")
    shards = [
        jax.ShapeDtypeStruct((rows, wide + 2 * span), query.dtype),
        jax.ShapeDtypeStruct(output.shape, output.dtype),
    ]
    sizes = {"all": 32, "dp": 8, "expert": 4}
    plan = tuple((whose, r.shape[0], ps) for r, whose, ps in jobs)
    plan += tuple(("dp", s.shape[0], pieces) for s in shards)
    lines = sum(len(ps) for _, _, ps in plan)
    hbm = pl.BlockSpec(memory_space=pltpu.HBM)
    gathered = [
        jax.ShapeDtypeStruct((sizes[whose] * r.shape[0], r.shape[1]), r.dtype)
        for r, (whose, _, _) in zip([r for r, _, _ in jobs] + shards, plan)
    ]
    out = pl.pallas_call(
        functools.partial(weights_kernel, plan),
        out_shape=shards + gathered,
        in_specs=[hbm] * (len(jobs) + 3),
        out_specs=[hbm] * (2 + len(gathered)),
        scratch_shapes=[
            pltpu.SemaphoreType.DMA((110 * lines,)),
            pltpu.SemaphoreType.DMA((lines, 32)),
            pltpu.SemaphoreType.DMA((len(plan),)),
            pltpu.SemaphoreType.DMA((8,)),
        ],
        compiler_params=pltpu.CompilerParams(collective_id=collective_id, has_side_effects=True),
        name="gather_weights",
    )(*[r for r, _, _ in jobs], query, keyvalue, output)
    return out[2:]


def attention_bias(bias, block, rows, width, prefix):
    query = block * rows + lax.broadcasted_iota(jnp.int32, (rows, width), 0)
    key = lax.broadcasted_iota(jnp.int32, (rows, width), 1)
    bias[:, :width] = jnp.where((key <= query) | (key < prefix), 0.0, NEG)


def pick_expert(ref, lane, experts, span, chosen):
    total = None
    for e in range(experts):
        cols = ref[:, pl.ds(pl.multiple_of(e * span + lane, HEAD_DIM), HEAD_DIM)]
        term = jnp.where(chosen == e, cols.astype(jnp.float32), 0.0)
        total = term if total is None else total + term
    return total.astype(jnp.bfloat16)


def key_limits(blocks, rows):
    return [max((i + 1) * rows, blocks * rows // 2) for i in range(blocks)]


def for_each_limit(blocks, rows, body):
    block = pl.program_id(0)
    limits = key_limits(blocks, rows)
    for width in sorted(set(limits)):
        members = [i for i, limit in enumerate(limits) if limit == width]
        pl.when((block >= members[0]) & (block <= members[-1]))(lambda width=width: body(width))


def attention_kernel(experts, prefix, q, k, v, side, mixed, log_total, bias):
    rows, span = q.shape[0], k.shape[1]
    heads = span // HEAD_DIM
    block = pl.program_id(0)
    chosen = [side[:, 0:1], side[:, 1:2]]
    gates = [side[:, 2:3], side[:, 3:4]]

    def body(width):
        attention_bias(bias, block, rows, width, prefix[0])

        @pl.loop(0, heads)
        def _(head):
            lane = head * HEAD_DIM
            lanes = pl.ds(pl.multiple_of(lane, HEAD_DIM), HEAD_DIM)
            weighted = []
            for j in range(2):
                query = pick_expert(q, lane, experts, span, chosen[j])
                scores = lax.dot_general(
                    query, k[:width, lanes], ACROSS, preferred_element_type=jnp.float32
                )
                scores = scores * (HEAD_DIM**-0.5) + bias[:, :width]
                largest = jnp.max(scores, axis=1, keepdims=True)
                exponent = jnp.exp(scores - largest)
                total = jnp.sum(exponent, axis=1, keepdims=True)
                low = (exponent * (1.0 / total)).astype(jnp.bfloat16)
                out = jnp.dot(low, v[:width, lanes], preferred_element_type=jnp.float32)
                weighted.append(out * gates[j])
                at = pl.ds(pl.multiple_of((2 * head + j) * HEAD_DIM, HEAD_DIM), HEAD_DIM)
                log_total[:, at] = jnp.broadcast_to(
                    largest + jnp.log(total), (rows, HEAD_DIM)
                )
            for e in range(experts):
                cols = jnp.where(chosen[0] == e, weighted[0], 0.0) + jnp.where(
                    chosen[1] == e, weighted[1], 0.0
                )
                at = pl.ds(pl.multiple_of(e * span + lane, HEAD_DIM), HEAD_DIM)
                mixed[:, at] = cols.astype(jnp.bfloat16)

    for_each_limit(k.shape[0] // rows, rows, body)


def attention(projected, side, prefix, experts, rows):
    length = projected.shape[0]
    span = projected.shape[1] // (experts + 2)
    wide = experts * span
    return pl.pallas_call(
        functools.partial(attention_kernel, experts),
        grid=(length // rows,),
        in_specs=[
            pl.BlockSpec(memory_space=pltpu.SMEM),
            pl.BlockSpec((rows, wide), lambda i: (i, 0)),
            pl.BlockSpec((length, span), lambda i: (0, experts)),
            pl.BlockSpec((length, span), lambda i: (0, experts + 1)),
            pl.BlockSpec((rows, 128), lambda i: (i, 0)),
        ],
        out_specs=[
            pl.BlockSpec((rows, wide), lambda i: (i, 0)),
            pl.BlockSpec((rows, 2 * span), lambda i: (i, 0)),
        ],
        out_shape=[
            jax.ShapeDtypeStruct((length, wide), jnp.bfloat16),
            jax.ShapeDtypeStruct((length, 2 * span), jnp.float32),
        ],
        scratch_shapes=[pltpu.VMEM((rows, length), jnp.float32)],
        compiler_params=pltpu.CompilerParams(vmem_limit_bytes=48 * 2**20),
        name="attention",
    )(prefix, projected, projected, projected, side)


class AttentionBack(Nothing):
    operands, results, rooms = 4, 2, 11
    turns = 4

    def __init__(self, length, total, experts, rows):
        self.length, self.experts, self.rows = length, experts, rows
        self.span = total // (experts + 2)
        low, f32 = jnp.bfloat16, jnp.float32
        self.heads = self.span // HEAD_DIM
        self.blocks = length // rows
        self.shapes = [
            jax.ShapeDtypeStruct((length, total), low),
            jax.ShapeDtypeStruct((length, 128), f32),
        ]
        self.scratch = [
            pltpu.VMEM((length, total), low),
            pltpu.VMEM((length, 128), f32),
            pltpu.VMEM((length, 2 * self.span), f32),
            pltpu.VMEM((length, experts * self.span), low),
            pltpu.VMEM((length, total), low),
            pltpu.VMEM((length, 128), f32),
            pltpu.VMEM((rows, length), f32),
            pltpu.VMEM((length, self.span), f32),
            pltpu.VMEM((length, self.span), f32),
            pltpu.SemaphoreType.DMA((4,)),
            pltpu.SemaphoreType.DMA((2,)),
        ]

    def loads(self, given, own):
        return [pltpu.make_async_copy(given[i], own[i], own[9].at[i]) for i in range(4)]

    def start(self, given, made, own):
        for load in self.loads(given, own):
            load.start()
        for ref in (own[5], own[7], own[8]):
            ref[...] = jnp.zeros_like(ref)
        return self.blocks * self.heads

    def run(self, given, made, own, first, last):
        if first == 0:
            for load in self.loads(given, own):
                load.wait()

        @pl.loop(first, last)
        def _(step):
            block = step // self.heads
            limits = key_limits(self.blocks, self.rows)
            for width in sorted(set(limits)):
                members = [i for i, limit in enumerate(limits) if limit == width]

                @pl.when((block >= members[0]) & (block <= members[-1]))
                def _(width=width):
                    self.step(own, block, step % self.heads, width)

    def step(self, own, block, head, width):
        qkv, side_ref, log_total, dmix, dprojected, dgate, bias, dk, dv = own[:9]
        experts, span, rows = self.experts, self.span, self.rows
        scaling = HEAD_DIM**-0.5
        row_at = pl.ds(pl.multiple_of(block * rows, rows), rows)
        side = side_ref[row_at, :]
        chosen = [side[:, 0:1], side[:, 1:2]]
        gates = [side[:, 2:3], side[:, 3:4]]
        column = lax.broadcasted_iota(jnp.int32, (rows, 128), 1)
        query_at = block * rows + lax.broadcasted_iota(jnp.int32, (rows, width), 0)
        key_at = lax.broadcasted_iota(jnp.int32, (rows, width), 1)
        reach = key_at.astype(jnp.float32) < side[:, 4:5]
        bias[:, :width] = jnp.where((key_at <= query_at) | reach, 0.0, NEG)
        lane = head * HEAD_DIM
        lanes = lambda base: pl.ds(pl.multiple_of(base + lane, HEAD_DIM), HEAD_DIM)
        keys = qkv[:width, lanes(experts * span)]
        values = qkv[:width, lanes((experts + 1) * span)]
        dqueries = []
        for j in range(2):
            query = pick_expert(qkv.at[row_at], lane, experts, span, chosen[j])
            dm = pick_expert(dmix.at[row_at], lane, experts, span, chosen[j])
            at = pl.ds(pl.multiple_of((2 * head + j) * HEAD_DIM, HEAD_DIM), HEAD_DIM)
            logs = jnp.tile(log_total[row_at, at], (1, width // HEAD_DIM))
            scores = lax.dot_general(query, keys, ACROSS, preferred_element_type=jnp.float32)
            probs = jnp.exp(scores * scaling + bias[:, :width] - logs)
            dprobs = lax.dot_general(dm, values, ACROSS, preferred_element_type=jnp.float32)
            inner = jnp.sum(probs * dprobs, axis=1, keepdims=True)
            dgate[row_at, :] += jnp.where(column == j, inner, 0.0)
            probs = probs * gates[j]
            dscores = (probs * (dprobs - inner)).astype(jnp.bfloat16)
            low = probs.astype(jnp.bfloat16)
            dqueries.append(jnp.dot(dscores, keys, preferred_element_type=jnp.float32) * scaling)
            dk[:width, lanes(0)] += lax.dot_general(
                dscores, query, DOWNWARD, preferred_element_type=jnp.float32
            )
            dv[:width, lanes(0)] += lax.dot_general(
                low, dm, DOWNWARD, preferred_element_type=jnp.float32
            )
        for e in range(experts):
            cols = jnp.where(chosen[0] == e, dqueries[0], 0.0) + jnp.where(
                chosen[1] == e, dqueries[1], 0.0
            )
            dprojected[row_at, lanes(e * span)] = cols.astype(jnp.bfloat16)

    def end(self, given, made, own):
        dprojected, dgate, dk, dv = own[4], own[5], own[7], own[8]
        wide = self.experts * self.span
        dprojected[:, wide : wide + self.span] = (dk[...] * HEAD_DIM**-0.5).astype(jnp.bfloat16)
        dprojected[:, wide + self.span :] = dv[...].astype(jnp.bfloat16)
        copies = [
            pltpu.make_async_copy(dprojected, made[0], own[10].at[0]),
            pltpu.make_async_copy(dgate, made[1], own[10].at[1]),
        ]
        for copy in copies:
            copy.start()
        for copy in copies:
            copy.wait()


def chip_in_turn(u, z_here):
    u = jnp.asarray(u, jnp.int32)
    turn, q = u // 4, u % 4
    flip = lambda *at: ((q == at[0]) | (q == at[1])).astype(jnp.int32)
    k, xr, yr = turn + (q == 3) - (q == 0), flip(0, 1), flip(0, 2)
    k = jnp.where(u == 0, 0, jnp.minimum(k, CHIPS_Z - 1))
    last = 4 * CHIPS_Z - 1
    xr = jnp.where(u == 0, 0, jnp.where(u == last, 1, xr))
    yr = jnp.where(u == 0, 0, jnp.where(u == last, 1, yr))
    inner = (z_here == 1) | (z_here == 2)
    near = jnp.where(inner, jnp.where(k == 3, 3, jnp.where(k == 2, 0, k + 1)), k)
    return jnp.where(z_here < 2, near, CHIPS_Z - 1 - near), xr, yr


def block_in_turn(u, place):
    z, xr, yr = chip_in_turn(u, place.at["z"])
    x = place.at["x"] + xr * (1 - 2 * place.at["x"])
    y = place.at["y"] + yr * (1 - 2 * place.at["y"])
    return (z * 2 + y) * 4 + x * 2


class BranchRows(Nothing):
    operands, results, rooms = 3, 1, 8

    def __init__(self, tok, slot_count, blocks, hidden, padded, width):
        self.tok, self.slot_count, self.hidden = tok, slot_count, hidden
        low = jnp.bfloat16
        self.chips = blocks // 2
        self.shapes = [jax.ShapeDtypeStruct((blocks * tok, width), low)]
        self.scratch = [
            pltpu.VMEM((padded, width), low),
            pltpu.VMEM((blocks, tok), jnp.int32),
            pltpu.VMEM((2, 2 * slot_count, padded), low),
            pltpu.VMEM((2 * slot_count, width), low),
            pltpu.VMEM((2, 2 * tok, width), low),
            pltpu.SemaphoreType.DMA((2,)),
            pltpu.SemaphoreType.DMA((2,)),
            pltpu.SemaphoreType.DMA((2,)),
        ]

    def whole(self, given, own):
        return [
            pltpu.make_async_copy(given[1], own[0].at[pl.ds(0, self.hidden)], own[5].at[0]),
            pltpu.make_async_copy(given[2], own[1], own[5].at[1]),
        ]

    def take(self, given, own, u):
        rows = pl.ds(pl.multiple_of(u * 2 * self.slot_count, 64), 2 * self.slot_count)
        return pltpu.make_async_copy(given[0].at[rows], own[2].at[u % 2], own[6].at[u % 2])

    def put(self, made, own, u):
        rows = pl.ds(block_in_turn(u, Place()) * self.tok, 2 * self.tok)
        return pltpu.make_async_copy(own[4].at[u % 2], made[0].at[rows], own[7].at[u % 2])

    def start(self, given, made, own):
        for copy in self.whole(given, own):
            copy.start()
        self.take(given, own, jnp.int32(0)).start()
        own[0][self.hidden :, :] = jnp.zeros_like(own[0][self.hidden :, :])
        return self.chips

    def run(self, given, made, own, first, last):
        if first == last:
            return
        if first == 0:
            for copy in self.whole(given, own):
                copy.wait()
        w_down, slots, acts, outs, placed = own[:5]

        @pl.loop(first, last)
        def _(u):
            s = u % 2

            @pl.when(u + 1 < self.chips)
            def _():
                self.take(given, own, u + 1).start()

            self.take(given, own, u).wait()

            @pl.when(u >= 2)
            def _():
                self.put(made, own, u - 2).wait()

            @pl.loop(0, outs.shape[1] // 256)
            def _(n):
                cols = pl.ds(pl.multiple_of(n * 256, 256), 256)
                outs[:, cols] = jnp.dot(
                    acts[s], w_down[:, cols], preferred_element_type=jnp.float32
                ).astype(jnp.bfloat16)

            block = block_in_turn(u, Place())
            for b in range(2):
                row = slots[pl.ds(block + b, 1), :]
                number = lax.broadcasted_iota(jnp.int32, (self.slot_count, self.tok), 0)
                table = (number == row).astype(jnp.float32).T.astype(jnp.bfloat16)
                placed[s, pl.ds(b * self.tok, self.tok), :] = jnp.dot(
                    table,
                    outs[pl.ds(b * self.slot_count, self.slot_count), :],
                    preferred_element_type=jnp.float32,
                ).astype(jnp.bfloat16)
            self.put(made, own, u).start()

    def end(self, given, made, own):
        for u in (self.chips - 2, self.chips - 1):
            self.put(made, own, jnp.int32(u)).wait()


def expert_slots(first, second, my_index):
    tok_rows = first.shape[1]
    chosen = ((first == my_index) | (second == my_index)).astype(jnp.float32)
    before = jnp.triu(jnp.ones((tok_rows, tok_rows), jnp.float32), 1)
    slots = jnp.where(chosen > 0, jnp.dot(chosen, before), -1.0).astype(jnp.int32)
    return slots, first + second - my_index


def feed_kernel(
    tok,
    slot_count,
    own_rows,
    cots_left,
    cots_right,
    gate_weight,
    up_weight,
    down_weight,
    router_rows,
    slots,
    others,
    everyone,
    dx_part,
    x_kept,
    g_kept,
    d_kept,
    a_kept,
    dgate,
    w_in,
    w_down,
    rows_buf,
    cots_buf,
    xs,
    gs,
    pre,
    back,
    ds,
    acts,
    dx_buf,
    dxs,
    send_sems,
    arrive_sems,
    own_sem,
    weight_sems,
    load_sems,
    keep_sems,
):
    place = Place()
    z_here = place.at["z"]
    hidden = gate_weight.shape[0]
    padded = w_down.shape[0]
    width, cut = own_rows.shape[1], cots_left.shape[1]
    half = tok // 2
    chips = 4 * CHIPS_Z
    pair = 2 * slot_count
    f32, low = jnp.float32, jnp.bfloat16

    loads = [
        pltpu.make_async_copy(gate_weight, w_in.at[pl.ds(0, hidden)], weight_sems.at[0]),
        pltpu.make_async_copy(
            router_rows, w_in.at[pl.ds(hidden, padded - hidden)], weight_sems.at[1]
        ),
        pltpu.make_async_copy(up_weight, w_in.at[pl.ds(padded, hidden)], weight_sems.at[2]),
        pltpu.make_async_copy(down_weight, w_down.at[pl.ds(0, hidden)], weight_sems.at[3]),
        pltpu.make_async_copy(
            own_rows, everyone.at[pl.ds(place.block("all", z_here, {}) * tok, tok)], own_sem
        ),
    ]
    for load in loads:
        load.start()
    w_in[padded + hidden :, :] = jnp.zeros((padded - hidden, width), low)
    w_down[hidden:, :] = jnp.zeros((padded - hidden, width), low)
    enter(place, "cxyz")

    def chip(u):
        return chip_in_turn(u, z_here)

    def first_block(u):
        return block_in_turn(u, place)

    def part(p, u, core):
        return everyone.at[pl.ds((first_block(u) + core) * tok + p * half, half)]

    def remote(source, target, number, mark, device):
        return pltpu.make_async_remote_copy(
            src_ref=source,
            dst_ref=target,
            send_sem=send_sems.at[number],
            recv_sem=arrive_sems.at[mark],
            device_id=device,
            device_id_type=MESH,
        )

    def routes(u, p):
        z, xr, yr = chip(u)
        plain = (xr + yr) == 0
        mark = (p * CHIPS_Z + z) * 8
        here = xr * 4 + yr * 2
        base = (u * 2 + p) * 5
        own = z == z_here
        right = plain & (z <= z_here) & (z_here < CHIPS_Z - 1)
        left = plain & (z >= z_here) & (z_here > 0)
        over_x = plain if p == 0 else xr == 0
        over_y = yr == 0 if p == 0 else plain
        return [
            (right, base, mark, place.along(1)),
            (left, base + 1, mark, place.along(-1)),
            (over_x, base + 2, mark + 4 + yr * 2, place.across("x")),
            (over_y, base + 3, mark + xr * 4 + 2, place.across("y")),
            (None, base + 4, mark + here + 1, place.across("c")),
        ]

    def hand_on(u, sources, pieces=(0, 1)):
        for p in pieces:
            for condition, number, mark, device in routes(u, p):
                target = part(p, u, place.at["c"])
                source = target if sources is None else sources[p]
                on(
                    condition,
                    lambda source=source, target=target, number=number, mark=mark, device=device: remote(
                        source, target, number, mark, device
                    ).start(),
                )

    def sibling_came(u):
        z, xr, yr = chip(u)
        for p in range(2):
            ref = part(p, u, 1 - place.at["c"])
            mark = (p * CHIPS_Z + z) * 8 + xr * 4 + yr * 2 + 1
            remote(ref, ref, 0, mark, place.across("c")).wait_recv()

    def take_in(u, p):
        z, xr, yr = chip(u)
        ref = part(p, u, place.at["c"])
        mark = (p * CHIPS_Z + z) * 8 + xr * 4 + yr * 2
        remote(ref, ref, 0, mark, place.across("c")).wait_recv()
        hand_on(u, None, (p,))

    def fetch(u):
        at = pl.ds(first_block(u) * tok, 2 * tok)
        return [
            pltpu.make_async_copy(everyone.at[at], rows_buf.at[u % 2], load_sems.at[u % 2, 0]),
            pltpu.make_async_copy(
                cots_left.at[at], cots_buf.at[u % 2, :, pl.ds(0, cut)], load_sems.at[u % 2, 1]
            ),
            pltpu.make_async_copy(
                cots_right.at[at],
                cots_buf.at[u % 2, :, pl.ds(cut, width - cut)],
                load_sems.at[u % 2, 2],
            ),
        ]

    def keep(u):
        rows = pl.ds(u * pair, pair)
        blocks = pl.ds(first_block(u) * tok, 2 * tok)
        s = u % 2
        return [
            pltpu.make_async_copy(xs.at[s], x_kept.at[rows], keep_sems.at[s, 0]),
            pltpu.make_async_copy(gs.at[s], g_kept.at[rows], keep_sems.at[s, 1]),
            pltpu.make_async_copy(ds.at[s], d_kept.at[rows], keep_sems.at[s, 2]),
            pltpu.make_async_copy(acts.at[s], a_kept.at[rows], keep_sems.at[s, 3]),
            pltpu.make_async_copy(dx_buf.at[s], dx_part.at[blocks], keep_sems.at[s, 4]),
        ]

    hand_on(0, [own_rows.at[pl.ds(0, half)], own_rows.at[pl.ds(half, half)]])
    loads[4].wait()
    sibling_came(0)
    for copy in fetch(0):
        copy.start()
    for p in range(2):
        take_in(1, p)
    for load in loads[:4]:
        load.wait()

    def compute(u):
        s = u % 2
        block = first_block(u)
        spread = []
        for b in range(2):
            row = slots[pl.ds(block + b, 1), :]
            table = lax.broadcasted_iota(jnp.int32, (slot_count, tok), 0) == row
            table = table.astype(f32)
            spread.append(table)
            at = pl.ds(b * slot_count, slot_count)
            from_rows = pl.ds(b * tok, tok)
            xs[s, at, :] = jnp.dot(
                table.astype(low), rows_buf[s, from_rows, :], preferred_element_type=f32
            ).astype(low)
            gs[s, at, :] = jnp.dot(
                table.astype(low), cots_buf[s, from_rows, :], preferred_element_type=f32
            ).astype(low)

        @pl.loop(0, 2 * padded // 256)
        def _(n):
            at = pl.ds(pl.multiple_of(n * 256, 256), 256)
            pre[:, at] = lax.dot_general(xs[s], w_in[at, :], ACROSS, preferred_element_type=f32)

        @pl.when(u + 2 < chips)
        def _():
            take_in(u + 2, 1)

        @pl.loop(0, padded // 256)
        def _(n):
            at = pl.ds(pl.multiple_of(n * 256, 256), 256)
            back[:, at] = lax.dot_general(gs[s], w_down[at, :], ACROSS, preferred_element_type=f32)

        for b in range(2):
            at = pl.ds(b * slot_count, slot_count)
            last = pre[at, padded - 128 : padded]
            column = lax.broadcasted_iota(jnp.int32, (slot_count, 128), 1) - (
                hidden - (padded - 128)
            )
            other = jnp.sum(
                spread[b] * others[pl.ds(block + b, 1), :].astype(f32), axis=1, keepdims=True
            )
            mine = jnp.sum(jnp.where(column == place.expert, last, 0.0), axis=1, keepdims=True)
            theirs = jnp.sum(
                jnp.where(column == other.astype(jnp.int32), last, 0.0), axis=1, keepdims=True
            )
            gate = 1.0 / (1.0 + jnp.exp(theirs - mine))
            inner = jnp.zeros((slot_count, 1), f32)
            for n in range(padded // 256):
                cols = pl.ds(n * 256, 256)
                pre_gate, pre_up = pre[at, cols], pre[at, pl.ds(padded + n * 256, 256)]
                dact = back[at, cols]
                sig = 1.0 / (1.0 + jnp.exp(-pre_gate))
                silu = pre_gate * sig
                act = silu * pre_up
                acts[s, at, cols] = (act * gate).astype(low)
                inner += jnp.sum(act * dact, axis=1, keepdims=True)
                dact = dact * gate
                ds[s, at, cols] = (dact * pre_up * sig * (1.0 + pre_gate * (1.0 - sig))).astype(low)
                ds[s, at, pl.ds(padded + n * 256, 256)] = (dact * silu).astype(low)
            dgate[pl.ds(block + b, 1), :] = jnp.sum(spread[b] * inner, axis=0, keepdims=True)

        @pl.loop(0, width // 256)
        def _(n):
            cols = pl.ds(pl.multiple_of(n * 256, 256), 256)
            dxs[:, cols] = jnp.dot(ds[s], w_in[:, cols], preferred_element_type=f32).astype(low)

        for b in range(2):
            at = pl.ds(b * slot_count, slot_count)
            back_table = spread[b].T.astype(low)
            to = pl.ds(b * tok, tok)
            dx_buf[s, to, :] = jnp.dot(
                back_table, dxs[at, :], preferred_element_type=f32
            ).astype(low)

    @pl.loop(0, chips)
    def _(u):
        @pl.when(u + 1 < chips)
        def _():
            sibling_came(u + 1)
            for copy in fetch(u + 1):
                copy.start()

        @pl.when(u + 2 < chips)
        def _():
            take_in(u + 2, 0)

        for copy in fetch(u):
            copy.wait()

        @pl.when(u >= 2)
        def _():
            for copy in keep(u - 2):
                copy.wait()

        compute(u)
        for copy in keep(u):
            copy.start()

    for u in (chips - 2, chips - 1):
        for copy in keep(jnp.int32(u)):
            copy.wait()

    @pl.loop(0, chips)
    def _(u):
        for p in range(2):
            for condition, number, mark, device in routes(u, p):
                ref = part(p, u, place.at["c"])
                on(
                    condition,
                    lambda ref=ref, number=number, mark=mark, device=device: remote(
                        ref, ref, number, mark, device
                    ).wait_send(),
                )


def feed(
    own_rows,
    cots_left,
    cots_right,
    gate_weight,
    up_weight,
    down_weight,
    router_rows,
    slots,
    others,
    slot_count,
):
    tok, width = own_rows.shape
    hidden = gate_weight.shape[0]
    padded = hidden + router_rows.shape[0]
    total = cots_left.shape[0]
    kept = total // tok * slot_count
    low = jnp.bfloat16
    hbm = pl.BlockSpec(memory_space=pltpu.HBM)
    vmem = pl.BlockSpec(memory_space=pltpu.VMEM)
    shape = jax.ShapeDtypeStruct
    pair = 2 * slot_count
    chips = 4 * CHIPS_Z
    return pl.pallas_call(
        functools.partial(feed_kernel, tok, slot_count),
        in_specs=[hbm] * 7 + [vmem] * 2,
        out_specs=[hbm] * 6 + [vmem],
        out_shape=[
            shape((total, width), low),
            shape((total, width), low),
            shape((kept, width), low),
            shape((kept, width), low),
            shape((kept, 2 * padded), low),
            shape((kept, padded), low),
            shape(slots.shape, jnp.float32),
        ],
        scratch_shapes=[
            pltpu.VMEM((2 * padded, width), low),
            pltpu.VMEM((padded, width), low),
            pltpu.VMEM((2, 2 * tok, width), low),
            pltpu.VMEM((2, 2 * tok, width), low),
            pltpu.VMEM((2, pair, width), low),
            pltpu.VMEM((2, pair, width), low),
            pltpu.VMEM((pair, 2 * padded), jnp.float32),
            pltpu.VMEM((pair, padded), jnp.float32),
            pltpu.VMEM((2, pair, 2 * padded), low),
            pltpu.VMEM((2, pair, padded), low),
            pltpu.VMEM((2, 2 * tok, width), low),
            pltpu.VMEM((pair, width), low),
            pltpu.SemaphoreType.DMA((10 * chips,)),
            pltpu.SemaphoreType.DMA((16 * CHIPS_Z,)),
            pltpu.SemaphoreType.DMA,
            pltpu.SemaphoreType.DMA((4,)),
            pltpu.SemaphoreType.DMA((2, 3)),
            pltpu.SemaphoreType.DMA((2, 6)),
        ],
        compiler_params=pltpu.CompilerParams(
            collective_id=3, has_side_effects=True, vmem_limit_bytes=60 * 2**20
        ),
        name="feed_forward",
    )(
        own_rows,
        cots_left,
        cots_right,
        gate_weight,
        up_weight,
        down_weight,
        router_rows,
        slots,
        others,
    )


def per_device_torus(
    tokens,
    cotangent,
    attention_routes,
    feedforward_routes,
    prefix_length,
    gain_attention,
    gain_feedforward,
    keyvalue_weight,
    router_weight,
    query_weight,
    output_weight,
    gate_weight,
    up_weight,
    down_weight,
):
    my_index = lax.axis_index("expert")
    group_size = lax.axis_size("expert")
    dp_size = lax.axis_size("dp")
    inputs = tokens[0].astype(jnp.float32)
    tok_rows, model_width = inputs.shape
    slot_count = 5 * 2 * tok_rows // (4 * group_size)
    query_width = HEADS * HEAD_DIM
    span = query_width // group_size
    low = jnp.bfloat16
    f32 = jnp.float32

    normed_attention, unit_attention, factor_attention = norm_parts(inputs, gain_attention)
    attention_in = normed_attention.astype(low)
    quarters = lambda order: tuple(
        (i * tok_rows // 4, tok_rows // 4, order) for i in range(4)
    )
    rows_in = keyvalue_weight.shape[0]
    route_shard = feedforward_routes[0].T.astype(low).reshape(-1, 128)
    early = model_width * 5 // 8
    router_shard = router_weight.T.reshape(-1, 128)
    whole = lambda a: ((0, a.shape[0], "zy"),)
    cut = rows_in * 13 // 16
    sequence_in, cots_left, every_route, router_full, in_weight, out_weight = gather_weights(
        [
            (attention_in, "expert", quarters("xc")),
            (cotangent[0, :, :early], "all", quarters("zyxc")),
            (route_shard, "dp", whole(route_shard)),
            (router_shard, "dp", whole(router_shard)),
        ],
        query_weight[0],
        keyvalue_weight,
        output_weight[0],
        ((0, cut, "zy"), (cut, rows_in - cut, "yz")),
        1,
    )
    cots_late, sequence_in = lax.optimization_barrier((cotangent[0, :, early:], sequence_in))
    cots_right = lax.all_gather(cots_late, ("dp", "expert"), axis=0, tiled=True)
    every_route = every_route.reshape(dp_size, 2, group_size, tok_rows).astype(jnp.int32)
    router_full = (
        router_full.reshape(dp_size, 2 * group_size, rows_in)
        .transpose(0, 2, 1)
        .reshape(-1, 2 * group_size)
    )
    attention_cols = router_full[:, :group_size]
    feedforward_cols = router_full[:, group_size:]
    projected = jnp.dot(sequence_in, in_weight, preferred_element_type=f32).astype(low)
    attend_matches_all = expert_matches(attention_routes[0], group_size)
    attend_logits = jnp.dot(sequence_in, attention_cols, preferred_element_type=f32)
    attend_weights_all, _ = pair_gates(attend_logits, attend_matches_all)
    reach = jnp.broadcast_to(prefix_length.astype(f32)[None], (attend_logits.shape[0], 1))
    side = jnp.concatenate([attention_routes[0].astype(f32), attend_weights_all, reach], axis=1)
    side = jnp.pad(side, ((0, 0), (0, 128 - side.shape[1])))
    mixed, log_total = attention(projected, side, prefix_length, group_size, tok_rows)
    attend_part = jnp.dot(mixed, out_weight, preferred_element_type=f32).astype(low)
    attended = scatter(attend_part, "expert", quarters("cx"), 2, "sum_attention")
    hidden = inputs + attended
    normed_feed, unit_feed, factor_feed = norm_parts(hidden, gain_feedforward)
    feed_in = normed_feed.astype(low)
    everywhere = lambda a, b: ((0, tok_rows // 2, a), (tok_rows // 2, tok_rows // 2, b))
    mine = lambda a: lax.dynamic_slice_in_dim(a, my_index * tok_rows, tok_rows, 0)
    feed_matches = expert_matches(mine(feedforward_routes[0]), group_size)
    feed_logits = jnp.dot(feed_in, feedforward_cols, preferred_element_type=f32)
    feed_weights, _ = pair_gates(feed_logits, feed_matches)
    slots, others = expert_slots(
        every_route[:, 0].reshape(-1, tok_rows), every_route[:, 1].reshape(-1, tok_rows), my_index
    )
    hidden_rows = gate_weight.shape[1]
    padded = -(-hidden_rows // 256) * 256
    router_rows = jnp.pad(
        feedforward_cols.T, ((0, padded - hidden_rows - group_size), (0, 0))
    )
    _, dx_part, kept_rows, kept_cots, kept_back, kept_act, token_dgate = feed(
        feed_in,
        cots_left,
        cots_right,
        gate_weight[0],
        up_weight[0],
        down_weight[0],
        router_rows,
        slots,
        others,
        slot_count,
    )
    own_row = (jnp.arange(group_size) == my_index).astype(f32)[None, :, None]
    feed_dgate = lax.psum_scatter(
        (token_dgate[:, None, :] * own_row).reshape(-1, tok_rows),
        ("dp", "expert"),
        scatter_dimension=0,
        tiled=True,
    ).T
    feed_home, grad_gate, grad_up, grad_down = scatter(
        dx_part,
        "all",
        everywhere("cxyz", "cyxz"),
        4,
        "sum_rows",
        WeightGrads(kept_rows.shape[0], padded, hidden_rows, model_width),
        (kept_back, kept_rows, kept_act, kept_cots),
    )
    gradient = cotangent[0].astype(f32)
    feed_dlogits = gates_back(feed_dgate, feed_weights, feed_matches)
    feed_dnorm = feed_home + jnp.dot(feed_dlogits, feedforward_cols.astype(f32).T, precision=HIGH)
    grad_gain_feed = jnp.sum(feed_dnorm * unit_feed, axis=0)
    hidden_grad = gradient + norm_back(feed_dnorm, gain_feedforward, unit_feed, factor_feed)

    sequence_grad, out_part = gather(
        [(hidden_grad.astype(low), "expert", quarters("xc"))],
        5,
        "gather_cotangents",
        BranchRows(tok_rows, slot_count, slots.shape[0], hidden_rows, padded, model_width),
        (kept_act, down_weight[0], slots),
    )
    dmix = lax.dot_general(sequence_grad, out_weight, ACROSS, preferred_element_type=f32).astype(low)
    length, total = projected.shape
    columns = model_width // 2
    first_sum, dprojected, gate_parts, grad_out = scatter(
        out_part,
        "all",
        everywhere("cxyz", "cyxz"),
        7,
        "sum_output_left",
        InTurn(
            AttentionBack(length, total, group_size, tok_rows),
            LowGrad(length, query_width, model_width, 4),
        ),
        (projected, side, log_total, dmix, mixed, sequence_grad),
        (0, columns),
    )
    second_sum, attend_dx = scatter(
        out_part,
        "all",
        everywhere("cxyz", "cyxz"),
        8,
        "sum_output_right",
        RowGrads(length, total, model_width),
        (dprojected, in_weight, gate_parts),
        (columns, model_width - columns),
    )
    attend_home, out_rows, grad_in = sum_with_output(
        attend_dx,
        quarters("cx"),
        grad_out,
        ((0, rows_in, "yz"),),
        9,
        LowGrad(length, model_width, total, 4),
        (sequence_in, dprojected),
    )
    pair_dgate = attend_home[:, model_width : model_width + 2]
    attend_home = attend_home[:, :model_width]
    layer_output = hidden + jnp.concatenate([first_sum, second_sum], axis=1)
    matches = mine(attend_matches_all)
    weights = mine(attend_weights_all)
    dselected = weights * (pair_dgate - jnp.sum(weights * pair_dgate, axis=1, keepdims=True))
    attend_dlogits = jnp.sum(dselected[:, :, None] * matches, axis=1)
    attend_dnorm = attend_home + jnp.dot(
        attend_dlogits, attention_cols.astype(f32).T, precision=HIGH
    )
    grad_gain_attend = jnp.sum(attend_dnorm * unit_attention, axis=0)
    grad_tokens = hidden_grad + norm_back(
        attend_dnorm, gain_attention, unit_attention, factor_attention
    )
    small = jnp.concatenate(
        [
            lax.dot_general(attend_dlogits, attention_in.astype(f32), DOWNWARD, precision=HIGH),
            lax.dot_general(feed_dlogits, feed_in.astype(f32), DOWNWARD, precision=HIGH),
            grad_gain_attend[None],
            grad_gain_feed[None],
        ],
        axis=0,
    )
    small = lax.psum(small.astype(f32), ("dp", "expert"))
    small = lax.dynamic_slice_in_dim(small, lax.axis_index("dp") * rows_in, rows_in, 1)

    grad_query, grad_keyvalue, grad_projection = sum_weights(
        grad_in, out_rows, ((0, rows_in, "yz"),), 6
    )
    return (
        layer_output.astype(low)[None],
        grad_tokens[None],
        small[2 * group_size],
        small[2 * group_size + 1],
        grad_keyvalue,
        small[: 2 * group_size].T,
        grad_query[None],
        grad_projection[None],
        grad_gate[None],
        grad_up[None],
        grad_down[None],
    )


def solution(mesh):
    in_specs = (
        P("dp", "expert", None),
        P("dp", "expert", None),
        P("dp", None, None),
        P("dp", None, None),
        P("dp"),
        P(),
        P(),
        P("dp", None),
        P("dp", None),
        P("expert", "dp", None),
        P("expert", "dp", None),
        P("expert", "dp", None),
        P("expert", "dp", None),
        P("expert", "dp", None),
    )
    out_specs = (
        P("dp", "expert", None),
        P("dp", "expert", None),
        P("dp"),
        P("dp"),
        P("dp", None),
        P("dp", None),
        P("expert", "dp", None),
        P("expert", "dp", None),
        P("expert", "dp", None),
        P("expert", "dp", None),
        P("expert", "dp", None),
    )
    torus = (mesh.shape["dp"], mesh.shape["expert"]) == (8, 4)
    body = per_device_torus if torus else per_device
    return jax.shard_map(
        body, mesh=mesh, in_specs=in_specs, out_specs=out_specs, check_vma=False
    )
```
